32 devices in a mesh: shard: 4 (over y, x), head: 4 (over z), tensor: 2 (over core).
Axes of the slice: x: 2, y: 2, z: 4, core: 2. Of those that a mesh axis runs over, the one named last changes fastest.
Arguments:
- tokens: bfloat16 [1152, 4, 2048], P(None, 'shard', ('head', 'tensor')), may hold values from -6 to 6
- seq_lengths: int32 [16], replicated, may hold values from 1 to 1024, as said below
- dealing: int32 [16], replicated, may hold values from 0 to 15, as said below
- gain_mixer: float32 [2048], replicated, may hold values from 0.5 to 1.5
- w_query: bfloat16 [2048, 2048], P('shard', ('head', 'tensor')), may hold values from -0.125 to 0.125
- w_key: bfloat16 [2048, 2048], P('shard', ('head', 'tensor')), may hold values from -0.125 to 0.125
- w_value: bfloat16 [2048, 2048], P('shard', ('head', 'tensor')), may hold values from -0.125 to 0.125
- w_gate: bfloat16 [2048, 2048], P('shard', ('head', 'tensor')), may hold values from -0.125 to 0.125
- w_beta: bfloat16 [2048, 16], P('shard', ('head', 'tensor')), may hold values from -0.125 to 0.125
- conv_weight: float32 [4, 3, 2048], P(None, None, ('head', 'tensor')), may hold values from -3 to 3
- gain_heads: float32 [128], replicated, may hold values from 0.5 to 1.5
- w_out: bfloat16 [2048, 2048], P(('head', 'tensor'), 'shard'), may hold values from -0.25 to 0.25
- gain_ffn: float32 [2048], replicated, may hold values from 0.5 to 1.5
- w_up_gate: bfloat16 [2048, 5632], P('shard', ('head', 'tensor')), may hold values from -0.125 to 0.125
- w_up: bfloat16 [2048, 5632], P('shard', ('head', 'tensor')), may hold values from -0.125 to 0.125
- w_down: bfloat16 [5632, 2048], P(('head', 'tensor'), 'shard'), may hold values from -0.15625 to 0.15625
- cotangent: bfloat16 [5120, 2048], P('shard', ('head', 'tensor')), may hold values from -6 to 6
Outputs:
- block_out: bfloat16 [5120, 2048], P('shard', ('head', 'tensor'))
- d_tokens: float32 [1152, 4, 2048], P(None, 'shard', ('head', 'tensor'))
- d_gain_mixer: float32 [2048], replicated
- d_w_query: float32 [2048, 2048], P('shard', ('head', 'tensor'))
- d_w_key: float32 [2048, 2048], P('shard', ('head', 'tensor'))
- d_w_value: float32 [2048, 2048], P('shard', ('head', 'tensor'))
- d_w_gate: float32 [2048, 2048], P('shard', ('head', 'tensor'))
- d_w_beta: float32 [2048, 16], P('shard', ('head', 'tensor'))
- d_conv_weight: float32 [4, 3, 2048], replicated
- d_gain_heads: float32 [128], replicated
- d_w_out: float32 [2048, 2048], P(('head', 'tensor'), 'shard')
- d_gain_ffn: float32 [2048], replicated
- d_w_up_gate: float32 [2048, 5632], P('shard', ('head', 'tensor'))
- d_w_up: float32 [2048, 5632], P('shard', ('head', 'tensor'))
- d_w_down: float32 [5632, 2048], P(('head', 'tensor'), 'shard')
The draws below stay inside these ranges and needn't reach their ends.
Inputs may be any that keep to these rules, and one draw needn't show every extreme that they name: `seq_lengths`: the sequences at dealt positions 4 g to 4 g + 3 have lengths that sum to 1152; rounded up to multiples of 64 they sum to at most 1280, which some group reaches; some sequence has 1024 tokens. `dealing`: a permutation of the 16 sequence numbers.
All inputs are finite; a program needn't handle non-finite values.
Results may differ from the reference program's by a relative error of at most 0.015.
Values may be sent and summed in bfloat16 or wider, within the bound.
A program may use at most 256 MiB of HBM per device.

```python
import jax
import jax.numpy as jnp
from jax import lax

D = 2048
H = 16
HD = 128
FF = 5632
CONV = 4
BLOCK = 64
SEQ_DEV = 4
REAL_DEV = 1152
CAP = 1280
NSEQ = 16
TOKENS = 4608
N_SHARD = 4


def deal_plan(key):
    base = jax.random.fold_in(key, 1234)
    keys = jax.random.split(base, 6)
    groups = NSEQ // SEQ_DEV
    spare = REAL_DEV // BLOCK - SEQ_DEV
    units = jax.random.randint(keys[0], (groups, spare), 0, SEQ_DEV)
    counts = 1 + jnp.sum((units[:, :, None] == jnp.arange(SEQ_DEV)[None, None, :]).astype(jnp.int32), axis=1)
    lift_one = jax.random.randint(keys[1], (groups,), 1 - BLOCK, BLOCK)
    lift_two = jax.random.randint(keys[2], (groups,), 1 - BLOCK, BLOCK)
    lens = counts * BLOCK + jnp.stack([lift_one, -lift_one, lift_two, -lift_two], axis=1)
    first = jax.random.randint(keys[3], (), 0, groups)
    second = (first + 1 + jax.random.randint(keys[4], (), 0, groups - 1)) % groups
    longest = jnp.array([16 * BLOCK, BLOCK, BLOCK // 2, BLOCK - BLOCK // 2], jnp.int32)
    fullest = jnp.array([15 * BLOCK + 1, BLOCK + 1, BLOCK - 1, BLOCK - 1], jnp.int32)
    group_ids = jnp.arange(groups)[:, None]
    lens = jnp.where(group_ids == first, longest[None, :], jnp.where(group_ids == second, fullest[None, :], lens))
    dealt = lens.reshape(-1).astype(jnp.int32)
    order = jax.random.permutation(keys[5], groups * SEQ_DEV).astype(jnp.int32)
    natural = jnp.zeros((groups * SEQ_DEV,), jnp.int32).at[order].set(dealt)
    return (natural, order)


def draw_seq_lengths(key, part):
    return deal_plan(key)[0]


def draw_dealing(key, part):
    return deal_plan(key)[1]


def block_scale(rng, extent, shards, smallest, top_value):
    def one(axis_at, blocks):
        draws = jax.random.uniform(jax.random.fold_in(jax.random.fold_in(rng, 6), axis_at), (blocks,), jnp.float32, smallest / len(shards), top_value / len(shards))
        return jnp.repeat(jnp.exp(draws), extent[axis_at] // blocks).reshape((-1,) + (1,) * (len(extent) - axis_at - 1))

    level = one(*shards[0])
    for cut in shards[1:]:
        level = level * one(*cut)
    return level


def bell_draw(own_key, shape, scale, reach, pieces=(), held_as=jnp.bfloat16):
    loudness = block_scale(own_key, shape, pieces, -0.22, 0.18) if pieces else 1.0
    values = jax.random.normal(own_key, shape, jnp.float32) * scale * loudness
    return jnp.minimum(jnp.maximum(values, -reach), reach).astype(held_as)


def setup_inputs(seed: int = 0) -> dict:
    key_list = jax.random.split(jax.random.key(seed), 18)
    tokens = bell_draw(key_list[0], (REAL_DEV, N_SHARD, D), 1.0, 6.0, ((1, 4), (2, 8)))
    seq_lengths = draw_seq_lengths(jax.random.fold_in(key_list[17], 71), 0)
    dealing = draw_dealing(jax.random.fold_in(key_list[17], 71), 0)
    gain_mixer = jnp.clip(1.0 + 0.1 * jax.random.normal(key_list[3], (D,), jnp.float32), 0.5, 1.5)
    w_query = bell_draw(key_list[4], (D, D), D ** -0.5, 0.125, ((0, 4), (1, 8)))
    w_key = bell_draw(key_list[5], (D, D), D ** -0.5, 0.125, ((0, 4), (1, 8)))
    w_value = bell_draw(key_list[6], (D, D), D ** -0.5, 0.125, ((0, 4), (1, 8)))
    w_gate = bell_draw(key_list[7], (D, D), D ** -0.5, 0.125, ((0, 4), (1, 8)))
    w_beta = bell_draw(key_list[8], (D, H), D ** -0.5, 0.125, ((0, 4), (1, 8)))
    conv_weight = bell_draw(key_list[9], (CONV, 3, D), 0.5, 3.0, ((2, 8),), jnp.float32)
    gain_heads = jnp.clip(1.0 + 0.1 * jax.random.normal(key_list[10], (HD,), jnp.float32), 0.5, 1.5)
    w_out = bell_draw(key_list[11], (D, D), (D // 4) ** -0.5, 0.25, ((0, 8), (1, 4)))
    gain_ffn = jnp.clip(1.0 + 0.1 * jax.random.normal(key_list[12], (D,), jnp.float32), 0.5, 1.5)
    w_up_gate = bell_draw(key_list[13], (D, FF), D ** -0.5, 0.125, ((0, 4), (1, 8)))
    w_up = bell_draw(key_list[14], (D, FF), D ** -0.5, 0.125, ((0, 4), (1, 8)))
    w_down = bell_draw(key_list[15], (FF, D), (FF // 4) ** -0.5, 0.15625, ((0, 8), (1, 4)))
    cotangent = bell_draw(key_list[16], (N_SHARD * CAP, D), 1.0, 6.0, ((0, 4), (1, 8)))
    return dict(tokens=tokens, seq_lengths=seq_lengths, dealing=dealing, gain_mixer=gain_mixer, w_query=w_query, w_key=w_key, w_value=w_value, w_gate=w_gate, w_beta=w_beta, conv_weight=conv_weight, gain_heads=gain_heads, w_out=w_out, gain_ffn=gain_ffn, w_up_gate=w_up_gate, w_up=w_up, w_down=w_down, cotangent=cotangent)


EPSILON = 1e-06
HEAD_FLOOR = 0.01
HIGHEST = lax.Precision.HIGHEST

@jax.custom_vjp
def low(v):
    return lax.optimization_barrier(v.astype(jnp.bfloat16)).astype(jnp.float32)

@jax.custom_vjp
def low_back(v):
    return v

def low_keep(v):
    return (low(v), None)

def low_pass(kept, grad):
    return (grad,)

def back_keep(v):
    return (v, None)

def back_low(kept, grad):
    return (low(grad),)
low.defvjp(low_keep, low_pass)
low_back.defvjp(back_keep, back_low)

def int_sum(values, along_axis):
    return lax.optimization_barrier(jnp.sum(values, axis=along_axis)).astype(jnp.int32)

def layout(seq_lengths, dealing, group_idx):
    total_seqs = seq_lengths.shape[0]
    lengths = seq_lengths.astype(jnp.int32)
    starts = (jnp.cumsum(lengths, dtype=jnp.int32) - lengths).astype(jnp.int32)
    chosen = lax.dynamic_slice_in_dim(dealing.astype(jnp.int32), (group_idx * SEQ_DEV).astype(jnp.int32), SEQ_DEV)
    picked = (chosen[:, None] == jnp.arange(total_seqs, dtype=jnp.int32)[None, :]).astype(jnp.int32)
    own_length = int_sum(picked * lengths[None, :], 1)
    own_start = int_sum(picked * starts[None, :], 1)
    padded = (own_length + BLOCK - 1) // BLOCK * BLOCK
    buffer_start = (jnp.cumsum(padded, dtype=jnp.int32) - padded).astype(jnp.int32)
    row_ids = jnp.arange(CAP, dtype=jnp.int32)
    member = int_sum((row_ids[:, None] >= buffer_start[None, :]).astype(jnp.int32), 1) - 1
    owned_by = (member[:, None] == jnp.arange(SEQ_DEV, dtype=jnp.int32)[None, :]).astype(jnp.int32)
    position = row_ids - int_sum(owned_by * buffer_start[None, :], 1)
    row_length = int_sum(owned_by * own_length[None, :], 1)
    seq_first = int_sum(owned_by * own_start[None, :], 1)
    filled = position < row_length
    return (seq_first + position, position, filled, seq_first, own_start, own_length)

def matmul(left, right):
    return jnp.dot(left, right, precision=HIGHEST)

def short_conv(stacked, weight, position):
    summed = weight[0][None] * stacked
    for offset in range(1, CONV):
        shifted = jnp.concatenate([jnp.zeros((offset,) + stacked.shape[1:], jnp.float32), stacked[:-offset]], axis=0)
        summed = summed + weight[offset][None] * shifted * (position >= offset).astype(jnp.float32)[:, None, None]
    return summed

def delta_rule(queries, key_rows, value_rows, beta_rows, persist):
    row_count, head_count, head_size = queries.shape
    blocks = row_count // BLOCK

    def to_blocks(values):
        return values.reshape(blocks, BLOCK, head_count, -1).transpose(0, 2, 1, 3)
    q_blk = to_blocks(queries)
    k_blk = to_blocks(key_rows)
    v_blk = to_blocks(value_rows)
    b_blk = to_blocks(beta_rows[..., None])
    key_grams = jnp.einsum('nhid,nhjd->nhij', k_blk, k_blk, precision=HIGHEST)
    strict = jnp.tril(jnp.ones((BLOCK, BLOCK), jnp.float32), -1)
    lower_incl = jnp.tril(jnp.ones((BLOCK, BLOCK), jnp.float32))
    identity = jnp.eye(BLOCK, dtype=jnp.float32)
    system = identity + strict * (b_blk * key_grams)
    inverse = lax.linalg.triangular_solve(system, jnp.broadcast_to(identity, system.shape), left_side=True, lower=True, unit_diagonal=True)
    w_blk = jnp.einsum('nhij,nhjd->nhid', inverse, b_blk * k_blk, precision=HIGHEST)
    u_blk = jnp.einsum('nhij,nhjd->nhid', inverse, b_blk * v_blk, precision=HIGHEST)
    scores = jnp.einsum('nhid,nhjd->nhij', q_blk, k_blk, precision=HIGHEST) * lower_incl

    def advance(memory, inputs):
        q_part, k_part, w_part, u_part, s_part, p_part = inputs
        memory = memory * p_part
        fresh_vals = u_part - jnp.einsum('hid,hde->hie', w_part, memory, precision=HIGHEST)
        output = jnp.einsum('hid,hde->hie', q_part, memory, precision=HIGHEST) + jnp.einsum('hij,hje->hie', s_part, fresh_vals, precision=HIGHEST)
        memory = memory + jnp.einsum('hid,hie->hde', k_part, fresh_vals, precision=HIGHEST)
        return (memory, output)
    start_mem = jnp.zeros((head_count, head_size, head_size), jnp.float32)
    _, outputs = lax.scan(advance, start_mem, (q_blk, k_blk, w_blk, u_blk, scores, persist))
    return outputs.transpose(0, 2, 1, 3).reshape(row_count, head_count, head_size)

def mixer_piece(q_in, k_in, v_in, g_in, b_in, conv_in, gain_in, position, filled_f, persist):
    row_count = q_in.shape[0]
    head_count = q_in.shape[1] // HD
    stacked = jnp.stack([q_in, k_in, v_in], axis=1)
    active = jax.nn.silu(short_conv(stacked, conv_in, position)) * filled_f[:, None, None]

    def unit_norm(values):
        values = values.reshape(row_count, head_count, HD)
        return values * lax.rsqrt(lax.optimization_barrier(jnp.sum(values * values, axis=2, keepdims=True)) + EPSILON)
    queries = unit_norm(active[:, 0])
    key_rows = unit_norm(active[:, 1])
    value_rows = active[:, 2].reshape(row_count, head_count, HD)
    beta_rows = jax.nn.sigmoid(b_in)
    core_out = delta_rule(queries, key_rows, value_rows, beta_rows, persist)
    normal = core_out * lax.rsqrt(jnp.maximum(lax.optimization_barrier(jnp.mean(core_out * core_out, axis=2, keepdims=True)), HEAD_FLOOR)) * gain_in
    gate_rows = jax.nn.silu(g_in.reshape(row_count, head_count, HD))
    return (normal * gate_rows).reshape(row_count, head_count * HD)

def residual_block(params, dealt_rows, position, filled):
    gain_mixer, w_query, w_key, w_value, w_gate, w_beta, conv_weight, gain_heads, w_out, gain_ffn, w_up_gate, w_up, w_down = params
    filled_f = filled.astype(jnp.float32)
    persist = (position.reshape(-1, BLOCK)[:, 0] != 0).astype(jnp.float32)
    scale_one = lax.rsqrt(lax.optimization_barrier(jnp.mean(dealt_rows * dealt_rows, axis=1, keepdims=True)) + EPSILON)
    normed = low(dealt_rows * scale_one * gain_mixer)
    q_pre = low_back(matmul(normed, w_query))
    k_pre = low_back(matmul(normed, w_key))
    v_pre = low_back(matmul(normed, w_value))
    g_pre = low_back(matmul(normed, w_gate))
    beta_pre = matmul(normed, w_beta)
    mixed = low(mixer_piece(q_pre, k_pre, v_pre, g_pre, beta_pre, conv_weight, gain_heads, position, filled_f, persist))
    branch = low_back(matmul(mixed, w_out))
    hidden = dealt_rows + branch
    held_low = low(hidden)
    scale_two = lax.rsqrt(lax.optimization_barrier(jnp.mean(held_low * held_low, axis=1, keepdims=True)) + EPSILON)
    normed_two = low(held_low * scale_two * gain_ffn)
    gate_act = low_back(matmul(normed_two, w_up_gate))
    up_act = low_back(matmul(normed_two, w_up))
    product = low(jax.nn.silu(gate_act) * up_act)
    return hidden + matmul(product, w_down)

def reference(tokens, seq_lengths, dealing, gain_mixer, w_query, w_key, w_value, w_gate, w_beta, conv_weight, gain_heads, w_out, gain_ffn, w_up_gate, w_up, w_down, cotangent):
    group_ids = jnp.arange(N_SHARD, dtype=jnp.int32)
    plans = jax.vmap(lambda group_idx: layout(seq_lengths, dealing, group_idx))(group_ids)
    natural, position, filled = (plans[0], plans[1], plans[2])
    source_rows = jnp.where(filled, natural, 0).astype(jnp.int32)
    packed = tokens.astype(jnp.float32).reshape(TOKENS, D)
    params = tuple((weight_arr.astype(jnp.float32) for weight_arr in (gain_mixer, w_query, w_key, w_value, w_gate, w_beta, conv_weight, gain_heads, w_out, gain_ffn, w_up_gate, w_up, w_down)))

    def forward(packed_in, params_in):
        dealt_rows = jnp.where(filled[:, :, None], packed_in[source_rows], 0.0)
        step_fn = jax.checkpoint(residual_block)

        def per_group(carried, inputs):
            group_rows, group_pos, group_fill = inputs
            return (carried, step_fn(params_in, group_rows, group_pos, group_fill))
        _, outputs = lax.scan(per_group, jnp.zeros((), jnp.float32), (dealt_rows, position, filled))
        return outputs.reshape(N_SHARD * CAP, D)
    result, pullback = jax.vjp(forward, packed, params)
    d_packed, d_params = pullback(cotangent.astype(jnp.float32))
    return (result.astype(jnp.bfloat16), d_packed.reshape(REAL_DEV, N_SHARD, D), d_params[0], d_params[1], d_params[2], d_params[3], d_params[4], d_params[5], d_params[6], d_params[7], d_params[8], d_params[9], d_params[10], d_params[11], d_params[12])
```

```python
import functools
import jax
import jax.numpy as jnp
from jax import lax
from jax.experimental import pallas as pl
from jax.experimental.pallas import tpu as pltpu

from jax.sharding import PartitionSpec as P

D = 2048
HD = 128
CONV = 4
BLOCK = 64
SEQ_DEV = 4
REAL_DEV = 1152
CAP = 1280
NB = CAP // BLOCK
EPSILON = 1e-06
HEAD_FLOOR = 0.01
F32 = jnp.float32
BF = jnp.bfloat16

def split(x):
    hi = x.astype(BF)
    return hi, (x - hi.astype(F32)).astype(BF)

NN=(((1,),(0,)),((),())); NT=(((1,),(1,)),((),())); TN=(((0,),(0,)),((),()))

def dg(a, b, dims):
    return lax.dot_general(a, b, dims, preferred_element_type=F32)

def d3(a, b, dims=NN):
    ah, al = split(a); bh, bl = split(b)
    return dg(ah, bh, dims) + (dg(ah, bl, dims) + dg(al, bh, dims))

def masks():
    ri = lax.broadcasted_iota(jnp.int32, (BLOCK, BLOCK), 0)
    ci = lax.broadcasted_iota(jnp.int32, (BLOCK, BLOCK), 1)
    return ri, ci

def sigmoid(x):
    return 1.0 / (1.0 + jnp.exp(-x))

def conv_rows(cur, tail, wt, pos):
    ext = jnp.concatenate([tail, cur], axis=0)
    out = wt[0] * cur
    for j in range(1, CONV):
        sh = pltpu.roll(ext, j, axis=0)[8:]
        out = out + wt[j] * jnp.where(pos >= j, sh, 0.0)
    return out

def inverses(lmats, ri, ci):
    apart = ri ^ ci
    xs = [jnp.where(apart == 0, 1.0, 0.0) - jnp.where(apart == 1, m, 0.0) for m in lmats]
    s = 2
    while s < BLOCK:
        at = (apart >= s) & (apart < 2 * s)
        ys = [d3(x, jnp.where(at, m, 0.0)) for x, m in zip(xs, lmats)]
        xs = [x - d3(y, x) for x, y in zip(xs, ys)]
        s *= 2
    return xs

def fwd_kernel(persist, pre, pos_ref, fill_ref, cw, gain, mixed, c_out, qk, w_out, u_out, u2_out, o_out, p_out, t_out, m_out, s_out, b_s):
    ri, ci = masks()
    heads = 2
    def phase_a(n, tails):
        r = pl.ds(pl.multiple_of(n * BLOCK, BLOCK), BLOCK)
        pos = pos_ref[r, :]; fil = fill_ref[r, :]
        new_tails = []
        acts = []
        for i in range(3):
            cur = pre[r, i*256:(i+1)*256]
            wt = [cw[j*3+i:j*3+i+1, :] for j in range(CONV)]
            cc = conv_rows(cur, tails[i], wt, pos)
            c_out[r, i*256:(i+1)*256] = cc
            acts.append(cc * sigmoid(cc) * fil)
            new_tails.append(cur[BLOCK-8:])
        beta = sigmoid(pre[r, 1024:1152])
        for h in range(heads):
            hs = slice(h*HD, (h+1)*HD)
            yq = acts[0][:, hs]; yk = acts[1][:, hs]; v = acts[2][:, hs]
            q = yq * lax.rsqrt(jnp.sum(yq*yq, axis=1, keepdims=True) + EPSILON)
            k = yk * lax.rsqrt(jnp.sum(yk*yk, axis=1, keepdims=True) + EPSILON)
            b = beta[:, h:h+1]
            qk[r, h*HD:(h+1)*HD] = q
            qk[r, 256+h*HD:256+(h+1)*HD] = k
            lmat = jnp.where(ri > ci, b * d3(k, k, NT), 0.0)
            p_out[n*2+h] = jnp.where(ri >= ci, d3(q, k, NT), 0.0)
            t_out[n*2+h] = lmat
            u_out[r, hs] = b*v
            w_out[r, hs] = b*k
        return tuple(new_tails)
    z8 = jnp.zeros((8, 256), F32)
    lax.fori_loop(0, NB, phase_a, (z8, z8, z8))
    GRP = 8
    def phase_t(i, _):
        ts = inverses([t_out[i*GRP+j] for j in range(GRP)], ri, ci)
        for j in range(GRP):
            t_out[i*GRP+j] = ts[j]
        return 0
    lax.fori_loop(0, 2*NB//GRP, phase_t, 0)
    def phase_w(i, _):
        for jj in range(2):
            n = i*2+jj
            r = pl.ds(pl.multiple_of(n * BLOCK, BLOCK), BLOCK)
            for h in range(heads):
                hs = slice(h*HD, (h+1)*HD)
                e = n*2+h
                wu = d3(t_out[e], jnp.concatenate([w_out[r, hs], u_out[r, hs]], axis=1))
                mb = d3(qk[r, 256+h*HD:256+(h+1)*HD], wu, TN)
                w_out[r, hs] = wu[:, :HD]; u_out[r, hs] = wu[:, HD:]
                m_out[e] = mb[:, :HD]; b_s[e] = mb[:, HD:]
        return 0
    lax.fori_loop(0, NB//2, phase_w, 0)
    def phase_b(n, ss):
        out = []
        for h in range(heads):
            e = n*2+h
            s = ss[h] * persist[n]
            s_out[e] = s
            out.append(s - d3(m_out[e], s) + b_s[e])
        return tuple(out)
    zs = jnp.zeros((HD, HD), F32)
    lax.fori_loop(0, NB, phase_b, (zs, zs))
    def phase_c(n, _):
        r = pl.ds(pl.multiple_of(n * BLOCK, BLOCK), BLOCK)
        for h in range(heads):
            hs = slice(h*HD, (h+1)*HD)
            e = n*2+h
            wq = jnp.concatenate([w_out[r, hs], qk[r, hs]], axis=0)
            rr = d3(wq, s_out[e])
            u2 = u_out[r, hs] - rr[:BLOCK]
            o = rr[BLOCK:] + d3(p_out[e], u2)
            u2_out[r, hs] = u2
            o_out[r, hs] = o
            ms = jnp.mean(o*o, axis=1, keepdims=True)
            sc = lax.rsqrt(jnp.maximum(ms, HEAD_FLOOR))
            gg = pre[r, 768+h*HD:768+(h+1)*HD]
            mixed[r, hs] = (o * sc * gain[...] * (gg * sigmoid(gg))).astype(BF)
        return 0
    lax.fori_loop(0, NB, phase_c, 0)

def sds(*s, dt=F32): return jax.ShapeDtypeStruct(s, dt)
VM = pl.BlockSpec(memory_space=pltpu.VMEM)
SM = pl.BlockSpec(memory_space=pltpu.SMEM)

def mixer_fwd(persist, pre, pos, fil, cw, gain):
    outs = (sds(CAP,256,dt=BF), sds(CAP,768), sds(CAP,512), sds(CAP,256), sds(CAP,256), sds(CAP,256), sds(CAP,256),
            sds(2*NB,BLOCK,BLOCK), sds(2*NB,BLOCK,BLOCK), sds(2*NB,HD,HD), sds(2*NB,HD,HD))
    return pl.pallas_call(fwd_kernel, out_shape=outs, in_specs=[SM]+[VM]*5, out_specs=[VM]*len(outs),
        scratch_shapes=[pltpu.VMEM((2*NB,HD,HD),F32)],
        compiler_params=pltpu.CompilerParams(vmem_limit_bytes=56*2**20), cost_estimate=pl.CostEstimate(flops=0, bytes_accessed=140 * 2**20, transcendentals=0),
        name="mixer_forward")(persist, pre, pos, fil, cw, gain)

def bwd_kernel(persist, dmix, pre, pos_ref, fill_ref, cw, gain, c_in, qk, w_in, u_in, u2_in, o_in, p_in, t_in, m_in, s_in,
               dpre, dcw, dgain, e_s, do_s):
    ri, ci = masks()
    heads = 2
    lane = lax.broadcasted_iota(jnp.int32, (BLOCK, HD), 1)
    dgain[...] = jnp.zeros_like(dgain)
    dcw[...] = jnp.zeros_like(dcw)
    def phase_a(n, _):
        r = pl.ds(pl.multiple_of(n * BLOCK, BLOCK), BLOCK)
        for h in range(heads):
            hs = slice(h*HD, (h+1)*HD)
            e = n*2+h
            o = o_in[r, hs]; dm = dmix[r, hs]
            gg = pre[r, 768+h*HD:768+(h+1)*HD]
            sg = sigmoid(gg); si = gg*sg
            ms = jnp.mean(o*o, axis=1, keepdims=True)
            sc = lax.rsqrt(jnp.maximum(ms, HEAD_FLOOR))
            on = o*sc
            gn = gain[...]
            dpre[r, 768+h*HD:768+(h+1)*HD] = (dm * on * gn * (sg * (1.0 + gg*(1.0-sg)))).astype(BF)
            dgs = dm * on * si
            dgain[...] += jnp.sum(dgs.reshape(8, 8, HD), axis=0)
            dn = dm * gn * si
            corr = jnp.where(ms > HEAD_FLOOR, jnp.mean(dn*on, axis=1, keepdims=True), 0.0)
            do = sc * (dn - on*corr)
            do_s[r, hs] = do
            pdo = d3(p_in[e], do, TN)
            qw = jnp.concatenate([qk[r, hs], w_in[r, hs]], axis=0)
            dd = jnp.concatenate([do, -pdo], axis=0)
            e_s[e] = d3(qw, dd, TN)
        return 0
    lax.fori_loop(0, NB, phase_a, 0)
    def phase_b(i, ds):
        n = NB-1-i
        out = []
        for h in range(heads):
            e = n*2+h
            d = ds[h]
            ee = e_s[e]
            e_s[e] = d
            out.append((d - d3(m_in[e], d, TN) + ee) * persist[n])
        return tuple(out)
    zs = jnp.zeros((HD, HD), F32)
    lax.fori_loop(0, NB, phase_b, (zs, zs))
    def phase_c(i, heads_dc):
        n = NB-1-i
        r = pl.ds(pl.multiple_of(n * BLOCK, BLOCK), BLOCK)
        pos = pos_ref[r, :]; fil = fill_ref[r, :]
        beta_t = sigmoid(pre[r, 1024:1152])
        dacts = [[], [], []]
        dbt = jnp.zeros((BLOCK, HD), F32)
        for h in range(heads):
            hs = slice(h*HD, (h+1)*HD)
            e = n*2+h
            q = qk[r, hs]; k = qk[r, 256+h*HD:256+(h+1)*HD]
            w = w_in[r, hs]; u = u_in[r, hs]; u2 = u2_in[r, hs]
            do = do_s[r, hs]; p = p_in[e]; t = t_in[e]; s = s_in[e]; ds = e_s[e]
            cv = c_in[r, 512+h*HD:512+(h+1)*HD]
            v = cv * sigmoid(cv) * fil
            b = beta_t[:, h:h+1]
            du2 = d3(p, do, TN) + d3(k, ds)
            dp = jnp.where(ri >= ci, d3(do, u2, NT), 0.0)
            xs = d3(jnp.concatenate([do, -du2], axis=0), s, NT)
            dq = xs[:BLOCK] + d3(dp, k)
            dw = xs[BLOCK:]
            dk = d3(dp, q, TN) + d3(u2, ds, NT)
            xx = d3(t, jnp.concatenate([dw, du2], axis=1), TN)
            xw = xx[:, :HD]; xu = xx[:, HD:]
            wu = jnp.concatenate([w, u], axis=1)
            mm = jnp.where(ri > ci, -d3(xx, wu, NT), 0.0)
            g = d3(k, k, NT)
            db = jnp.sum(mm*g, axis=1, keepdims=True)
            bm = b*mm
            dk = dk + d3(bm + bm.T, k) + b*xw
            db = db + jnp.sum(xw*k + xu*v, axis=1, keepdims=True)
            dv = b*xu
            dbt = jnp.where(lane == h, db, dbt)
            cq = c_in[r, hs]; ck = c_in[r, 256+h*HD:256+(h+1)*HD]
            sq = sigmoid(cq); sk = sigmoid(ck); sv = sigmoid(cv)
            yq = cq*sq*fil; yk = ck*sk*fil
            rq = lax.rsqrt(jnp.sum(yq*yq, axis=1, keepdims=True) + EPSILON)
            rk = lax.rsqrt(jnp.sum(yk*yk, axis=1, keepdims=True) + EPSILON)
            dyq = rq*(dq - q*jnp.sum(dq*q, axis=1, keepdims=True))
            dyk = rk*(dk - k*jnp.sum(dk*k, axis=1, keepdims=True))
            dacts[0].append(dyq*fil*(sq*(1.0+cq*(1.0-sq))))
            dacts[1].append(dyk*fil*(sk*(1.0+ck*(1.0-sk))))
            dacts[2].append(dv*fil*(sv*(1.0+cv*(1.0-sv))))
        dpre[r, 1024:1152] = (dbt*beta_t*(1.0-beta_t)).astype(BF)
        nxt = jnp.minimum(n+1, NB-1)
        posx = jnp.concatenate([pos, pos_ref[pl.ds(pl.multiple_of(nxt*BLOCK, BLOCK), 8), :]], axis=0)
        prv = jnp.maximum(n*BLOCK-8, 0)
        new = []
        for i in range(3):
            dc = jnp.concatenate(dacts[i], axis=1)
            ext = jnp.concatenate([dc, heads_dc[i]], axis=0)
            cur = pre[r, i*256:(i+1)*256]
            tail = pre[pl.ds(pl.multiple_of(prv, 8), 8), i*256:(i+1)*256]
            xext = jnp.concatenate([tail, cur], axis=0)
            dx = cw[i:i+1, :]*dc
            dcw[i] += jnp.sum((dc*cur).reshape(8, 8, 256), axis=0)
            for j in range(1, CONV):
                z = jnp.where(posx >= j, ext, 0.0)
                dx = dx + cw[j*3+i:j*3+i+1, :]*pltpu.roll(z, BLOCK+8-j, axis=0)[:BLOCK]
                sh = pltpu.roll(xext, j, axis=0)[8:]
                dcw[j*3+i] += jnp.sum(jnp.where(pos >= j, dc*sh, 0.0).reshape(8, 8, 256), axis=0)
            dpre[r, i*256:(i+1)*256] = dx.astype(BF)
            new.append(dc[:8])
        return tuple(new)
    z8 = jnp.zeros((8, 256), F32)
    lax.fori_loop(0, NB, phase_c, (z8, z8, z8))

def mixer_bwd(persist, dmix, pre, pos, fil, cw, gain, saved):
    outs = (sds(CAP,1152,dt=BF), sds(12,8,256), sds(8,HD))
    return pl.pallas_call(bwd_kernel, out_shape=outs, in_specs=[SM]+[VM]*(6+len(saved)), out_specs=[VM]*3,
        scratch_shapes=[pltpu.VMEM((2*NB,HD,HD),F32), pltpu.VMEM((CAP,256),F32)],
        compiler_params=pltpu.CompilerParams(vmem_limit_bytes=58*2**20), cost_estimate=pl.CostEstimate(flops=0, bytes_accessed=200 * 2**20, transcendentals=0),
        name="mixer_backward")(persist, dmix, pre, pos, fil, cw, gain, *saved)


MESH = pl.DeviceIdType.MESH
LINK_COST = 150 * 2**20
HBM = pl.BlockSpec(memory_space=pltpu.HBM)


def places():
    s, h, t = lax.axis_index("shard"), lax.axis_index("head"), lax.axis_index("tensor")
    return h, t, (s, h + 1, t), (s, h - 1, t), (s, h, 1 - t)


def shard_peers(m):
    s, h, t = lax.axis_index("shard"), lax.axis_index("head"), lax.axis_index("tensor")
    return [((lax.rem(s + i, m), h, t), lax.rem(s + i, m)) for i in range(1, m)]


class Carry:
    def __init__(self, kinds, m, ins, outs, send, recv, here):
        self.kinds, self.m, self.ins, self.outs = kinds, m, ins, outs
        self.send, self.recv, self.here = send, recv, here
        self.me = lax.axis_index("shard")

    def part(self, e, src):
        if self.kinds[e] == "gather":
            rows = self.ins[e].shape[0]
            return self.outs[e].at[pl.ds(pl.multiple_of(src * rows, rows), rows)]
        return self.outs[e].at[src]

    def given(self, e, dst):
        if self.kinds[e] == "columns":
            w = self.ins[e].shape[1] // self.m
            return self.ins[e].at[:, pl.ds(pl.multiple_of(dst * w, w), w)]
        return self.ins[e] if self.kinds[e] == "gather" else self.ins[e].at[dst]

    def copy(self, e, i, p):
        return pltpu.make_async_remote_copy(src_ref=self.given(e, p[1]), dst_ref=self.part(e, self.me), send_sem=self.send.at[e, i],
                                            recv_sem=self.recv.at[e, self.me], device_id=p[0], device_id_type=MESH)

    def local(self, e):
        return pltpu.make_async_copy(self.given(e, self.me), self.part(e, self.me), self.here.at[e])

    def greet(self):
        barrier = pltpu.get_barrier_semaphore()
        if self.kinds:
            for p, _ in shard_peers(self.m):
                pl.semaphore_signal(barrier, inc=1, device_id=p, device_id_type=MESH)
        return self.m - 1 if self.kinds else 0

    def start(self):
        for e in range(len(self.kinds)):
            for i, p in enumerate(shard_peers(self.m)):
                self.copy(e, i, p).start()
            self.local(e).start()

    def wait(self):
        for e in range(len(self.kinds)):
            self.local(e).wait()
            for i, p in enumerate(shard_peers(self.m)):
                self.copy(e, i, p).wait_send()
                pltpu.make_async_remote_copy(src_ref=self.given(e, p[1]), dst_ref=self.part(e, p[1]), send_sem=self.send.at[e, i],
                                             recv_sem=self.recv.at[e, p[1]], device_id=p[0], device_id_type=MESH).wait_recv()


def carried(kinds, m, arrays):
    dma = pltpu.SemaphoreType.DMA
    give = {"gather": lambda a: (m * a.shape[0], a.shape[1]), "swap": lambda a: a.shape,
            "columns": lambda a: (m, a.shape[0], a.shape[1] // m)}
    shapes = [jax.ShapeDtypeStruct(give[k](a), a.dtype) for k, a in zip(kinds, arrays)]
    e = len(kinds)
    return shapes, ([dma((e, m)), dma((e, m)), dma((e,))] if e else [])


def carry_of(kinds, m, refs, n_in, n_out):
    e = len(kinds)
    ins, refs = refs[:n_in], refs[n_in:]
    c_in, refs = refs[:e], refs[e:]
    outs, refs = refs[:n_out], refs[n_out:]
    c_out, refs = refs[:e], refs[e:]
    sems = (refs[-3:] if e else (None,) * 3)
    scratch = refs[:-3] if e else refs
    return ins, outs, scratch, Carry(kinds, m, c_in, c_out, *sems)


def greet(n, h, up, down, across, more=0):
    barrier = pltpu.get_barrier_semaphore()
    pl.semaphore_signal(barrier, inc=1, device_id=across, device_id_type=MESH)

    @pl.when(h < n - 1)
    def _():
        pl.semaphore_signal(barrier, inc=1, device_id=up, device_id_type=MESH)

    @pl.when(h > 0)
    def _():
        pl.semaphore_signal(barrier, inc=1, device_id=down, device_id_type=MESH)

    pl.semaphore_wait(barrier, 1 + more + (h < n - 1).astype(jnp.int32) + (h > 0).astype(jnp.int32))


def gather_kernel(n, width, m, kinds, *refs):
    (x,), (out,), (here, up_s, up_r, down_s, down_r, core_s, core_r), carry = carry_of(kinds, m, refs, 1, 1)
    h, t, up, down, across = places()

    def cols(j):
        return out.at[:, pl.ds(pl.multiple_of((j * 2 + t) * width, width), width)]

    def other(j):
        return out.at[:, pl.ds(pl.multiple_of((j * 2 + 1 - t) * width, width), width)]

    def send(j, src, ss, rs, to):
        return pltpu.make_async_remote_copy(src_ref=src, dst_ref=cols(j), send_sem=ss.at[j], recv_sem=rs.at[j],
                                            device_id=to, device_id_type=MESH)

    greet(n, h, up, down, across, carry.greet())
    local = pltpu.make_async_copy(x, cols(h), here)
    local.start()

    @pl.when(h < n - 1)
    def _():
        send(h, x, up_s, up_r, up).start()

    @pl.when(h > 0)
    def _():
        send(h, x, down_s, down_r, down).start()

    send(h, x, core_s, core_r, across).start()
    carry.start()
    for k in range(1, n):
        below, above = h - k, h + k

        @pl.when(below >= 0)
        def _():
            send(below, cols(below), up_s, up_r, up).wait_recv()

            @pl.when(h < n - 1)
            def _():
                send(below, cols(below), up_s, up_r, up).start()

            send(below, cols(below), core_s, core_r, across).start()

        @pl.when(above < n)
        def _():
            send(above, cols(above), down_s, down_r, down).wait_recv()

            @pl.when(h > 0)
            def _():
                send(above, cols(above), down_s, down_r, down).start()

            send(above, cols(above), core_s, core_r, across).start()

    for j in range(n):
        back = pltpu.make_async_remote_copy(src_ref=cols(j), dst_ref=other(j), send_sem=core_s.at[j], recv_sem=core_r.at[j],
                                            device_id=across, device_id_type=MESH)
        back.wait_recv()
        back.wait_send()

        @pl.when((j <= h) & (h < n - 1))
        def _():
            send(j, cols(j), up_s, up_r, up).wait_send()

        @pl.when((j >= h) & (h > 0))
        def _():
            send(j, cols(j), down_s, down_r, down).wait_send()

    local.wait()
    carry.wait()


def z_gather(n, piece, collective_id, name, m=1, kinds=(), arrays=()):
    rows, width = piece.shape
    dma = pltpu.SemaphoreType.DMA
    shapes, sems = carried(kinds, m, arrays)
    out = pl.pallas_call(
        functools.partial(gather_kernel, n, width, m, kinds),
        out_shape=[jax.ShapeDtypeStruct((rows, 2 * n * width), piece.dtype)] + shapes,
        in_specs=[HBM] * (1 + len(shapes)), out_specs=[HBM] * (1 + len(shapes)),
        scratch_shapes=[dma] + [dma((n,))] * 6 + sems,
        compiler_params=pltpu.CompilerParams(collective_id=collective_id, has_side_effects=True),
        cost_estimate=pl.CostEstimate(flops=0, bytes_accessed=LINK_COST, transcendentals=0),
        name=name,
    )(piece, *arrays)
    return out if kinds else out[0]


STEP = 128


def group_peers(n):
    s, h, t = lax.axis_index("shard"), lax.axis_index("head"), lax.axis_index("tensor")
    peers = []
    for i in range(1, 2 * n):
        hh, tt = lax.rem(h + i // 2, n), lax.rem(t + i % 2, 2)
        peers.append(((s, hh, tt), hh * 2 + tt))
    return peers


def greet_group(n, more=0):
    barrier = pltpu.get_barrier_semaphore()
    for p, _ in group_peers(n):
        pl.semaphore_signal(barrier, inc=1, device_id=p, device_id_type=MESH)
    pl.semaphore_wait(barrier, 2 * n - 1 + more)


def scatter_kernel(n, width, m, kinds, *refs):
    (part,), (out,), scratch, carry = carry_of(kinds, m, refs, 1, 1)
    mine, theirs, from_below, from_above, here, core_s, core_r, up_s, up_r, down_s, down_r = scratch
    h, t, up, down, across = places()

    def cols(j, c):
        return part.at[:, pl.ds(pl.multiple_of((j * 2 + c) * width, width), width)]

    def swap(j):
        return pltpu.make_async_remote_copy(src_ref=cols(j, 1 - t), dst_ref=theirs.at[j], send_sem=core_s.at[j],
                                            recv_sem=core_r.at[j], device_id=across, device_id_type=MESH)

    def own(j):
        return pltpu.make_async_copy(cols(j, t), mine.at[j], here.at[j])

    def rise(k):
        return pltpu.make_async_remote_copy(src_ref=mine.at[n - 1 - k], dst_ref=from_below.at[k], send_sem=up_s.at[k],
                                            recv_sem=up_r.at[k], device_id=up, device_id_type=MESH)

    def fall(k):
        return pltpu.make_async_remote_copy(src_ref=mine.at[k], dst_ref=from_above.at[k], send_sem=down_s.at[k],
                                            recv_sem=down_r.at[k], device_id=down, device_id_type=MESH)

    def total(j, extra):
        def step(i, c):
            r = pl.ds(pl.multiple_of(i * STEP, STEP), STEP)
            v = mine[j, r, :].astype(F32) + theirs[j, r, :].astype(F32)
            if extra is not None:
                v = v + extra(r).astype(F32)
            mine[j, r, :] = v.astype(BF)
            return c
        lax.fori_loop(0, CAP // STEP, step, 0)

    order = [j for i in range(n // 2) for j in (n - 1 - i, i)]
    for j in order:
        own(j).start()
    greet(n, h, up, down, across, carry.greet())
    for j in order:
        swap(j).start()
    carry.start()

    def arrive(j):
        own(j).wait()
        swap(j).wait_recv()

    for tick in range(2 * n - 2):
        ku = tick - h
        tu = n - 1 - ku

        @pl.when((ku >= 0) & (tu > h))
        def _():
            arrive(tu)

            @pl.when(h == 0)
            def _():
                total(tu, None)

            @pl.when(h > 0)
            def _():
                rise(ku).wait_recv()
                total(tu, lambda r: from_below[ku, r, :])

            rise(ku).start()

        kd = tick - (n - 1 - h)

        @pl.when((kd >= 0) & (kd < h))
        def _():
            arrive(kd)

            @pl.when(h == n - 1)
            def _():
                total(kd, None)

            @pl.when(h < n - 1)
            def _():
                fall(kd).wait_recv()
                total(kd, lambda r: from_above[kd, r, :])

            fall(kd).start()

    arrive(h)

    def final(get):
        def step(i, c):
            r = pl.ds(pl.multiple_of(i * STEP, STEP), STEP)
            out[r, :] = get(r)
            return c
        lax.fori_loop(0, CAP // STEP, step, 0)

    final(lambda r: mine[h, r, :].astype(F32) + theirs[h, r, :].astype(F32))

    @pl.when(h > 0)
    def _():
        rise(n - 1 - h).wait_recv()
        final(lambda r: out[r, :] + from_below[n - 1 - h, r, :].astype(F32))

    @pl.when(h < n - 1)
    def _():
        fall(h).wait_recv()
        final(lambda r: out[r, :] + from_above[h, r, :].astype(F32))

    for j in range(n):
        swap(j).wait_send()
    for k in range(n - 1):
        @pl.when(n - 1 - k > h)
        def _():
            rise(k).wait_send()

        @pl.when(k < h)
        def _():
            fall(k).wait_send()
    carry.wait()


def z_scatter(n, part, collective_id, name, m=1, kinds=(), arrays=()):
    rows, width = part.shape[0], part.shape[1] // (2 * n)
    dma = pltpu.SemaphoreType.DMA
    shapes, sems = carried(kinds, m, arrays)
    out = pl.pallas_call(
        functools.partial(scatter_kernel, n, width, m, kinds),
        out_shape=[jax.ShapeDtypeStruct((rows, width), F32)] + shapes,
        in_specs=[HBM] * (1 + len(shapes)), out_specs=[VM] + [HBM] * len(shapes),
        scratch_shapes=[pltpu.VMEM((n, rows, width), BF)] * 2 + [pltpu.VMEM((n - 1, rows, width), BF)] * 2
        + [dma((n,))] * 3 + [dma((n - 1,))] * 4 + sems,
        compiler_params=pltpu.CompilerParams(collective_id=collective_id, has_side_effects=True, vmem_limit_bytes=32 * 2**20),
        cost_estimate=pl.CostEstimate(flops=0, bytes_accessed=LINK_COST, transcendentals=0),
        name=name,
    )(part, *arrays)
    return out if kinds else out[0]


def scatter_norm_kernel(n, width, m, kinds, *refs):
    (part, kept, scale, base, gain), (out, low, dgain), scratch, carry = carry_of(kinds, m, refs, 5, 3)
    (acc, tots, tot_s, tot_r, mine, theirs, from_below, from_above,
     here, core_s, core_r, up_s, up_r, down_s, down_r) = scratch
    h, t, up, down, across = places()

    def cols(j, c):
        return part.at[:, pl.ds(pl.multiple_of((j * 2 + c) * width, width), width)]

    def swap(j):
        return pltpu.make_async_remote_copy(src_ref=cols(j, 1 - t), dst_ref=theirs.at[j], send_sem=core_s.at[j],
                                            recv_sem=core_r.at[j], device_id=across, device_id_type=MESH)

    def own(j):
        return pltpu.make_async_copy(cols(j, t), mine.at[j], here.at[j])

    def rise(k):
        return pltpu.make_async_remote_copy(src_ref=mine.at[n - 1 - k], dst_ref=from_below.at[k], send_sem=up_s.at[k],
                                            recv_sem=up_r.at[k], device_id=up, device_id_type=MESH)

    def fall(k):
        return pltpu.make_async_remote_copy(src_ref=mine.at[k], dst_ref=from_above.at[k], send_sem=down_s.at[k],
                                            recv_sem=down_r.at[k], device_id=down, device_id_type=MESH)

    def total(j, extra):
        def step(i, c):
            r = pl.ds(pl.multiple_of(i * STEP, STEP), STEP)
            v = mine[j, r, :].astype(F32) + theirs[j, r, :].astype(F32)
            if extra is not None:
                v = v + extra(r).astype(F32)
            mine[j, r, :] = v.astype(BF)
            return c
        lax.fori_loop(0, CAP // STEP, step, 0)

    order = [j for i in range(n // 2) for j in (n - 1 - i, i)]
    for j in order:
        own(j).start()
    greet_group(n, carry.greet())
    for j in order:
        swap(j).start()
    carry.start()

    def arrive(j):
        own(j).wait()
        swap(j).wait_recv()

    for tick in range(2 * n - 2):
        ku = tick - h
        tu = n - 1 - ku

        @pl.when((ku >= 0) & (tu > h))
        def _():
            arrive(tu)

            @pl.when(h == 0)
            def _():
                total(tu, None)

            @pl.when(h > 0)
            def _():
                rise(ku).wait_recv()
                total(tu, lambda r: from_below[ku, r, :])

            rise(ku).start()

        kd = tick - (n - 1 - h)

        @pl.when((kd >= 0) & (kd < h))
        def _():
            arrive(kd)

            @pl.when(h == n - 1)
            def _():
                total(kd, None)

            @pl.when(h < n - 1)
            def _():
                fall(kd).wait_recv()
                total(kd, lambda r: from_above[kd, r, :])

            fall(kd).start()

    arrive(h)

    def final(get):
        def step(i, c):
            r = pl.ds(pl.multiple_of(i * STEP, STEP), STEP)
            acc[r, :] = get(r)
            return c
        lax.fori_loop(0, CAP // STEP, step, 0)

    final(lambda r: mine[h, r, :].astype(F32) + theirs[h, r, :].astype(F32))

    @pl.when(h > 0)
    def _():
        rise(n - 1 - h).wait_recv()
        final(lambda r: acc[r, :] + from_below[n - 1 - h, r, :].astype(F32))

    @pl.when(h < n - 1)
    def _():
        fall(h).wait_recv()
        final(lambda r: acc[r, :] + from_above[h, r, :].astype(F32))

    me = h * 2 + t
    gains = gain[...]
    ones = jnp.ones((8, width), BF)

    def share(i, c):
        r = pl.ds(pl.multiple_of(i * STEP, STEP), STEP)
        hi, lo = split(acc[r, :] * gains * kept[r, :].astype(F32))
        tots[me, :, r] = dg(ones, hi, NT) + dg(ones, lo, NT)
        return c
    lax.fori_loop(0, CAP // STEP, share, 0)
    peers = group_peers(n)
    sends = [pltpu.make_async_remote_copy(src_ref=tots.at[me], dst_ref=tots.at[me], send_sem=tot_s.at[i], recv_sem=tot_r.at[me],
                                          device_id=p[0], device_id_type=MESH) for i, p in enumerate(peers)]
    for c in sends:
        c.start()
    for i, p in enumerate(peers):
        pltpu.make_async_remote_copy(src_ref=tots.at[me], dst_ref=tots.at[p[1]], send_sem=tot_s.at[i], recv_sem=tot_r.at[p[1]],
                                     device_id=p[0], device_id_type=MESH).wait_recv()
    dgain[...] = jnp.zeros_like(dgain)
    eighth = jnp.full((8, 128), 0.125, BF)

    def close(i, c):
        r = pl.ds(pl.multiple_of(i * STEP, STEP), STEP)
        row = tots[0, :, r]
        for d in range(1, 2 * n):
            row = row + tots[d, :, r]
        hi, lo = split(row)
        total_r = dg(hi, eighth, TN) + dg(lo, eighth, TN)
        sc = scale[r, :]
        kp = kept[r, :].astype(F32)
        dn = acc[r, :]
        back = base[r, :].astype(F32) + sc * (gains * dn) - kp * jnp.tile((sc * sc * sc) * (total_r * (1.0 / D)), (1, width // 128))
        out[r, :] = back
        low[r, :] = back.astype(BF)
        dgain[...] += jnp.sum((dn * kp * sc).reshape(STEP // 8, 8, width), axis=0)
        return c
    lax.fori_loop(0, CAP // STEP, close, 0)
    for c in sends:
        c.wait_send()

    for j in range(n):
        swap(j).wait_send()
    for k in range(n - 1):
        @pl.when(n - 1 - k > h)
        def _():
            rise(k).wait_send()

        @pl.when(k < h)
        def _():
            fall(k).wait_send()
    carry.wait()


def z_scatter_norm(n, part, kept, scale, base, gain, collective_id, name, m=1, kinds=(), arrays=()):
    rows, width = part.shape[0], part.shape[1] // (2 * n)
    dma = pltpu.SemaphoreType.DMA
    shapes, sems = carried(kinds, m, arrays)
    return pl.pallas_call(
        functools.partial(scatter_norm_kernel, n, width, m, kinds),
        out_shape=[jax.ShapeDtypeStruct((rows, width), F32), jax.ShapeDtypeStruct((rows, width), BF),
                   jax.ShapeDtypeStruct((8, width), F32)] + shapes,
        in_specs=[HBM] + [VM] * 4 + [HBM] * len(shapes), out_specs=[VM] * 3 + [HBM] * len(shapes),
        scratch_shapes=[pltpu.VMEM((rows, width), F32), pltpu.VMEM((2 * n, 8, rows), F32), dma((2 * n,)), dma((2 * n,))]
        + [pltpu.VMEM((n, rows, width), BF)] * 2 + [pltpu.VMEM((n - 1, rows, width), BF)] * 2
        + [dma((n,))] * 3 + [dma((n - 1,))] * 4 + sems,
        compiler_params=pltpu.CompilerParams(collective_id=collective_id, has_side_effects=True, vmem_limit_bytes=40 * 2**20),
        cost_estimate=pl.CostEstimate(flops=0, bytes_accessed=LINK_COST, transcendentals=0),
        name=name,
    )(part, kept, scale, base, gain, *arrays)


def small_kernel(n, m, x, out, held, total, shard_s, shard_r, group_s, group_r):
    s, h, t = lax.axis_index("shard"), lax.axis_index("head"), lax.axis_index("tensor")
    barrier = pltpu.get_barrier_semaphore()
    others = [lax.rem(s + i, m) for i in range(1, m)]
    peers = group_peers(n)
    for o in others:
        pl.semaphore_signal(barrier, inc=1, device_id=(o, h, t), device_id_type=MESH)
    for p, _ in peers:
        pl.semaphore_signal(barrier, inc=1, device_id=p, device_id_type=MESH)
    pl.semaphore_wait(barrier, m - 1 + 2 * n - 1)

    def over(i, o):
        return pltpu.make_async_remote_copy(src_ref=x, dst_ref=held.at[i], send_sem=shard_s.at[i], recv_sem=shard_r.at[i],
                                            device_id=(o, h, t), device_id_type=MESH)

    def along(i, p):
        return pltpu.make_async_remote_copy(src_ref=total, dst_ref=out.at[h * 2 + t], send_sem=group_s.at[i],
                                            recv_sem=group_r.at[h * 2 + t], device_id=p[0], device_id_type=MESH)

    for i, o in enumerate(others):
        over(i, o).start()
    for i, o in enumerate(others):
        over(i, o).wait_recv()
    v = x[...]
    for i in range(m - 1):
        v = v + held[i]
    total[...] = v
    out[h * 2 + t] = v
    for i, p in enumerate(peers):
        along(i, p).start()
    for i, p in enumerate(peers):
        pltpu.make_async_remote_copy(src_ref=total, dst_ref=out.at[p[1]], send_sem=group_s.at[i], recv_sem=group_r.at[p[1]],
                                     device_id=p[0], device_id_type=MESH).wait_recv()
    for i, o in enumerate(others):
        over(i, o).wait_send()
    for i, p in enumerate(peers):
        along(i, p).wait_send()


def sum_small(n, m, x, collective_id):
    dma = pltpu.SemaphoreType.DMA
    return pl.pallas_call(
        functools.partial(small_kernel, n, m),
        out_shape=jax.ShapeDtypeStruct((2 * n,) + x.shape, F32),
        in_specs=[VM], out_specs=VM,
        scratch_shapes=[pltpu.VMEM((m - 1,) + x.shape, F32), pltpu.VMEM(x.shape, F32), dma((m - 1,)), dma((m - 1,)),
                        dma((2 * n,)), dma((2 * n,))],
        compiler_params=pltpu.CompilerParams(collective_id=collective_id, has_side_effects=True),
        name="sum_small",
    )(x)


PRE = 1152
GROUP = ("head", "tensor")


def int_sum(values, along_axis):
    return jnp.sum(values, axis=along_axis)


def before(values):
    at = jnp.arange(values.shape[0], dtype=jnp.int32)
    return int_sum(jnp.where(at[None, :] < at[:, None], values[None, :], 0), 1)


def layout(seq_lengths, starts, dealing, group_idx):
    total_seqs = seq_lengths.shape[0]
    chosen = lax.dynamic_slice_in_dim(dealing, group_idx * SEQ_DEV, SEQ_DEV)
    picked = (chosen[:, None] == jnp.arange(total_seqs, dtype=jnp.int32)[None, :]).astype(jnp.int32)
    own_length = int_sum(picked * seq_lengths[None, :], 1)
    own_start = int_sum(picked * starts[None, :], 1)
    padded = (own_length + BLOCK - 1) // BLOCK * BLOCK
    buffer_start = before(padded)
    row_ids = jnp.arange(CAP, dtype=jnp.int32)
    member = int_sum((row_ids[:, None] >= buffer_start[None, :]).astype(jnp.int32), 1) - 1
    owned_by = (member[:, None] == jnp.arange(SEQ_DEV, dtype=jnp.int32)[None, :]).astype(jnp.int32)
    position = row_ids - int_sum(owned_by * buffer_start[None, :], 1)
    row_length = int_sum(owned_by * own_length[None, :], 1)
    seq_first = int_sum(owned_by * own_start[None, :], 1)
    filled = position < row_length
    return (seq_first + position, position, filled, seq_first, own_start, own_length)


def congruent(lower_end, upper_end, residue, modulus):
    return (upper_end - 1 - residue) // modulus - (lower_end - 1 - residue) // modulus


def mm(left, right, dims=NN):
    return lax.dot_general(left, right, dims, preferred_element_type=F32)


def full_rows(piece_in):
    return lax.all_gather(piece_in, GROUP, axis=1, tiled=True)


def shares(partial_sum):
    return lax.psum_scatter(partial_sum.astype(BF), GROUP, scatter_dimension=1, tiled=True).astype(F32)


def column_blocks(grad, m):
    rows, wide = grad.shape[0], grad.shape[1] // m
    if wide % 128 == 0:
        return "columns", grad
    return "swap", grad.reshape(rows, m, wide).transpose(1, 0, 2)


def sum_blocks(blocks):
    return jnp.sum(blocks.astype(F32), axis=0)


def body(tokens, seq_lengths, dealing, gain_mixer, w_query, w_key, w_value, w_gate, w_beta, conv_weight,
         gain_heads, w_out, gain_ffn, w_up_gate, w_up, w_down, cotangent):
    shards = lax.axis_size("shard")
    device = lax.axis_index("shard")
    width = tokens.shape[2]
    col_start = lax.axis_index(GROUP) * width
    ff = w_up.shape[1]
    per_peer = CAP // shards + SEQ_DEV
    slots = shards * per_peer
    total_seqs = seq_lengths.shape[0]

    w_piece = jnp.concatenate(
        [w_query, w_key, w_value, w_gate, w_beta, jnp.zeros((w_beta.shape[0], PRE - 4 * width - w_beta.shape[1]), BF)], axis=1)

    starts = before(seq_lengths)
    finish = starts + seq_lengths
    own_rows = tokens.reshape(REAL_DEV, width)
    own_ids = jnp.arange(REAL_DEV, dtype=jnp.int32)
    packed_ids = own_ids * shards + device
    inside = ((packed_ids[:, None] >= starts[None, :]) & (packed_ids[:, None] < finish[None, :])).astype(jnp.int32)
    seq_ids = jnp.arange(total_seqs, dtype=jnp.int32)
    matches = (dealing[:, None] == seq_ids[None, :]).astype(jnp.int32)
    seq_home = int_sum(matches * (seq_ids // SEQ_DEV)[:, None], 0)
    held = congruent(starts, finish, device, shards)
    ahead = (seq_home[:, None] == seq_home[None, :]) & (seq_ids[None, :] < seq_ids[:, None])
    seq_slot = (seq_home * per_peer + int_sum(jnp.where(ahead, held[None, :], 0), 1)
                - 1 - (starts - 1 - device) // shards)
    sent_slot = int_sum(inside * seq_slot[None, :], 1) + own_ids
    slot_ids = jnp.arange(slots, dtype=jnp.int32)
    send_pick = (slot_ids[:, None] == sent_slot[None, :]).astype(BF)
    outbox = mm(send_pick, own_rows).astype(BF)
    arrived = lax.all_to_all(outbox.reshape(shards, per_peer, width), "shard", split_axis=0, concat_axis=0, tiled=True)
    natural, position, filled, seq_first, own_start, own_length = layout(seq_lengths, starts, dealing, device)
    source = natural % shards
    earlier = own_start[None, :] < seq_first[:, None]
    span_counts = congruent(own_start[None, :], (own_start + own_length)[None, :], source[:, None], shards)
    arrival = int_sum(jnp.where(earlier, span_counts, 0), 1) + congruent(seq_first, natural, source, shards)
    recv_slot = jnp.where(filled, source * per_peer + arrival, -1)
    recv_pick = (recv_slot[:, None] == slot_ids[None, :]).astype(BF)
    x_rows = mm(recv_pick, arrived.reshape(slots, width)).astype(BF)
    filled_f = filled.astype(F32)[:, None]
    persist = (position.reshape(-1, BLOCK)[:, 0] != 0).astype(F32)
    pos = position[:, None]
    taps = conv_weight.reshape(3 * CONV, width)
    head_gain = gain_heads[None, :]

    n = lax.axis_size("head")
    rows_full, w_in = z_gather(n, x_rows, 1, "gather_rows", shards, ("gather",), (w_piece,))
    rows_full, cot_piece, w_down, w_out = lax.optimization_barrier((rows_full, cotangent, w_down, w_out))
    w_o = lax.all_gather(w_out, "shard", axis=1, tiled=True)
    cot_full = full_rows(cot_piece)
    w_d = lax.all_gather(w_down, "shard", axis=1, tiled=True)
    rows_full = rows_full.astype(F32)
    scale_one = lax.rsqrt(jnp.mean(rows_full * rows_full, axis=1) + EPSILON)
    normed = (rows_full * scale_one[:, None] * gain_mixer[None, :]).astype(BF)
    pre = mm(normed, w_in)
    mixed, *saved = mixer_fwd(persist, pre, pos, filled_f, taps, head_gain)
    branch_part, cot_full = lax.optimization_barrier((mm(mixed, w_o).astype(BF), cot_full))
    branch, w_ug = z_scatter(n, branch_part, 2, "scatter_branch", shards, ("gather",), (w_up_gate,))
    dealt_f32 = x_rows.astype(F32)
    hidden = dealt_f32 + branch
    held_low = hidden.astype(BF)
    held_full, w_u = z_gather(n, held_low, 3, "gather_held", shards, ("gather",), (w_up,))
    held_full = held_full.astype(F32)
    scale_two = lax.rsqrt(jnp.mean(held_full * held_full, axis=1) + EPSILON)
    normed_two = (held_full * scale_two[:, None] * gain_ffn[None, :]).astype(BF)
    gate_act = mm(normed_two, w_ug)
    up_act = mm(normed_two, w_u)
    sig = jax.nn.sigmoid(gate_act)
    product = (gate_act * sig * up_act).astype(BF)
    d_product = mm(cot_full, w_d, NT)
    d_gate = (d_product * up_act * sig * (1.0 + gate_act * (1.0 - sig))).astype(BF)
    d_up = (d_product * gate_act * sig).astype(BF)
    d_normed_two = (mm(d_gate, w_ug, NT) + mm(d_up, w_u, NT)).astype(BF)
    down_kind, d_w_down = column_blocks(mm(product, cot_full, TN).astype(BF), shards)
    blocks = (shards, w_up.shape[0], ff)
    d_w_ug = mm(normed_two, d_gate, TN).astype(BF).reshape(blocks)
    ffn_gain_part = lax.dynamic_slice_in_dim(gain_ffn, col_start, width)[None, :]
    d_hidden, d_hidden_low, ffn_gain_grad, d_w_ug, d_w_down = z_scatter_norm(
        n, d_normed_two, held_low, scale_two[:, None], cotangent, ffn_gain_part, 4, "scatter_normed_two", shards,
        ("swap", down_kind), (d_w_ug, d_w_down))
    d_w_u = mm(normed_two, d_up, TN).astype(BF).reshape(blocks)
    d_branch_full, d_w_u = z_gather(n, d_hidden_low, 5, "gather_branch", shards, ("swap",), (d_w_u,))
    out_part = mm(product, w_d).astype(BF)
    out_part, d_branch_full = lax.optimization_barrier((out_part, d_branch_full))
    out_sum = shares(out_part)
    d_mixed = mm(d_branch_full, w_o, NT)
    out_kind, d_w_out = column_blocks(mm(mixed, d_branch_full, TN).astype(BF), shards)
    d_pre, d_taps, d_head_gain = mixer_bwd(persist, d_mixed, pre, pos, filled_f, taps, head_gain, saved)
    d_normed = mm(d_pre, w_in, NT).astype(BF)
    d_w_in = mm(normed, d_pre, TN).astype(BF).reshape(shards, w_piece.shape[0], PRE)
    d_normed, out_sum = lax.optimization_barrier((d_normed, out_sum))
    block_out = (hidden + out_sum).astype(BF)
    mixer_gain_part = lax.dynamic_slice_in_dim(gain_mixer, col_start, width)[None, :]
    _, d_dealt, mixer_gain_grad, d_w_in, d_w_out = z_scatter_norm(
        n, d_normed, x_rows, scale_one[:, None], d_hidden, mixer_gain_part, 6, "scatter_normed", shards,
        ("swap", out_kind), (d_w_in, d_w_out))
    d_w_out = sum_blocks(d_w_out)
    d_w_in = sum_blocks(d_w_in)
    outbox_back = mm(recv_pick, d_dealt, TN).astype(BF)
    arrived_back = lax.all_to_all(outbox_back.reshape(shards, per_peer, width), "shard", split_axis=0, concat_axis=0, tiled=True)
    d_tokens = mm(send_pick, arrived_back.reshape(slots, width), TN).reshape(REAL_DEV, 1, width)

    small = jnp.concatenate([
        jnp.sum(d_taps, axis=1), jnp.sum(mixer_gain_grad, axis=0)[None, :], jnp.sum(ffn_gain_grad, axis=0)[None, :],
        jnp.pad(jnp.sum(d_head_gain, axis=0), (0, width - HD))[None, :],
        jnp.zeros((1, width), F32)], axis=0)
    summed = sum_small(n, shards, small, 7)
    by_row = summed.transpose(1, 0, 2).reshape(16, D)
    d_conv = by_row[:12].reshape(CONV, 3, D)
    d_gain_heads = jnp.sum(summed[:, 14, :HD], axis=0)
    cut = [0, width, 2 * width, 3 * width, 4 * width]
    return (
        block_out, d_tokens, by_row[12],
        d_w_in[:, cut[0]:cut[1]], d_w_in[:, cut[1]:cut[2]], d_w_in[:, cut[2]:cut[3]], d_w_in[:, cut[3]:cut[4]],
        d_w_in[:, 4 * width:4 * width + w_beta.shape[1]],
        d_conv, d_gain_heads, d_w_out, by_row[13],
        sum_blocks(d_w_ug), sum_blocks(d_w_u), sum_blocks(d_w_down),
    )


def solution(mesh):
    feat = ("head", "tensor")
    placed = (
        P(None, "shard", feat), P(), P(), P(),
        P("shard", feat), P("shard", feat), P("shard", feat), P("shard", feat), P("shard", feat),
        P(None, None, feat), P(), P(feat, "shard"), P(),
        P("shard", feat), P("shard", feat), P(feat, "shard"), P("shard", feat),
    )
    given = (
        P("shard", feat), P(None, "shard", feat), P(),
        P("shard", feat), P("shard", feat), P("shard", feat), P("shard", feat), P("shard", feat),
        P(), P(), P(feat, "shard"), P(),
        P("shard", feat), P("shard", feat), P(feat, "shard"),
    )
    return jax.shard_map(body, mesh=mesh, in_specs=placed, out_specs=given, check_vma=False)
```

```python
import functools
import jax
import jax.numpy as jnp
from jax import lax
from jax.experimental import pallas as pl
from jax.experimental.pallas import tpu as pltpu

from jax.sharding import PartitionSpec as P

D = 2048
HD = 128
CONV = 4
BLOCK = 64
SEQ_DEV = 4
REAL_DEV = 1152
CAP = 1280
NB = CAP // BLOCK
EPSILON = 1e-06
HEAD_FLOOR = 0.01
F32 = jnp.float32
BF = jnp.bfloat16

def split(x):
    hi = x.astype(BF)
    return hi, (x - hi.astype(F32)).astype(BF)

NN=(((1,),(0,)),((),())); NT=(((1,),(1,)),((),())); TN=(((0,),(0,)),((),()))

def dg(a, b, dims):
    return lax.dot_general(a, b, dims, preferred_element_type=F32)

def d3(a, b, dims=NN):
    ah, al = split(a); bh, bl = split(b)
    return dg(ah, bh, dims) + (dg(ah, bl, dims) + dg(al, bh, dims))

def twice(step):
    return lambda i, c: step(2 * i + 1, step(2 * i, c))

def masks():
    ri = lax.broadcasted_iota(jnp.int32, (BLOCK, BLOCK), 0)
    ci = lax.broadcasted_iota(jnp.int32, (BLOCK, BLOCK), 1)
    return ri, ci

def sigmoid(x):
    return 1.0 / (1.0 + jnp.exp(-x))

def conv_rows(cur, tail, wt, pos):
    ext = jnp.concatenate([tail, cur], axis=0)
    out = wt[0] * cur
    for j in range(1, CONV):
        sh = pltpu.roll(ext, j, axis=0)[8:]
        out = out + wt[j] * jnp.where(pos >= j, sh, 0.0)
    return out

def inverses(lmats, ri, ci):
    apart = ri ^ ci
    xs = [jnp.where(apart == 0, 1.0, 0.0) - jnp.where(apart == 1, m, 0.0) for m in lmats]
    s = 2
    while s < BLOCK:
        at = (apart >= s) & (apart < 2 * s)
        ys = [d3(x, jnp.where(at, m, 0.0)) for x, m in zip(xs, lmats)]
        xs = [x - d3(y, x) for x, y in zip(xs, ys)]
        s *= 2
    return xs

def fwd_kernel(persist, pre, pos_ref, fill_ref, cw, gain, mixed, c_out, qk, w_out, u_out, u2_out, o_out, p_out, t_out, m_out, s_out, b_s):
    ri, ci = masks()
    heads = 2
    def phase_a(n, tails):
        r = pl.ds(pl.multiple_of(n * BLOCK, BLOCK), BLOCK)
        pos = pos_ref[r, :]; fil = fill_ref[r, :]
        new_tails = []
        acts = []
        for i in range(3):
            cur = pre[r, i*256:(i+1)*256]
            wt = [cw[j*3+i:j*3+i+1, :] for j in range(CONV)]
            cc = conv_rows(cur, tails[i], wt, pos)
            c_out[r, i*256:(i+1)*256] = cc
            acts.append(cc * sigmoid(cc) * fil)
            new_tails.append(cur[BLOCK-8:])
        beta = sigmoid(pre[r, 1024:1152])
        for h in range(heads):
            hs = slice(h*HD, (h+1)*HD)
            yq = acts[0][:, hs]; yk = acts[1][:, hs]; v = acts[2][:, hs]
            q = yq * lax.rsqrt(jnp.sum(yq*yq, axis=1, keepdims=True) + EPSILON)
            k = yk * lax.rsqrt(jnp.sum(yk*yk, axis=1, keepdims=True) + EPSILON)
            b = beta[:, h:h+1]
            qk[r, h*HD:(h+1)*HD] = q
            qk[r, 256+h*HD:256+(h+1)*HD] = k
            lmat = jnp.where(ri > ci, b * d3(k, k, NT), 0.0)
            p_out[n*2+h] = jnp.where(ri >= ci, d3(q, k, NT), 0.0)
            t_out[n*2+h] = lmat
            u_out[r, hs] = b*v
            w_out[r, hs] = b*k
        return tuple(new_tails)
    z8 = jnp.zeros((8, 256), F32)
    lax.fori_loop(0, NB // 2, twice(phase_a), (z8, z8, z8))
    GRP = 8
    def phase_t(i, _):
        ts = inverses([t_out[i*GRP+j] for j in range(GRP)], ri, ci)
        for j in range(GRP):
            t_out[i*GRP+j] = ts[j]
        return 0
    lax.fori_loop(0, 2*NB//GRP, phase_t, 0)
    def phase_w(i, _):
        todo = [(n, pl.ds(pl.multiple_of(n * BLOCK, BLOCK), BLOCK), h, slice(h*HD, (h+1)*HD)) for n in (2*i, 2*i+1) for h in range(heads)]
        wu = [d3(t_out[n*2+h], jnp.concatenate([w_out[r, c], u_out[r, c]], axis=1)) for n, r, h, c in todo]
        mb = [d3(qk[r, 256+h*HD:256+(h+1)*HD], x, TN) for x, (n, r, h, c) in zip(wu, todo)]
        for x, y, (n, r, h, c) in zip(wu, mb, todo):
            w_out[r, c] = x[:, :HD]; u_out[r, c] = x[:, HD:]
            m_out[n*2+h] = y[:, :HD]; b_s[n*2+h] = y[:, HD:]
        return 0
    lax.fori_loop(0, NB//2, phase_w, 0)
    def phase_b(n, ss):
        out = []
        for h in range(heads):
            e = n*2+h
            s = ss[h] * persist[n]
            s_out[e] = s
            out.append(s - d3(m_out[e], s) + b_s[e])
        return tuple(out)
    zs = jnp.zeros((HD, HD), F32)
    lax.fori_loop(0, NB, phase_b, (zs, zs))
    def phase_c(i, _):
        todo = [(n, pl.ds(pl.multiple_of(n * BLOCK, BLOCK), BLOCK), h, slice(h*HD, (h+1)*HD)) for n in (2*i, 2*i+1) for h in range(heads)]
        rr = [d3(jnp.concatenate([w_out[r, c], qk[r, c]], axis=0), s_out[n*2+h]) for n, r, h, c in todo]
        u2 = [u_out[r, c] - v[:BLOCK] for v, (n, r, h, c) in zip(rr, todo)]
        os_ = [v[BLOCK:] + d3(p_out[n*2+h], u) for v, u, (n, r, h, c) in zip(rr, u2, todo)]
        for o, u, (n, r, h, c) in zip(os_, u2, todo):
            u2_out[r, c] = u
            o_out[r, c] = o
            ms = jnp.mean(o*o, axis=1, keepdims=True)
            sc = lax.rsqrt(jnp.maximum(ms, HEAD_FLOOR))
            gg = pre[r, 768+h*HD:768+(h+1)*HD]
            mixed[r, c] = (o * sc * gain[...] * (gg * sigmoid(gg))).astype(BF)
        return 0
    lax.fori_loop(0, NB // 2, phase_c, 0)

def sds(*s, dt=F32): return jax.ShapeDtypeStruct(s, dt)
VM = pl.BlockSpec(memory_space=pltpu.VMEM)
SM = pl.BlockSpec(memory_space=pltpu.SMEM)

def mixer_fwd(persist, pre, pos, fil, cw, gain):
    outs = (sds(CAP,256,dt=BF), sds(CAP,768), sds(CAP,512), sds(CAP,256), sds(CAP,256), sds(CAP,256), sds(CAP,256),
            sds(2*NB,BLOCK,BLOCK), sds(2*NB,BLOCK,BLOCK), sds(2*NB,HD,HD), sds(2*NB,HD,HD))
    return pl.pallas_call(fwd_kernel, out_shape=outs, in_specs=[SM]+[VM]*5, out_specs=[VM]*len(outs),
        scratch_shapes=[pltpu.VMEM((2*NB,HD,HD),F32)],
        compiler_params=pltpu.CompilerParams(vmem_limit_bytes=56*2**20), cost_estimate=pl.CostEstimate(flops=0, bytes_accessed=140 * 2**20, transcendentals=0),
        name="mixer_forward")(persist, pre, pos, fil, cw, gain)

def bwd_kernel(persist, dmix, pre, pos_ref, fill_ref, cw, gain, c_in, qk, w_in, u_in, u2_in, o_in, p_in, t_in, m_in, s_in,
               dpre, dcw, dgain, e_s, do_s):
    ri, ci = masks()
    heads = 2
    lane = lax.broadcasted_iota(jnp.int32, (BLOCK, HD), 1)
    dgain[...] = jnp.zeros_like(dgain)
    dcw[...] = jnp.zeros_like(dcw)
    def phase_a(n, _):
        r = pl.ds(pl.multiple_of(n * BLOCK, BLOCK), BLOCK)
        for h in range(heads):
            hs = slice(h*HD, (h+1)*HD)
            e = n*2+h
            o = o_in[r, hs]; dm = dmix[r, hs]
            gg = pre[r, 768+h*HD:768+(h+1)*HD]
            sg = sigmoid(gg); si = gg*sg
            ms = jnp.mean(o*o, axis=1, keepdims=True)
            sc = lax.rsqrt(jnp.maximum(ms, HEAD_FLOOR))
            on = o*sc
            gn = gain[...]
            dpre[r, 768+h*HD:768+(h+1)*HD] = (dm * on * gn * (sg * (1.0 + gg*(1.0-sg)))).astype(BF)
            dgs = dm * on * si
            dgain[...] += jnp.sum(dgs.reshape(8, 8, HD), axis=0)
            dn = dm * gn * si
            corr = jnp.where(ms > HEAD_FLOOR, jnp.mean(dn*on, axis=1, keepdims=True), 0.0)
            do = sc * (dn - on*corr)
            do_s[r, hs] = do
            pdo = d3(p_in[e], do, TN)
            qw = jnp.concatenate([qk[r, hs], w_in[r, hs]], axis=0)
            dd = jnp.concatenate([do, -pdo], axis=0)
            e_s[e] = d3(qw, dd, TN)
        return 0
    lax.fori_loop(0, NB // 2, twice(phase_a), 0)
    def phase_b(i, ds):
        n = NB-1-i
        out = []
        for h in range(heads):
            e = n*2+h
            d = ds[h]
            ee = e_s[e]
            e_s[e] = d
            out.append((d - d3(m_in[e], d, TN) + ee) * persist[n])
        return tuple(out)
    zs = jnp.zeros((HD, HD), F32)
    lax.fori_loop(0, NB, phase_b, (zs, zs))
    def phase_c(i, heads_dc):
        blocks = (NB - 1 - 2 * i, NB - 2 - 2 * i)
        todo = [(n, pl.ds(pl.multiple_of(n * BLOCK, BLOCK), BLOCK), h, slice(h*HD, (h+1)*HD)) for n in blocks for h in range(heads)]
        def every(f, *lists):
            return [f(*v) for v in zip(*lists)]
        ns, rs, hh, hs = zip(*todo)
        es = [n*2+h for n, h in zip(ns, hh)]
        fil = [fill_ref[r, :] for r in rs]
        beta_t = [sigmoid(pre[r, 1024:1152]) for r in rs]
        q = [qk[r, c] for r, c in zip(rs, hs)]
        k = [qk[r, 256+h*HD:256+(h+1)*HD] for r, h in zip(rs, hh)]
        w = [w_in[r, c] for r, c in zip(rs, hs)]
        u = [u_in[r, c] for r, c in zip(rs, hs)]
        u2 = [u2_in[r, c] for r, c in zip(rs, hs)]
        do = [do_s[r, c] for r, c in zip(rs, hs)]
        p = [p_in[e] for e in es]
        t = [t_in[e] for e in es]
        s = [s_in[e] for e in es]
        ds = [e_s[e] for e in es]
        b = [x[:, h:h+1] for x, h in zip(beta_t, hh)]
        du2 = every(lambda p, do, k, ds: d3(p, do, TN) + d3(k, ds), p, do, k, ds)
        dp = every(lambda do, u2: jnp.where(ri >= ci, d3(do, u2, NT), 0.0), do, u2)
        g = every(lambda k: d3(k, k, NT), k)
        xs = every(lambda do, du2, s: d3(jnp.concatenate([do, -du2], axis=0), s, NT), do, du2, s)
        dq = every(lambda xs, dp, k: xs[:BLOCK] + d3(dp, k), xs, dp, k)
        xx = every(lambda t, xs, du2: d3(t, jnp.concatenate([xs[BLOCK:], du2], axis=1), TN), t, xs, du2)
        dk = every(lambda dp, q, u2, ds: d3(dp, q, TN) + d3(u2, ds, NT), dp, q, u2, ds)
        mm = every(lambda xx, w, u: jnp.where(ri > ci, -d3(xx, jnp.concatenate([w, u], axis=1), NT), 0.0), xx, w, u)
        cv = [c_in[r, 512+h*HD:512+(h+1)*HD] for r, h in zip(rs, hh)]
        sv = every(sigmoid, cv)
        bm = every(lambda b, mm: b*mm, b, mm)
        dk = every(lambda dk, bm, k, b, xx: dk + d3(bm + bm.T, k) + b*xx[:, :HD], dk, bm, k, b, xx)
        db = every(lambda mm, g, xx, k, cv, sv, fil: jnp.sum(mm*g, axis=1, keepdims=True)
                   + jnp.sum(xx[:, :HD]*k + xx[:, HD:]*(cv*sv*fil), axis=1, keepdims=True), mm, g, xx, k, cv, sv, fil)
        cq = [c_in[r, c] for r, c in zip(rs, hs)]
        ck = [c_in[r, 256+h*HD:256+(h+1)*HD] for r, h in zip(rs, hh)]
        def unit_back(c, fil, n, d):
            sg = sigmoid(c)
            y = c*sg*fil
            r = lax.rsqrt(jnp.sum(y*y, axis=1, keepdims=True) + EPSILON)
            return r*(d - n*jnp.sum(d*n, axis=1, keepdims=True))*fil*(sg*(1.0+c*(1.0-sg)))
        aq = every(unit_back, cq, fil, q, dq)
        ak = every(unit_back, ck, fil, k, dk)
        av = every(lambda b, xx, fil, sv, cv: b*xx[:, HD:]*fil*(sv*(1.0+cv*(1.0-sv))), b, xx, fil, sv, cv)
        for j, n in enumerate(blocks):
            r = rs[2*j]
            dbt = jnp.where(lane == 0, db[2*j], jnp.where(lane == 1, db[2*j+1], 0.0))
            dpre[r, 1024:1152] = (dbt*beta_t[2*j]*(1.0-beta_t[2*j])).astype(BF)
            pos = pos_ref[r, :]
            nxt = jnp.minimum(n+1, NB-1)
            posx = jnp.concatenate([pos, pos_ref[pl.ds(pl.multiple_of(nxt*BLOCK, BLOCK), 8), :]], axis=0)
            prv = jnp.maximum(n*BLOCK-8, 0)
            new = []
            for i, acts in enumerate((aq, ak, av)):
                dc = jnp.concatenate(acts[2*j:2*j+2], axis=1)
                ext = jnp.concatenate([dc, heads_dc[i]], axis=0)
                cur = pre[r, i*256:(i+1)*256]
                tail = pre[pl.ds(pl.multiple_of(prv, 8), 8), i*256:(i+1)*256]
                xext = jnp.concatenate([tail, cur], axis=0)
                dx = cw[i:i+1, :]*dc
                dcw[i] += jnp.sum((dc*cur).reshape(8, 8, 256), axis=0)
                for o in range(1, CONV):
                    z = jnp.where(posx >= o, ext, 0.0)
                    dx = dx + cw[o*3+i:o*3+i+1, :]*pltpu.roll(z, BLOCK+8-o, axis=0)[:BLOCK]
                    sh = pltpu.roll(xext, o, axis=0)[8:]
                    dcw[o*3+i] += jnp.sum(jnp.where(pos >= o, dc*sh, 0.0).reshape(8, 8, 256), axis=0)
                dpre[r, i*256:(i+1)*256] = dx.astype(BF)
                new.append(dc[:8])
            heads_dc = tuple(new)
        return heads_dc
    z8 = jnp.zeros((8, 256), F32)
    lax.fori_loop(0, NB // 2, phase_c, (z8, z8, z8))

def mixer_bwd(persist, dmix, pre, pos, fil, cw, gain, saved):
    outs = (sds(CAP,1152,dt=BF), sds(12,8,256), sds(8,HD))
    return pl.pallas_call(bwd_kernel, out_shape=outs, in_specs=[SM]+[VM]*(6+len(saved)), out_specs=[VM]*3,
        scratch_shapes=[pltpu.VMEM((2*NB,HD,HD),F32), pltpu.VMEM((CAP,256),F32)],
        compiler_params=pltpu.CompilerParams(vmem_limit_bytes=58*2**20), cost_estimate=pl.CostEstimate(flops=0, bytes_accessed=200 * 2**20, transcendentals=0),
        name="mixer_backward")(persist, dmix, pre, pos, fil, cw, gain, *saved)


MESH = pl.DeviceIdType.MESH
LINK_COST = 150 * 2**20
HBM = pl.BlockSpec(memory_space=pltpu.HBM)


def places():
    s, h, t = lax.axis_index("shard"), lax.axis_index("head"), lax.axis_index("tensor")
    return h, t, (s, h + 1, t), (s, h - 1, t), (s, h, 1 - t)


def shard_peers(m):
    s, h, t = lax.axis_index("shard"), lax.axis_index("head"), lax.axis_index("tensor")
    return [((lax.rem(s + i, m), h, t), lax.rem(s + i, m)) for i in range(1, m)]


class Carry:
    def __init__(self, hops, kinds, m, ins, outs, send, recv, here):
        self.hops, self.kinds, self.m, self.ins, self.outs = hops, kinds, m, ins, outs
        self.send, self.recv, self.here = send, recv, here
        s, self.h, self.t = lax.axis_index("shard"), lax.axis_index("head"), lax.axis_index("tensor")
        self.me = s
        self.side = s + 1 - 2 * lax.rem(s, 2)
        self.over = lax.rem(s + 2, 4)
        self.corner = lax.rem(self.side + 2, 4)

    def relayed(self, e):
        return self.hops and self.m == 4 and self.kinds[e] in ("gather", "abreast")

    def part(self, e, src, half=None):
        rows = self.ins[e].shape[0]
        span = pl.ds(0, rows) if half is None else pl.ds(half * (rows // 2), rows // 2)
        if self.kinds[e] == "gather":
            first = src * rows + (0 if half is None else half * (rows // 2))
            return self.outs[e].at[pl.ds(pl.multiple_of(first, rows // 2), span.size)]
        if self.kinds[e] == "abreast":
            w = self.ins[e].shape[1]
            return self.outs[e].at[span, pl.ds(pl.multiple_of(src * w, w), w)]
        return self.outs[e].at[src]

    def given(self, e, dst):
        if self.kinds[e] == "columns":
            w = self.ins[e].shape[1] // self.m
            return self.ins[e].at[:, pl.ds(pl.multiple_of(dst * w, w), w)]
        return self.ins[e].at[dst] if self.kinds[e] == "swap" else self.ins[e]

    def move(self, e, src, dst, i, j, to):
        return pltpu.make_async_remote_copy(src_ref=src, dst_ref=dst, send_sem=self.send.at[e, i], recv_sem=self.recv.at[e, j],
                                            device_id=(to, self.h, self.t), device_id_type=MESH)

    def copy(self, e, i, to):
        return self.move(e, self.given(e, to), self.part(e, self.me), i, self.me, to)

    def came(self, e, src):
        return self.move(e, self.given(e, src), self.part(e, src), 0, src, src)

    def hand(self, e, half):
        src, to = (self.side, self.over) if half == 0 else (self.over, self.side)
        piece = self.part(e, src, half)
        return self.move(e, piece, piece, 2 + half, src if half == 0 else self.m, to)

    def handed(self, e, half):
        piece = self.part(e, self.corner, half)
        return self.move(e, piece, piece, 2 + half, self.corner if half == 0 else self.m, self.over if half == 0 else self.side)

    def local(self, e):
        return pltpu.make_async_copy(self.given(e, self.me), self.part(e, self.me), self.here.at[e])

    def targets(self, e):
        return [self.side, self.over] if self.relayed(e) else [p[1] for p in shard_peers(self.m)]

    def greet(self):
        barrier = pltpu.get_barrier_semaphore()
        if self.kinds:
            for p, _ in shard_peers(self.m):
                pl.semaphore_signal(barrier, inc=1, device_id=p, device_id_type=MESH)
        return self.m - 1 if self.kinds else 0

    def start(self):
        for e in range(len(self.kinds)):
            for i, to in enumerate(self.targets(e)):
                self.copy(e, i, to).start()
            self.local(e).start()

    def relay(self, e):
        if e < len(self.kinds) and self.relayed(e):
            self.came(e, self.side).wait_recv()
            self.hand(e, 0).start()
            self.came(e, self.over).wait_recv()
            self.hand(e, 1).start()

    def wait(self):
        for e in range(len(self.kinds)):
            self.local(e).wait()
            for i, to in enumerate(self.targets(e)):
                self.copy(e, i, to).wait_send()
                if not self.relayed(e):
                    self.came(e, to).wait_recv()
            if self.relayed(e):
                for half in range(2):
                    self.handed(e, half).wait_recv()
                    self.hand(e, half).wait_send()


def carried(kinds, m, arrays):
    dma = pltpu.SemaphoreType.DMA
    give = {"gather": lambda a: (m * a.shape[0], a.shape[1]), "swap": lambda a: a.shape,
            "abreast": lambda a: (a.shape[0], m * a.shape[1]), "pile": lambda a: (m,) + a.shape,
            "columns": lambda a: (m, a.shape[0], a.shape[1] // m)}
    shapes = [jax.ShapeDtypeStruct(give[k](a), a.dtype) for k, a in zip(kinds, arrays)]
    e = len(kinds)
    return shapes, ([dma((e, m + 1)), dma((e, m + 1)), dma((e,))] if e else [])


def carry_of(kinds, m, refs, n_in, n_out, hops=False):
    e = len(kinds)
    ins, refs = refs[:n_in], refs[n_in:]
    c_in, refs = refs[:e], refs[e:]
    outs, refs = refs[:n_out], refs[n_out:]
    c_out, refs = refs[:e], refs[e:]
    sems = (refs[-3:] if e else (None,) * 3)
    scratch = refs[:-3] if e else refs
    return ins, outs, scratch, Carry(hops, kinds, m, c_in, c_out, *sems)


def greet(n, h, up, down, across, more=0):
    barrier = pltpu.get_barrier_semaphore()
    pl.semaphore_signal(barrier, inc=1, device_id=across, device_id_type=MESH)

    @pl.when(h < n - 1)
    def _():
        pl.semaphore_signal(barrier, inc=1, device_id=up, device_id_type=MESH)

    @pl.when(h > 0)
    def _():
        pl.semaphore_signal(barrier, inc=1, device_id=down, device_id_type=MESH)

    pl.semaphore_wait(barrier, 1 + more + (h < n - 1).astype(jnp.int32) + (h > 0).astype(jnp.int32))


def gather_kernel(n, width, m, kinds, *refs):
    (tokens, sent, place), (x, out), scratch, carry = carry_of(kinds, m, refs, 3, 2)
    outbox, inbox, deal_s, deal_r, here, up_s, up_r, down_s, down_r, core_s, core_r = scratch
    h, t, up, down, across = places()
    per_peer = outbox.shape[1]

    def cols(j):
        return out.at[:, pl.ds(pl.multiple_of((j * 2 + t) * width, width), width)]

    def other(j):
        return out.at[:, pl.ds(pl.multiple_of((j * 2 + 1 - t) * width, width), width)]

    def send(j, src, ss, rs, to):
        return pltpu.make_async_remote_copy(src_ref=src, dst_ref=cols(j), send_sem=ss.at[j], recv_sem=rs.at[j],
                                            device_id=to, device_id_type=MESH)

    greet(n, h, up, down, across, carry.greet())
    peers = shard_peers(m)
    mine = lax.axis_index("shard")
    ids = lax.broadcasted_iota(jnp.int32, (per_peer, sent.shape[1]), 0)

    def deal(i, p, src):
        return pltpu.make_async_remote_copy(src_ref=outbox.at[p[1]], dst_ref=inbox.at[src], send_sem=deal_s.at[i],
                                            recv_sem=deal_r.at[src], device_id=p[0], device_id_type=MESH)

    def pick(q):
        return dg(jnp.where(sent[...] - q * per_peer == ids, 1.0, 0.0).astype(BF), tokens[...], NN).astype(BF)

    for i, p in enumerate(peers):
        outbox[p[1]] = pick(p[1])
        deal(i, p, mine).start()
    carry.start()
    inbox[mine] = pick(mine)
    for i, p in enumerate(peers):
        deal(i, p, p[1]).wait_recv()
    lanes = lax.broadcasted_iota(jnp.int32, (STEP, m * per_peer), 1)

    def settle(i, c):
        r = pl.ds(pl.multiple_of(i * STEP, STEP), STEP)
        chosen = jnp.where(place[r, :] == lanes, 1.0, 0.0).astype(BF)
        x[r, :] = dg(chosen, inbox[...].reshape(m * per_peer, width), NN).astype(BF)
        return c

    lax.fori_loop(0, CAP // STEP, settle, 0)
    local = pltpu.make_async_copy(x, cols(h), here)
    local.start()

    @pl.when(h < n - 1)
    def _():
        send(h, x, up_s, up_r, up).start()

    @pl.when(h > 0)
    def _():
        send(h, x, down_s, down_r, down).start()

    send(h, x, core_s, core_r, across).start()
    for k in range(1, n):
        below, above = h - k, h + k

        @pl.when(below >= 0)
        def _():
            send(below, cols(below), up_s, up_r, up).wait_recv()

            @pl.when(h < n - 1)
            def _():
                send(below, cols(below), up_s, up_r, up).start()

            send(below, cols(below), core_s, core_r, across).start()

        @pl.when(above < n)
        def _():
            send(above, cols(above), down_s, down_r, down).wait_recv()

            @pl.when(h > 0)
            def _():
                send(above, cols(above), down_s, down_r, down).start()

            send(above, cols(above), core_s, core_r, across).start()

    for j in range(n):
        back = pltpu.make_async_remote_copy(src_ref=cols(j), dst_ref=other(j), send_sem=core_s.at[j], recv_sem=core_r.at[j],
                                            device_id=across, device_id_type=MESH)
        back.wait_recv()
        back.wait_send()

        @pl.when((j <= h) & (h < n - 1))
        def _():
            send(j, cols(j), up_s, up_r, up).wait_send()

        @pl.when((j >= h) & (h > 0))
        def _():
            send(j, cols(j), down_s, down_r, down).wait_send()

    local.wait()
    for i, p in enumerate(peers):
        deal(i, p, mine).wait_send()
    carry.wait()


def z_gather(n, tokens, sent, place, per_peer, collective_id, name, m, kinds, arrays):
    width = tokens.shape[1]
    dma = pltpu.SemaphoreType.DMA
    shapes, sems = carried(kinds, m, arrays)
    return pl.pallas_call(
        functools.partial(gather_kernel, n, width, m, kinds),
        out_shape=[jax.ShapeDtypeStruct((CAP, width), BF), jax.ShapeDtypeStruct((CAP, 2 * n * width), BF)] + shapes,
        in_specs=[VM] * 3 + [HBM] * len(shapes), out_specs=[VM, HBM] + [HBM] * len(shapes),
        scratch_shapes=[pltpu.VMEM((m, per_peer, width), BF)] * 2 + [dma((m,)), dma((m,)), dma] + [dma((n,))] * 6 + sems,
        compiler_params=pltpu.CompilerParams(collective_id=collective_id, has_side_effects=True, vmem_limit_bytes=32 * 2**20),
        cost_estimate=pl.CostEstimate(flops=0, bytes_accessed=LINK_COST, transcendentals=0),
        name=name,
    )(tokens, sent, place, *arrays)


STEP = 128


def group_peers(n):
    s, h, t = lax.axis_index("shard"), lax.axis_index("head"), lax.axis_index("tensor")
    peers = []
    for i in range(1, 2 * n):
        hh, tt = lax.rem(h + i // 2, n), lax.rem(t + i % 2, 2)
        peers.append(((s, hh, tt), hh * 2 + tt))
    return peers


def greet_group(n, more=0):
    barrier = pltpu.get_barrier_semaphore()
    for p, _ in group_peers(n):
        pl.semaphore_signal(barrier, inc=1, device_id=p, device_id_type=MESH)
    pl.semaphore_wait(barrier, 2 * n - 1 + more)


def finish_kernel(n, width, m, kinds, *refs):
    (part, kept, scale, base, gain, share, small, sent, place), (tokens, every), scratch, carry = carry_of(kinds, m, refs, 9, 2)
    (low, dgain, outbox, inbox, deal_s, deal_r, held, ours, shard_s, shard_r, group_s, group_r,
     acc, tots, tot_s, tot_r, mine, theirs, from_below, from_above,
     here, core_s, core_r, up_s, up_r, down_s, down_r) = scratch
    h, t, up, down, across = places()

    def cols(j, c):
        return part.at[:, pl.ds(pl.multiple_of((j * 2 + c) * width, width), width)]

    def swap(j):
        return pltpu.make_async_remote_copy(src_ref=cols(j, 1 - t), dst_ref=theirs.at[j], send_sem=core_s.at[j],
                                            recv_sem=core_r.at[j], device_id=across, device_id_type=MESH)

    def own(j):
        return pltpu.make_async_copy(cols(j, t), mine.at[j], here.at[j])

    def rise(k):
        return pltpu.make_async_remote_copy(src_ref=mine.at[n - 1 - k], dst_ref=from_below.at[k], send_sem=up_s.at[k],
                                            recv_sem=up_r.at[k], device_id=up, device_id_type=MESH)

    def fall(k):
        return pltpu.make_async_remote_copy(src_ref=mine.at[k], dst_ref=from_above.at[k], send_sem=down_s.at[k],
                                            recv_sem=down_r.at[k], device_id=down, device_id_type=MESH)

    def total(j, extra):
        def step(i, c):
            r = pl.ds(pl.multiple_of(i * STEP, STEP), STEP)
            v = mine[j, r, :].astype(F32) + theirs[j, r, :].astype(F32)
            if extra is not None:
                v = v + extra(r).astype(F32)
            mine[j, r, :] = v.astype(BF)
            return c
        lax.fori_loop(0, CAP // STEP, step, 0)

    order = [j for i in range(n // 2) for j in (n - 1 - i, i)]
    for j in order:
        own(j).start()
    greet_group(n, carry.greet())
    me = h * 2 + t
    peers = group_peers(n)

    def tot_copy(i, p, dst):
        return pltpu.make_async_remote_copy(src_ref=share, dst_ref=tots.at[dst], send_sem=tot_s.at[i], recv_sem=tot_r.at[dst],
                                            device_id=p, device_id_type=MESH)

    for i, p in enumerate(peers):
        tot_copy(i, p[0], me).start()
    for j in order:
        swap(j).start()
    carry.start()

    def arrive(j):
        own(j).wait()
        swap(j).wait_recv()

    for tick in range(2 * n - 2):
        ku = tick - h
        tu = n - 1 - ku

        @pl.when((ku >= 0) & (tu > h))
        def _():
            arrive(tu)

            @pl.when(h == 0)
            def _():
                total(tu, None)

            @pl.when(h > 0)
            def _():
                rise(ku).wait_recv()
                total(tu, lambda r: from_below[ku, r, :])

            rise(ku).start()

        kd = tick - (n - 1 - h)

        @pl.when((kd >= 0) & (kd < h))
        def _():
            arrive(kd)

            @pl.when(h == n - 1)
            def _():
                total(kd, None)

            @pl.when(h < n - 1)
            def _():
                fall(kd).wait_recv()
                total(kd, lambda r: from_above[kd, r, :])

            fall(kd).start()

    arrive(h)
    for i, p in enumerate(peers):
        tot_copy(i, p[0], p[1]).wait_recv()
    tots[me] = share[...]
    for i, p in enumerate(peers):
        tots[me] = tots[me] + tots[p[1]]
    dgain[...] = jnp.zeros_like(dgain)
    gains = gain[...]
    eighth = jnp.full((8, 128), 0.125, BF)

    def final(get):
        def step(i, c):
            r = pl.ds(pl.multiple_of(i * STEP, STEP), STEP)
            acc[r, :] = get(r)
            return c
        lax.fori_loop(0, CAP // STEP, step, 0)

    final(lambda r: mine[h, r, :].astype(F32) + theirs[h, r, :].astype(F32))

    def first(get):
        final(lambda r: acc[r, :] + get(r).astype(F32))

    @pl.when((h > 0) & (h < n - 1))
    def _():
        @pl.when(2 * h < n)
        def _():
            fall(h).wait_recv()
            first(lambda r: from_above[h, r, :])

        @pl.when(2 * h >= n)
        def _():
            rise(n - 1 - h).wait_recv()
            first(lambda r: from_below[n - 1 - h, r, :])

    by_below = (h > 0) & ((2 * h < n) | (h == n - 1))

    @pl.when(by_below)
    def _():
        rise(n - 1 - h).wait_recv()

    @pl.when(jnp.logical_not(by_below))
    def _():
        fall(h).wait_recv()

    def close(get):
        def step(i, c):
            r = pl.ds(pl.multiple_of(i * STEP, STEP), STEP)
            hi, lo = split(tots[me, i])
            total_r = dg(hi, eighth, TN) + dg(lo, eighth, TN)
            sc = scale[r, :]
            kp = kept[r, :].astype(F32)
            dn = acc[r, :] + get(r).astype(F32)
            back = base[r, :].astype(F32) + sc * (gains * dn) - kp * jnp.tile((sc * sc * sc) * (total_r * (1.0 / D)), (1, width // 128))
            low[r, :] = back.astype(BF)
            dgain[...] += jnp.sum((dn * kp * sc).reshape(STEP // 8, 8, width), axis=0)
            return c
        lax.fori_loop(0, CAP // STEP, step, 0)

    @pl.when(by_below)
    def _():
        close(lambda r: from_below[n - 1 - h, r, :])

    @pl.when(jnp.logical_not(by_below))
    def _():
        close(lambda r: from_above[h, r, :])

    for i, p in enumerate(peers):
        tot_copy(i, p[0], me).wait_send()

    others = shard_peers(m)
    shard = lax.axis_index("shard")
    per_peer = outbox.shape[1]
    ids = lax.broadcasted_iota(jnp.int32, (per_peer, place.shape[1]), 0)

    def back(i, p, src):
        return pltpu.make_async_remote_copy(src_ref=outbox.at[p[1]], dst_ref=inbox.at[src], send_sem=deal_s.at[i],
                                            recv_sem=deal_r.at[src], device_id=p[0], device_id_type=MESH)

    def pick(q):
        return dg(jnp.where(place[...] - q * per_peer == ids, 1.0, 0.0).astype(BF), low[...], NN).astype(BF)

    def over(i, p, src):
        return pltpu.make_async_remote_copy(src_ref=ours, dst_ref=held.at[src], send_sem=shard_s.at[i],
                                            recv_sem=shard_r.at[src], device_id=p[0], device_id_type=MESH)

    def along(i, p, src):
        return pltpu.make_async_remote_copy(src_ref=held.at[shard], dst_ref=every.at[src], send_sem=group_s.at[i],
                                            recv_sem=group_r.at[src], device_id=p[0], device_id_type=MESH)

    for i, p in enumerate(others):
        outbox[p[1]] = pick(p[1])
        back(i, p, shard).start()
    at = lax.broadcasted_iota(jnp.int32, small.shape, 0)
    ours[...] = small[...] + jnp.where(at == 12, jnp.sum(dgain[...], axis=0, keepdims=True), 0.0)
    for i, p in enumerate(others):
        over(i, p, shard).start()
    inbox[shard] = pick(shard)
    v = ours[...]
    for i, p in enumerate(others):
        over(i, p, p[1]).wait_recv()
        v = v + held[p[1]]
    held[shard] = v
    every[me] = v
    for i, p in enumerate(peers):
        along(i, p, me).start()
    for i, p in enumerate(others):
        back(i, p, p[1]).wait_recv()
    lanes = lax.broadcasted_iota(jnp.int32, (STEP, m * per_peer), 1)

    def settle(i, c):
        r = pl.ds(pl.multiple_of(i * STEP, STEP), STEP)
        chosen = jnp.where(sent[r, :] == lanes, 1.0, 0.0).astype(BF)
        tokens[r, :] = dg(chosen, inbox[...].reshape(m * per_peer, width), NN)
        return c

    lax.fori_loop(0, REAL_DEV // STEP, settle, 0)
    for i, p in enumerate(peers):
        along(i, p, p[1]).wait_recv()
        along(i, p, me).wait_send()
    for i, p in enumerate(others):
        over(i, p, shard).wait_send()
        back(i, p, shard).wait_send()
    for j in range(n):
        swap(j).wait_send()
    for k in range(n - 1):
        @pl.when(n - 1 - k > h)
        def _():
            rise(k).wait_send()

        @pl.when(k < h)
        def _():
            fall(k).wait_send()
    carry.wait()


def z_finish(n, part, kept, scale, base, gain, share, small, sent, place, per_peer, collective_id, name, m, kinds, arrays):
    rows, width = part.shape[0], part.shape[1] // (2 * n)
    dma = pltpu.SemaphoreType.DMA
    shapes, sems = carried(kinds, m, arrays)
    return pl.pallas_call(
        functools.partial(finish_kernel, n, width, m, kinds),
        out_shape=[jax.ShapeDtypeStruct((REAL_DEV, width), F32), jax.ShapeDtypeStruct((2 * n,) + small.shape, F32)] + shapes,
        in_specs=[HBM] + [VM] * 8 + [HBM] * len(shapes), out_specs=[VM] * 2 + [HBM] * len(shapes),
        scratch_shapes=[pltpu.VMEM((rows, width), BF), pltpu.VMEM((8, width), F32)]
        + [pltpu.VMEM((m, per_peer, width), BF)] * 2 + [dma((m,))] * 2
        + [pltpu.VMEM((m,) + small.shape, F32), pltpu.VMEM(small.shape, F32), dma((m,)), dma((m,)), dma((2 * n,)), dma((2 * n,))]
        + [pltpu.VMEM((rows, width), F32), pltpu.VMEM((2 * n, rows // STEP, 8, STEP), F32), dma((2 * n,)), dma((2 * n,))]
        + [pltpu.VMEM((n, rows, width), BF)] * 2 + [pltpu.VMEM((n - 1, rows, width), BF)] * 2
        + [dma((n,))] * 3 + [dma((n - 1,))] * 4 + sems,
        compiler_params=pltpu.CompilerParams(collective_id=collective_id, has_side_effects=True, vmem_limit_bytes=48 * 2**20),
        cost_estimate=pl.CostEstimate(flops=0, bytes_accessed=LINK_COST, transcendentals=0),
        name=name,
    )(part, kept, scale, base, gain, share, small, sent, place, *arrays)


CHUNKS = 4
SUBS = 4
UNITS = CHUNKS * SUBS
UNIT = CAP // UNITS


def turn_kernel(n, width, m, kinds, norm, *refs):
    if norm:
        (part, kept, scale, base, gain, share), (out, full, low, dgain), scratch, carry = carry_of(kinds, m, refs, 6, 4)
        tots, tot_s, tot_r = scratch[-3:]
        scratch = scratch[:-3]
    else:
        (part, base), (out, full, low), scratch, carry = carry_of(kinds, m, refs, 2, 3, True)
    (mine, theirs, from_below, from_above, here, core_s, core_r, up_s, up_r, down_s, down_r,
     gu_s, gu_r, gd_s, gd_r, gc_s, gc_r, flat) = scratch
    h, t, up, down, across = places()
    me = h * 2 + t
    chunks = CHUNKS

    def rows(u):
        return pl.ds(pl.multiple_of(u * UNIT, UNIT), UNIT)

    def wide(r):
        return pl.ds(pl.multiple_of(r * SUBS * UNIT, SUBS * UNIT), SUBS * UNIT)

    def lanes(j, c):
        return pl.ds(pl.multiple_of((j * 2 + c) * width, width), width)

    def remote(src, dst, ss, rs, to):
        return pltpu.make_async_remote_copy(src_ref=src, dst_ref=dst, send_sem=ss, recv_sem=rs, device_id=to, device_id_type=MESH)

    def swap(j, r):
        return remote(part.at[wide(r), lanes(j, 1 - t)], theirs.at[j, wide(r)], core_s.at[j, r], core_r.at[j, r], across)

    def own(j, r):
        return pltpu.make_async_copy(part.at[wide(r), lanes(j, t)], mine.at[j, wide(r)], here.at[j, r])

    def rise(k, u):
        return remote(mine.at[n - 1 - k, rows(u)], from_below.at[k, rows(u)], up_s.at[k, u], up_r.at[k, u], up)

    def fall(k, u):
        return remote(mine.at[k, rows(u)], from_above.at[k, rows(u)], down_s.at[k, u], down_r.at[k, u], down)

    def spread(j, u, src, ss, rs, to):
        return remote(src, full.at[rows(u), lanes(j, t)], ss.at[j, u], rs.at[j, u], to)

    def piece(j, u):
        return full.at[rows(u), lanes(j, t)]

    def tot_copy(i, p, dst):
        return remote(share, tots.at[dst], tot_s.at[i], tot_r.at[dst], p)

    order = [j for i in range(n // 2) for j in (n - 1 - i, i)]
    for r in range(chunks):
        for j in order:
            own(j, r).start()
    if norm:
        greet_group(n, carry.greet())
        for i, p in enumerate(group_peers(n)):
            tot_copy(i, p[0], me).start()
        dgain[...] = jnp.zeros_like(dgain)
    else:
        greet(n, h, up, down, across, carry.greet())
    for r in range(chunks):
        for j in order:
            swap(j, r).start()
    carry.start()

    def arrive(j, r):
        own(j, r).wait()
        swap(j, r).wait_recv()

    def both(j, u):
        return mine[j, rows(u), :].astype(F32) + theirs[j, rows(u), :].astype(F32)

    def climb(o, r, s):
        u = SUBS * r + s

        @pl.when(h <= o)
        def _():
            ku = o - h
            tu = n - 1 - ku
            if s == 0:
                arrive(tu, r)

            @pl.when(h == 0)
            def _():
                mine[tu, rows(u), :] = both(tu, u).astype(BF)

            @pl.when(h > 0)
            def _():
                rise(ku, u).wait_recv()
                mine[tu, rows(u), :] = (both(tu, u) + from_below[ku, rows(u), :].astype(F32)).astype(BF)

            rise(ku, u).start()

        @pl.when(h >= n - 1 - o)
        def _():
            kd = o - (n - 1 - h)
            if s == 0:
                arrive(kd, r)

            @pl.when(h == n - 1)
            def _():
                mine[kd, rows(u), :] = both(kd, u).astype(BF)

            @pl.when(h < n - 1)
            def _():
                fall(kd, u).wait_recv()
                mine[kd, rows(u), :] = (both(kd, u) + from_above[kd, rows(u), :].astype(F32)).astype(BF)

            fall(kd, u).start()

    def gather_totals():
        for i, p in enumerate(group_peers(n)):
            tot_copy(i, p[0], p[1]).wait_recv()
        tots[me] = share[...]
        for i, p in enumerate(group_peers(n)):
            tots[me] = tots[me] + tots[p[1]]

    def last(r, s):
        u = SUBS * r + s
        if s == 0:
            arrive(h, r)
        flat[rows(u), :] = both(h, u)

        @pl.when(h > 0)
        def _():
            k = n - 1 - h
            rise(k, u).wait_recv()
            flat[rows(u), :] = flat[rows(u), :] + from_below[k, rows(u), :].astype(F32)

        @pl.when(h < n - 1)
        def _():
            fall(h, u).wait_recv()
            flat[rows(u), :] = flat[rows(u), :] + from_above[h, rows(u), :].astype(F32)

        if norm:
            close(u)
        else:
            v = base[rows(u), :].astype(F32) + flat[rows(u), :]
            out[rows(u), :] = v
            low[rows(u), :] = v.astype(BF)
            set_out(u)

    def close(u):
        hi, lo = split(tots[me, u])
        eighth = jnp.full((8, 128), 0.125, BF)
        total_r = (dg(hi, eighth, TN) + dg(lo, eighth, TN))[:UNIT]
        sc = scale[rows(u), :]
        kp = kept[rows(u), :].astype(F32)
        dn = flat[rows(u), :]
        v = (base[rows(u), :].astype(F32) + sc * (gain[...] * dn)
             - kp * jnp.tile((sc * sc * sc) * (total_r * (1.0 / D)), (1, width // 128)))
        out[rows(u), :] = v
        low[rows(u), :] = v.astype(BF)
        dgain[...] += jnp.sum((dn * kp * sc).reshape(UNIT // 8, 8, width), axis=0)
        set_out(u)

    def set_out(u):
        src = low.at[rows(u)]

        @pl.when(h < n - 1)
        def _():
            spread(h, u, src, gu_s, gu_r, up).start()

        @pl.when(h > 0)
        def _():
            spread(h, u, src, gd_s, gd_r, down).start()

        spread(h, u, src, gc_s, gc_r, across).start()

    def pass_on(k, r, s):
        u = SUBS * r + s
        below, above = h - k, h + k

        @pl.when(below >= 0)
        def _():
            spread(below, u, piece(below, u), gu_s, gu_r, up).wait_recv()

            @pl.when(h < n - 1)
            def _():
                spread(below, u, piece(below, u), gu_s, gu_r, up).start()

            spread(below, u, piece(below, u), gc_s, gc_r, across).start()

        @pl.when(above < n)
        def _():
            spread(above, u, piece(above, u), gd_s, gd_r, down).wait_recv()

            @pl.when(h > 0)
            def _():
                spread(above, u, piece(above, u), gd_s, gd_r, down).start()

            spread(above, u, piece(above, u), gc_s, gc_r, across).start()

    def at(o, r, s):
        if o < n - 1:
            climb(o, r, s)
        elif o == n - 1:
            if norm and s == 0:
                @pl.when(r == 0)
                def _():
                    gather_totals()
            last(r, s)
        elif o < 2 * n - 1:
            pass_on(o - n + 1, r, s)

    def period(r, c):
        for e in range(len(kinds)):
            @pl.when(r == e + 1)
            def _():
                carry.relay(e)

        for o in range(n):
            for s in range(SUBS):
                @pl.when(r > 0)
                def _():
                    at(o + n, r - 1, s)

                @pl.when(r < chunks)
                def _():
                    at(o, r, s)
        return c

    lax.fori_loop(0, chunks + 1, period, 0)
    mine_out = pltpu.make_async_copy(low, full.at[:, lanes(h, t)], here.at[0, 0])
    mine_out.start()

    def drain(u, c):
        for j in range(n):
            back = remote(piece(j, u), full.at[rows(u), lanes(j, 1 - t)], gc_s.at[j, u], gc_r.at[j, u], across)
            back.wait_recv()
            back.wait_send()

            @pl.when((j <= h) & (h < n - 1))
            def _():
                spread(j, u, piece(j, u), gu_s, gu_r, up).wait_send()

            @pl.when((j >= h) & (h > 0))
            def _():
                spread(j, u, piece(j, u), gd_s, gd_r, down).wait_send()

        for k in range(n - 1):
            @pl.when(n - 1 - k > h)
            def _():
                rise(k, u).wait_send()

            @pl.when(k < h)
            def _():
                fall(k, u).wait_send()

        return c

    if norm:
        for i, p in enumerate(group_peers(n)):
            tot_copy(i, p[0], me).wait_send()
    lax.fori_loop(0, UNITS, drain, 0)
    for r in range(chunks):
        for j in range(n):
            swap(j, r).wait_send()
    mine_out.wait()
    carry.wait()


def z_turn(n, part, base, collective_id, name, m=1, kinds=(), arrays=(), norm=None):
    rows, width = part.shape[0], part.shape[1] // (2 * n)
    dma = pltpu.SemaphoreType.DMA
    shapes, sems = carried(kinds, m, arrays)
    shape = jax.ShapeDtypeStruct
    ins = [part, base] if norm is None else [part, norm[0], norm[1], base, norm[2], norm[3]]
    outs = [shape((rows, width), F32), shape((rows, 2 * n * width), BF), shape((rows, width), BF)]
    out_specs = [VM, HBM, VM]
    more = []
    if norm is not None:
        outs, out_specs = outs + [shape((8, width), F32)], out_specs + [VM]
        more = [pltpu.VMEM((2 * n, UNITS, 8, 128), F32), dma((2 * n,)), dma((2 * n,))]
    return pl.pallas_call(
        functools.partial(turn_kernel, n, width, m, kinds, norm is not None),
        out_shape=outs + shapes,
        in_specs=[HBM] + [VM] * (len(ins) - 1) + [HBM] * len(shapes), out_specs=out_specs + [HBM] * len(shapes),
        scratch_shapes=[pltpu.VMEM((n, rows, width), BF)] * 2 + [pltpu.VMEM((n - 1, rows, width), BF)] * 2
        + [dma((n, CHUNKS))] * 3 + [dma((n - 1, UNITS))] * 4 + [dma((n, UNITS))] * 6 + [pltpu.VMEM((rows, width), F32)]
        + more + sems,
        compiler_params=pltpu.CompilerParams(collective_id=collective_id, has_side_effects=True, vmem_limit_bytes=40 * 2**20),
        cost_estimate=pl.CostEstimate(flops=0, bytes_accessed=LINK_COST, transcendentals=0),
        name=name,
    )(*ins, *arrays)


PRE = 1152
GROUP = ("head", "tensor")


def int_sum(values, along_axis):
    return jnp.sum(values, axis=along_axis)


def before(values):
    at = jnp.arange(values.shape[0], dtype=jnp.int32)
    return int_sum(jnp.where(at[None, :] < at[:, None], values[None, :], 0), 1)


def layout(seq_lengths, starts, dealing, group_idx):
    total_seqs = seq_lengths.shape[0]
    chosen = lax.dynamic_slice_in_dim(dealing, group_idx * SEQ_DEV, SEQ_DEV)
    picked = (chosen[:, None] == jnp.arange(total_seqs, dtype=jnp.int32)[None, :]).astype(jnp.int32)
    own_length = int_sum(picked * seq_lengths[None, :], 1)
    own_start = int_sum(picked * starts[None, :], 1)
    padded = (own_length + BLOCK - 1) // BLOCK * BLOCK
    buffer_start = before(padded)
    row_ids = jnp.arange(CAP, dtype=jnp.int32)
    member = int_sum((row_ids[:, None] >= buffer_start[None, :]).astype(jnp.int32), 1) - 1
    owned_by = (member[:, None] == jnp.arange(SEQ_DEV, dtype=jnp.int32)[None, :]).astype(jnp.int32)
    position = row_ids - int_sum(owned_by * buffer_start[None, :], 1)
    row_length = int_sum(owned_by * own_length[None, :], 1)
    seq_first = int_sum(owned_by * own_start[None, :], 1)
    filled = position < row_length
    return (seq_first + position, position, filled, seq_first, own_start, own_length)


def congruent(lower_end, upper_end, residue, modulus):
    return (upper_end - 1 - residue) // modulus - (lower_end - 1 - residue) // modulus


def mm(left, right, dims=NN):
    return lax.dot_general(left, right, dims, preferred_element_type=F32)


def full_rows(piece_in):
    return lax.all_gather(piece_in, GROUP, axis=1, tiled=True)


def shares(partial_sum):
    return lax.psum_scatter(partial_sum.astype(BF), GROUP, scatter_dimension=1, tiled=True).astype(F32)


def column_blocks(grad, m):
    rows, wide = grad.shape[0], grad.shape[1] // m
    if wide % 128 == 0:
        return "columns", grad
    return "swap", grad.reshape(rows, m, wide).transpose(1, 0, 2)


def side_by_side(wide):
    return "abreast" if wide % 128 == 0 else "pile"


def level(weights):
    if weights.ndim == 2:
        return weights
    return weights.transpose(1, 0, 2).reshape(weights.shape[1], -1)


def swap_ring(*grads):
    shards, device = lax.axis_size("shard"), lax.axis_index("shard")
    wide = grads[0].shape[1] // shards

    def block(i):
        at = lax.rem(device + i, shards) * wide
        return jnp.concatenate([lax.dynamic_slice_in_dim(g, at, wide, 1) for g in grads], axis=0)

    total = block(0).astype(F32)
    for i in range(1, shards):
        total = total + lax.ppermute(block(i), "shard", [(a, (a + i) % shards) for a in range(shards)]).astype(F32)
    ends = [0]
    for g in grads:
        ends.append(ends[-1] + g.shape[0])
    return [total[i:j] for i, j in zip(ends, ends[1:])]


def along_lanes(values, units):
    rows = values.reshape(units, 1, -1)
    return jnp.broadcast_to(jnp.pad(rows, ((0, 0), (0, 0), (0, 128 - rows.shape[2]))), (units, 8, 128))


def sum_blocks(blocks):
    return jnp.sum(blocks.astype(F32), axis=0)


def body(tokens, seq_lengths, dealing, gain_mixer, w_query, w_key, w_value, w_gate, w_beta, conv_weight,
         gain_heads, w_out, gain_ffn, w_up_gate, w_up, w_down, cotangent):
    shards = lax.axis_size("shard")
    device = lax.axis_index("shard")
    width = tokens.shape[2]
    col_start = lax.axis_index(GROUP) * width
    per_peer = (CAP // shards + SEQ_DEV + 15) // 16 * 16
    total_seqs = seq_lengths.shape[0]

    w_piece = jnp.concatenate(
        [w_query, w_key, w_value, w_gate, w_beta, jnp.zeros((w_beta.shape[0], PRE - 4 * width - w_beta.shape[1]), BF)], axis=1)

    starts = before(seq_lengths)
    finish = starts + seq_lengths
    own_rows = tokens.reshape(REAL_DEV, width)
    own_ids = jnp.arange(REAL_DEV, dtype=jnp.int32)
    packed_ids = own_ids * shards + device
    inside = ((packed_ids[:, None] >= starts[None, :]) & (packed_ids[:, None] < finish[None, :])).astype(jnp.int32)
    seq_ids = jnp.arange(total_seqs, dtype=jnp.int32)
    matches = (dealing[:, None] == seq_ids[None, :]).astype(jnp.int32)
    seq_home = int_sum(matches * (seq_ids // SEQ_DEV)[:, None], 0)
    held = congruent(starts, finish, device, shards)
    ahead = (seq_home[:, None] == seq_home[None, :]) & (seq_ids[None, :] < seq_ids[:, None])
    seq_slot = (seq_home * per_peer + int_sum(jnp.where(ahead, held[None, :], 0), 1)
                - 1 - (starts - 1 - device) // shards)
    sent_slot = int_sum(inside * seq_slot[None, :], 1) + own_ids
    natural, position, filled, seq_first, own_start, own_length = layout(seq_lengths, starts, dealing, device)
    source = natural % shards
    earlier = own_start[None, :] < seq_first[:, None]
    span_counts = congruent(own_start[None, :], (own_start + own_length)[None, :], source[:, None], shards)
    arrival = int_sum(jnp.where(earlier, span_counts, 0), 1) + congruent(seq_first, natural, source, shards)
    recv_slot = jnp.where(filled, source * per_peer + arrival, -1)
    filled_f = filled.astype(F32)[:, None]
    persist = (position.reshape(-1, BLOCK)[:, 0] != 0).astype(F32)
    pos = position[:, None]
    taps = conv_weight.reshape(3 * CONV, width)
    head_gain = gain_heads[None, :]

    n = lax.axis_size("head")
    side = side_by_side(w_up.shape[0])
    x_rows, rows_full, w_in, w_o = z_gather(
        n, own_rows, sent_slot[None, :], recv_slot[:, None], per_peer, 1, "gather_rows", shards, ("gather", side), (w_piece, w_out))
    w_o = level(w_o)
    rows_full, cot_piece = lax.optimization_barrier((rows_full, cotangent))
    cot_full = full_rows(cot_piece)
    rows_full = rows_full.astype(F32)
    scale_one = lax.rsqrt(jnp.mean(rows_full * rows_full, axis=1) + EPSILON)
    normed = lax.optimization_barrier((rows_full * scale_one[:, None] * gain_mixer[None, :]).astype(BF))
    pre = mm(normed, w_in)
    mixed, *saved = mixer_fwd(persist, pre, pos, filled_f, taps, head_gain)
    branch_part, cot_full = lax.optimization_barrier((mm(mixed, w_o).astype(BF), cot_full))
    hidden, held_full, held_low, w_ug, w_u, w_d = z_turn(
        n, branch_part, x_rows, 2, "turn_branch", shards, (side,) * 3, (w_up_gate.T, w_up.T, w_down))
    w_ug, w_u, w_d = level(w_ug), level(w_u), level(w_d)
    held_full = held_full.astype(F32)
    scale_two = lax.rsqrt(jnp.mean(held_full * held_full, axis=1) + EPSILON)
    normed_two = lax.optimization_barrier((held_full * scale_two[:, None] * gain_ffn[None, :]).astype(BF))
    gate_act = mm(normed_two, w_ug, NT)
    up_act = mm(normed_two, w_u, NT)
    sig = jax.nn.sigmoid(gate_act)
    product = (gate_act * sig * up_act).astype(BF)
    d_product = mm(cot_full, w_d, NT)
    d_gate = (d_product * up_act * sig * (1.0 + gate_act * (1.0 - sig))).astype(BF)
    d_up = (d_product * gate_act * sig).astype(BF)
    share_two = jnp.sum(d_gate.astype(F32) * gate_act + d_up.astype(F32) * up_act, axis=1) / scale_two
    d_normed_two = (mm(d_gate, w_ug) + mm(d_up, w_u)).astype(BF)
    down_kind, d_w_down = column_blocks(mm(product, cot_full, TN).astype(BF), shards)
    gate_kind, d_w_ug = column_blocks(mm(d_gate, normed_two, TN).astype(BF), shards)
    d_w_u = mm(d_up, normed_two, TN).astype(BF)
    ffn_gain_part = lax.dynamic_slice_in_dim(gain_ffn, col_start, width)[None, :]
    d_hidden, d_branch_full, _, ffn_gain_grad, d_w_ug, d_w_down = z_turn(
        n, d_normed_two, cotangent, 4, "turn_normed_two", shards, (gate_kind, down_kind), (d_w_ug, d_w_down),
        norm=(held_low, scale_two[:, None], ffn_gain_part, along_lanes(share_two, UNITS)))
    out_part = mm(product, w_d).astype(BF)
    out_part, d_branch_full = lax.optimization_barrier((out_part, d_branch_full))
    d_w_u, d_w_out = swap_ring(d_w_u, mm(mixed, d_branch_full, TN).astype(BF))
    out_sum = shares(out_part)
    d_mixed = mm(d_branch_full, w_o, NT)
    d_pre, d_taps, d_head_gain = mixer_bwd(persist, d_mixed, pre, pos, filled_f, taps, head_gain, saved)
    d_normed = mm(d_pre, w_in, NT).astype(BF)
    share_one = jnp.sum(d_pre.astype(F32) * pre, axis=1) / scale_one
    d_w_in = mm(normed, d_pre, TN).astype(BF).reshape(shards, w_piece.shape[0], PRE)
    d_normed, out_sum = lax.optimization_barrier((d_normed, out_sum))
    block_out = (hidden + out_sum).astype(BF)
    mixer_gain_part = lax.dynamic_slice_in_dim(gain_mixer, col_start, width)[None, :]
    small = jnp.concatenate([
        jnp.sum(d_taps, axis=1), jnp.zeros((1, width), F32), jnp.sum(ffn_gain_grad, axis=0)[None, :],
        jnp.pad(jnp.sum(d_head_gain, axis=0), (0, width - HD))[None, :],
        jnp.zeros((1, width), F32)], axis=0)
    d_tokens, summed, d_w_in = z_finish(
        n, d_normed, x_rows, scale_one[:, None], d_hidden, mixer_gain_part, along_lanes(share_one, CAP // STEP), small,
        sent_slot[:, None], recv_slot[None, :], per_peer, 6, "finish_rows", shards, ("swap",), (d_w_in,))
    d_tokens = d_tokens.reshape(REAL_DEV, 1, width)
    d_w_in = sum_blocks(d_w_in)
    by_row = summed.transpose(1, 0, 2).reshape(16, D)
    d_conv = by_row[:12].reshape(CONV, 3, D)
    d_gain_heads = jnp.sum(summed[:, 14, :HD], axis=0)
    cut = [0, width, 2 * width, 3 * width, 4 * width]
    return (
        block_out, d_tokens, by_row[12],
        d_w_in[:, cut[0]:cut[1]], d_w_in[:, cut[1]:cut[2]], d_w_in[:, cut[2]:cut[3]], d_w_in[:, cut[3]:cut[4]],
        d_w_in[:, 4 * width:4 * width + w_beta.shape[1]],
        d_conv, d_gain_heads, d_w_out, by_row[13],
        sum_blocks(d_w_ug).T, d_w_u.T, sum_blocks(d_w_down),
    )


def solution(mesh):
    feat = ("head", "tensor")
    placed = (
        P(None, "shard", feat), P(), P(), P(),
        P("shard", feat), P("shard", feat), P("shard", feat), P("shard", feat), P("shard", feat),
        P(None, None, feat), P(), P(feat, "shard"), P(),
        P("shard", feat), P("shard", feat), P(feat, "shard"), P("shard", feat),
    )
    given = (
        P("shard", feat), P(None, "shard", feat), P(),
        P("shard", feat), P("shard", feat), P("shard", feat), P("shard", feat), P("shard", feat),
        P(), P(), P(feat, "shard"), P(),
        P("shard", feat), P("shard", feat), P(feat, "shard"),
    )
    return jax.shard_map(body, mesh=mesh, in_specs=placed, out_specs=given, check_vma=False)
```

```python
import functools
import jax
import jax.numpy as jnp
from jax import lax
from jax.experimental import pallas as pl
from jax.experimental.pallas import tpu as pltpu

from jax.sharding import PartitionSpec as P

D = 2048
HD = 128
CONV = 4
BLOCK = 64
SEQ_DEV = 4
REAL_DEV = 1152
CAP = 1280
NB = CAP // BLOCK
EPSILON = 1e-06
HEAD_FLOOR = 0.01
F32 = jnp.float32
BF = jnp.bfloat16

def split(x):
    hi = x.astype(BF)
    return hi, (x - hi.astype(F32)).astype(BF)

NN=(((1,),(0,)),((),())); NT=(((1,),(1,)),((),())); TN=(((0,),(0,)),((),()))

def dg(a, b, dims):
    return lax.dot_general(a, b, dims, preferred_element_type=F32)

def d3(a, b, dims=NN):
    ah, al = split(a); bh, bl = split(b)
    return dg(ah, bh, dims) + (dg(ah, bl, dims) + dg(al, bh, dims))

def twice(step):
    return lambda i, c: step(2 * i + 1, step(2 * i, c))

def goes_on(pos_ref, n):
    first = pos_ref[pl.ds(pl.multiple_of(n * BLOCK, BLOCK), 8), :][:1]
    return jnp.where(first != 0, 1.0, 0.0)

def masks():
    ri = lax.broadcasted_iota(jnp.int32, (BLOCK, BLOCK), 0)
    ci = lax.broadcasted_iota(jnp.int32, (BLOCK, BLOCK), 1)
    return ri, ci

def sigmoid(x):
    return 1.0 / (1.0 + jnp.exp(-x))

def conv_rows(cur, tail, wt, pos):
    ext = jnp.concatenate([tail, cur], axis=0)
    out = wt[0] * cur
    for j in range(1, CONV):
        sh = pltpu.roll(ext, j, axis=0)[8:]
        out = out + wt[j] * jnp.where(pos >= j, sh, 0.0)
    return out

def inverses(lmats, ri, ci):
    apart = ri ^ ci
    xs = [jnp.where(apart == 0, 1.0, 0.0) - jnp.where(apart == 1, m, 0.0) for m in lmats]
    s = 2
    while s < BLOCK:
        at = (apart >= s) & (apart < 2 * s)
        ys = [d3(x, jnp.where(at, m, 0.0)) for x, m in zip(xs, lmats)]
        xs = [x - d3(y, x) for x, y in zip(xs, ys)]
        s *= 2
    return xs

def fwd_kernel(pre, pos_ref, fill_ref, cw, gain, mixed, *refs):
    given, (c_out, qk, w_out, u_out, u2_out, o_out, p_out, t_out, m_out, s_out, b_s), sem = refs[:10], refs[10:21], refs[21]
    held = (c_out, qk, w_out, u_out, u2_out, o_out, p_out, t_out, m_out, s_out)

    def keep(*which):
        for i in which:
            pltpu.make_async_copy(held[i], given[i], sem.at[i]).start()

    ri, ci = masks()
    heads = 2
    def phase_a(n, tails):
        r = pl.ds(pl.multiple_of(n * BLOCK, BLOCK), BLOCK)
        pos = pos_ref[r, :]; fil = fill_ref[r, :]
        new_tails = []
        acts = []
        for i in range(3):
            cur = pre[r, i*256:(i+1)*256]
            wt = [cw[j*3+i:j*3+i+1, :] for j in range(CONV)]
            cc = conv_rows(cur, tails[i], wt, pos)
            c_out[r, i*256:(i+1)*256] = cc
            acts.append(cc * sigmoid(cc) * fil)
            new_tails.append(cur[BLOCK-8:])
        beta = sigmoid(pre[r, 1024:1152])
        for h in range(heads):
            hs = slice(h*HD, (h+1)*HD)
            yq = acts[0][:, hs]; yk = acts[1][:, hs]; v = acts[2][:, hs]
            q = yq * lax.rsqrt(jnp.sum(yq*yq, axis=1, keepdims=True) + EPSILON)
            k = yk * lax.rsqrt(jnp.sum(yk*yk, axis=1, keepdims=True) + EPSILON)
            b = beta[:, h:h+1]
            qk[r, h*HD:(h+1)*HD] = q
            qk[r, 256+h*HD:256+(h+1)*HD] = k
            lmat = jnp.where(ri > ci, b * d3(k, k, NT), 0.0)
            p_out[n*2+h] = jnp.where(ri >= ci, d3(q, k, NT), 0.0)
            t_out[n*2+h] = lmat
            u_out[r, hs] = b*v
            w_out[r, hs] = b*k
        return tuple(new_tails)
    z8 = jnp.zeros((8, 256), F32)
    lax.fori_loop(0, NB // 2, twice(phase_a), (z8, z8, z8))
    keep(0, 1, 6)
    GRP = 8
    def phase_t(i, _):
        ts = inverses([t_out[i*GRP+j] for j in range(GRP)], ri, ci)
        for j in range(GRP):
            t_out[i*GRP+j] = ts[j]
        return 0
    lax.fori_loop(0, 2*NB//GRP, phase_t, 0)
    keep(7)
    def phase_w(i, _):
        todo = [(n, pl.ds(pl.multiple_of(n * BLOCK, BLOCK), BLOCK), h, slice(h*HD, (h+1)*HD)) for n in (2*i, 2*i+1) for h in range(heads)]
        wu = [d3(t_out[n*2+h], jnp.concatenate([w_out[r, c], u_out[r, c]], axis=1)) for n, r, h, c in todo]
        mb = [d3(qk[r, 256+h*HD:256+(h+1)*HD], x, TN) for x, (n, r, h, c) in zip(wu, todo)]
        for x, y, (n, r, h, c) in zip(wu, mb, todo):
            w_out[r, c] = x[:, :HD]; u_out[r, c] = x[:, HD:]
            m_out[n*2+h] = y[:, :HD]; b_s[n*2+h] = y[:, HD:]
        return 0
    lax.fori_loop(0, NB//2, phase_w, 0)
    keep(2, 3, 8)
    def phase_b(n, ss):
        out = []
        for h in range(heads):
            e = n*2+h
            s = ss[h] * goes_on(pos_ref, n)
            s_out[e] = s
            out.append(s - d3(m_out[e], s) + b_s[e])
        return tuple(out)
    zs = jnp.zeros((HD, HD), F32)
    lax.fori_loop(0, NB, phase_b, (zs, zs))
    keep(9)
    def phase_c(i, _):
        todo = [(n, pl.ds(pl.multiple_of(n * BLOCK, BLOCK), BLOCK), h, slice(h*HD, (h+1)*HD)) for n in (2*i, 2*i+1) for h in range(heads)]
        rr = [d3(jnp.concatenate([w_out[r, c], qk[r, c]], axis=0), s_out[n*2+h]) for n, r, h, c in todo]
        u2 = [u_out[r, c] - v[:BLOCK] for v, (n, r, h, c) in zip(rr, todo)]
        os_ = [v[BLOCK:] + d3(p_out[n*2+h], u) for v, u, (n, r, h, c) in zip(rr, u2, todo)]
        for o, u, (n, r, h, c) in zip(os_, u2, todo):
            u2_out[r, c] = u
            o_out[r, c] = o
            ms = jnp.mean(o*o, axis=1, keepdims=True)
            sc = lax.rsqrt(jnp.maximum(ms, HEAD_FLOOR))
            gg = pre[r, 768+h*HD:768+(h+1)*HD]
            mixed[r, c] = (o * sc * gain[...] * (gg * sigmoid(gg))).astype(BF)
        return 0
    lax.fori_loop(0, NB // 2, phase_c, 0)
    keep(4, 5)
    for i in range(10):
        pltpu.make_async_copy(held[i], given[i], sem.at[i]).wait()

def sds(*s, dt=F32): return jax.ShapeDtypeStruct(s, dt)
VM = pl.BlockSpec(memory_space=pltpu.VMEM)
SM = pl.BlockSpec(memory_space=pltpu.SMEM)

def mixer_fwd(pre, pos, fil, cw, gain):
    outs = (sds(CAP,256,dt=BF), sds(CAP,768), sds(CAP,512), sds(CAP,256), sds(CAP,256), sds(CAP,256), sds(CAP,256),
            sds(2*NB,BLOCK,BLOCK), sds(2*NB,BLOCK,BLOCK), sds(2*NB,HD,HD), sds(2*NB,HD,HD))
    return pl.pallas_call(fwd_kernel, out_shape=outs, in_specs=[VM]*5, out_specs=[VM]+[pl.BlockSpec(memory_space=pltpu.HBM)]*(len(outs)-1),
        scratch_shapes=[pltpu.VMEM(o.shape,F32) for o in outs[1:]]+[pltpu.VMEM((2*NB,HD,HD),F32), pltpu.SemaphoreType.DMA((10,))],
        compiler_params=pltpu.CompilerParams(vmem_limit_bytes=60*2**20), cost_estimate=pl.CostEstimate(flops=0, bytes_accessed=140 * 2**20, transcendentals=0),
        name="mixer_forward")(pre, pos, fil, cw, gain)

def bwd_kernel(dmix, pre, pos_ref, fill_ref, cw, gain, *refs):
    kept, (dpre, dcw, dgain), held, (e_s, do_s, sem) = refs[:10], refs[10:13], refs[13:23], refs[23:]
    c_in, qk, w_in, u_in, u2_in, o_in, p_in, t_in, m_in, s_in = held

    def fetch(i):
        return pltpu.make_async_copy(kept[i], held[i], sem.at[i])

    for i in (5, 6, 1, 2, 8, 7, 9, 0, 3, 4):
        fetch(i).start()
    for i in (5, 6, 1, 2):
        fetch(i).wait()
    ri, ci = masks()
    heads = 2
    lane = lax.broadcasted_iota(jnp.int32, (BLOCK, HD), 1)
    dgain[...] = jnp.zeros_like(dgain)
    dcw[...] = jnp.zeros_like(dcw)
    def phase_a(n, _):
        r = pl.ds(pl.multiple_of(n * BLOCK, BLOCK), BLOCK)
        for h in range(heads):
            hs = slice(h*HD, (h+1)*HD)
            e = n*2+h
            o = o_in[r, hs]; dm = dmix[r, hs]
            gg = pre[r, 768+h*HD:768+(h+1)*HD]
            sg = sigmoid(gg); si = gg*sg
            ms = jnp.mean(o*o, axis=1, keepdims=True)
            sc = lax.rsqrt(jnp.maximum(ms, HEAD_FLOOR))
            on = o*sc
            gn = gain[...]
            dpre[r, 768+h*HD:768+(h+1)*HD] = (dm * on * gn * (sg * (1.0 + gg*(1.0-sg)))).astype(BF)
            dgs = dm * on * si
            dgain[...] += jnp.sum(dgs.reshape(8, 8, HD), axis=0)
            dn = dm * gn * si
            corr = jnp.where(ms > HEAD_FLOOR, jnp.mean(dn*on, axis=1, keepdims=True), 0.0)
            do = sc * (dn - on*corr)
            do_s[r, hs] = do
            pdo = d3(p_in[e], do, TN)
            qw = jnp.concatenate([qk[r, hs], w_in[r, hs]], axis=0)
            dd = jnp.concatenate([do, -pdo], axis=0)
            e_s[e] = d3(qw, dd, TN)
        return 0
    lax.fori_loop(0, NB // 2, twice(phase_a), 0)
    fetch(8).wait()

    def phase_b(i, ds):
        n = NB-1-i
        out = []
        for h in range(heads):
            e = n*2+h
            d = ds[h]
            ee = e_s[e]
            e_s[e] = d
            out.append((d - d3(m_in[e], d, TN) + ee) * goes_on(pos_ref, n))
        return tuple(out)
    zs = jnp.zeros((HD, HD), F32)
    lax.fori_loop(0, NB, phase_b, (zs, zs))
    for i in (7, 9, 0, 3, 4):
        fetch(i).wait()

    def phase_c(i, heads_dc):
        blocks = (NB - 1 - 2 * i, NB - 2 - 2 * i)
        todo = [(n, pl.ds(pl.multiple_of(n * BLOCK, BLOCK), BLOCK), h, slice(h*HD, (h+1)*HD)) for n in blocks for h in range(heads)]
        def every(f, *lists):
            return [f(*v) for v in zip(*lists)]
        ns, rs, hh, hs = zip(*todo)
        es = [n*2+h for n, h in zip(ns, hh)]
        fil = [fill_ref[r, :] for r in rs]
        beta_t = [sigmoid(pre[r, 1024:1152]) for r in rs]
        q = [qk[r, c] for r, c in zip(rs, hs)]
        k = [qk[r, 256+h*HD:256+(h+1)*HD] for r, h in zip(rs, hh)]
        w = [w_in[r, c] for r, c in zip(rs, hs)]
        u = [u_in[r, c] for r, c in zip(rs, hs)]
        u2 = [u2_in[r, c] for r, c in zip(rs, hs)]
        do = [do_s[r, c] for r, c in zip(rs, hs)]
        p = [p_in[e] for e in es]
        t = [t_in[e] for e in es]
        s = [s_in[e] for e in es]
        ds = [e_s[e] for e in es]
        b = [x[:, h:h+1] for x, h in zip(beta_t, hh)]
        du2 = every(lambda p, do, k, ds: d3(p, do, TN) + d3(k, ds), p, do, k, ds)
        dp = every(lambda do, u2: jnp.where(ri >= ci, d3(do, u2, NT), 0.0), do, u2)
        g = every(lambda k: d3(k, k, NT), k)
        xs = every(lambda do, du2, s: d3(jnp.concatenate([do, -du2], axis=0), s, NT), do, du2, s)
        dq = every(lambda xs, dp, k: xs[:BLOCK] + d3(dp, k), xs, dp, k)
        xx = every(lambda t, xs, du2: d3(t, jnp.concatenate([xs[BLOCK:], du2], axis=1), TN), t, xs, du2)
        dk = every(lambda dp, q, u2, ds: d3(dp, q, TN) + d3(u2, ds, NT), dp, q, u2, ds)
        mm = every(lambda xx, w, u: jnp.where(ri > ci, -d3(xx, jnp.concatenate([w, u], axis=1), NT), 0.0), xx, w, u)
        cv = [c_in[r, 512+h*HD:512+(h+1)*HD] for r, h in zip(rs, hh)]
        sv = every(sigmoid, cv)
        bm = every(lambda b, mm: b*mm, b, mm)
        dk = every(lambda dk, bm, k, b, xx: dk + d3(bm + bm.T, k) + b*xx[:, :HD], dk, bm, k, b, xx)
        db = every(lambda mm, g, xx, k, cv, sv, fil: jnp.sum(mm*g, axis=1, keepdims=True)
                   + jnp.sum(xx[:, :HD]*k + xx[:, HD:]*(cv*sv*fil), axis=1, keepdims=True), mm, g, xx, k, cv, sv, fil)
        cq = [c_in[r, c] for r, c in zip(rs, hs)]
        ck = [c_in[r, 256+h*HD:256+(h+1)*HD] for r, h in zip(rs, hh)]
        def unit_back(c, fil, n, d):
            sg = sigmoid(c)
            y = c*sg*fil
            r = lax.rsqrt(jnp.sum(y*y, axis=1, keepdims=True) + EPSILON)
            return r*(d - n*jnp.sum(d*n, axis=1, keepdims=True))*fil*(sg*(1.0+c*(1.0-sg)))
        aq = every(unit_back, cq, fil, q, dq)
        ak = every(unit_back, ck, fil, k, dk)
        av = every(lambda b, xx, fil, sv, cv: b*xx[:, HD:]*fil*(sv*(1.0+cv*(1.0-sv))), b, xx, fil, sv, cv)
        for j, n in enumerate(blocks):
            r = rs[2*j]
            dbt = jnp.where(lane == 0, db[2*j], jnp.where(lane == 1, db[2*j+1], 0.0))
            dpre[r, 1024:1152] = (dbt*beta_t[2*j]*(1.0-beta_t[2*j])).astype(BF)
            pos = pos_ref[r, :]
            nxt = jnp.minimum(n+1, NB-1)
            posx = jnp.concatenate([pos, pos_ref[pl.ds(pl.multiple_of(nxt*BLOCK, BLOCK), 8), :]], axis=0)
            prv = jnp.maximum(n*BLOCK-8, 0)
            new = []
            for i, acts in enumerate((aq, ak, av)):
                dc = jnp.concatenate(acts[2*j:2*j+2], axis=1)
                ext = jnp.concatenate([dc, heads_dc[i]], axis=0)
                cur = pre[r, i*256:(i+1)*256]
                tail = pre[pl.ds(pl.multiple_of(prv, 8), 8), i*256:(i+1)*256]
                xext = jnp.concatenate([tail, cur], axis=0)
                dx = cw[i:i+1, :]*dc
                dcw[i] += jnp.sum((dc*cur).reshape(8, 8, 256), axis=0)
                for o in range(1, CONV):
                    z = jnp.where(posx >= o, ext, 0.0)
                    dx = dx + cw[o*3+i:o*3+i+1, :]*pltpu.roll(z, BLOCK+8-o, axis=0)[:BLOCK]
                    sh = pltpu.roll(xext, o, axis=0)[8:]
                    dcw[o*3+i] += jnp.sum(jnp.where(pos >= o, dc*sh, 0.0).reshape(8, 8, 256), axis=0)
                dpre[r, i*256:(i+1)*256] = dx.astype(BF)
                new.append(dc[:8])
            heads_dc = tuple(new)
        return heads_dc
    z8 = jnp.zeros((8, 256), F32)
    lax.fori_loop(0, NB // 2, phase_c, (z8, z8, z8))

def mixer_bwd(dmix, pre, pos, fil, cw, gain, saved):
    outs = (sds(CAP,1152,dt=BF), sds(12,8,256), sds(8,HD))
    return pl.pallas_call(bwd_kernel, out_shape=outs, in_specs=[VM]*6+[pl.BlockSpec(memory_space=pltpu.HBM)]*len(saved), out_specs=[VM]*3,
        scratch_shapes=[pltpu.VMEM(a.shape, F32) for a in saved]+[pltpu.VMEM((2*NB,HD,HD),F32), pltpu.VMEM((CAP,256),F32), pltpu.SemaphoreType.DMA((10,))],
        compiler_params=pltpu.CompilerParams(vmem_limit_bytes=60*2**20), cost_estimate=pl.CostEstimate(flops=0, bytes_accessed=200 * 2**20, transcendentals=0),
        name="mixer_backward")(dmix, pre, pos, fil, cw, gain, *saved)


MESH = pl.DeviceIdType.MESH
ROOM = 60 * 2**20
LINK_COST = 150 * 2**20
HBM = pl.BlockSpec(memory_space=pltpu.HBM)


def places():
    s, h, t = lax.axis_index("shard"), lax.axis_index("head"), lax.axis_index("tensor")
    return h, t, (s, h + 1, t), (s, h - 1, t), (s, h, 1 - t)


def shard_peers(m):
    s, h, t = lax.axis_index("shard"), lax.axis_index("head"), lax.axis_index("tensor")
    return [((lax.rem(s + i, m), h, t), lax.rem(s + i, m)) for i in range(1, m)]


class Carry:
    def __init__(self, hops, kinds, m, ins, outs, send, recv, here):
        self.hops, self.kinds, self.m, self.ins, self.outs = hops, kinds, m, ins, outs
        self.send, self.recv, self.here = send, recv, here
        s, self.h, self.t = lax.axis_index("shard"), lax.axis_index("head"), lax.axis_index("tensor")
        self.me = s
        self.side = s + 1 - 2 * lax.rem(s, 2)
        self.over = lax.rem(s + 2, 4)
        self.corner = lax.rem(self.side + 2, 4)

    def relayed(self, e):
        return self.hops and self.m == 4 and self.kinds[e] in ("gather", "abreast")

    def part(self, e, src, half=None):
        rows = self.ins[e].shape[0]
        span = pl.ds(0, rows) if half is None else pl.ds(half * (rows // 2), rows // 2)
        if self.kinds[e] == "gather":
            first = src * rows + (0 if half is None else half * (rows // 2))
            return self.outs[e].at[pl.ds(pl.multiple_of(first, rows // 2), span.size)]
        if self.kinds[e] == "abreast":
            w = self.ins[e].shape[1]
            return self.outs[e].at[span, pl.ds(pl.multiple_of(src * w, w), w)]
        return self.outs[e].at[src]

    def given(self, e, dst):
        if self.kinds[e] == "columns":
            w = self.ins[e].shape[1] // self.m
            return self.ins[e].at[:, pl.ds(pl.multiple_of(dst * w, w), w)]
        return self.ins[e].at[dst] if self.kinds[e] == "swap" else self.ins[e]

    def move(self, e, src, dst, i, j, to):
        return pltpu.make_async_remote_copy(src_ref=src, dst_ref=dst, send_sem=self.send.at[e, i], recv_sem=self.recv.at[e, j],
                                            device_id=(to, self.h, self.t), device_id_type=MESH)

    def copy(self, e, i, to):
        return self.move(e, self.given(e, to), self.part(e, self.me), i, self.me, to)

    def came(self, e, src):
        return self.move(e, self.given(e, src), self.part(e, src), 0, src, src)

    def hand(self, e, half):
        src, to = (self.side, self.over) if half == 0 else (self.over, self.side)
        piece = self.part(e, src, half)
        return self.move(e, piece, piece, 2 + half, src if half == 0 else self.m, to)

    def handed(self, e, half):
        piece = self.part(e, self.corner, half)
        return self.move(e, piece, piece, 2 + half, self.corner if half == 0 else self.m, self.over if half == 0 else self.side)

    def local(self, e):
        return pltpu.make_async_copy(self.given(e, self.me), self.part(e, self.me), self.here.at[e])

    def targets(self, e):
        return [self.side, self.over] if self.relayed(e) else [p[1] for p in shard_peers(self.m)]

    def greet(self):
        barrier = pltpu.get_barrier_semaphore()
        if self.kinds:
            for p, _ in shard_peers(self.m):
                pl.semaphore_signal(barrier, inc=1, device_id=p, device_id_type=MESH)
        return self.m - 1 if self.kinds else 0

    def start(self):
        for e in range(len(self.kinds)):
            for i, to in enumerate(self.targets(e)):
                self.copy(e, i, to).start()
            self.local(e).start()

    def relay(self, e):
        if e < len(self.kinds) and self.relayed(e):
            self.came(e, self.side).wait_recv()
            self.hand(e, 0).start()
            self.came(e, self.over).wait_recv()
            self.hand(e, 1).start()

    def wait(self):
        for e in range(len(self.kinds)):
            self.local(e).wait()
            for i, to in enumerate(self.targets(e)):
                self.copy(e, i, to).wait_send()
                if not self.relayed(e):
                    self.came(e, to).wait_recv()
            if self.relayed(e):
                for half in range(2):
                    self.handed(e, half).wait_recv()
                    self.hand(e, half).wait_send()


def carried(kinds, m, arrays):
    dma = pltpu.SemaphoreType.DMA
    give = {"gather": lambda a: (m * a.shape[0], a.shape[1]), "swap": lambda a: a.shape,
            "abreast": lambda a: (a.shape[0], m * a.shape[1]), "pile": lambda a: (m,) + a.shape,
            "columns": lambda a: (m, a.shape[0], a.shape[1] // m)}
    shapes = [jax.ShapeDtypeStruct(give[k](a), a.dtype) for k, a in zip(kinds, arrays)]
    e = len(kinds)
    return shapes, ([dma((e, m + 1)), dma((e, m + 1)), dma((e,))] if e else [])


def carry_of(kinds, m, refs, n_in, n_out, hops=False):
    e = len(kinds)
    ins, refs = refs[:n_in], refs[n_in:]
    c_in, refs = refs[:e], refs[e:]
    outs, refs = refs[:n_out], refs[n_out:]
    c_out, refs = refs[:e], refs[e:]
    sems = (refs[-3:] if e else (None,) * 3)
    scratch = refs[:-3] if e else refs
    return ins, outs, scratch, Carry(hops, kinds, m, c_in, c_out, *sems)


def greet(n, h, up, down, across, more=0):
    barrier = pltpu.get_barrier_semaphore()
    pl.semaphore_signal(barrier, inc=1, device_id=across, device_id_type=MESH)

    @pl.when(h < n - 1)
    def _():
        pl.semaphore_signal(barrier, inc=1, device_id=up, device_id_type=MESH)

    @pl.when(h > 0)
    def _():
        pl.semaphore_signal(barrier, inc=1, device_id=down, device_id_type=MESH)

    pl.semaphore_wait(barrier, 1 + more + (h < n - 1).astype(jnp.int32) + (h > 0).astype(jnp.int32))


class Plan:
    def __init__(self, m, per_peer, lengths, dealing, starts):
        self.m, self.per_peer, self.lengths, self.dealing, self.starts = m, per_peer, lengths, dealing, starts
        self.shift = m.bit_length() - 1
        self.device = lax.axis_index("shard")

        def begin(q, total):
            starts[q] = total
            return total + lengths[q]

        lax.fori_loop(0, lengths.shape[0], begin, jnp.int32(0))

    def under(self, row, residue):
        return lax.shift_right_arithmetic(row - 1 - residue + self.m, self.shift + jnp.zeros_like(row))

    def members(self, g):
        at = [self.dealing[g * SEQ_DEV + i] for i in range(SEQ_DEV)]
        return [(self.starts[q], self.lengths[q]) for q in at]

    def sent(self, ids):
        packed = ids * self.m + self.device

        def group(g, slot):
            seqs = self.members(g)
            counts = [self.under(s + n, self.device) - self.under(s, self.device) for s, n in seqs]
            for s, n in seqs:
                first = g * self.per_peer - self.under(s, self.device)
                for (other, _), count in zip(seqs, counts):
                    first = first + jnp.where(other < s, count, 0)
                slot = slot + jnp.where((packed >= s) & (packed < s + n), first, 0)
            return slot

        return lax.fori_loop(0, self.lengths.shape[0] // SEQ_DEV, group, ids)

    def rows(self, ids):
        seqs = self.members(self.device)
        place, start, length, below = ids, jnp.zeros_like(ids), jnp.zeros_like(ids), jnp.int32(0)
        for s, n in seqs:
            here = ids >= below
            place = jnp.where(here, ids - below, place)
            start = jnp.where(here, s, start)
            length = jnp.where(here, n, length)
            below = below + lax.shift_right_arithmetic(n + BLOCK - 1, jnp.int32(6)) * BLOCK
        filled = place < length
        natural = start + place
        source = natural & (self.m - 1)
        slot = source * self.per_peer + self.under(natural, source) - self.under(start, source)
        for s, n in seqs:
            span = self.under(jnp.zeros_like(ids) + (s + n), source) - self.under(jnp.zeros_like(ids) + s, source)
            slot = slot + jnp.where(s < start, span, 0)
        return place, filled, jnp.where(filled, slot, -1)


def gather_kernel(n, width, m, kinds, *refs):
    (lengths, dealing, tokens), (x, out, sent_at, slot_at, pos_at, fill_at), scratch, carry = carry_of(kinds, m, refs, 3, 6)
    place_at, starts, outbox, inbox, deal_s, deal_r, here, up_s, up_r, down_s, down_r, core_s, core_r = scratch
    h, t, up, down, across = places()
    per_peer = outbox.shape[1]

    def cols(j):
        return out.at[:, pl.ds(pl.multiple_of((j * 2 + t) * width, width), width)]

    def other(j):
        return out.at[:, pl.ds(pl.multiple_of((j * 2 + 1 - t) * width, width), width)]

    def send(j, src, ss, rs, to):
        return pltpu.make_async_remote_copy(src_ref=src, dst_ref=cols(j), send_sem=ss.at[j], recv_sem=rs.at[j],
                                            device_id=to, device_id_type=MESH)

    greet(n, h, up, down, across, carry.greet())
    plan = Plan(m, per_peer, lengths, dealing, starts)
    peers = shard_peers(m)
    mine = lax.axis_index("shard")
    sent = plan.sent(lax.broadcasted_iota(jnp.int32, (1, REAL_DEV), 1))
    ids = lax.broadcasted_iota(jnp.int32, (per_peer, REAL_DEV), 0)

    def deal(i, p, src):
        return pltpu.make_async_remote_copy(src_ref=outbox.at[p[1]], dst_ref=inbox.at[src], send_sem=deal_s.at[i],
                                            recv_sem=deal_r.at[src], device_id=p[0], device_id_type=MESH)

    def pick(q):
        return dg(jnp.where(sent - q * per_peer == ids, 1.0, 0.0).astype(BF), tokens[...], NN).astype(BF)

    for i, p in enumerate(peers):
        outbox[p[1]] = pick(p[1])
        deal(i, p, mine).start()
    carry.start()
    inbox[mine] = pick(mine)
    place_at[...] = plan.rows(lax.broadcasted_iota(jnp.int32, (CAP, 1), 0))[2]
    for i, p in enumerate(peers):
        deal(i, p, p[1]).wait_recv()
    lanes = lax.broadcasted_iota(jnp.int32, (STEP, m * per_peer), 1)

    def settle(i, c):
        r = pl.ds(pl.multiple_of(i * STEP, STEP), STEP)
        chosen = jnp.where(place_at[r, :] == lanes, 1.0, 0.0).astype(BF)
        x[r, :] = dg(chosen, inbox[...].reshape(m * per_peer, width), NN).astype(BF)
        return c

    lax.fori_loop(0, CAP // STEP, settle, 0)
    local = pltpu.make_async_copy(x, cols(h), here)
    local.start()

    @pl.when(h < n - 1)
    def _():
        send(h, x, up_s, up_r, up).start()

    @pl.when(h > 0)
    def _():
        send(h, x, down_s, down_r, down).start()

    send(h, x, core_s, core_r, across).start()
    sent_at[...] = plan.sent(lax.broadcasted_iota(jnp.int32, (REAL_DEV, 1), 0))
    slot_at[...] = plan.rows(lax.broadcasted_iota(jnp.int32, (1, CAP), 1))[2]
    position, filled, _ = plan.rows(lax.broadcasted_iota(jnp.int32, (CAP, 1), 0))
    pos_at[...] = position
    fill_at[...] = jnp.where(filled, 1.0, 0.0)
    for k in range(1, n):
        below, above = h - k, h + k

        @pl.when(below >= 0)
        def _():
            send(below, cols(below), up_s, up_r, up).wait_recv()

            @pl.when(h < n - 1)
            def _():
                send(below, cols(below), up_s, up_r, up).start()

            send(below, cols(below), core_s, core_r, across).start()

        @pl.when(above < n)
        def _():
            send(above, cols(above), down_s, down_r, down).wait_recv()

            @pl.when(h > 0)
            def _():
                send(above, cols(above), down_s, down_r, down).start()

            send(above, cols(above), core_s, core_r, across).start()

    for j in range(n):
        back = pltpu.make_async_remote_copy(src_ref=cols(j), dst_ref=other(j), send_sem=core_s.at[j], recv_sem=core_r.at[j],
                                            device_id=across, device_id_type=MESH)
        back.wait_recv()
        back.wait_send()

        @pl.when((j <= h) & (h < n - 1))
        def _():
            send(j, cols(j), up_s, up_r, up).wait_send()

        @pl.when((j >= h) & (h > 0))
        def _():
            send(j, cols(j), down_s, down_r, down).wait_send()

    local.wait()
    for i, p in enumerate(peers):
        deal(i, p, mine).wait_send()
    carry.wait()


def z_gather(n, lengths, dealing, tokens, per_peer, collective_id, name, m, kinds, arrays):
    width = tokens.shape[1]
    dma = pltpu.SemaphoreType.DMA
    sd = jax.ShapeDtypeStruct
    shapes, sems = carried(kinds, m, arrays)
    return pl.pallas_call(
        functools.partial(gather_kernel, n, width, m, kinds),
        out_shape=[sd((CAP, width), BF), sd((CAP, 2 * n * width), BF), sd((REAL_DEV, 1), jnp.int32), sd((1, CAP), jnp.int32),
                   sd((CAP, 1), jnp.int32), sd((CAP, 1), F32)] + shapes,
        in_specs=[SM, SM, VM] + [HBM] * len(shapes), out_specs=[VM, HBM] + [VM] * 4 + [HBM] * len(shapes),
        scratch_shapes=[pltpu.VMEM((CAP, 1), jnp.int32), pltpu.SMEM(lengths.shape, jnp.int32)]
        + [pltpu.VMEM((m, per_peer, width), BF)] * 2 + [dma((m,)), dma((m,)), dma] + [dma((n,))] * 6 + sems,
        compiler_params=pltpu.CompilerParams(collective_id=collective_id, has_side_effects=True, vmem_limit_bytes=ROOM),
        cost_estimate=pl.CostEstimate(flops=0, bytes_accessed=LINK_COST, transcendentals=0),
        name=name,
    )(lengths, dealing, tokens, *arrays)


STEP = 128


def group_peers(n):
    s, h, t = lax.axis_index("shard"), lax.axis_index("head"), lax.axis_index("tensor")
    peers = []
    for i in range(1, 2 * n):
        hh, tt = lax.rem(h + i // 2, n), lax.rem(t + i % 2, 2)
        peers.append(((s, hh, tt), hh * 2 + tt))
    return peers


def greet_group(n, more=0):
    barrier = pltpu.get_barrier_semaphore()
    for p, _ in group_peers(n):
        pl.semaphore_signal(barrier, inc=1, device_id=p, device_id_type=MESH)
    pl.semaphore_wait(barrier, 2 * n - 1 + more)


def finish_kernel(n, width, m, kinds, *refs):
    (part, kept, scale, base, gain, share, small, sent, place), (tokens, every), scratch, carry = carry_of(kinds, m, refs, 9, 2)
    (low, dgain, outbox, inbox, deal_s, deal_r, held, ours, shard_s, shard_r, group_s, group_r,
     acc, tots, tot_s, tot_r, mine, theirs, from_below, from_above,
     here, core_s, core_r, up_s, up_r, down_s, down_r) = scratch
    h, t, up, down, across = places()

    def cols(j, c):
        return part.at[:, pl.ds(pl.multiple_of((j * 2 + c) * width, width), width)]

    def swap(j):
        return pltpu.make_async_remote_copy(src_ref=cols(j, 1 - t), dst_ref=theirs.at[j], send_sem=core_s.at[j],
                                            recv_sem=core_r.at[j], device_id=across, device_id_type=MESH)

    def own(j):
        return pltpu.make_async_copy(cols(j, t), mine.at[j], here.at[j])

    def rise(k):
        return pltpu.make_async_remote_copy(src_ref=mine.at[n - 1 - k], dst_ref=from_below.at[k], send_sem=up_s.at[k],
                                            recv_sem=up_r.at[k], device_id=up, device_id_type=MESH)

    def fall(k):
        return pltpu.make_async_remote_copy(src_ref=mine.at[k], dst_ref=from_above.at[k], send_sem=down_s.at[k],
                                            recv_sem=down_r.at[k], device_id=down, device_id_type=MESH)

    def total(j, extra):
        def step(i, c):
            r = pl.ds(pl.multiple_of(i * STEP, STEP), STEP)
            v = mine[j, r, :].astype(F32) + theirs[j, r, :].astype(F32)
            if extra is not None:
                v = v + extra(r).astype(F32)
            mine[j, r, :] = v.astype(BF)
            return c
        lax.fori_loop(0, CAP // STEP, step, 0)

    order = [j for i in range(n // 2) for j in (n - 1 - i, i)]
    for j in order:
        own(j).start()
    greet_group(n, carry.greet())
    me = h * 2 + t
    peers = group_peers(n)

    def tot_copy(i, p, dst):
        return pltpu.make_async_remote_copy(src_ref=share, dst_ref=tots.at[dst], send_sem=tot_s.at[i], recv_sem=tot_r.at[dst],
                                            device_id=p, device_id_type=MESH)

    for i, p in enumerate(peers):
        tot_copy(i, p[0], me).start()
    for j in order:
        swap(j).start()
    carry.start()

    def arrive(j):
        own(j).wait()
        swap(j).wait_recv()

    for tick in range(2 * n - 2):
        ku = tick - h
        tu = n - 1 - ku

        @pl.when((ku >= 0) & (tu > h))
        def _():
            arrive(tu)

            @pl.when(h == 0)
            def _():
                total(tu, None)

            @pl.when(h > 0)
            def _():
                rise(ku).wait_recv()
                total(tu, lambda r: from_below[ku, r, :])

            rise(ku).start()

        kd = tick - (n - 1 - h)

        @pl.when((kd >= 0) & (kd < h))
        def _():
            arrive(kd)

            @pl.when(h == n - 1)
            def _():
                total(kd, None)

            @pl.when(h < n - 1)
            def _():
                fall(kd).wait_recv()
                total(kd, lambda r: from_above[kd, r, :])

            fall(kd).start()

    arrive(h)
    for i, p in enumerate(peers):
        tot_copy(i, p[0], p[1]).wait_recv()
    tots[me] = share[...]
    for i, p in enumerate(peers):
        tots[me] = tots[me] + tots[p[1]]
    dgain[...] = jnp.zeros_like(dgain)
    gains = gain[...]
    eighth = jnp.full((8, 128), 0.125, BF)

    def final(get):
        def step(i, c):
            r = pl.ds(pl.multiple_of(i * STEP, STEP), STEP)
            acc[r, :] = get(r)
            return c
        lax.fori_loop(0, CAP // STEP, step, 0)

    final(lambda r: mine[h, r, :].astype(F32) + theirs[h, r, :].astype(F32))

    def first(get):
        final(lambda r: acc[r, :] + get(r).astype(F32))

    @pl.when((h > 0) & (h < n - 1))
    def _():
        @pl.when(2 * h < n)
        def _():
            fall(h).wait_recv()
            first(lambda r: from_above[h, r, :])

        @pl.when(2 * h >= n)
        def _():
            rise(n - 1 - h).wait_recv()
            first(lambda r: from_below[n - 1 - h, r, :])

    by_below = (h > 0) & ((2 * h < n) | (h == n - 1))

    @pl.when(by_below)
    def _():
        rise(n - 1 - h).wait_recv()

    @pl.when(jnp.logical_not(by_below))
    def _():
        fall(h).wait_recv()

    def close(get):
        def step(i, c):
            r = pl.ds(pl.multiple_of(i * STEP, STEP), STEP)
            hi, lo = split(tots[me, i])
            total_r = dg(hi, eighth, TN) + dg(lo, eighth, TN)
            sc = scale[r, :]
            kp = kept[r, :].astype(F32)
            dn = acc[r, :] + get(r).astype(F32)
            back = base[r, :].astype(F32) + sc * (gains * dn) - kp * jnp.tile((sc * sc * sc) * (total_r * (1.0 / D)), (1, width // 128))
            low[r, :] = back.astype(BF)
            dgain[...] += jnp.sum((dn * kp * sc).reshape(STEP // 8, 8, width), axis=0)
            return c
        lax.fori_loop(0, CAP // STEP, step, 0)

    @pl.when(by_below)
    def _():
        close(lambda r: from_below[n - 1 - h, r, :])

    @pl.when(jnp.logical_not(by_below))
    def _():
        close(lambda r: from_above[h, r, :])

    for i, p in enumerate(peers):
        tot_copy(i, p[0], me).wait_send()

    others = shard_peers(m)
    shard = lax.axis_index("shard")
    per_peer = outbox.shape[1]
    ids = lax.broadcasted_iota(jnp.int32, (per_peer, place.shape[1]), 0)

    def back(i, p, src):
        return pltpu.make_async_remote_copy(src_ref=outbox.at[p[1]], dst_ref=inbox.at[src], send_sem=deal_s.at[i],
                                            recv_sem=deal_r.at[src], device_id=p[0], device_id_type=MESH)

    def pick(q):
        return dg(jnp.where(place[...] - q * per_peer == ids, 1.0, 0.0).astype(BF), low[...], NN).astype(BF)

    def over(i, p, src):
        return pltpu.make_async_remote_copy(src_ref=ours, dst_ref=held.at[src], send_sem=shard_s.at[i],
                                            recv_sem=shard_r.at[src], device_id=p[0], device_id_type=MESH)

    def along(i, p, src):
        return pltpu.make_async_remote_copy(src_ref=held.at[shard], dst_ref=every.at[src], send_sem=group_s.at[i],
                                            recv_sem=group_r.at[src], device_id=p[0], device_id_type=MESH)

    for i, p in enumerate(others):
        outbox[p[1]] = pick(p[1])
        back(i, p, shard).start()
    at = lax.broadcasted_iota(jnp.int32, small.shape, 0)
    ours[...] = small[...] + jnp.where(at == 12, jnp.sum(dgain[...], axis=0, keepdims=True), 0.0)
    for i, p in enumerate(others):
        over(i, p, shard).start()
    inbox[shard] = pick(shard)
    v = ours[...]
    for i, p in enumerate(others):
        over(i, p, p[1]).wait_recv()
        v = v + held[p[1]]
    held[shard] = v
    every[me] = v
    for i, p in enumerate(peers):
        along(i, p, me).start()
    for i, p in enumerate(others):
        back(i, p, p[1]).wait_recv()
    lanes = lax.broadcasted_iota(jnp.int32, (STEP, m * per_peer), 1)

    def settle(i, c):
        r = pl.ds(pl.multiple_of(i * STEP, STEP), STEP)
        chosen = jnp.where(sent[r, :] == lanes, 1.0, 0.0).astype(BF)
        tokens[r, :] = dg(chosen, inbox[...].reshape(m * per_peer, width), NN)
        return c

    lax.fori_loop(0, REAL_DEV // STEP, settle, 0)
    for i, p in enumerate(peers):
        along(i, p, p[1]).wait_recv()
        along(i, p, me).wait_send()
    for i, p in enumerate(others):
        over(i, p, shard).wait_send()
        back(i, p, shard).wait_send()
    for j in range(n):
        swap(j).wait_send()
    for k in range(n - 1):
        @pl.when(n - 1 - k > h)
        def _():
            rise(k).wait_send()

        @pl.when(k < h)
        def _():
            fall(k).wait_send()
    carry.wait()


def z_finish(n, part, kept, scale, base, gain, share, small, sent, place, per_peer, collective_id, name, m, kinds, arrays):
    rows, width = part.shape[0], part.shape[1] // (2 * n)
    dma = pltpu.SemaphoreType.DMA
    shapes, sems = carried(kinds, m, arrays)
    return pl.pallas_call(
        functools.partial(finish_kernel, n, width, m, kinds),
        out_shape=[jax.ShapeDtypeStruct((REAL_DEV, width), F32), jax.ShapeDtypeStruct((2 * n,) + small.shape, F32)] + shapes,
        in_specs=[HBM] + [VM] * 8 + [HBM] * len(shapes), out_specs=[VM] * 2 + [HBM] * len(shapes),
        scratch_shapes=[pltpu.VMEM((rows, width), BF), pltpu.VMEM((8, width), F32)]
        + [pltpu.VMEM((m, per_peer, width), BF)] * 2 + [dma((m,))] * 2
        + [pltpu.VMEM((m,) + small.shape, F32), pltpu.VMEM(small.shape, F32), dma((m,)), dma((m,)), dma((2 * n,)), dma((2 * n,))]
        + [pltpu.VMEM((rows, width), F32), pltpu.VMEM((2 * n, rows // STEP, 8, STEP), F32), dma((2 * n,)), dma((2 * n,))]
        + [pltpu.VMEM((n, rows, width), BF)] * 2 + [pltpu.VMEM((n - 1, rows, width), BF)] * 2
        + [dma((n,))] * 3 + [dma((n - 1,))] * 4 + sems,
        compiler_params=pltpu.CompilerParams(collective_id=collective_id, has_side_effects=True, vmem_limit_bytes=ROOM),
        cost_estimate=pl.CostEstimate(flops=0, bytes_accessed=LINK_COST, transcendentals=0),
        name=name,
    )(part, kept, scale, base, gain, share, small, sent, place, *arrays)


CHUNKS = 4
SUBS = 4
UNITS = CHUNKS * SUBS
UNIT = CAP // UNITS


def turn_kernel(n, width, m, kinds, norm, *refs):
    if norm:
        (part, kept, scale, base, gain, share), (out, full, low, dgain), scratch, carry = carry_of(kinds, m, refs, 6, 4)
        tots, tot_s, tot_r = scratch[-3:]
        scratch = scratch[:-3]
    else:
        (part, base), (out, full, low), scratch, carry = carry_of(kinds, m, refs, 2, 3, True)
    (mine, theirs, from_below, from_above, here, core_s, core_r, up_s, up_r, down_s, down_r,
     gu_s, gu_r, gd_s, gd_r, gc_s, gc_r, flat) = scratch
    h, t, up, down, across = places()
    me = h * 2 + t
    chunks = CHUNKS

    def rows(u):
        return pl.ds(pl.multiple_of(u * UNIT, UNIT), UNIT)

    def wide(r):
        return pl.ds(pl.multiple_of(r * SUBS * UNIT, SUBS * UNIT), SUBS * UNIT)

    def lanes(j, c):
        return pl.ds(pl.multiple_of((j * 2 + c) * width, width), width)

    def remote(src, dst, ss, rs, to):
        return pltpu.make_async_remote_copy(src_ref=src, dst_ref=dst, send_sem=ss, recv_sem=rs, device_id=to, device_id_type=MESH)

    def swap(j, r):
        return remote(part.at[wide(r), lanes(j, 1 - t)], theirs.at[j, wide(r)], core_s.at[j, r], core_r.at[j, r], across)

    def own(j, r):
        return pltpu.make_async_copy(part.at[wide(r), lanes(j, t)], mine.at[j, wide(r)], here.at[j, r])

    def rise(k, u):
        return remote(mine.at[n - 1 - k, rows(u)], from_below.at[k, rows(u)], up_s.at[k, u], up_r.at[k, u], up)

    def fall(k, u):
        return remote(mine.at[k, rows(u)], from_above.at[k, rows(u)], down_s.at[k, u], down_r.at[k, u], down)

    def spread(j, u, src, ss, rs, to):
        return remote(src, full.at[rows(u), lanes(j, t)], ss.at[j, u], rs.at[j, u], to)

    def piece(j, u):
        return full.at[rows(u), lanes(j, t)]

    def tot_copy(i, p, dst):
        return remote(share, tots.at[dst], tot_s.at[i], tot_r.at[dst], p)

    order = [j for i in range(n // 2) for j in (n - 1 - i, i)]
    for r in range(chunks):
        for j in order:
            own(j, r).start()
    if norm:
        greet_group(n, carry.greet())
        for i, p in enumerate(group_peers(n)):
            tot_copy(i, p[0], me).start()
        dgain[...] = jnp.zeros_like(dgain)
    else:
        greet(n, h, up, down, across, carry.greet())
    for r in range(chunks):
        for j in order:
            swap(j, r).start()
    carry.start()

    def arrive(j, r):
        own(j, r).wait()
        swap(j, r).wait_recv()

    def both(j, u):
        return mine[j, rows(u), :].astype(F32) + theirs[j, rows(u), :].astype(F32)

    def climb(o, r, s):
        u = SUBS * r + s

        @pl.when(h <= o)
        def _():
            ku = o - h
            tu = n - 1 - ku
            if s == 0:
                arrive(tu, r)

            @pl.when(h == 0)
            def _():
                mine[tu, rows(u), :] = both(tu, u).astype(BF)

            @pl.when(h > 0)
            def _():
                rise(ku, u).wait_recv()
                mine[tu, rows(u), :] = (both(tu, u) + from_below[ku, rows(u), :].astype(F32)).astype(BF)

            rise(ku, u).start()

        @pl.when(h >= n - 1 - o)
        def _():
            kd = o - (n - 1 - h)
            if s == 0:
                arrive(kd, r)

            @pl.when(h == n - 1)
            def _():
                mine[kd, rows(u), :] = both(kd, u).astype(BF)

            @pl.when(h < n - 1)
            def _():
                fall(kd, u).wait_recv()
                mine[kd, rows(u), :] = (both(kd, u) + from_above[kd, rows(u), :].astype(F32)).astype(BF)

            fall(kd, u).start()

    def gather_totals():
        for i, p in enumerate(group_peers(n)):
            tot_copy(i, p[0], p[1]).wait_recv()
        tots[me] = share[...]
        for i, p in enumerate(group_peers(n)):
            tots[me] = tots[me] + tots[p[1]]

    def last(r, s):
        u = SUBS * r + s
        if s == 0:
            arrive(h, r)
        flat[rows(u), :] = both(h, u)

        @pl.when(h > 0)
        def _():
            k = n - 1 - h
            rise(k, u).wait_recv()
            flat[rows(u), :] = flat[rows(u), :] + from_below[k, rows(u), :].astype(F32)

        @pl.when(h < n - 1)
        def _():
            fall(h, u).wait_recv()
            flat[rows(u), :] = flat[rows(u), :] + from_above[h, rows(u), :].astype(F32)

        if norm:
            close(u)
        else:
            v = base[rows(u), :].astype(F32) + flat[rows(u), :]
            out[rows(u), :] = v
            low[rows(u), :] = v.astype(BF)
            set_out(u)

    def close(u):
        hi, lo = split(tots[me, u])
        eighth = jnp.full((8, 128), 0.125, BF)
        total_r = (dg(hi, eighth, TN) + dg(lo, eighth, TN))[:UNIT]
        sc = scale[rows(u), :]
        kp = kept[rows(u), :].astype(F32)
        dn = flat[rows(u), :]
        v = (base[rows(u), :].astype(F32) + sc * (gain[...] * dn)
             - kp * jnp.tile((sc * sc * sc) * (total_r * (1.0 / D)), (1, width // 128)))
        out[rows(u), :] = v
        low[rows(u), :] = v.astype(BF)
        dgain[...] += jnp.sum((dn * kp * sc).reshape(UNIT // 8, 8, width), axis=0)
        set_out(u)

    def set_out(u):
        src = low.at[rows(u)]

        @pl.when(h < n - 1)
        def _():
            spread(h, u, src, gu_s, gu_r, up).start()

        @pl.when(h > 0)
        def _():
            spread(h, u, src, gd_s, gd_r, down).start()

        spread(h, u, src, gc_s, gc_r, across).start()

    def pass_on(k, r, s):
        u = SUBS * r + s
        below, above = h - k, h + k

        @pl.when(below >= 0)
        def _():
            spread(below, u, piece(below, u), gu_s, gu_r, up).wait_recv()

            @pl.when(h < n - 1)
            def _():
                spread(below, u, piece(below, u), gu_s, gu_r, up).start()

            spread(below, u, piece(below, u), gc_s, gc_r, across).start()

        @pl.when(above < n)
        def _():
            spread(above, u, piece(above, u), gd_s, gd_r, down).wait_recv()

            @pl.when(h > 0)
            def _():
                spread(above, u, piece(above, u), gd_s, gd_r, down).start()

            spread(above, u, piece(above, u), gc_s, gc_r, across).start()

    def at(o, r, s):
        if o < n - 1:
            climb(o, r, s)
        elif o == n - 1:
            if norm and s == 0:
                @pl.when(r == 0)
                def _():
                    gather_totals()
            last(r, s)
        elif o < 2 * n - 1:
            pass_on(o - n + 1, r, s)

    def period(r, c):
        for e in range(len(kinds)):
            @pl.when(r == e + 1)
            def _():
                carry.relay(e)

        for o in range(n):
            for s in range(SUBS):
                @pl.when(r > 0)
                def _():
                    at(o + n, r - 1, s)

                @pl.when(r < chunks)
                def _():
                    at(o, r, s)
        return c

    lax.fori_loop(0, chunks + 1, period, 0)
    mine_out = pltpu.make_async_copy(low, full.at[:, lanes(h, t)], here.at[0, 0])
    mine_out.start()

    def drain(u, c):
        for j in range(n):
            back = remote(piece(j, u), full.at[rows(u), lanes(j, 1 - t)], gc_s.at[j, u], gc_r.at[j, u], across)
            back.wait_recv()
            back.wait_send()

            @pl.when((j <= h) & (h < n - 1))
            def _():
                spread(j, u, piece(j, u), gu_s, gu_r, up).wait_send()

            @pl.when((j >= h) & (h > 0))
            def _():
                spread(j, u, piece(j, u), gd_s, gd_r, down).wait_send()

        for k in range(n - 1):
            @pl.when(n - 1 - k > h)
            def _():
                rise(k, u).wait_send()

            @pl.when(k < h)
            def _():
                fall(k, u).wait_send()

        return c

    if norm:
        for i, p in enumerate(group_peers(n)):
            tot_copy(i, p[0], me).wait_send()
    lax.fori_loop(0, UNITS, drain, 0)
    for r in range(chunks):
        for j in range(n):
            swap(j, r).wait_send()
    mine_out.wait()
    carry.wait()


def z_turn(n, part, base, collective_id, name, m=1, kinds=(), arrays=(), norm=None):
    rows, width = part.shape[0], part.shape[1] // (2 * n)
    dma = pltpu.SemaphoreType.DMA
    shapes, sems = carried(kinds, m, arrays)
    shape = jax.ShapeDtypeStruct
    ins = [part, base] if norm is None else [part, norm[0], norm[1], base, norm[2], norm[3]]
    outs = [shape((rows, width), F32), shape((rows, 2 * n * width), BF), shape((rows, width), BF)]
    out_specs = [VM, HBM, VM]
    more = []
    if norm is not None:
        outs, out_specs = outs + [shape((8, width), F32)], out_specs + [VM]
        more = [pltpu.VMEM((2 * n, UNITS, 8, 128), F32), dma((2 * n,)), dma((2 * n,))]
    return pl.pallas_call(
        functools.partial(turn_kernel, n, width, m, kinds, norm is not None),
        out_shape=outs + shapes,
        in_specs=[HBM] + [VM] * (len(ins) - 1) + [HBM] * len(shapes), out_specs=out_specs + [HBM] * len(shapes),
        scratch_shapes=[pltpu.VMEM((n, rows, width), BF)] * 2 + [pltpu.VMEM((n - 1, rows, width), BF)] * 2
        + [dma((n, CHUNKS))] * 3 + [dma((n - 1, UNITS))] * 4 + [dma((n, UNITS))] * 6 + [pltpu.VMEM((rows, width), F32)]
        + more + sems,
        compiler_params=pltpu.CompilerParams(collective_id=collective_id, has_side_effects=True, vmem_limit_bytes=ROOM),
        cost_estimate=pl.CostEstimate(flops=0, bytes_accessed=LINK_COST, transcendentals=0),
        name=name,
    )(*ins, *arrays)


def rows_spec(rows, cols):
    return pl.BlockSpec((rows, cols), lambda i: (i, 0))


def fixed_spec(*shape):
    return pl.BlockSpec(shape, lambda i: (0,) * len(shape), pipeline_mode=pl.Buffered(1))


def by_rows(kernel, rows, ins, fixed, outs, lanes, flops, name):
    specs = [rows_spec(rows, a.shape[1]) for a in ins] + [fixed_spec(*a.shape) for a in fixed]
    out_specs = [rows_spec(rows, o.shape[1]) for o in outs]
    shapes = list(outs)
    if lanes:
        out_specs.append(pl.BlockSpec((lanes * rows // CAP, 8, 128), lambda i: (i, 0, 0)))
        shapes.append(jax.ShapeDtypeStruct((lanes, 8, 128), F32))
    return pl.pallas_call(
        kernel, grid=(CAP // rows,), out_shape=shapes, in_specs=specs, out_specs=out_specs,
        compiler_params=pltpu.CompilerParams(dimension_semantics=("arbitrary",), vmem_limit_bytes=ROOM),
        cost_estimate=pl.CostEstimate(flops=flops, bytes_accessed=20 * 2**20, transcendentals=0),
        name=name,
    )(*ins, *fixed)


def lane_sums(values, share):
    units, rows = share.shape[0], values.shape[0] // share.shape[0]
    hi, lo = split(values)
    ones = jnp.ones((8, values.shape[1]), BF)
    for i in range(units):
        r = slice(i * rows, (i + 1) * rows)
        share[i, :, :rows] = dg(ones, hi[r], NT) + dg(ones, lo[r], NT)
        if rows < 128:
            share[i, :, rows:] = jnp.zeros((8, 128 - rows), F32)


def normal(x, gain):
    x = x.astype(F32)
    scale = lax.rsqrt(jnp.mean(x * x, axis=1, keepdims=True) + EPSILON)
    return scale, (x * scale * gain).astype(BF)


def project_kernel(x, gain, w, pre, normed, scale):
    sc, nb = normal(x[...], gain[...])
    scale[...] = sc
    normed[...] = nb
    pre[...] = dg(nb, w[...], NN)


def project(rows_full, gain, w_in):
    sd = jax.ShapeDtypeStruct
    outs = [sd((CAP, w_in.shape[1]), F32), sd((CAP, D), BF), sd((CAP, 1), F32)]
    return by_rows(project_kernel, 256, [rows_full], [gain, w_in], outs, 0, 2 * CAP * D * w_in.shape[1], "project")


def ffn_kernel(x, cot, gain, w_ug, w_u, w_d, normed, product, d_gate, d_up, d_normed, scale, share):
    sc, nb = normal(x[...], gain[...])
    scale[...] = sc
    normed[...] = nb
    gate = dg(nb, w_ug[...], NT)
    up = dg(nb, w_u[...], NT)
    sig = sigmoid(gate)
    act = gate * sig
    product[...] = (act * up).astype(BF)
    d_product = dg(cot[...], w_d[...], NT)
    dgt = (d_product * up * sig * (1.0 + gate * (1.0 - sig))).astype(BF)
    dup = (d_product * act).astype(BF)
    d_gate[...] = dgt
    d_up[...] = dup
    d_normed[...] = (dg(dgt, w_ug[...], NN) + dg(dup, w_u[...], NN)).astype(BF)
    lane_sums((dgt.astype(F32) * gate + dup.astype(F32) * up) / sc, share)


def ffn(held_full, cot_full, gain, w_ug, w_u, w_d):
    sd = jax.ShapeDtypeStruct
    ff = w_u.shape[0]
    outs = [sd((CAP, D), BF)] + [sd((CAP, ff), BF)] * 3 + [sd((CAP, D), BF), sd((CAP, 1), F32)]
    return by_rows(ffn_kernel, CAP // CHUNKS, [held_full, cot_full], [gain, w_ug, w_u, w_d], outs, UNITS,
                   10 * CAP * D * ff, "feed_forward")


def unproject_kernel(d_pre, pre, scale, w, d_normed, share):
    d = d_pre[...]
    d_normed[...] = dg(d, w[...], NT).astype(BF)
    lane_sums(d.astype(F32) * pre[...] / scale[...], share)


def unproject(d_pre, pre, scale, w_in):
    outs = [jax.ShapeDtypeStruct((CAP, D), BF)]
    return by_rows(unproject_kernel, 256, [d_pre, pre, scale], [w_in], outs, CAP // STEP, 2 * CAP * D * w_in.shape[1], "unproject")


PRE = 1152
GROUP = ("head", "tensor")


def mm(left, right, dims=NN):
    return lax.dot_general(left, right, dims, preferred_element_type=F32)


def full_rows(piece_in):
    return lax.all_gather(piece_in, GROUP, axis=1, tiled=True)


def shares(partial_sum):
    return lax.psum_scatter(partial_sum.astype(BF), GROUP, scatter_dimension=1, tiled=True).astype(F32)


def column_blocks(grad, m):
    rows, wide = grad.shape[0], grad.shape[1] // m
    if wide % 128 == 0:
        return "columns", grad
    return "swap", grad.reshape(rows, m, wide).transpose(1, 0, 2)


def side_by_side(wide):
    return "abreast" if wide % 128 == 0 else "pile"


def level(weights):
    if weights.ndim == 2:
        return weights
    return weights.transpose(1, 0, 2).reshape(weights.shape[1], -1)


def swap_ring(*grads):
    shards, device = lax.axis_size("shard"), lax.axis_index("shard")
    wide = grads[0].shape[1] // shards

    def block(i):
        at = lax.rem(device + i, shards) * wide
        return jnp.concatenate([lax.dynamic_slice_in_dim(g, at, wide, 1) for g in grads], axis=0)

    total = block(0).astype(F32)
    for i in range(1, shards):
        total = total + lax.ppermute(block(i), "shard", [(a, (a + i) % shards) for a in range(shards)]).astype(F32)
    ends = [0]
    for g in grads:
        ends.append(ends[-1] + g.shape[0])
    return [total[i:j] for i, j in zip(ends, ends[1:])]


def sum_blocks(blocks):
    return jnp.sum(blocks.astype(F32), axis=0)


def body(tokens, seq_lengths, dealing, gain_mixer, w_query, w_key, w_value, w_gate, w_beta, conv_weight,
         gain_heads, w_out, gain_ffn, w_up_gate, w_up, w_down, cotangent):
    shards = lax.axis_size("shard")
    width = tokens.shape[2]
    col_start = lax.axis_index(GROUP) * width
    per_peer = (CAP // shards + SEQ_DEV + 15) // 16 * 16

    w_piece = jnp.concatenate(
        [w_query, w_key, w_value, w_gate, w_beta, jnp.zeros((w_beta.shape[0], PRE - 4 * width - w_beta.shape[1]), BF)], axis=1)

    own_rows = tokens.reshape(REAL_DEV, width)
    taps = conv_weight.reshape(3 * CONV, width)
    head_gain = gain_heads[None, :]

    n = lax.axis_size("head")
    side = side_by_side(w_up.shape[0])
    x_rows, rows_full, sent_slot, recv_slot, pos, filled_f, w_in, w_o = z_gather(
        n, seq_lengths, dealing, own_rows, per_peer, 1, "gather_rows", shards, ("gather", side), (w_piece, w_out))
    w_o = level(w_o)
    rows_full, cot_piece = lax.optimization_barrier((rows_full, cotangent))
    cot_full = full_rows(cot_piece)
    pre, normed, scale_one = project(rows_full, gain_mixer[None, :], w_in)
    mixed, *saved = mixer_fwd(pre, pos, filled_f, taps, head_gain)
    branch_part, cot_full = lax.optimization_barrier((mm(mixed, w_o).astype(BF), cot_full))
    hidden, held_full, held_low, w_ug, w_u, w_d = z_turn(
        n, branch_part, x_rows, 2, "turn_branch", shards, (side,) * 3, (w_up_gate.T, w_up.T, w_down))
    w_ug, w_u, w_d = level(w_ug), level(w_u), level(w_d)
    normed_two, product, d_gate, d_up, d_normed_two, scale_two, share_two = ffn(
        held_full, cot_full, gain_ffn[None, :], w_ug, w_u, w_d)
    down_kind, d_w_down = column_blocks(mm(product, cot_full, TN).astype(BF), shards)
    gate_kind, d_w_ug = column_blocks(mm(d_gate, normed_two, TN).astype(BF), shards)
    d_w_u = mm(d_up, normed_two, TN).astype(BF)
    ffn_gain_part = lax.dynamic_slice_in_dim(gain_ffn, col_start, width)[None, :]
    d_hidden, d_branch_full, _, ffn_gain_grad, d_w_ug, d_w_down = z_turn(
        n, d_normed_two, cotangent, 4, "turn_normed_two", shards, (gate_kind, down_kind), (d_w_ug, d_w_down),
        norm=(held_low, scale_two, ffn_gain_part, share_two))
    out_part = mm(product, w_d).astype(BF)
    out_part, d_branch_full = lax.optimization_barrier((out_part, d_branch_full))
    d_w_u, d_w_out = swap_ring(d_w_u, mm(mixed, d_branch_full, TN).astype(BF))
    out_sum = shares(out_part)
    d_mixed = mm(d_branch_full, w_o, NT)
    d_pre, d_taps, d_head_gain = mixer_bwd(d_mixed, pre, pos, filled_f, taps, head_gain, saved)
    d_normed, share_one = unproject(d_pre, pre, scale_one, w_in)
    d_w_in = mm(normed, d_pre, TN).astype(BF).reshape(shards, w_piece.shape[0], PRE)
    d_normed, out_sum = lax.optimization_barrier((d_normed, out_sum))
    block_out = (hidden + out_sum).astype(BF)
    mixer_gain_part = lax.dynamic_slice_in_dim(gain_mixer, col_start, width)[None, :]
    small = jnp.concatenate([
        jnp.sum(d_taps, axis=1), jnp.zeros((1, width), F32), jnp.sum(ffn_gain_grad, axis=0)[None, :],
        jnp.pad(jnp.sum(d_head_gain, axis=0), (0, width - HD))[None, :],
        jnp.zeros((1, width), F32)], axis=0)
    d_tokens, summed, d_w_in = z_finish(
        n, d_normed, x_rows, scale_one, d_hidden, mixer_gain_part, share_one, small,
        sent_slot, recv_slot, per_peer, 6, "finish_rows", shards, ("swap",), (d_w_in,))
    d_tokens = d_tokens.reshape(REAL_DEV, 1, width)
    d_w_in = sum_blocks(d_w_in)
    by_row = summed.transpose(1, 0, 2).reshape(16, D)
    d_conv = by_row[:12].reshape(CONV, 3, D)
    d_gain_heads = jnp.sum(summed[:, 14, :HD], axis=0)
    cut = [0, width, 2 * width, 3 * width, 4 * width]
    return (
        block_out, d_tokens, by_row[12],
        d_w_in[:, cut[0]:cut[1]], d_w_in[:, cut[1]:cut[2]], d_w_in[:, cut[2]:cut[3]], d_w_in[:, cut[3]:cut[4]],
        d_w_in[:, 4 * width:4 * width + w_beta.shape[1]],
        d_conv, d_gain_heads, d_w_out, by_row[13],
        sum_blocks(d_w_ug).T, d_w_u.T, sum_blocks(d_w_down),
    )


def solution(mesh):
    feat = ("head", "tensor")
    placed = (
        P(None, "shard", feat), P(), P(), P(),
        P("shard", feat), P("shard", feat), P("shard", feat), P("shard", feat), P("shard", feat),
        P(None, None, feat), P(), P(feat, "shard"), P(),
        P("shard", feat), P("shard", feat), P(feat, "shard"), P("shard", feat),
    )
    given = (
        P("shard", feat), P(None, "shard", feat), P(),
        P("shard", feat), P("shard", feat), P("shard", feat), P("shard", feat), P("shard", feat),
        P(), P(), P(feat, "shard"), P(),
        P("shard", feat), P("shard", feat), P(feat, "shard"),
    )
    return jax.shard_map(body, mesh=mesh, in_specs=placed, out_specs=given, check_vma=False)
```

```python
import functools
import jax
import jax.numpy as jnp
from jax import lax
from jax.experimental import pallas as pl
from jax.experimental.pallas import tpu as pltpu

from jax.sharding import PartitionSpec as P

D = 2048
HD = 128
CONV = 4
BLOCK = 64
SEQ_DEV = 4
REAL_DEV = 1152
CAP = 1280
NB = CAP // BLOCK
EPSILON = 1e-06
HEAD_FLOOR = 0.01
F32 = jnp.float32
BF = jnp.bfloat16

def split(x):
    hi = x.astype(BF)
    return hi, (x - hi.astype(F32)).astype(BF)

NN=(((1,),(0,)),((),())); NT=(((1,),(1,)),((),())); TN=(((0,),(0,)),((),()))

def dg(a, b, dims):
    return lax.dot_general(a, b, dims, preferred_element_type=F32)

def d3(a, b, dims=NN):
    ah, al = split(a); bh, bl = split(b)
    return dg(ah, bh, dims) + (dg(ah, bl, dims) + dg(al, bh, dims))

def four_times(step):
    return lambda i, c: step(4 * i + 3, step(4 * i + 2, step(4 * i + 1, step(4 * i, c))))

def goes_on(pos_ref, n):
    first = pos_ref[pl.ds(pl.multiple_of(n * BLOCK, BLOCK), 8), :][:1]
    return jnp.where(first != 0, 1.0, 0.0)

def masks():
    ri = lax.broadcasted_iota(jnp.int32, (BLOCK, BLOCK), 0)
    ci = lax.broadcasted_iota(jnp.int32, (BLOCK, BLOCK), 1)
    return ri, ci

def sigmoid(x):
    return 1.0 / (1.0 + jnp.exp(-x))

def conv_rows(cur, tail, wt, pos):
    ext = jnp.concatenate([tail, cur], axis=0)
    out = wt[0] * cur
    for j in range(1, CONV):
        sh = pltpu.roll(ext, j, axis=0)[8:]
        out = out + wt[j] * jnp.where(pos >= j, sh, 0.0)
    return out

def inverses(lmats, ri, ci):
    apart = ri ^ ci
    xs = [jnp.where(apart == 0, 1.0, 0.0) - jnp.where(apart == 1, m, 0.0) for m in lmats]
    s = 2
    while s < BLOCK:
        at = (apart >= s) & (apart < 2 * s)
        ys = [d3(x, jnp.where(at, m, 0.0)) for x, m in zip(xs, lmats)]
        xs = [x - d3(y, x) for x, y in zip(xs, ys)]
        s *= 2
    return xs

def fwd_kernel(pre, pos_ref, fill_ref, cw, gain, mixed, *refs):
    given, (c_out, qk, w_out, u_out, u2_out, o_out, p_out, t_out, m_out, s_out, b_s), sem = refs[:10], refs[10:21], refs[21]
    held = (c_out, qk, w_out, u_out, u2_out, o_out, p_out, t_out, m_out, s_out)

    def keep(*which):
        for i in which:
            pltpu.make_async_copy(held[i], given[i], sem.at[i]).start()

    ri, ci = masks()
    heads = 2
    def phase_a(n, tails):
        r = pl.ds(pl.multiple_of(n * BLOCK, BLOCK), BLOCK)
        pos = pos_ref[r, :]; fil = fill_ref[r, :]
        new_tails = []
        acts = []
        for i in range(3):
            cur = pre[r, i*256:(i+1)*256]
            wt = [cw[j*3+i:j*3+i+1, :] for j in range(CONV)]
            cc = conv_rows(cur, tails[i], wt, pos)
            c_out[r, i*256:(i+1)*256] = cc
            acts.append(cc * sigmoid(cc) * fil)
            new_tails.append(cur[BLOCK-8:])
        beta = sigmoid(pre[r, 1024:1152])
        for h in range(heads):
            hs = slice(h*HD, (h+1)*HD)
            yq = acts[0][:, hs]; yk = acts[1][:, hs]; v = acts[2][:, hs]
            q = yq * lax.rsqrt(jnp.sum(yq*yq, axis=1, keepdims=True) + EPSILON)
            k = yk * lax.rsqrt(jnp.sum(yk*yk, axis=1, keepdims=True) + EPSILON)
            b = beta[:, h:h+1]
            qk[r, h*HD:(h+1)*HD] = q
            qk[r, 256+h*HD:256+(h+1)*HD] = k
            lmat = jnp.where(ri > ci, b * d3(k, k, NT), 0.0)
            p_out[n*2+h] = jnp.where(ri >= ci, d3(q, k, NT), 0.0)
            t_out[n*2+h] = lmat
            u_out[r, hs] = b*v
            w_out[r, hs] = b*k
        return tuple(new_tails)
    z8 = jnp.zeros((8, 256), F32)
    lax.fori_loop(0, NB // 4, four_times(phase_a), (z8, z8, z8))
    keep(0, 1, 6)
    GRP = 20
    def phase_t(i, _):
        ts = inverses([t_out[i*GRP+j] for j in range(GRP)], ri, ci)
        for j in range(GRP):
            t_out[i*GRP+j] = ts[j]
        return 0
    lax.fori_loop(0, 2*NB//GRP, phase_t, 0)
    keep(7)
    def phase_w(i, _):
        todo = [(n, pl.ds(pl.multiple_of(n * BLOCK, BLOCK), BLOCK), h, slice(h*HD, (h+1)*HD)) for n in (4*i, 4*i+1, 4*i+2, 4*i+3) for h in range(heads)]
        wu = [d3(t_out[n*2+h], jnp.concatenate([w_out[r, c], u_out[r, c]], axis=1)) for n, r, h, c in todo]
        mb = [d3(qk[r, 256+h*HD:256+(h+1)*HD], x, TN) for x, (n, r, h, c) in zip(wu, todo)]
        for x, y, (n, r, h, c) in zip(wu, mb, todo):
            w_out[r, c] = x[:, :HD]; u_out[r, c] = x[:, HD:]
            m_out[n*2+h] = y[:, :HD]; b_s[n*2+h] = y[:, HD:]
        return 0
    lax.fori_loop(0, NB//4, phase_w, 0)
    keep(2, 3, 8)
    def phase_b(n, ss):
        out = []
        for h in range(heads):
            e = n*2+h
            s = ss[h] * goes_on(pos_ref, n)
            s_out[e] = s
            out.append(s - d3(m_out[e], s) + b_s[e])
        return tuple(out)
    zs = jnp.zeros((HD, HD), F32)
    lax.fori_loop(0, NB, phase_b, (zs, zs))
    keep(9)
    def phase_c(i, _):
        todo = [(n, pl.ds(pl.multiple_of(n * BLOCK, BLOCK), BLOCK), h, slice(h*HD, (h+1)*HD)) for n in (4*i, 4*i+1, 4*i+2, 4*i+3) for h in range(heads)]
        rr = [d3(jnp.concatenate([w_out[r, c], qk[r, c]], axis=0), s_out[n*2+h]) for n, r, h, c in todo]
        u2 = [u_out[r, c] - v[:BLOCK] for v, (n, r, h, c) in zip(rr, todo)]
        os_ = [v[BLOCK:] + d3(p_out[n*2+h], u) for v, u, (n, r, h, c) in zip(rr, u2, todo)]
        for o, u, (n, r, h, c) in zip(os_, u2, todo):
            u2_out[r, c] = u
            o_out[r, c] = o
            ms = jnp.mean(o*o, axis=1, keepdims=True)
            sc = lax.rsqrt(jnp.maximum(ms, HEAD_FLOOR))
            gg = pre[r, 768+h*HD:768+(h+1)*HD]
            mixed[r, c] = (o * sc * gain[...] * (gg * sigmoid(gg))).astype(BF)
        return 0
    lax.fori_loop(0, NB // 4, phase_c, 0)
    keep(4, 5)
    for i in range(10):
        pltpu.make_async_copy(held[i], given[i], sem.at[i]).wait()

def sds(*s, dt=F32): return jax.ShapeDtypeStruct(s, dt)
VM = pl.BlockSpec(memory_space=pltpu.VMEM)
SM = pl.BlockSpec(memory_space=pltpu.SMEM)

def mixer_fwd(pre, pos, fil, cw, gain):
    outs = (sds(CAP,256,dt=BF), sds(CAP,768), sds(CAP,512), sds(CAP,256), sds(CAP,256), sds(CAP,256), sds(CAP,256),
            sds(2*NB,BLOCK,BLOCK), sds(2*NB,BLOCK,BLOCK), sds(2*NB,HD,HD), sds(2*NB,HD,HD))
    return pl.pallas_call(fwd_kernel, out_shape=outs, in_specs=[VM]*5, out_specs=[VM]+[pl.BlockSpec(memory_space=pltpu.HBM)]*(len(outs)-1),
        scratch_shapes=[pltpu.VMEM(o.shape,F32) for o in outs[1:]]+[pltpu.VMEM((2*NB,HD,HD),F32), pltpu.SemaphoreType.DMA((10,))],
        compiler_params=pltpu.CompilerParams(vmem_limit_bytes=60*2**20), cost_estimate=pl.CostEstimate(flops=0, bytes_accessed=140 * 2**20, transcendentals=0),
        name="mixer_forward")(pre, pos, fil, cw, gain)

def bwd_kernel(dmix, pre, pos_ref, fill_ref, cw, gain, *refs):
    kept, (dpre, dcw, dgain), held, (e_s, do_s, sem) = refs[:10], refs[10:13], refs[13:23], refs[23:]
    c_in, qk, w_in, u_in, u2_in, o_in, p_in, t_in, m_in, s_in = held

    def fetch(i):
        return pltpu.make_async_copy(kept[i], held[i], sem.at[i])

    for i in (5, 6, 1, 2, 8, 7, 9, 0, 3, 4):
        fetch(i).start()
    for i in (5, 6, 1, 2):
        fetch(i).wait()
    ri, ci = masks()
    heads = 2
    lane = lax.broadcasted_iota(jnp.int32, (BLOCK, HD), 1)
    dgain[...] = jnp.zeros_like(dgain)
    dcw[...] = jnp.zeros_like(dcw)
    def phase_a(n, _):
        r = pl.ds(pl.multiple_of(n * BLOCK, BLOCK), BLOCK)
        for h in range(heads):
            hs = slice(h*HD, (h+1)*HD)
            e = n*2+h
            o = o_in[r, hs]; dm = dmix[r, hs]
            gg = pre[r, 768+h*HD:768+(h+1)*HD]
            sg = sigmoid(gg); si = gg*sg
            ms = jnp.mean(o*o, axis=1, keepdims=True)
            sc = lax.rsqrt(jnp.maximum(ms, HEAD_FLOOR))
            on = o*sc
            gn = gain[...]
            dpre[r, 768+h*HD:768+(h+1)*HD] = (dm * on * gn * (sg * (1.0 + gg*(1.0-sg)))).astype(BF)
            dgs = dm * on * si
            dgain[...] += jnp.sum(dgs.reshape(8, 8, HD), axis=0)
            dn = dm * gn * si
            corr = jnp.where(ms > HEAD_FLOOR, jnp.mean(dn*on, axis=1, keepdims=True), 0.0)
            do = sc * (dn - on*corr)
            do_s[r, hs] = do
            pdo = d3(p_in[e], do, TN)
            qw = jnp.concatenate([qk[r, hs], w_in[r, hs]], axis=0)
            dd = jnp.concatenate([do, -pdo], axis=0)
            e_s[e] = d3(qw, dd, TN)
        return 0
    lax.fori_loop(0, NB // 4, four_times(phase_a), 0)
    fetch(8).wait()

    def phase_b(i, ds):
        n = NB-1-i
        out = []
        for h in range(heads):
            e = n*2+h
            d = ds[h]
            ee = e_s[e]
            e_s[e] = d
            out.append((d - d3(m_in[e], d, TN) + ee) * goes_on(pos_ref, n))
        return tuple(out)
    zs = jnp.zeros((HD, HD), F32)
    lax.fori_loop(0, NB, phase_b, (zs, zs))
    for i in (7, 9, 0, 3, 4):
        fetch(i).wait()

    def phase_c(i, heads_dc):
        blocks = tuple(NB - 1 - j - 4 * i for j in range(4))
        todo = [(n, pl.ds(pl.multiple_of(n * BLOCK, BLOCK), BLOCK), h, slice(h*HD, (h+1)*HD)) for n in blocks for h in range(heads)]
        def every(f, *lists):
            return [f(*v) for v in zip(*lists)]
        ns, rs, hh, hs = zip(*todo)
        es = [n*2+h for n, h in zip(ns, hh)]
        fil = [fill_ref[r, :] for r in rs]
        beta_t = [sigmoid(pre[r, 1024:1152]) for r in rs]
        q = [qk[r, c] for r, c in zip(rs, hs)]
        k = [qk[r, 256+h*HD:256+(h+1)*HD] for r, h in zip(rs, hh)]
        w = [w_in[r, c] for r, c in zip(rs, hs)]
        u = [u_in[r, c] for r, c in zip(rs, hs)]
        u2 = [u2_in[r, c] for r, c in zip(rs, hs)]
        do = [do_s[r, c] for r, c in zip(rs, hs)]
        p = [p_in[e] for e in es]
        t = [t_in[e] for e in es]
        s = [s_in[e] for e in es]
        ds = [e_s[e] for e in es]
        b = [x[:, h:h+1] for x, h in zip(beta_t, hh)]
        du2 = every(lambda p, do, k, ds: d3(p, do, TN) + d3(k, ds), p, do, k, ds)
        dp = every(lambda do, u2: jnp.where(ri >= ci, d3(do, u2, NT), 0.0), do, u2)
        g = every(lambda k: d3(k, k, NT), k)
        xs = every(lambda do, du2, s: d3(jnp.concatenate([do, -du2], axis=0), s, NT), do, du2, s)
        dq = every(lambda xs, dp, k: xs[:BLOCK] + d3(dp, k), xs, dp, k)
        xx = every(lambda t, xs, du2: d3(t, jnp.concatenate([xs[BLOCK:], du2], axis=1), TN), t, xs, du2)
        dk = every(lambda dp, q, u2, ds: d3(dp, q, TN) + d3(u2, ds, NT), dp, q, u2, ds)
        mm = every(lambda xx, w, u: jnp.where(ri > ci, -d3(xx, jnp.concatenate([w, u], axis=1), NT), 0.0), xx, w, u)
        cv = [c_in[r, 512+h*HD:512+(h+1)*HD] for r, h in zip(rs, hh)]
        sv = every(sigmoid, cv)
        bm = every(lambda b, mm: b*mm, b, mm)
        dk = every(lambda dk, bm, k, b, xx: dk + d3(bm + bm.T, k) + b*xx[:, :HD], dk, bm, k, b, xx)
        db = every(lambda mm, g, xx, k, cv, sv, fil: jnp.sum(mm*g, axis=1, keepdims=True)
                   + jnp.sum(xx[:, :HD]*k + xx[:, HD:]*(cv*sv*fil), axis=1, keepdims=True), mm, g, xx, k, cv, sv, fil)
        cq = [c_in[r, c] for r, c in zip(rs, hs)]
        ck = [c_in[r, 256+h*HD:256+(h+1)*HD] for r, h in zip(rs, hh)]
        def unit_back(c, fil, n, d):
            sg = sigmoid(c)
            y = c*sg*fil
            r = lax.rsqrt(jnp.sum(y*y, axis=1, keepdims=True) + EPSILON)
            return r*(d - n*jnp.sum(d*n, axis=1, keepdims=True))*fil*(sg*(1.0+c*(1.0-sg)))
        aq = every(unit_back, cq, fil, q, dq)
        ak = every(unit_back, ck, fil, k, dk)
        av = every(lambda b, xx, fil, sv, cv: b*xx[:, HD:]*fil*(sv*(1.0+cv*(1.0-sv))), b, xx, fil, sv, cv)
        for j, n in enumerate(blocks):
            r = rs[2*j]
            dbt = jnp.where(lane == 0, db[2*j], jnp.where(lane == 1, db[2*j+1], 0.0))
            dpre[r, 1024:1152] = (dbt*beta_t[2*j]*(1.0-beta_t[2*j])).astype(BF)
            pos = pos_ref[r, :]
            nxt = jnp.minimum(n+1, NB-1)
            posx = jnp.concatenate([pos, pos_ref[pl.ds(pl.multiple_of(nxt*BLOCK, BLOCK), 8), :]], axis=0)
            prv = jnp.maximum(n*BLOCK-8, 0)
            new = []
            for i, acts in enumerate((aq, ak, av)):
                dc = jnp.concatenate(acts[2*j:2*j+2], axis=1)
                ext = jnp.concatenate([dc, heads_dc[i]], axis=0)
                cur = pre[r, i*256:(i+1)*256]
                tail = pre[pl.ds(pl.multiple_of(prv, 8), 8), i*256:(i+1)*256]
                xext = jnp.concatenate([tail, cur], axis=0)
                dx = cw[i:i+1, :]*dc
                dcw[i] += jnp.sum((dc*cur).reshape(8, 8, 256), axis=0)
                for o in range(1, CONV):
                    z = jnp.where(posx >= o, ext, 0.0)
                    dx = dx + cw[o*3+i:o*3+i+1, :]*pltpu.roll(z, BLOCK+8-o, axis=0)[:BLOCK]
                    sh = pltpu.roll(xext, o, axis=0)[8:]
                    dcw[o*3+i] += jnp.sum(jnp.where(pos >= o, dc*sh, 0.0).reshape(8, 8, 256), axis=0)
                dpre[r, i*256:(i+1)*256] = dx.astype(BF)
                new.append(dc[:8])
            heads_dc = tuple(new)
        return heads_dc
    z8 = jnp.zeros((8, 256), F32)
    lax.fori_loop(0, NB // 4, phase_c, (z8, z8, z8))

def mixer_bwd(dmix, pre, pos, fil, cw, gain, saved):
    outs = (sds(CAP,1152,dt=BF), sds(12,8,256), sds(8,HD))
    return pl.pallas_call(bwd_kernel, out_shape=outs, in_specs=[VM]*6+[pl.BlockSpec(memory_space=pltpu.HBM)]*len(saved), out_specs=[VM]*3,
        scratch_shapes=[pltpu.VMEM(a.shape, F32) for a in saved]+[pltpu.VMEM((2*NB,HD,HD),F32), pltpu.VMEM((CAP,256),F32), pltpu.SemaphoreType.DMA((10,))],
        compiler_params=pltpu.CompilerParams(vmem_limit_bytes=60*2**20), cost_estimate=pl.CostEstimate(flops=0, bytes_accessed=200 * 2**20, transcendentals=0),
        name="mixer_backward")(dmix, pre, pos, fil, cw, gain, *saved)


MESH = pl.DeviceIdType.MESH
ROOM = 60 * 2**20
LINK_COST = 150 * 2**20
HBM = pl.BlockSpec(memory_space=pltpu.HBM)


def places():
    s, h, t = lax.axis_index("shard"), lax.axis_index("head"), lax.axis_index("tensor")
    return h, t, (s, h + 1, t), (s, h - 1, t), (s, h, 1 - t)


def shard_peers(m):
    s, h, t = lax.axis_index("shard"), lax.axis_index("head"), lax.axis_index("tensor")
    return [((lax.rem(s + i, m), h, t), lax.rem(s + i, m)) for i in range(1, m)]


def greet_shard(m):
    barrier = pltpu.get_barrier_semaphore()
    for p, _ in shard_peers(m):
        pl.semaphore_signal(barrier, inc=1, device_id=p, device_id_type=MESH)
    return m - 1


class Carry:
    def __init__(self, hops, kinds, m, ins, outs, send, recv, here):
        self.hops, self.kinds, self.m, self.ins, self.outs = hops, kinds, m, ins, outs
        self.send, self.recv, self.here = send, recv, here
        s, self.h, self.t = lax.axis_index("shard"), lax.axis_index("head"), lax.axis_index("tensor")
        self.me = s
        self.side = s + 1 - 2 * lax.rem(s, 2)
        self.over = lax.rem(s + 2, 4)
        self.corner = lax.rem(self.side + 2, 4)

    def relayed(self, e):
        return self.hops and self.m == 4 and self.kinds[e] in ("gather", "abreast")

    def part(self, e, src, half=None):
        rows = self.ins[e].shape[0]
        span = pl.ds(0, rows) if half is None else pl.ds(half * (rows // 2), rows // 2)
        if self.kinds[e] == "gather":
            first = src * rows + (0 if half is None else half * (rows // 2))
            return self.outs[e].at[pl.ds(pl.multiple_of(first, rows // 2), span.size)]
        if self.kinds[e] == "abreast":
            w = self.ins[e].shape[1]
            return self.outs[e].at[span, pl.ds(pl.multiple_of(src * w, w), w)]
        return self.outs[e].at[src]

    def given(self, e, dst):
        if self.kinds[e] == "columns":
            w = self.ins[e].shape[1] // self.m
            return self.ins[e].at[:, pl.ds(pl.multiple_of(dst * w, w), w)]
        return self.ins[e].at[dst] if self.kinds[e] == "swap" else self.ins[e]

    def move(self, e, src, dst, i, j, to):
        return pltpu.make_async_remote_copy(src_ref=src, dst_ref=dst, send_sem=self.send.at[e, i], recv_sem=self.recv.at[e, j],
                                            device_id=(to, self.h, self.t), device_id_type=MESH)

    def copy(self, e, i, to):
        return self.move(e, self.given(e, to), self.part(e, self.me), i, self.me, to)

    def came(self, e, src):
        return self.move(e, self.given(e, src), self.part(e, src), 0, src, src)

    def hand(self, e, half):
        src, to = (self.side, self.over) if half == 0 else (self.over, self.side)
        piece = self.part(e, src, half)
        return self.move(e, piece, piece, 2 + half, src if half == 0 else self.m, to)

    def handed(self, e, half):
        piece = self.part(e, self.corner, half)
        return self.move(e, piece, piece, 2 + half, self.corner if half == 0 else self.m, self.over if half == 0 else self.side)

    def local(self, e):
        return pltpu.make_async_copy(self.given(e, self.me), self.part(e, self.me), self.here.at[e])

    def targets(self, e):
        return [self.side, self.over] if self.relayed(e) else [p[1] for p in shard_peers(self.m)]

    def greet(self):
        return greet_shard(self.m) if self.kinds else 0

    def start(self):
        for e in range(len(self.kinds)):
            for i, to in enumerate(self.targets(e)):
                self.copy(e, i, to).start()
            self.local(e).start()

    def relay(self, e):
        if e < len(self.kinds) and self.relayed(e):
            self.came(e, self.side).wait_recv()
            self.hand(e, 0).start()
            self.came(e, self.over).wait_recv()
            self.hand(e, 1).start()

    def wait(self):
        for e in range(len(self.kinds)):
            self.local(e).wait()
            for i, to in enumerate(self.targets(e)):
                self.copy(e, i, to).wait_send()
                if not self.relayed(e):
                    self.came(e, to).wait_recv()
            if self.relayed(e):
                for half in range(2):
                    self.handed(e, half).wait_recv()
                    self.hand(e, half).wait_send()


def carried(kinds, m, arrays):
    dma = pltpu.SemaphoreType.DMA
    give = {"gather": lambda a: (m * a.shape[0], a.shape[1]), "swap": lambda a: a.shape,
            "abreast": lambda a: (a.shape[0], m * a.shape[1]), "pile": lambda a: (m,) + a.shape,
            "columns": lambda a: (m, a.shape[0], a.shape[1] // m)}
    shapes = [jax.ShapeDtypeStruct(give[k](a), a.dtype) for k, a in zip(kinds, arrays)]
    e = len(kinds)
    return shapes, ([dma((e, m + 1)), dma((e, m + 1)), dma((e,))] if e else [])


def carry_of(kinds, m, refs, n_in, n_out, hops=False):
    e = len(kinds)
    ins, refs = refs[:n_in], refs[n_in:]
    c_in, refs = refs[:e], refs[e:]
    outs, refs = refs[:n_out], refs[n_out:]
    c_out, refs = refs[:e], refs[e:]
    sems = (refs[-3:] if e else (None,) * 3)
    scratch = refs[:-3] if e else refs
    return ins, outs, scratch, Carry(hops, kinds, m, c_in, c_out, *sems)


def greet(n, h, up, down, across, more=0):
    barrier = pltpu.get_barrier_semaphore()
    pl.semaphore_signal(barrier, inc=1, device_id=across, device_id_type=MESH)

    @pl.when(h < n - 1)
    def _():
        pl.semaphore_signal(barrier, inc=1, device_id=up, device_id_type=MESH)

    @pl.when(h > 0)
    def _():
        pl.semaphore_signal(barrier, inc=1, device_id=down, device_id_type=MESH)

    pl.semaphore_wait(barrier, 1 + more + (h < n - 1).astype(jnp.int32) + (h > 0).astype(jnp.int32))


class Plan:
    def __init__(self, m, per_peer, lengths, dealing, starts):
        self.m, self.per_peer, self.lengths, self.dealing, self.starts = m, per_peer, lengths, dealing, starts
        self.shift = m.bit_length() - 1
        self.device = lax.axis_index("shard")

        def begin(q, total):
            starts[q] = total
            return total + lengths[q]

        lax.fori_loop(0, lengths.shape[0], begin, jnp.int32(0))

    def under(self, row, residue):
        return lax.shift_right_arithmetic(row - 1 - residue + self.m, self.shift + jnp.zeros_like(row))

    def members(self, g):
        at = [self.dealing[g * SEQ_DEV + i] for i in range(SEQ_DEV)]
        return [(self.starts[q], self.lengths[q]) for q in at]

    def sent(self, ids):
        packed = ids * self.m + self.device

        def group(g, slot):
            seqs = self.members(g)
            counts = [self.under(s + n, self.device) - self.under(s, self.device) for s, n in seqs]
            for s, n in seqs:
                first = g * self.per_peer - self.under(s, self.device)
                for (other, _), count in zip(seqs, counts):
                    first = first + jnp.where(other < s, count, 0)
                slot = slot + jnp.where((packed >= s) & (packed < s + n), first, 0)
            return slot

        return lax.fori_loop(0, self.lengths.shape[0] // SEQ_DEV, group, ids)

    def rows(self, ids):
        seqs = self.members(self.device)
        place, start, length, below = ids, jnp.zeros_like(ids), jnp.zeros_like(ids), jnp.int32(0)
        for s, n in seqs:
            here = ids >= below
            place = jnp.where(here, ids - below, place)
            start = jnp.where(here, s, start)
            length = jnp.where(here, n, length)
            below = below + lax.shift_right_arithmetic(n + BLOCK - 1, jnp.int32(6)) * BLOCK
        filled = place < length
        natural = start + place
        source = natural & (self.m - 1)
        slot = source * self.per_peer + self.under(natural, source) - self.under(start, source)
        for s, n in seqs:
            span = self.under(jnp.zeros_like(ids) + (s + n), source) - self.under(jnp.zeros_like(ids) + s, source)
            slot = slot + jnp.where(s < start, span, 0)
        return place, filled, jnp.where(filled, slot, -1)


def gather_kernel(n, width, m, kinds, *refs):
    (lengths, dealing, tokens), (x, out, sent_at, slot_at, pos_at, fill_at), scratch, carry = carry_of(kinds, m, refs, 3, 6)
    place_at, starts, outbox, inbox, deal_s, deal_r, here, up_s, up_r, down_s, down_r, core_s, core_r = scratch
    h, t, up, down, across = places()
    per_peer = outbox.shape[1]

    def cols(j):
        return out.at[:, pl.ds(pl.multiple_of((j * 2 + t) * width, width), width)]

    def other(j):
        return out.at[:, pl.ds(pl.multiple_of((j * 2 + 1 - t) * width, width), width)]

    def send(j, src, ss, rs, to):
        return pltpu.make_async_remote_copy(src_ref=src, dst_ref=cols(j), send_sem=ss.at[j], recv_sem=rs.at[j],
                                            device_id=to, device_id_type=MESH)

    greet(n, h, up, down, across, carry.greet())
    plan = Plan(m, per_peer, lengths, dealing, starts)
    peers = shard_peers(m)
    mine = lax.axis_index("shard")
    sent = plan.sent(lax.broadcasted_iota(jnp.int32, (1, REAL_DEV), 1))
    ids = lax.broadcasted_iota(jnp.int32, (per_peer, REAL_DEV), 0)

    def deal(i, p, src):
        return pltpu.make_async_remote_copy(src_ref=outbox.at[p[1]], dst_ref=inbox.at[src], send_sem=deal_s.at[i],
                                            recv_sem=deal_r.at[src], device_id=p[0], device_id_type=MESH)

    def pick(q):
        return dg(jnp.where(sent - q * per_peer == ids, 1.0, 0.0).astype(BF), tokens[...], NN).astype(BF)

    for i, p in enumerate(peers):
        outbox[p[1]] = pick(p[1])
        deal(i, p, mine).start()
    carry.start()
    inbox[mine] = pick(mine)
    place_at[...] = plan.rows(lax.broadcasted_iota(jnp.int32, (CAP, 1), 0))[2]
    for i, p in enumerate(peers):
        deal(i, p, p[1]).wait_recv()
    lanes = lax.broadcasted_iota(jnp.int32, (STEP, m * per_peer), 1)

    def settle(i, c):
        r = pl.ds(pl.multiple_of(i * STEP, STEP), STEP)
        chosen = jnp.where(place_at[r, :] == lanes, 1.0, 0.0).astype(BF)
        x[r, :] = dg(chosen, inbox[...].reshape(m * per_peer, width), NN).astype(BF)
        return c

    lax.fori_loop(0, CAP // STEP, settle, 0)
    local = pltpu.make_async_copy(x, cols(h), here)
    local.start()

    @pl.when(h < n - 1)
    def _():
        send(h, x, up_s, up_r, up).start()

    @pl.when(h > 0)
    def _():
        send(h, x, down_s, down_r, down).start()

    send(h, x, core_s, core_r, across).start()
    sent_at[...] = plan.sent(lax.broadcasted_iota(jnp.int32, (REAL_DEV, 1), 0))
    slot_at[...] = plan.rows(lax.broadcasted_iota(jnp.int32, (1, CAP), 1))[2]
    position, filled, _ = plan.rows(lax.broadcasted_iota(jnp.int32, (CAP, 1), 0))
    pos_at[...] = position
    fill_at[...] = jnp.where(filled, 1.0, 0.0)
    for k in range(1, n):
        below, above = h - k, h + k

        @pl.when(below >= 0)
        def _():
            send(below, cols(below), up_s, up_r, up).wait_recv()

            @pl.when(h < n - 1)
            def _():
                send(below, cols(below), up_s, up_r, up).start()

            send(below, cols(below), core_s, core_r, across).start()

        @pl.when(above < n)
        def _():
            send(above, cols(above), down_s, down_r, down).wait_recv()

            @pl.when(h > 0)
            def _():
                send(above, cols(above), down_s, down_r, down).start()

            send(above, cols(above), core_s, core_r, across).start()

    for j in range(n):
        back = pltpu.make_async_remote_copy(src_ref=cols(j), dst_ref=other(j), send_sem=core_s.at[j], recv_sem=core_r.at[j],
                                            device_id=across, device_id_type=MESH)
        back.wait_recv()
        back.wait_send()

        @pl.when((j <= h) & (h < n - 1))
        def _():
            send(j, cols(j), up_s, up_r, up).wait_send()

        @pl.when((j >= h) & (h > 0))
        def _():
            send(j, cols(j), down_s, down_r, down).wait_send()

    local.wait()
    for i, p in enumerate(peers):
        deal(i, p, mine).wait_send()
    carry.wait()


def z_gather(n, lengths, dealing, tokens, per_peer, collective_id, name, m, kinds, arrays):
    width = tokens.shape[1]
    dma = pltpu.SemaphoreType.DMA
    sd = jax.ShapeDtypeStruct
    shapes, sems = carried(kinds, m, arrays)
    return pl.pallas_call(
        functools.partial(gather_kernel, n, width, m, kinds),
        out_shape=[sd((CAP, width), BF), sd((CAP, 2 * n * width), BF), sd((REAL_DEV, 1), jnp.int32), sd((1, CAP), jnp.int32),
                   sd((CAP, 1), jnp.int32), sd((CAP, 1), F32)] + shapes,
        in_specs=[SM, SM, VM] + [HBM] * len(shapes), out_specs=[VM, HBM] + [VM] * 4 + [HBM] * len(shapes),
        scratch_shapes=[pltpu.VMEM((CAP, 1), jnp.int32), pltpu.SMEM(lengths.shape, jnp.int32)]
        + [pltpu.VMEM((m, per_peer, width), BF)] * 2 + [dma((m,)), dma((m,)), dma] + [dma((n,))] * 6 + sems,
        compiler_params=pltpu.CompilerParams(collective_id=collective_id, has_side_effects=True, vmem_limit_bytes=ROOM),
        cost_estimate=pl.CostEstimate(flops=0, bytes_accessed=LINK_COST, transcendentals=0),
        name=name,
    )(lengths, dealing, tokens, *arrays)


STEP = 128


def group_peers(n):
    s, h, t = lax.axis_index("shard"), lax.axis_index("head"), lax.axis_index("tensor")
    peers = []
    for i in range(1, 2 * n):
        hh, tt = lax.rem(h + i // 2, n), lax.rem(t + i % 2, 2)
        peers.append(((s, hh, tt), hh * 2 + tt))
    return peers


def greet_group(n, more=0):
    barrier = pltpu.get_barrier_semaphore()
    for p, _ in group_peers(n):
        pl.semaphore_signal(barrier, inc=1, device_id=p, device_id_type=MESH)
    pl.semaphore_wait(barrier, 2 * n - 1 + more)


def finish_kernel(n, width, m, kinds, fill, piles, *refs):
    (part, kept, scale, base, gain, share, small, sent, place, *left), (tokens, every, *grads), scratch, carry = carry_of(
        kinds, m, refs, 9 + piles + 2 * fill, 2 + piles + fill)
    stacks, left = left[:piles], left[piles:]
    added, grads = grads[:piles], grads[piles:]
    *scratch, pile_sem = scratch
    heaps, scratch = scratch[:piles], scratch[piles:]
    if fill:
        *scratch, l_buf, r_buf, blocks, l_sem, r_sem, w_s, w_r, w_own = scratch
    (low, dgain, outbox, inbox, deal_s, deal_r, held, ours, shard_s, shard_r, group_s, group_r,
     acc, tots, tot_s, tot_r, mine, theirs, from_below, from_above,
     here, core_s, core_r, up_s, up_r, down_s, down_r) = scratch
    h, t, up, down, across = places()

    def cols(j, c):
        return part.at[:, pl.ds(pl.multiple_of((j * 2 + c) * width, width), width)]

    def swap(j):
        return pltpu.make_async_remote_copy(src_ref=cols(j, 1 - t), dst_ref=theirs.at[j], send_sem=core_s.at[j],
                                            recv_sem=core_r.at[j], device_id=across, device_id_type=MESH)

    def own(j):
        return pltpu.make_async_copy(cols(j, t), mine.at[j], here.at[j])

    def rise(k):
        return pltpu.make_async_remote_copy(src_ref=mine.at[n - 1 - k], dst_ref=from_below.at[k], send_sem=up_s.at[k],
                                            recv_sem=up_r.at[k], device_id=up, device_id_type=MESH)

    def fall(k):
        return pltpu.make_async_remote_copy(src_ref=mine.at[k], dst_ref=from_above.at[k], send_sem=down_s.at[k],
                                            recv_sem=down_r.at[k], device_id=down, device_id_type=MESH)

    def total(j, extra):
        def step(i, c):
            r = pl.ds(pl.multiple_of(i * STEP, STEP), STEP)
            v = mine[j, r, :].astype(F32) + theirs[j, r, :].astype(F32)
            if extra is not None:
                v = v + extra(r).astype(F32)
            mine[j, r, :] = v.astype(BF)
            return c
        lax.fori_loop(0, CAP // STEP, step, 0)

    order = [j for i in range(n // 2) for j in (n - 1 - i, i)]
    for j in order:
        own(j).start()

    def load(i):
        return pltpu.make_async_copy(stacks[i], heaps[i], pile_sem.at[i])

    def add_up(i):
        load(i).wait()
        tall = heaps[i].shape[1] // 4

        def step(q, c):
            r = pl.ds(pl.multiple_of(q * tall, tall), tall)
            v = heaps[i][0, r, :].astype(F32)
            for b in range(1, m):
                v = v + heaps[i][b, r, :].astype(F32)
            added[i][r, :] = v
            return c

        lax.fori_loop(0, 4, step, 0)

    for i in range(piles):
        load(i).start()
    greet_group(n, greet_shard(m))
    me = h * 2 + t
    peers = group_peers(n)

    def tot_copy(i, p, dst):
        return pltpu.make_async_remote_copy(src_ref=share, dst_ref=tots.at[dst], send_sem=tot_s.at[i], recv_sem=tot_r.at[dst],
                                            device_id=p, device_id_type=MESH)

    for i, p in enumerate(peers):
        tot_copy(i, p[0], me).start()
    for j in order:
        swap(j).start()
    carry.start()
    shard = lax.axis_index("shard")
    others = shard_peers(m)
    if fill:
        lhs, rhs = left
        wide = lhs.shape[1] // m

        def columns(q):
            return lhs.at[:, pl.ds(pl.multiple_of(q * wide, wide), wide)]

        def fetch(i, q):
            return pltpu.make_async_copy(columns(q), l_buf.at[i], l_sem.at[i])

        def grad(i, p, src):
            return pltpu.make_async_remote_copy(src_ref=blocks.at[i], dst_ref=grads[0].at[src], send_sem=w_s.at[i],
                                                recv_sem=w_r.at[src], device_id=p[0], device_id_type=MESH)

        own_grad = pltpu.make_async_copy(blocks.at[m - 1], grads[0].at[shard], w_own)
        whole = pltpu.make_async_copy(rhs, r_buf, r_sem)
        whole.start()
        for i, p in enumerate(others):
            fetch(i, p[1]).start()
        fetch(m - 1, shard).start()

        def multiply(i):
            if i == 0:
                whole.wait()
            fetch(i, shard).wait()
            blocks[i] = dg(l_buf[i], r_buf[...], TN).astype(BF)
            if i < m - 1:
                grad(i, others[i], shard).start()
            else:
                own_grad.start()

        multiply(0)

    def arrive(j):
        own(j).wait()
        swap(j).wait_recv()

    for tick in range(2 * n - 2):
        ku = tick - h
        tu = n - 1 - ku

        @pl.when((ku >= 0) & (tu > h))
        def _():
            arrive(tu)

            @pl.when(h == 0)
            def _():
                total(tu, None)

            @pl.when(h > 0)
            def _():
                rise(ku).wait_recv()
                total(tu, lambda r: from_below[ku, r, :])

            rise(ku).start()

        kd = tick - (n - 1 - h)

        @pl.when((kd >= 0) & (kd < h))
        def _():
            arrive(kd)

            @pl.when(h == n - 1)
            def _():
                total(kd, None)

            @pl.when(h < n - 1)
            def _():
                fall(kd).wait_recv()
                total(kd, lambda r: from_above[kd, r, :])

            fall(kd).start()

        if fill and tick + 1 < m:
            multiply(tick + 1)

        if tick >= 2 * n - 2 - piles:
            add_up(tick - (2 * n - 2 - piles))

    if fill:
        for i in range(2 * n - 1, m):
            multiply(i)
    arrive(h)
    for i, p in enumerate(peers):
        tot_copy(i, p[0], p[1]).wait_recv()
    tots[me] = share[...]
    for i, p in enumerate(peers):
        tots[me] = tots[me] + tots[p[1]]
    dgain[...] = jnp.zeros_like(dgain)
    gains = gain[...]
    eighth = jnp.full((8, 128), 0.125, BF)

    def final(get):
        def step(i, c):
            r = pl.ds(pl.multiple_of(i * STEP, STEP), STEP)
            acc[r, :] = get(r)
            return c
        lax.fori_loop(0, CAP // STEP, step, 0)

    final(lambda r: mine[h, r, :].astype(F32) + theirs[h, r, :].astype(F32))

    def first(get):
        final(lambda r: acc[r, :] + get(r).astype(F32))

    @pl.when((h > 0) & (h < n - 1))
    def _():
        @pl.when(2 * h < n)
        def _():
            fall(h).wait_recv()
            first(lambda r: from_above[h, r, :])

        @pl.when(2 * h >= n)
        def _():
            rise(n - 1 - h).wait_recv()
            first(lambda r: from_below[n - 1 - h, r, :])

    by_below = (h > 0) & ((2 * h < n) | (h == n - 1))

    @pl.when(by_below)
    def _():
        rise(n - 1 - h).wait_recv()

    @pl.when(jnp.logical_not(by_below))
    def _():
        fall(h).wait_recv()

    def close(get):
        def step(i, c):
            r = pl.ds(pl.multiple_of(i * STEP, STEP), STEP)
            hi, lo = split(tots[me, i])
            total_r = dg(hi, eighth, TN) + dg(lo, eighth, TN)
            sc = scale[r, :]
            kp = kept[r, :].astype(F32)
            dn = acc[r, :] + get(r).astype(F32)
            back = base[r, :].astype(F32) + sc * (gains * dn) - kp * jnp.tile((sc * sc * sc) * (total_r * (1.0 / D)), (1, width // 128))
            low[r, :] = back.astype(BF)
            dgain[...] += jnp.sum((dn * kp * sc).reshape(STEP // 8, 8, width), axis=0)
            return c
        lax.fori_loop(0, CAP // STEP, step, 0)

    @pl.when(by_below)
    def _():
        close(lambda r: from_below[n - 1 - h, r, :])

    @pl.when(jnp.logical_not(by_below))
    def _():
        close(lambda r: from_above[h, r, :])

    for i, p in enumerate(peers):
        tot_copy(i, p[0], me).wait_send()

    per_peer = outbox.shape[1]
    ids = lax.broadcasted_iota(jnp.int32, (per_peer, place.shape[1]), 0)

    def back(i, p, src):
        return pltpu.make_async_remote_copy(src_ref=outbox.at[p[1]], dst_ref=inbox.at[src], send_sem=deal_s.at[i],
                                            recv_sem=deal_r.at[src], device_id=p[0], device_id_type=MESH)

    def pick(q):
        return dg(jnp.where(place[...] - q * per_peer == ids, 1.0, 0.0).astype(BF), low[...], NN).astype(BF)

    def over(i, p, src):
        return pltpu.make_async_remote_copy(src_ref=ours, dst_ref=held.at[src], send_sem=shard_s.at[i],
                                            recv_sem=shard_r.at[src], device_id=p[0], device_id_type=MESH)

    def along(i, p, src):
        return pltpu.make_async_remote_copy(src_ref=held.at[shard], dst_ref=every.at[src], send_sem=group_s.at[i],
                                            recv_sem=group_r.at[src], device_id=p[0], device_id_type=MESH)

    for i, p in enumerate(others):
        outbox[p[1]] = pick(p[1])
        back(i, p, shard).start()
    at = lax.broadcasted_iota(jnp.int32, small.shape, 0)
    ours[...] = small[...] + jnp.where(at == 12, jnp.sum(dgain[...], axis=0, keepdims=True), 0.0)
    for i, p in enumerate(others):
        over(i, p, shard).start()
    inbox[shard] = pick(shard)
    v = ours[...]
    for i, p in enumerate(others):
        over(i, p, p[1]).wait_recv()
        v = v + held[p[1]]
    held[shard] = v
    every[me] = v
    for i, p in enumerate(peers):
        along(i, p, me).start()
    for i, p in enumerate(others):
        back(i, p, p[1]).wait_recv()
    lanes = lax.broadcasted_iota(jnp.int32, (STEP, m * per_peer), 1)

    def settle(i, c):
        r = pl.ds(pl.multiple_of(i * STEP, STEP), STEP)
        chosen = jnp.where(sent[r, :] == lanes, 1.0, 0.0).astype(BF)
        tokens[r, :, :] = dg(chosen, inbox[...].reshape(m * per_peer, width), NN).reshape(STEP, 1, width)
        return c

    lax.fori_loop(0, REAL_DEV // STEP, settle, 0)
    for i, p in enumerate(peers):
        along(i, p, p[1]).wait_recv()
        along(i, p, me).wait_send()
    for i, p in enumerate(others):
        over(i, p, shard).wait_send()
        back(i, p, shard).wait_send()
    for j in range(n):
        swap(j).wait_send()
    for k in range(n - 1):
        @pl.when(n - 1 - k > h)
        def _():
            rise(k).wait_send()

        @pl.when(k < h)
        def _():
            fall(k).wait_send()
    carry.wait()
    if fill:
        own_grad.wait()
        for i, p in enumerate(others):
            grad(i, p, p[1]).wait_recv()
            grad(i, p, shard).wait_send()


def z_finish(n, part, kept, scale, base, gain, share, small, sent, place, per_peer, collective_id, name, m, lhs, rhs, stacks):
    rows, width = part.shape[0], part.shape[1] // (2 * n)
    dma = pltpu.SemaphoreType.DMA
    wide = lhs.shape[1] // m
    fill = wide % 128 == 0
    if fill:
        kinds, arrays, extra = (), (), [lhs, rhs]
        made = [jax.ShapeDtypeStruct((m, wide, rhs.shape[1]), BF)]
        room = [pltpu.VMEM((m, rows, wide), BF), pltpu.VMEM(rhs.shape, BF), pltpu.VMEM(made[0].shape, BF),
                dma((m,)), dma, dma((m,)), dma((m,)), dma]
    else:
        kinds, arrays = ("swap",), (dg(lhs, rhs, TN).astype(BF).reshape(m, wide, rhs.shape[1]),)
        extra, made, room = [], [], []
    shapes, sems = carried(kinds, m, arrays)
    return pl.pallas_call(
        functools.partial(finish_kernel, n, width, m, kinds, int(fill), len(stacks)),
        out_shape=[jax.ShapeDtypeStruct((REAL_DEV, 1, width), F32), jax.ShapeDtypeStruct((2 * n,) + small.shape, F32)]
        + [jax.ShapeDtypeStruct(a.shape[1:], F32) for a in stacks] + made + shapes,
        in_specs=[HBM] + [VM] * 8 + [HBM] * (len(stacks) + len(extra) + len(shapes)),
        out_specs=[VM] * (2 + len(stacks)) + [HBM] * (len(made) + len(shapes)),
        scratch_shapes=[pltpu.VMEM(a.shape, BF) for a in stacks] + [pltpu.VMEM((rows, width), BF), pltpu.VMEM((8, width), F32)]
        + [pltpu.VMEM((m, per_peer, width), BF)] * 2 + [dma((m,))] * 2
        + [pltpu.VMEM((m,) + small.shape, F32), pltpu.VMEM(small.shape, F32), dma((m,)), dma((m,)), dma((2 * n,)), dma((2 * n,))]
        + [pltpu.VMEM((rows, width), F32), pltpu.VMEM((2 * n, rows // STEP, 8, STEP), F32), dma((2 * n,)), dma((2 * n,))]
        + [pltpu.VMEM((n, rows, width), BF)] * 2 + [pltpu.VMEM((n - 1, rows, width), BF)] * 2
        + [dma((n,))] * 3 + [dma((n - 1,))] * 4 + room + [dma((len(stacks),))] + sems,
        compiler_params=pltpu.CompilerParams(collective_id=collective_id, has_side_effects=True, vmem_limit_bytes=ROOM),
        cost_estimate=pl.CostEstimate(flops=0, bytes_accessed=LINK_COST, transcendentals=0),
        name=name,
    )(part, kept, scale, base, gain, share, small, sent, place, *stacks, *extra, *arrays)


CHUNKS = 4
SUBS = 4
UNITS = CHUNKS * SUBS
UNIT = CAP // UNITS


def turn_kernel(n, width, m, kinds, norm, *refs):
    if norm:
        (part, kept, scale, base, gain, share), (out, full, low, dgain), scratch, carry = carry_of(kinds, m, refs, 6, 4)
        tots, tot_s, tot_r = scratch[-3:]
        scratch = scratch[:-3]
    else:
        (part, base), (out, full, low), scratch, carry = carry_of(kinds, m, refs, 2, 3, True)
    (mine, theirs, from_below, from_above, here, core_s, core_r, up_s, up_r, down_s, down_r,
     gu_s, gu_r, gd_s, gd_r, gc_s, gc_r, flat) = scratch
    h, t, up, down, across = places()
    me = h * 2 + t
    chunks = CHUNKS

    def rows(u):
        return pl.ds(pl.multiple_of(u * UNIT, UNIT), UNIT)

    def wide(r):
        return pl.ds(pl.multiple_of(r * SUBS * UNIT, SUBS * UNIT), SUBS * UNIT)

    def lanes(j, c):
        return pl.ds(pl.multiple_of((j * 2 + c) * width, width), width)

    def remote(src, dst, ss, rs, to):
        return pltpu.make_async_remote_copy(src_ref=src, dst_ref=dst, send_sem=ss, recv_sem=rs, device_id=to, device_id_type=MESH)

    def swap(j, r):
        return remote(part.at[wide(r), lanes(j, 1 - t)], theirs.at[j, wide(r)], core_s.at[j, r], core_r.at[j, r], across)

    def own(j, r):
        return pltpu.make_async_copy(part.at[wide(r), lanes(j, t)], mine.at[j, wide(r)], here.at[j, r])

    def rise(k, u):
        return remote(mine.at[n - 1 - k, rows(u)], from_below.at[k, rows(u)], up_s.at[k, u], up_r.at[k, u], up)

    def fall(k, u):
        return remote(mine.at[k, rows(u)], from_above.at[k, rows(u)], down_s.at[k, u], down_r.at[k, u], down)

    def spread(j, u, src, ss, rs, to):
        return remote(src, full.at[rows(u), lanes(j, t)], ss.at[j, u], rs.at[j, u], to)

    def piece(j, u):
        return full.at[rows(u), lanes(j, t)]

    def tot_copy(i, p, dst):
        return remote(share, tots.at[dst], tot_s.at[i], tot_r.at[dst], p)

    order = [j for i in range(n // 2) for j in (n - 1 - i, i)]
    for r in range(chunks):
        for j in order:
            own(j, r).start()
    if norm:
        greet_group(n, carry.greet())
        for i, p in enumerate(group_peers(n)):
            tot_copy(i, p[0], me).start()
        dgain[...] = jnp.zeros_like(dgain)
    else:
        greet(n, h, up, down, across, carry.greet())
    for r in range(chunks):
        for j in order:
            swap(j, r).start()
    carry.start()

    def arrive(j, r):
        own(j, r).wait()
        swap(j, r).wait_recv()

    def both(j, u):
        return mine[j, rows(u), :].astype(F32) + theirs[j, rows(u), :].astype(F32)

    def climb(o, r, s):
        u = SUBS * r + s

        @pl.when(h <= o)
        def _():
            ku = o - h
            tu = n - 1 - ku
            if s == 0:
                arrive(tu, r)

            @pl.when(h == 0)
            def _():
                mine[tu, rows(u), :] = both(tu, u).astype(BF)

            @pl.when(h > 0)
            def _():
                rise(ku, u).wait_recv()
                mine[tu, rows(u), :] = (both(tu, u) + from_below[ku, rows(u), :].astype(F32)).astype(BF)

            rise(ku, u).start()

        @pl.when(h >= n - 1 - o)
        def _():
            kd = o - (n - 1 - h)
            if s == 0:
                arrive(kd, r)

            @pl.when(h == n - 1)
            def _():
                mine[kd, rows(u), :] = both(kd, u).astype(BF)

            @pl.when(h < n - 1)
            def _():
                fall(kd, u).wait_recv()
                mine[kd, rows(u), :] = (both(kd, u) + from_above[kd, rows(u), :].astype(F32)).astype(BF)

            fall(kd, u).start()

    def gather_totals():
        for i, p in enumerate(group_peers(n)):
            tot_copy(i, p[0], p[1]).wait_recv()
        tots[me] = share[...]
        for i, p in enumerate(group_peers(n)):
            tots[me] = tots[me] + tots[p[1]]

    def last(r, s):
        u = SUBS * r + s
        if s == 0:
            arrive(h, r)
        flat[rows(u), :] = both(h, u)

        @pl.when(h > 0)
        def _():
            k = n - 1 - h
            rise(k, u).wait_recv()
            flat[rows(u), :] = flat[rows(u), :] + from_below[k, rows(u), :].astype(F32)

        @pl.when(h < n - 1)
        def _():
            fall(h, u).wait_recv()
            flat[rows(u), :] = flat[rows(u), :] + from_above[h, rows(u), :].astype(F32)

        if norm:
            close(u)
        else:
            v = base[rows(u), :].astype(F32) + flat[rows(u), :]
            out[rows(u), :] = v
            low[rows(u), :] = v.astype(BF)
            set_out(u)

    def close(u):
        hi, lo = split(tots[me, u])
        eighth = jnp.full((8, 128), 0.125, BF)
        total_r = (dg(hi, eighth, TN) + dg(lo, eighth, TN))[:UNIT]
        sc = scale[rows(u), :]
        kp = kept[rows(u), :].astype(F32)
        dn = flat[rows(u), :]
        v = (base[rows(u), :].astype(F32) + sc * (gain[...] * dn)
             - kp * jnp.tile((sc * sc * sc) * (total_r * (1.0 / D)), (1, width // 128)))
        out[rows(u), :] = v
        low[rows(u), :] = v.astype(BF)
        dgain[...] += jnp.sum((dn * kp * sc).reshape(UNIT // 8, 8, width), axis=0)
        set_out(u)

    def set_out(u):
        src = low.at[rows(u)]

        @pl.when(h < n - 1)
        def _():
            spread(h, u, src, gu_s, gu_r, up).start()

        @pl.when(h > 0)
        def _():
            spread(h, u, src, gd_s, gd_r, down).start()

        spread(h, u, src, gc_s, gc_r, across).start()

    def pass_on(k, r, s):
        u = SUBS * r + s
        below, above = h - k, h + k

        @pl.when(below >= 0)
        def _():
            spread(below, u, piece(below, u), gu_s, gu_r, up).wait_recv()

            @pl.when(h < n - 1)
            def _():
                spread(below, u, piece(below, u), gu_s, gu_r, up).start()

            spread(below, u, piece(below, u), gc_s, gc_r, across).start()

        @pl.when(above < n)
        def _():
            spread(above, u, piece(above, u), gd_s, gd_r, down).wait_recv()

            @pl.when(h > 0)
            def _():
                spread(above, u, piece(above, u), gd_s, gd_r, down).start()

            spread(above, u, piece(above, u), gc_s, gc_r, across).start()

    def at(o, r, s):
        if o < n - 1:
            climb(o, r, s)
        elif o == n - 1:
            if norm and s == 0:
                @pl.when(r == 0)
                def _():
                    gather_totals()
            last(r, s)
        elif o < 2 * n - 1:
            pass_on(o - n + 1, r, s)

    def period(r, c):
        for e in range(len(kinds)):
            @pl.when(r == e + 1)
            def _():
                carry.relay(e)

        for o in range(n):
            for s in range(SUBS):
                @pl.when(r > 0)
                def _():
                    at(o + n, r - 1, s)

                @pl.when(r < chunks)
                def _():
                    at(o, r, s)
        return c

    lax.fori_loop(0, chunks + 1, period, 0)
    mine_out = pltpu.make_async_copy(low, full.at[:, lanes(h, t)], here.at[0, 0])
    mine_out.start()

    def drain(u, c):
        for j in range(n):
            back = remote(piece(j, u), full.at[rows(u), lanes(j, 1 - t)], gc_s.at[j, u], gc_r.at[j, u], across)
            back.wait_recv()
            back.wait_send()

            @pl.when((j <= h) & (h < n - 1))
            def _():
                spread(j, u, piece(j, u), gu_s, gu_r, up).wait_send()

            @pl.when((j >= h) & (h > 0))
            def _():
                spread(j, u, piece(j, u), gd_s, gd_r, down).wait_send()

        for k in range(n - 1):
            @pl.when(n - 1 - k > h)
            def _():
                rise(k, u).wait_send()

            @pl.when(k < h)
            def _():
                fall(k, u).wait_send()

        return c

    if norm:
        for i, p in enumerate(group_peers(n)):
            tot_copy(i, p[0], me).wait_send()
    lax.fori_loop(0, UNITS, drain, 0)
    for r in range(chunks):
        for j in range(n):
            swap(j, r).wait_send()
    mine_out.wait()
    carry.wait()


def z_turn(n, part, base, collective_id, name, m=1, kinds=(), arrays=(), norm=None):
    rows, width = part.shape[0], part.shape[1] // (2 * n)
    dma = pltpu.SemaphoreType.DMA
    shapes, sems = carried(kinds, m, arrays)
    shape = jax.ShapeDtypeStruct
    ins = [part, base] if norm is None else [part, norm[0], norm[1], base, norm[2], norm[3]]
    outs = [shape((rows, width), F32), shape((rows, 2 * n * width), BF), shape((rows, width), BF)]
    out_specs = [VM, HBM, VM]
    more = []
    if norm is not None:
        outs, out_specs = outs + [shape((8, width), F32)], out_specs + [VM]
        more = [pltpu.VMEM((2 * n, UNITS, 8, 128), F32), dma((2 * n,)), dma((2 * n,))]
    return pl.pallas_call(
        functools.partial(turn_kernel, n, width, m, kinds, norm is not None),
        out_shape=outs + shapes,
        in_specs=[HBM] + [VM] * (len(ins) - 1) + [HBM] * len(shapes), out_specs=out_specs + [HBM] * len(shapes),
        scratch_shapes=[pltpu.VMEM((n, rows, width), BF)] * 2 + [pltpu.VMEM((n - 1, rows, width), BF)] * 2
        + [dma((n, CHUNKS))] * 3 + [dma((n - 1, UNITS))] * 4 + [dma((n, UNITS))] * 6 + [pltpu.VMEM((rows, width), F32)]
        + more + sems,
        compiler_params=pltpu.CompilerParams(collective_id=collective_id, has_side_effects=True, vmem_limit_bytes=ROOM),
        cost_estimate=pl.CostEstimate(flops=0, bytes_accessed=LINK_COST, transcendentals=0),
        name=name,
    )(*ins, *arrays)


def rows_spec(rows, cols):
    return pl.BlockSpec((rows, cols), lambda i: (i, 0))


def fixed_spec(*shape):
    return pl.BlockSpec(shape, lambda i: (0,) * len(shape), pipeline_mode=pl.Buffered(1))


def by_rows(kernel, rows, ins, fixed, outs, lanes, flops, name):
    specs = [rows_spec(rows, a.shape[1]) for a in ins] + [fixed_spec(*a.shape) for a in fixed]
    out_specs = [rows_spec(rows, o.shape[1]) for o in outs]
    shapes = list(outs)
    if lanes:
        out_specs.append(pl.BlockSpec((lanes * rows // CAP, 8, 128), lambda i: (i, 0, 0)))
        shapes.append(jax.ShapeDtypeStruct((lanes, 8, 128), F32))
    return pl.pallas_call(
        kernel, grid=(CAP // rows,), out_shape=shapes, in_specs=specs, out_specs=out_specs,
        compiler_params=pltpu.CompilerParams(dimension_semantics=("arbitrary",), vmem_limit_bytes=ROOM),
        cost_estimate=pl.CostEstimate(flops=flops, bytes_accessed=20 * 2**20, transcendentals=0),
        name=name,
    )(*ins, *fixed)


def lane_sums(values, share):
    units, rows = share.shape[0], values.shape[0] // share.shape[0]
    hi, lo = split(values)
    ones = jnp.ones((8, values.shape[1]), BF)
    for i in range(units):
        r = slice(i * rows, (i + 1) * rows)
        share[i, :, :rows] = dg(ones, hi[r], NT) + dg(ones, lo[r], NT)
        if rows < 128:
            share[i, :, rows:] = jnp.zeros((8, 128 - rows), F32)


def normal(x, gain):
    x = x.astype(F32)
    scale = lax.rsqrt(jnp.mean(x * x, axis=1, keepdims=True) + EPSILON)
    return scale, (x * scale * gain).astype(BF)


def project_kernel(x, gain, w, pre, normed, scale):
    sc, nb = normal(x[...], gain[...])
    scale[...] = sc
    normed[...] = nb
    pre[...] = dg(nb, w[...], NN)


def project(rows_full, gain, w_in):
    sd = jax.ShapeDtypeStruct
    outs = [sd((CAP, w_in.shape[1]), F32), sd((CAP, D), BF), sd((CAP, 1), F32)]
    return by_rows(project_kernel, 256, [rows_full], [gain, w_in], outs, 0, 2 * CAP * D * w_in.shape[1], "project")


def ffn_kernel(x, cot, gain, w_ug, w_u, w_d, normed, product, d_gate, d_up, d_normed, scale, share):
    sc, nb = normal(x[...], gain[...])
    scale[...] = sc
    normed[...] = nb
    gate = dg(nb, w_ug[...], NT)
    up = dg(nb, w_u[...], NT)
    sig = sigmoid(gate)
    act = gate * sig
    product[...] = (act * up).astype(BF)
    d_product = dg(cot[...], w_d[...], NT)
    dgt = (d_product * up * sig * (1.0 + gate * (1.0 - sig))).astype(BF)
    dup = (d_product * act).astype(BF)
    d_gate[...] = dgt
    d_up[...] = dup
    d_normed[...] = (dg(dgt, w_ug[...], NN) + dg(dup, w_u[...], NN)).astype(BF)
    lane_sums((dgt.astype(F32) * gate + dup.astype(F32) * up) / sc, share)


def ffn(held_full, cot_full, gain, w_ug, w_u, w_d):
    sd = jax.ShapeDtypeStruct
    ff = w_u.shape[0]
    outs = [sd((CAP, D), BF)] + [sd((CAP, ff), BF)] * 3 + [sd((CAP, D), BF), sd((CAP, 1), F32)]
    return by_rows(ffn_kernel, CAP // CHUNKS, [held_full, cot_full], [gain, w_ug, w_u, w_d], outs, UNITS,
                   10 * CAP * D * ff, "feed_forward")


def unproject_kernel(d_pre, pre, scale, w, d_normed, share):
    d = d_pre[...]
    d_normed[...] = dg(d, w[...], NT).astype(BF)
    lane_sums(d.astype(F32) * pre[...] / scale[...], share)


def unproject(d_pre, pre, scale, w_in):
    outs = [jax.ShapeDtypeStruct((CAP, D), BF)]
    return by_rows(unproject_kernel, 256, [d_pre, pre, scale], [w_in], outs, CAP // STEP, 2 * CAP * D * w_in.shape[1], "unproject")


def blocks_kernel(shard, a, x, b, y, *outs):
    tall = a.shape[1]
    first, second = dg(a[...], x[...], TN).astype(BF), dg(b[...], y[...], TN).astype(BF)
    for i, out in enumerate(outs):
        @pl.when(pl.program_id(0) == i)
        def _():
            out[:tall] = first
            out[tall:] = second


def grad_blocks(m, device, a, x, b, y):
    wide, tall = x.shape[1] // m, a.shape[1] + b.shape[1]
    if wide % 128:
        both = jnp.concatenate([dg(a, x, TN), dg(b, y, TN)], axis=0).astype(BF)
        return [lax.dynamic_slice_in_dim(both, lax.rem(device + i, m) * wide, wide, 1) for i in range(m)]

    def side(i, shard):
        return (0, lax.rem(shard[0] + i, m))

    def fixed(i, shard):
        return (0, 0)

    return pl.pallas_call(
        blocks_kernel,
        grid_spec=pltpu.PrefetchScalarGridSpec(
            num_scalar_prefetch=1, grid=(m,),
            in_specs=[pl.BlockSpec(a.shape, fixed, pipeline_mode=pl.Buffered(1)), pl.BlockSpec((CAP, wide), side),
                      pl.BlockSpec(b.shape, fixed, pipeline_mode=pl.Buffered(1)), pl.BlockSpec((CAP, wide), side)],
            out_specs=[pl.BlockSpec((tall, wide), fixed)] * m),
        out_shape=[jax.ShapeDtypeStruct((tall, wide), BF)] * m,
        compiler_params=pltpu.CompilerParams(dimension_semantics=("arbitrary",), vmem_limit_bytes=ROOM),
        cost_estimate=pl.CostEstimate(flops=2 * CAP * tall * x.shape[1], bytes_accessed=12 * 2**20, transcendentals=0),
        name="gradient_blocks",
    )(device[None], a, x, b, y)


PRE = 1152
GROUP = ("head", "tensor")


def mm(left, right, dims=NN):
    return lax.dot_general(left, right, dims, preferred_element_type=F32)


def full_rows(piece_in):
    return lax.all_gather(piece_in, GROUP, axis=1, tiled=True)


def shares(partial_sum):
    return lax.psum_scatter(partial_sum.astype(BF), GROUP, scatter_dimension=1, tiled=True).astype(F32)


def column_blocks(grad, m):
    rows, wide = grad.shape[0], grad.shape[1] // m
    if wide % 128 == 0:
        return "columns", grad
    return "swap", grad.reshape(rows, m, wide).transpose(1, 0, 2)


def side_by_side(wide):
    return "abreast" if wide % 128 == 0 else "pile"


def level(weights):
    if weights.ndim == 2:
        return weights
    return weights.transpose(1, 0, 2).reshape(weights.shape[1], -1)


def gather_ring(piece):
    shards, device = lax.axis_size("shard"), lax.axis_index("shard")
    wide = piece.shape[1]
    whole = jnp.zeros((piece.shape[0], shards * wide), piece.dtype)
    for i in range(shards):
        came = lax.ppermute(piece, "shard", [(o, (o + i) % shards) for o in range(shards)]) if i else piece
        whole = lax.dynamic_update_slice_in_dim(whole, came, lax.rem(device - i + shards, shards) * wide, 1)
    return whole


def swap_ring(a, x, b, y):
    shards, device = lax.axis_size("shard"), lax.axis_index("shard")
    blocks = grad_blocks(shards, device, a, x, b, y)
    total = blocks[0].astype(F32)
    for i in range(1, shards):
        total = total + lax.ppermute(blocks[i], "shard", [(o, (o + i) % shards) for o in range(shards)]).astype(F32)
    return total[:a.shape[1]], total[a.shape[1]:]


def sum_blocks(blocks):
    return jnp.sum(blocks.astype(F32), axis=0)


def body(tokens, seq_lengths, dealing, gain_mixer, w_query, w_key, w_value, w_gate, w_beta, conv_weight,
         gain_heads, w_out, gain_ffn, w_up_gate, w_up, w_down, cotangent):
    shards = lax.axis_size("shard")
    width = tokens.shape[2]
    col_start = lax.axis_index(GROUP) * width
    per_peer = (CAP // shards + SEQ_DEV + 15) // 16 * 16

    w_piece = jnp.concatenate(
        [w_query, w_key, w_value, w_gate, w_beta, jnp.zeros((w_beta.shape[0], PRE - 4 * width - w_beta.shape[1]), BF)], axis=1)

    own_rows = tokens.reshape(REAL_DEV, width)
    taps = conv_weight.reshape(3 * CONV, width)
    head_gain = gain_heads[None, :]

    n = lax.axis_size("head")
    side = side_by_side(w_up.shape[0])
    x_rows, rows_full, sent_slot, recv_slot, pos, filled_f, w_in = z_gather(
        n, seq_lengths, dealing, own_rows, per_peer, 1, "gather_rows", shards, ("gather",), (w_piece,))
    rows_full, cot_piece, w_out = lax.optimization_barrier((rows_full, cotangent, w_out))
    w_o = gather_ring(w_out)
    cot_full = full_rows(cot_piece)
    pre, normed, scale_one = project(rows_full, gain_mixer[None, :], w_in)
    mixed, *saved = mixer_fwd(pre, pos, filled_f, taps, head_gain)
    branch_part, cot_full = lax.optimization_barrier((mm(mixed, w_o).astype(BF), cot_full))
    hidden, held_full, held_low, w_ug, w_u, w_d = z_turn(
        n, branch_part, x_rows, 2, "turn_branch", shards, (side,) * 3, (w_up_gate.T, w_up.T, w_down))
    w_ug, w_u, w_d = level(w_ug), level(w_u), level(w_d)
    normed_two, product, d_gate, d_up, d_normed_two, scale_two, share_two = ffn(
        held_full, cot_full, gain_ffn[None, :], w_ug, w_u, w_d)
    down_kind, d_w_down = column_blocks(mm(product, cot_full, TN).astype(BF), shards)
    gate_kind, d_w_ug = column_blocks(mm(d_gate, normed_two, TN).astype(BF), shards)
    ffn_gain_part = lax.dynamic_slice_in_dim(gain_ffn, col_start, width)[None, :]
    d_hidden, d_branch_full, _, ffn_gain_grad, d_w_ug, d_w_down = z_turn(
        n, d_normed_two, cotangent, 4, "turn_normed_two", shards, (gate_kind, down_kind), (d_w_ug, d_w_down),
        norm=(held_low, scale_two, ffn_gain_part, share_two))
    out_part = mm(product, w_d).astype(BF)
    out_part, d_branch_full = lax.optimization_barrier((out_part, d_branch_full))
    d_w_u, d_w_out = swap_ring(d_up, normed_two, mixed, d_branch_full)
    out_sum = shares(out_part)
    d_mixed = mm(d_branch_full, w_o, NT)
    d_pre, d_taps, d_head_gain = mixer_bwd(d_mixed, pre, pos, filled_f, taps, head_gain, saved)
    d_normed, share_one = unproject(d_pre, pre, scale_one, w_in)
    d_normed, out_sum = lax.optimization_barrier((d_normed, out_sum))
    block_out = (hidden + out_sum).astype(BF)
    mixer_gain_part = lax.dynamic_slice_in_dim(gain_mixer, col_start, width)[None, :]
    small = jnp.concatenate([
        jnp.sum(d_taps, axis=1), jnp.zeros((1, width), F32), jnp.sum(ffn_gain_grad, axis=0)[None, :],
        jnp.pad(jnp.sum(d_head_gain, axis=0), (0, width - HD))[None, :],
        jnp.zeros((1, width), F32)], axis=0)
    d_tokens, summed, d_w_ug, d_w_down, d_w_in = z_finish(
        n, d_normed, x_rows, scale_one, d_hidden, mixer_gain_part, share_one, small,
        sent_slot, recv_slot, per_peer, 6, "finish_rows", shards, normed, d_pre, (d_w_ug, d_w_down))
    d_w_in = sum_blocks(d_w_in)
    by_row = summed.transpose(1, 0, 2).reshape(16, D)
    d_conv = by_row[:12].reshape(CONV, 3, D)
    d_gain_heads = jnp.sum(summed[:, 14, :HD], axis=0)
    cut = [0, width, 2 * width, 3 * width, 4 * width]
    return (
        block_out, d_tokens, by_row[12],
        d_w_in[:, cut[0]:cut[1]], d_w_in[:, cut[1]:cut[2]], d_w_in[:, cut[2]:cut[3]], d_w_in[:, cut[3]:cut[4]],
        d_w_in[:, 4 * width:4 * width + w_beta.shape[1]],
        d_conv, d_gain_heads, d_w_out, by_row[13],
        d_w_ug.T, d_w_u.T, d_w_down,
    )


def solution(mesh):
    feat = ("head", "tensor")
    placed = (
        P(None, "shard", feat), P(), P(), P(),
        P("shard", feat), P("shard", feat), P("shard", feat), P("shard", feat), P("shard", feat),
        P(None, None, feat), P(), P(feat, "shard"), P(),
        P("shard", feat), P("shard", feat), P(feat, "shard"), P("shard", feat),
    )
    given = (
        P("shard", feat), P(None, "shard", feat), P(),
        P("shard", feat), P("shard", feat), P("shard", feat), P("shard", feat), P("shard", feat),
        P(), P(), P(feat, "shard"), P(),
        P("shard", feat), P("shard", feat), P(feat, "shard"),
    )
    return jax.shard_map(body, mesh=mesh, in_specs=placed, out_specs=given, check_vma=False)
```

```python
import functools
import jax
import jax.numpy as jnp
from jax import lax
from jax.experimental import pallas as pl
from jax.experimental.pallas import tpu as pltpu

from jax.sharding import PartitionSpec as P

D = 2048
HD = 128
CONV = 4
BLOCK = 64
SEQ_DEV = 4
REAL_DEV = 1152
CAP = 1280
NB = CAP // BLOCK
EPSILON = 1e-06
HEAD_FLOOR = 0.01
PRE = 1152
BETA = 16
F32 = jnp.float32
BF = jnp.bfloat16

def split(x):
    hi = x.astype(BF)
    return hi, (x - hi.astype(F32)).astype(BF)

NN=(((1,),(0,)),((),())); NT=(((1,),(1,)),((),())); TN=(((0,),(0,)),((),()))

def dg(a, b, dims):
    return lax.dot_general(a, b, dims, preferred_element_type=F32)

def d3(a, b, dims=NN):
    ah, al = split(a); bh, bl = split(b)
    return dg(ah, bh, dims) + (dg(ah, bl, dims) + dg(al, bh, dims))

def four_times(step):
    return lambda i, c: step(4 * i + 3, step(4 * i + 2, step(4 * i + 1, step(4 * i, c))))

def goes_on(pos_ref, n):
    first = pos_ref[pl.ds(pl.multiple_of(n * BLOCK, BLOCK), 8), :][:1]
    return jnp.where(first != 0, 1.0, 0.0)

def masks():
    ri = lax.broadcasted_iota(jnp.int32, (BLOCK, BLOCK), 0)
    ci = lax.broadcasted_iota(jnp.int32, (BLOCK, BLOCK), 1)
    return ri, ci

def sigmoid(x):
    return 1.0 / (1.0 + jnp.exp(-x))

def conv_rows(cur, tail, wt, pos):
    ext = jnp.concatenate([tail, cur], axis=0)
    out = wt[0] * cur
    for j in range(1, CONV):
        sh = pltpu.roll(ext, j, axis=0)[8:]
        out = out + wt[j] * jnp.where(pos >= j, sh, 0.0)
    return out

def inverses(lmats, ri, ci):
    apart = ri ^ ci
    xs = [jnp.where(apart == 0, 1.0, 0.0) - jnp.where(apart == 1, m, 0.0) for m in lmats]
    s = 2
    while s < BLOCK:
        at = (apart >= s) & (apart < 2 * s)
        ys = [d3(x, jnp.where(at, m, 0.0)) for x, m in zip(xs, lmats)]
        xs = [x - d3(y, x) for x, y in zip(xs, ys)]
        s *= 2
    return xs

def fwd_kernel(pre, pos_ref, fill_ref, cw, gain, mixed, *refs):
    given, (c_out, qk, w_out, u_out, u2_out, o_out, p_out, t_out, m_out, s_out, b_s), sem = refs[:10], refs[10:21], refs[21]
    held = (c_out, qk, w_out, u_out, u2_out, o_out, p_out, t_out, m_out, s_out)

    def keep(*which):
        for i in which:
            pltpu.make_async_copy(held[i], given[i], sem.at[i]).start()

    ri, ci = masks()
    heads = 2
    def phase_a(n, tails):
        r = pl.ds(pl.multiple_of(n * BLOCK, BLOCK), BLOCK)
        pos = pos_ref[r, :]; fil = fill_ref[r, :]
        new_tails = []
        acts = []
        for i in range(3):
            cur = pre[r, i*256:(i+1)*256]
            wt = [cw[j*3+i:j*3+i+1, :] for j in range(CONV)]
            cc = conv_rows(cur, tails[i], wt, pos)
            c_out[r, i*256:(i+1)*256] = cc
            acts.append(cc * sigmoid(cc) * fil)
            new_tails.append(cur[BLOCK-8:])
        beta = sigmoid(pre[r, 1024:1152])
        for h in range(heads):
            hs = slice(h*HD, (h+1)*HD)
            yq = acts[0][:, hs]; yk = acts[1][:, hs]; v = acts[2][:, hs]
            q = yq * lax.rsqrt(jnp.sum(yq*yq, axis=1, keepdims=True) + EPSILON)
            k = yk * lax.rsqrt(jnp.sum(yk*yk, axis=1, keepdims=True) + EPSILON)
            b = beta[:, h:h+1]
            qk[r, h*HD:(h+1)*HD] = q
            qk[r, 256+h*HD:256+(h+1)*HD] = k
            lmat = jnp.where(ri > ci, b * d3(k, k, NT), 0.0)
            p_out[n*2+h] = jnp.where(ri >= ci, d3(q, k, NT), 0.0)
            t_out[n*2+h] = lmat
            u_out[r, hs] = b*v
            w_out[r, hs] = b*k
        return tuple(new_tails)
    z8 = jnp.zeros((8, 256), F32)
    lax.fori_loop(0, NB // 4, four_times(phase_a), (z8, z8, z8))
    keep(0, 1, 6)
    GRP = 20
    def phase_t(i, _):
        ts = inverses([t_out[i*GRP+j] for j in range(GRP)], ri, ci)
        for j in range(GRP):
            t_out[i*GRP+j] = ts[j]
        return 0
    lax.fori_loop(0, 2*NB//GRP, phase_t, 0)
    keep(7)
    def phase_w(i, _):
        todo = [(n, pl.ds(pl.multiple_of(n * BLOCK, BLOCK), BLOCK), h, slice(h*HD, (h+1)*HD)) for n in (4*i, 4*i+1, 4*i+2, 4*i+3) for h in range(heads)]
        wu = [d3(t_out[n*2+h], jnp.concatenate([w_out[r, c], u_out[r, c]], axis=1)) for n, r, h, c in todo]
        mb = [d3(qk[r, 256+h*HD:256+(h+1)*HD], x, TN) for x, (n, r, h, c) in zip(wu, todo)]
        for x, y, (n, r, h, c) in zip(wu, mb, todo):
            w_out[r, c] = x[:, :HD]; u_out[r, c] = x[:, HD:]
            m_out[n*2+h] = y[:, :HD]; b_s[n*2+h] = y[:, HD:]
        return 0
    lax.fori_loop(0, NB//4, phase_w, 0)
    keep(2, 3, 8)
    def phase_b(n, ss):
        out = []
        for h in range(heads):
            e = n*2+h
            s = ss[h] * goes_on(pos_ref, n)
            s_out[e] = s
            out.append(s - d3(m_out[e], s) + b_s[e])
        return tuple(out)
    zs = jnp.zeros((HD, HD), F32)
    lax.fori_loop(0, NB, phase_b, (zs, zs))
    keep(9)
    def phase_c(i, _):
        todo = [(n, pl.ds(pl.multiple_of(n * BLOCK, BLOCK), BLOCK), h, slice(h*HD, (h+1)*HD)) for n in (4*i, 4*i+1, 4*i+2, 4*i+3) for h in range(heads)]
        rr = [d3(jnp.concatenate([w_out[r, c], qk[r, c]], axis=0), s_out[n*2+h]) for n, r, h, c in todo]
        u2 = [u_out[r, c] - v[:BLOCK] for v, (n, r, h, c) in zip(rr, todo)]
        os_ = [v[BLOCK:] + d3(p_out[n*2+h], u) for v, u, (n, r, h, c) in zip(rr, u2, todo)]
        for o, u, (n, r, h, c) in zip(os_, u2, todo):
            u2_out[r, c] = u
            o_out[r, c] = o
            ms = jnp.mean(o*o, axis=1, keepdims=True)
            sc = lax.rsqrt(jnp.maximum(ms, HEAD_FLOOR))
            gg = pre[r, 768+h*HD:768+(h+1)*HD]
            mixed[r, c] = (o * sc * gain[...] * (gg * sigmoid(gg))).astype(BF)
        return 0
    lax.fori_loop(0, NB // 4, phase_c, 0)
    keep(4, 5)
    for i in range(10):
        pltpu.make_async_copy(held[i], given[i], sem.at[i]).wait()

def sds(*s, dt=F32): return jax.ShapeDtypeStruct(s, dt)
VM = pl.BlockSpec(memory_space=pltpu.VMEM)
SM = pl.BlockSpec(memory_space=pltpu.SMEM)

def mixer_fwd(pre, pos, fil, cw, gain):
    outs = (sds(CAP,256,dt=BF), sds(CAP,768), sds(CAP,512), sds(CAP,256), sds(CAP,256), sds(CAP,256), sds(CAP,256),
            sds(2*NB,BLOCK,BLOCK), sds(2*NB,BLOCK,BLOCK), sds(2*NB,HD,HD), sds(2*NB,HD,HD))
    return pl.pallas_call(fwd_kernel, out_shape=outs, in_specs=[VM]*5, out_specs=[VM]+[pl.BlockSpec(memory_space=pltpu.HBM)]*(len(outs)-1),
        scratch_shapes=[pltpu.VMEM(o.shape,F32) for o in outs[1:]]+[pltpu.VMEM((2*NB,HD,HD),F32), pltpu.SemaphoreType.DMA((10,))],
        compiler_params=pltpu.CompilerParams(vmem_limit_bytes=60*2**20), cost_estimate=pl.CostEstimate(flops=0, bytes_accessed=140 * 2**20, transcendentals=0),
        name="mixer_forward")(pre, pos, fil, cw, gain)

def bwd_kernel(dmix, pre, pos_ref, fill_ref, cw, gain, *refs):
    kept, (dpre, dcw, dgain), held, (e_s, do_s, sem) = refs[:10], refs[10:13], refs[13:23], refs[23:]
    c_in, qk, w_in, u_in, u2_in, o_in, p_in, t_in, m_in, s_in = held

    def fetch(i):
        return pltpu.make_async_copy(kept[i], held[i], sem.at[i])

    for i in (5, 6, 1, 2, 8, 7, 9, 0, 3, 4):
        fetch(i).start()
    for i in (5, 6, 1, 2):
        fetch(i).wait()
    ri, ci = masks()
    heads = 2
    lane = lax.broadcasted_iota(jnp.int32, (BLOCK, HD), 1)
    dgain[...] = jnp.zeros_like(dgain)
    dcw[...] = jnp.zeros_like(dcw)
    def phase_a(n, _):
        r = pl.ds(pl.multiple_of(n * BLOCK, BLOCK), BLOCK)
        for h in range(heads):
            hs = slice(h*HD, (h+1)*HD)
            e = n*2+h
            o = o_in[r, hs]; dm = dmix[r, hs]
            gg = pre[r, 768+h*HD:768+(h+1)*HD]
            sg = sigmoid(gg); si = gg*sg
            ms = jnp.mean(o*o, axis=1, keepdims=True)
            sc = lax.rsqrt(jnp.maximum(ms, HEAD_FLOOR))
            on = o*sc
            gn = gain[...]
            dpre[r, 768+h*HD:768+(h+1)*HD] = (dm * on * gn * (sg * (1.0 + gg*(1.0-sg)))).astype(BF)
            dgs = dm * on * si
            dgain[...] += jnp.sum(dgs.reshape(8, 8, HD), axis=0)
            dn = dm * gn * si
            corr = jnp.where(ms > HEAD_FLOOR, jnp.mean(dn*on, axis=1, keepdims=True), 0.0)
            do = sc * (dn - on*corr)
            do_s[r, hs] = do
            pdo = d3(p_in[e], do, TN)
            qw = jnp.concatenate([qk[r, hs], w_in[r, hs]], axis=0)
            dd = jnp.concatenate([do, -pdo], axis=0)
            e_s[e] = d3(qw, dd, TN)
        return 0
    lax.fori_loop(0, NB // 4, four_times(phase_a), 0)
    fetch(8).wait()

    def phase_b(i, ds):
        n = NB-1-i
        out = []
        for h in range(heads):
            e = n*2+h
            d = ds[h]
            ee = e_s[e]
            e_s[e] = d
            out.append((d - d3(m_in[e], d, TN) + ee) * goes_on(pos_ref, n))
        return tuple(out)
    zs = jnp.zeros((HD, HD), F32)
    lax.fori_loop(0, NB, phase_b, (zs, zs))
    for i in (7, 9, 0, 3, 4):
        fetch(i).wait()

    def phase_c(i, heads_dc):
        blocks = tuple(NB - 1 - j - 4 * i for j in range(4))
        todo = [(n, pl.ds(pl.multiple_of(n * BLOCK, BLOCK), BLOCK), h, slice(h*HD, (h+1)*HD)) for n in blocks for h in range(heads)]
        def every(f, *lists):
            return [f(*v) for v in zip(*lists)]
        ns, rs, hh, hs = zip(*todo)
        es = [n*2+h for n, h in zip(ns, hh)]
        fil = [fill_ref[r, :] for r in rs]
        beta_t = [sigmoid(pre[r, 1024:1152]) for r in rs]
        q = [qk[r, c] for r, c in zip(rs, hs)]
        k = [qk[r, 256+h*HD:256+(h+1)*HD] for r, h in zip(rs, hh)]
        w = [w_in[r, c] for r, c in zip(rs, hs)]
        u = [u_in[r, c] for r, c in zip(rs, hs)]
        u2 = [u2_in[r, c] for r, c in zip(rs, hs)]
        do = [do_s[r, c] for r, c in zip(rs, hs)]
        p = [p_in[e] for e in es]
        t = [t_in[e] for e in es]
        s = [s_in[e] for e in es]
        ds = [e_s[e] for e in es]
        b = [x[:, h:h+1] for x, h in zip(beta_t, hh)]
        du2 = every(lambda p, do, k, ds: d3(p, do, TN) + d3(k, ds), p, do, k, ds)
        dp = every(lambda do, u2: jnp.where(ri >= ci, d3(do, u2, NT), 0.0), do, u2)
        g = every(lambda k: d3(k, k, NT), k)
        xs = every(lambda do, du2, s: d3(jnp.concatenate([do, -du2], axis=0), s, NT), do, du2, s)
        dq = every(lambda xs, dp, k: xs[:BLOCK] + d3(dp, k), xs, dp, k)
        xx = every(lambda t, xs, du2: d3(t, jnp.concatenate([xs[BLOCK:], du2], axis=1), TN), t, xs, du2)
        dk = every(lambda dp, q, u2, ds: d3(dp, q, TN) + d3(u2, ds, NT), dp, q, u2, ds)
        mm = every(lambda xx, w, u: jnp.where(ri > ci, -d3(xx, jnp.concatenate([w, u], axis=1), NT), 0.0), xx, w, u)
        cv = [c_in[r, 512+h*HD:512+(h+1)*HD] for r, h in zip(rs, hh)]
        sv = every(sigmoid, cv)
        bm = every(lambda b, mm: b*mm, b, mm)
        dk = every(lambda dk, bm, k, b, xx: dk + d3(bm + bm.T, k) + b*xx[:, :HD], dk, bm, k, b, xx)
        db = every(lambda mm, g, xx, k, cv, sv, fil: jnp.sum(mm*g, axis=1, keepdims=True)
                   + jnp.sum(xx[:, :HD]*k + xx[:, HD:]*(cv*sv*fil), axis=1, keepdims=True), mm, g, xx, k, cv, sv, fil)
        cq = [c_in[r, c] for r, c in zip(rs, hs)]
        ck = [c_in[r, 256+h*HD:256+(h+1)*HD] for r, h in zip(rs, hh)]
        def unit_back(c, fil, n, d):
            sg = sigmoid(c)
            y = c*sg*fil
            r = lax.rsqrt(jnp.sum(y*y, axis=1, keepdims=True) + EPSILON)
            return r*(d - n*jnp.sum(d*n, axis=1, keepdims=True))*fil*(sg*(1.0+c*(1.0-sg)))
        aq = every(unit_back, cq, fil, q, dq)
        ak = every(unit_back, ck, fil, k, dk)
        av = every(lambda b, xx, fil, sv, cv: b*xx[:, HD:]*fil*(sv*(1.0+cv*(1.0-sv))), b, xx, fil, sv, cv)
        for j, n in enumerate(blocks):
            r = rs[2*j]
            dbt = jnp.where(lane == 0, db[2*j], jnp.where(lane == 1, db[2*j+1], 0.0))
            dpre[r, 1024:1152] = (dbt*beta_t[2*j]*(1.0-beta_t[2*j])).astype(BF)
            pos = pos_ref[r, :]
            nxt = jnp.minimum(n+1, NB-1)
            posx = jnp.concatenate([pos, pos_ref[pl.ds(pl.multiple_of(nxt*BLOCK, BLOCK), 8), :]], axis=0)
            prv = jnp.maximum(n*BLOCK-8, 0)
            new = []
            for i, acts in enumerate((aq, ak, av)):
                dc = jnp.concatenate(acts[2*j:2*j+2], axis=1)
                ext = jnp.concatenate([dc, heads_dc[i]], axis=0)
                cur = pre[r, i*256:(i+1)*256]
                tail = pre[pl.ds(pl.multiple_of(prv, 8), 8), i*256:(i+1)*256]
                xext = jnp.concatenate([tail, cur], axis=0)
                dx = cw[i:i+1, :]*dc
                dcw[i] += jnp.sum((dc*cur).reshape(8, 8, 256), axis=0)
                for o in range(1, CONV):
                    z = jnp.where(posx >= o, ext, 0.0)
                    dx = dx + cw[o*3+i:o*3+i+1, :]*pltpu.roll(z, BLOCK+8-o, axis=0)[:BLOCK]
                    sh = pltpu.roll(xext, o, axis=0)[8:]
                    dcw[o*3+i] += jnp.sum(jnp.where(pos >= o, dc*sh, 0.0).reshape(8, 8, 256), axis=0)
                dpre[r, i*256:(i+1)*256] = dx.astype(BF)
                new.append(dc[:8])
            heads_dc = tuple(new)
        return heads_dc
    z8 = jnp.zeros((8, 256), F32)
    lax.fori_loop(0, NB // 4, phase_c, (z8, z8, z8))

def mixer_bwd(dmix, pre, pos, fil, cw, gain, saved):
    outs = (sds(CAP,1152,dt=BF), sds(12,8,256), sds(8,HD))
    return pl.pallas_call(bwd_kernel, out_shape=outs, in_specs=[VM]*6+[pl.BlockSpec(memory_space=pltpu.HBM)]*len(saved), out_specs=[VM]*3,
        scratch_shapes=[pltpu.VMEM(a.shape, F32) for a in saved]+[pltpu.VMEM((2*NB,HD,HD),F32), pltpu.VMEM((CAP,256),F32), pltpu.SemaphoreType.DMA((10,))],
        compiler_params=pltpu.CompilerParams(vmem_limit_bytes=60*2**20), cost_estimate=pl.CostEstimate(flops=0, bytes_accessed=200 * 2**20, transcendentals=0),
        name="mixer_backward")(dmix, pre, pos, fil, cw, gain, *saved)


MESH = pl.DeviceIdType.MESH
ROOM = 60 * 2**20
LINK_COST = 150 * 2**20
HBM = pl.BlockSpec(memory_space=pltpu.HBM)


def places():
    s, h, t = lax.axis_index("shard"), lax.axis_index("head"), lax.axis_index("tensor")
    return h, t, (s, h + 1, t), (s, h - 1, t), (s, h, 1 - t)


def shard_peers(m):
    s, h, t = lax.axis_index("shard"), lax.axis_index("head"), lax.axis_index("tensor")
    return [((lax.rem(s + i, m), h, t), lax.rem(s + i, m)) for i in range(1, m)]


def greet_shard(m):
    barrier = pltpu.get_barrier_semaphore()
    for p, _ in shard_peers(m):
        pl.semaphore_signal(barrier, inc=1, device_id=p, device_id_type=MESH)
    return m - 1


class Carry:
    def __init__(self, hops, kinds, m, ins, outs, send, recv, here):
        self.hops, self.kinds, self.m, self.ins, self.outs = hops, kinds, m, ins, outs
        self.send, self.recv, self.here = send, recv, here
        s, self.h, self.t = lax.axis_index("shard"), lax.axis_index("head"), lax.axis_index("tensor")
        self.me = s
        self.side = s + 1 - 2 * lax.rem(s, 2)
        self.over = lax.rem(s + 2, 4)
        self.corner = lax.rem(self.side + 2, 4)

    def relayed(self, e):
        return self.hops and self.m == 4 and self.kinds[e] in ("gather", "abreast")

    def part(self, e, src, half=None):
        rows = self.ins[e].shape[0]
        span = pl.ds(0, rows) if half is None else pl.ds(half * (rows // 2), rows // 2)
        if self.kinds[e] == "gather":
            first = src * rows + (0 if half is None else half * (rows // 2))
            return self.outs[e].at[pl.ds(pl.multiple_of(first, rows // 2), span.size)]
        if self.kinds[e] == "abreast":
            w = self.ins[e].shape[1]
            return self.outs[e].at[span, pl.ds(pl.multiple_of(src * w, w), w)]
        return self.outs[e].at[src]

    def given(self, e, dst):
        if self.kinds[e] == "columns":
            w = self.ins[e].shape[1] // self.m
            return self.ins[e].at[:, pl.ds(pl.multiple_of(dst * w, w), w)]
        return self.ins[e].at[dst] if self.kinds[e] == "swap" else self.ins[e]

    def move(self, e, src, dst, i, j, to):
        return pltpu.make_async_remote_copy(src_ref=src, dst_ref=dst, send_sem=self.send.at[e, i], recv_sem=self.recv.at[e, j],
                                            device_id=(to, self.h, self.t), device_id_type=MESH)

    def copy(self, e, i, to):
        return self.move(e, self.given(e, to), self.part(e, self.me), i, self.me, to)

    def came(self, e, src):
        return self.move(e, self.given(e, src), self.part(e, src), 0, src, src)

    def hand(self, e, half):
        src, to = (self.side, self.over) if half == 0 else (self.over, self.side)
        piece = self.part(e, src, half)
        return self.move(e, piece, piece, 2 + half, src if half == 0 else self.m, to)

    def handed(self, e, half):
        piece = self.part(e, self.corner, half)
        return self.move(e, piece, piece, 2 + half, self.corner if half == 0 else self.m, self.over if half == 0 else self.side)

    def local(self, e):
        return pltpu.make_async_copy(self.given(e, self.me), self.part(e, self.me), self.here.at[e])

    def targets(self, e):
        return [self.side, self.over] if self.relayed(e) else [p[1] for p in shard_peers(self.m)]

    def greet(self):
        return greet_shard(self.m) if self.kinds else 0

    def start(self):
        for e in range(len(self.kinds)):
            for i, to in enumerate(self.targets(e)):
                self.copy(e, i, to).start()
            self.local(e).start()

    def relay(self, e):
        if e < len(self.kinds) and self.relayed(e):
            self.came(e, self.side).wait_recv()
            self.hand(e, 0).start()
            self.came(e, self.over).wait_recv()
            self.hand(e, 1).start()

    def wait(self):
        for e in range(len(self.kinds)):
            self.local(e).wait()
            for i, to in enumerate(self.targets(e)):
                self.copy(e, i, to).wait_send()
                if not self.relayed(e):
                    self.came(e, to).wait_recv()
            if self.relayed(e):
                for half in range(2):
                    self.handed(e, half).wait_recv()
                    self.hand(e, half).wait_send()


def carried(kinds, m, arrays):
    dma = pltpu.SemaphoreType.DMA
    give = {"gather": lambda a: (m * a.shape[0], a.shape[1]), "swap": lambda a: a.shape,
            "abreast": lambda a: (a.shape[0], m * a.shape[1]), "pile": lambda a: (m,) + a.shape,
            "columns": lambda a: (m, a.shape[0], a.shape[1] // m)}
    shapes = [jax.ShapeDtypeStruct(give[k](a), a.dtype) for k, a in zip(kinds, arrays)]
    e = len(kinds)
    return shapes, ([dma((e, m + 1)), dma((e, m + 1)), dma((e,))] if e else [])


def carry_of(kinds, m, refs, n_in, n_out, hops=False):
    e = len(kinds)
    ins, refs = refs[:n_in], refs[n_in:]
    c_in, refs = refs[:e], refs[e:]
    outs, refs = refs[:n_out], refs[n_out:]
    c_out, refs = refs[:e], refs[e:]
    sems = (refs[-3:] if e else (None,) * 3)
    scratch = refs[:-3] if e else refs
    return ins, outs, scratch, Carry(hops, kinds, m, c_in, c_out, *sems)


def greet(n, h, up, down, across, more=0):
    barrier = pltpu.get_barrier_semaphore()
    pl.semaphore_signal(barrier, inc=1, device_id=across, device_id_type=MESH)

    @pl.when(h < n - 1)
    def _():
        pl.semaphore_signal(barrier, inc=1, device_id=up, device_id_type=MESH)

    @pl.when(h > 0)
    def _():
        pl.semaphore_signal(barrier, inc=1, device_id=down, device_id_type=MESH)

    pl.semaphore_wait(barrier, 1 + more + (h < n - 1).astype(jnp.int32) + (h > 0).astype(jnp.int32))


class Plan:
    def __init__(self, m, per_peer, lengths, dealing, starts):
        self.m, self.per_peer, self.lengths, self.dealing, self.starts = m, per_peer, lengths, dealing, starts
        self.shift = m.bit_length() - 1
        self.device = lax.axis_index("shard")

        def begin(q, total):
            starts[q] = total
            return total + lengths[q]

        lax.fori_loop(0, lengths.shape[0], begin, jnp.int32(0))

    def under(self, row, residue):
        return lax.shift_right_arithmetic(row - 1 - residue + self.m, self.shift + jnp.zeros_like(row))

    def members(self, g):
        at = [self.dealing[g * SEQ_DEV + i] for i in range(SEQ_DEV)]
        return [(self.starts[q], self.lengths[q]) for q in at]

    def sent(self, ids):
        packed = ids * self.m + self.device

        def group(g, slot):
            seqs = self.members(g)
            counts = [self.under(s + n, self.device) - self.under(s, self.device) for s, n in seqs]
            for s, n in seqs:
                first = g * self.per_peer - self.under(s, self.device)
                for (other, _), count in zip(seqs, counts):
                    first = first + jnp.where(other < s, count, 0)
                slot = slot + jnp.where((packed >= s) & (packed < s + n), first, 0)
            return slot

        return lax.fori_loop(0, self.lengths.shape[0] // SEQ_DEV, group, ids)

    def rows(self, ids):
        seqs = self.members(self.device)
        place, start, length, below = ids, jnp.zeros_like(ids), jnp.zeros_like(ids), jnp.int32(0)
        for s, n in seqs:
            here = ids >= below
            place = jnp.where(here, ids - below, place)
            start = jnp.where(here, s, start)
            length = jnp.where(here, n, length)
            below = below + lax.shift_right_arithmetic(n + BLOCK - 1, jnp.int32(6)) * BLOCK
        filled = place < length
        natural = start + place
        source = natural & (self.m - 1)
        slot = source * self.per_peer + self.under(natural, source) - self.under(start, source)
        for s, n in seqs:
            span = self.under(jnp.zeros_like(ids) + (s + n), source) - self.under(jnp.zeros_like(ids) + s, source)
            slot = slot + jnp.where(s < start, span, 0)
        return place, filled, jnp.where(filled, slot, -1)


def gather_kernel(n, width, m, kinds, *refs):
    (lengths, dealing, tokens), (x, out, sent_at, slot_at, pos_at, fill_at), scratch, carry = carry_of(kinds, m, refs, 3, 6)
    place_at, starts, outbox, inbox, deal_s, deal_r, here, up_s, up_r, down_s, down_r, core_s, core_r = scratch
    h, t, up, down, across = places()
    per_peer = outbox.shape[1]

    def cols(j):
        return out.at[:, pl.ds(pl.multiple_of((j * 2 + t) * width, width), width)]

    def other(j):
        return out.at[:, pl.ds(pl.multiple_of((j * 2 + 1 - t) * width, width), width)]

    def send(j, src, ss, rs, to):
        return pltpu.make_async_remote_copy(src_ref=src, dst_ref=cols(j), send_sem=ss.at[j], recv_sem=rs.at[j],
                                            device_id=to, device_id_type=MESH)

    greet(n, h, up, down, across, carry.greet())
    plan = Plan(m, per_peer, lengths, dealing, starts)
    peers = shard_peers(m)
    mine = lax.axis_index("shard")
    sent = plan.sent(lax.broadcasted_iota(jnp.int32, (1, REAL_DEV), 1))
    ids = lax.broadcasted_iota(jnp.int32, (per_peer, REAL_DEV), 0)

    def deal(i, p, src):
        return pltpu.make_async_remote_copy(src_ref=outbox.at[p[1]], dst_ref=inbox.at[src], send_sem=deal_s.at[i],
                                            recv_sem=deal_r.at[src], device_id=p[0], device_id_type=MESH)

    def pick(q):
        return dg(jnp.where(sent - q * per_peer == ids, 1.0, 0.0).astype(BF), tokens[...], NN).astype(BF)

    for i, p in enumerate(peers):
        outbox[p[1]] = pick(p[1])
        deal(i, p, mine).start()
    carry.start()
    inbox[mine] = pick(mine)
    place_at[...] = plan.rows(lax.broadcasted_iota(jnp.int32, (CAP, 1), 0))[2]
    for i, p in enumerate(peers):
        deal(i, p, p[1]).wait_recv()
    lanes = lax.broadcasted_iota(jnp.int32, (STEP, m * per_peer), 1)

    def settle(i, c):
        r = pl.ds(pl.multiple_of(i * STEP, STEP), STEP)
        chosen = jnp.where(place_at[r, :] == lanes, 1.0, 0.0).astype(BF)
        x[r, :] = dg(chosen, inbox[...].reshape(m * per_peer, width), NN).astype(BF)
        return c

    lax.fori_loop(0, CAP // STEP, settle, 0)
    local = pltpu.make_async_copy(x, cols(h), here)
    local.start()

    @pl.when(h < n - 1)
    def _():
        send(h, x, up_s, up_r, up).start()

    @pl.when(h > 0)
    def _():
        send(h, x, down_s, down_r, down).start()

    send(h, x, core_s, core_r, across).start()
    sent_at[...] = plan.sent(lax.broadcasted_iota(jnp.int32, (REAL_DEV, 1), 0))
    slot_at[...] = plan.rows(lax.broadcasted_iota(jnp.int32, (1, CAP), 1))[2]
    position, filled, _ = plan.rows(lax.broadcasted_iota(jnp.int32, (CAP, 1), 0))
    pos_at[...] = position
    fill_at[...] = jnp.where(filled, 1.0, 0.0)
    for k in range(1, n):
        below, above = h - k, h + k

        @pl.when(below >= 0)
        def _():
            send(below, cols(below), up_s, up_r, up).wait_recv()

            @pl.when(h < n - 1)
            def _():
                send(below, cols(below), up_s, up_r, up).start()

            send(below, cols(below), core_s, core_r, across).start()

        @pl.when(above < n)
        def _():
            send(above, cols(above), down_s, down_r, down).wait_recv()

            @pl.when(h > 0)
            def _():
                send(above, cols(above), down_s, down_r, down).start()

            send(above, cols(above), core_s, core_r, across).start()

    for j in range(n):
        back = pltpu.make_async_remote_copy(src_ref=cols(j), dst_ref=other(j), send_sem=core_s.at[j], recv_sem=core_r.at[j],
                                            device_id=across, device_id_type=MESH)
        back.wait_recv()
        back.wait_send()

        @pl.when((j <= h) & (h < n - 1))
        def _():
            send(j, cols(j), up_s, up_r, up).wait_send()

        @pl.when((j >= h) & (h > 0))
        def _():
            send(j, cols(j), down_s, down_r, down).wait_send()

    local.wait()
    for i, p in enumerate(peers):
        deal(i, p, mine).wait_send()
    carry.wait()


def z_gather(n, lengths, dealing, tokens, per_peer, collective_id, name, m, kinds, arrays):
    width = tokens.shape[1]
    dma = pltpu.SemaphoreType.DMA
    sd = jax.ShapeDtypeStruct
    shapes, sems = carried(kinds, m, arrays)
    return pl.pallas_call(
        functools.partial(gather_kernel, n, width, m, kinds),
        out_shape=[sd((CAP, width), BF), sd((CAP, 2 * n * width), BF), sd((REAL_DEV, 1), jnp.int32), sd((1, CAP), jnp.int32),
                   sd((CAP, 1), jnp.int32), sd((CAP, 1), F32)] + shapes,
        in_specs=[SM, SM, VM] + [HBM] * len(shapes), out_specs=[VM, HBM] + [VM] * 4 + [HBM] * len(shapes),
        scratch_shapes=[pltpu.VMEM((CAP, 1), jnp.int32), pltpu.SMEM(lengths.shape, jnp.int32)]
        + [pltpu.VMEM((m, per_peer, width), BF)] * 2 + [dma((m,)), dma((m,)), dma] + [dma((n,))] * 6 + sems,
        compiler_params=pltpu.CompilerParams(collective_id=collective_id, has_side_effects=True, vmem_limit_bytes=ROOM),
        cost_estimate=pl.CostEstimate(flops=0, bytes_accessed=LINK_COST, transcendentals=0),
        name=name,
    )(lengths, dealing, tokens, *arrays)


STEP = 128


def group_peers(n):
    s, h, t = lax.axis_index("shard"), lax.axis_index("head"), lax.axis_index("tensor")
    peers = []
    for i in range(1, 2 * n):
        hh, tt = lax.rem(h + i // 2, n), lax.rem(t + i % 2, 2)
        peers.append(((s, hh, tt), hh * 2 + tt))
    return peers


def greet_group(n, more=0):
    barrier = pltpu.get_barrier_semaphore()
    for p, _ in group_peers(n):
        pl.semaphore_signal(barrier, inc=1, device_id=p, device_id_type=MESH)
    pl.semaphore_wait(barrier, 2 * n - 1 + more)


def finish_kernel(n, width, m, kinds, fill, piles, *refs):
    (part, kept, scale, base, gain, share, small, sent, place, *left), (tokens, every, *grads), scratch, carry = carry_of(
        kinds, m, refs, 9 + piles + 2 * fill, 2 + piles + 2 * fill)
    stacks, left = left[:piles], left[piles:]
    added, grads = grads[:piles], grads[piles:]
    *scratch, pile_sem = scratch
    heaps, scratch = scratch[:piles], scratch[piles:]
    if fill:
        *scratch, l_buf, r_buf, blocks, strips, l_sem, r_sem, w_s, w_r, w_own = scratch
    (low, dgain, outbox, inbox, deal_s, deal_r, held, ours, shard_s, shard_r, group_s, group_r,
     acc, tots, tot_s, tot_r, mine, theirs, from_below, from_above,
     here, core_s, core_r, up_s, up_r, down_s, down_r) = scratch
    h, t, up, down, across = places()

    def cols(j, c):
        return part.at[:, pl.ds(pl.multiple_of((j * 2 + c) * width, width), width)]

    def swap(j):
        return pltpu.make_async_remote_copy(src_ref=cols(j, 1 - t), dst_ref=theirs.at[j], send_sem=core_s.at[j],
                                            recv_sem=core_r.at[j], device_id=across, device_id_type=MESH)

    def own(j):
        return pltpu.make_async_copy(cols(j, t), mine.at[j], here.at[j])

    def rise(k):
        return pltpu.make_async_remote_copy(src_ref=mine.at[n - 1 - k], dst_ref=from_below.at[k], send_sem=up_s.at[k],
                                            recv_sem=up_r.at[k], device_id=up, device_id_type=MESH)

    def fall(k):
        return pltpu.make_async_remote_copy(src_ref=mine.at[k], dst_ref=from_above.at[k], send_sem=down_s.at[k],
                                            recv_sem=down_r.at[k], device_id=down, device_id_type=MESH)

    def total(j, extra):
        def step(i, c):
            r = pl.ds(pl.multiple_of(i * STEP, STEP), STEP)
            v = mine[j, r, :].astype(F32) + theirs[j, r, :].astype(F32)
            if extra is not None:
                v = v + extra(r).astype(F32)
            mine[j, r, :] = v.astype(BF)
            return c
        lax.fori_loop(0, CAP // STEP, step, 0)

    order = [j for i in range(n // 2) for j in (n - 1 - i, i)]
    for j in order:
        own(j).start()

    def load(i):
        return pltpu.make_async_copy(stacks[i], heaps[i], pile_sem.at[i])

    def add_up(i):
        load(i).wait()
        tall = heaps[i].shape[1] // 4

        def step(q, c):
            r = pl.ds(pl.multiple_of(q * tall, tall), tall)
            v = heaps[i][0, r, :].astype(F32)
            for b in range(1, m):
                v = v + heaps[i][b, r, :].astype(F32)
            added[i][r, :] = v
            return c

        lax.fori_loop(0, 4, step, 0)

    for i in range(piles):
        load(i).start()
    greet_group(n, greet_shard(m))
    me = h * 2 + t
    peers = group_peers(n)

    def tot_copy(i, p, dst):
        return pltpu.make_async_remote_copy(src_ref=share, dst_ref=tots.at[dst], send_sem=tot_s.at[i], recv_sem=tot_r.at[dst],
                                            device_id=p, device_id_type=MESH)

    for i, p in enumerate(peers):
        tot_copy(i, p[0], me).start()
    for j in order:
        swap(j).start()
    carry.start()
    shard = lax.axis_index("shard")
    others = shard_peers(m)
    if fill:
        lhs, rhs = left
        wide = lhs.shape[1] // m

        def columns(q):
            return lhs.at[:, pl.ds(pl.multiple_of(q * wide, wide), wide)]

        def fetch(i, q):
            return pltpu.make_async_copy(columns(q), l_buf.at[i], l_sem.at[i])

        made = (blocks, strips)

        def grad(i, p, src):
            return [pltpu.make_async_remote_copy(src_ref=made[e].at[i], dst_ref=grads[e].at[src], send_sem=w_s.at[e, i],
                                                 recv_sem=w_r.at[e, src], device_id=p[0], device_id_type=MESH) for e in range(2)]

        own_grad = [pltpu.make_async_copy(made[e].at[m - 1], grads[e].at[shard], w_own.at[e]) for e in range(2)]
        whole = pltpu.make_async_copy(rhs, r_buf, r_sem)
        whole.start()
        for i, p in enumerate(others):
            fetch(i, p[1]).start()
        fetch(m - 1, shard).start()

        def multiply(i):
            if i == 0:
                whole.wait()
            fetch(i, shard).wait()
            main = blocks.shape[2]
            strips[i] = dg(r_buf[:, main:main + BETA], l_buf[i], TN).astype(BF)
            blocks[i] = dg(l_buf[i], r_buf[:, :main], TN).astype(BF)
            for c in (grad(i, others[i], shard) if i < m - 1 else own_grad):
                c.start()

        multiply(0)

    def arrive(j):
        own(j).wait()
        swap(j).wait_recv()

    for tick in range(2 * n - 2):
        ku = tick - h
        tu = n - 1 - ku

        @pl.when((ku >= 0) & (tu > h))
        def _():
            arrive(tu)

            @pl.when(h == 0)
            def _():
                total(tu, None)

            @pl.when(h > 0)
            def _():
                rise(ku).wait_recv()
                total(tu, lambda r: from_below[ku, r, :])

            rise(ku).start()

        kd = tick - (n - 1 - h)

        @pl.when((kd >= 0) & (kd < h))
        def _():
            arrive(kd)

            @pl.when(h == n - 1)
            def _():
                total(kd, None)

            @pl.when(h < n - 1)
            def _():
                fall(kd).wait_recv()
                total(kd, lambda r: from_above[kd, r, :])

            fall(kd).start()

        if fill and tick + 1 < m:
            multiply(tick + 1)

        if tick >= 2 * n - 2 - piles:
            add_up(tick - (2 * n - 2 - piles))

    if fill:
        for i in range(2 * n - 1, m):
            multiply(i)
    arrive(h)
    for i, p in enumerate(peers):
        tot_copy(i, p[0], p[1]).wait_recv()
    tots[me] = share[...]
    for i, p in enumerate(peers):
        tots[me] = tots[me] + tots[p[1]]
    dgain[...] = jnp.zeros_like(dgain)
    gains = gain[...]
    eighth = jnp.full((8, 128), 0.125, BF)

    def final(get):
        def step(i, c):
            r = pl.ds(pl.multiple_of(i * STEP, STEP), STEP)
            acc[r, :] = get(r)
            return c
        lax.fori_loop(0, CAP // STEP, step, 0)

    final(lambda r: mine[h, r, :].astype(F32) + theirs[h, r, :].astype(F32))

    def first(get):
        final(lambda r: acc[r, :] + get(r).astype(F32))

    @pl.when((h > 0) & (h < n - 1))
    def _():
        @pl.when(2 * h < n)
        def _():
            fall(h).wait_recv()
            first(lambda r: from_above[h, r, :])

        @pl.when(2 * h >= n)
        def _():
            rise(n - 1 - h).wait_recv()
            first(lambda r: from_below[n - 1 - h, r, :])

    by_below = (h > 0) & ((2 * h < n) | (h == n - 1))

    @pl.when(by_below)
    def _():
        rise(n - 1 - h).wait_recv()

    @pl.when(jnp.logical_not(by_below))
    def _():
        fall(h).wait_recv()

    def close(get):
        def step(i, c):
            r = pl.ds(pl.multiple_of(i * STEP, STEP), STEP)
            hi, lo = split(tots[me, i])
            total_r = dg(hi, eighth, TN) + dg(lo, eighth, TN)
            sc = scale[r, :]
            kp = kept[r, :].astype(F32)
            dn = acc[r, :] + get(r).astype(F32)
            back = base[r, :].astype(F32) + sc * (gains * dn) - kp * jnp.tile((sc * sc * sc) * (total_r * (1.0 / D)), (1, width // 128))
            low[r, :] = back.astype(BF)
            dgain[...] += jnp.sum((dn * kp * sc).reshape(STEP // 8, 8, width), axis=0)
            return c
        lax.fori_loop(0, CAP // STEP, step, 0)

    @pl.when(by_below)
    def _():
        close(lambda r: from_below[n - 1 - h, r, :])

    @pl.when(jnp.logical_not(by_below))
    def _():
        close(lambda r: from_above[h, r, :])

    for i, p in enumerate(peers):
        tot_copy(i, p[0], me).wait_send()

    per_peer = outbox.shape[1]
    ids = lax.broadcasted_iota(jnp.int32, (per_peer, place.shape[1]), 0)

    def back(i, p, src):
        return pltpu.make_async_remote_copy(src_ref=outbox.at[p[1]], dst_ref=inbox.at[src], send_sem=deal_s.at[i],
                                            recv_sem=deal_r.at[src], device_id=p[0], device_id_type=MESH)

    def pick(q):
        return dg(jnp.where(place[...] - q * per_peer == ids, 1.0, 0.0).astype(BF), low[...], NN).astype(BF)

    def over(i, p, src):
        return pltpu.make_async_remote_copy(src_ref=ours, dst_ref=held.at[src], send_sem=shard_s.at[i],
                                            recv_sem=shard_r.at[src], device_id=p[0], device_id_type=MESH)

    def along(i, p, src):
        return pltpu.make_async_remote_copy(src_ref=held.at[shard], dst_ref=every.at[src], send_sem=group_s.at[i],
                                            recv_sem=group_r.at[src], device_id=p[0], device_id_type=MESH)

    for i, p in enumerate(others):
        outbox[p[1]] = pick(p[1])
        back(i, p, shard).start()
    at = lax.broadcasted_iota(jnp.int32, small.shape, 0)
    ours[...] = small[...] + jnp.where(at == 12, jnp.sum(dgain[...], axis=0, keepdims=True), 0.0)
    for i, p in enumerate(others):
        over(i, p, shard).start()
    inbox[shard] = pick(shard)
    v = ours[...]
    for i, p in enumerate(others):
        over(i, p, p[1]).wait_recv()
        v = v + held[p[1]]
    held[shard] = v
    every[me] = v
    for i, p in enumerate(peers):
        along(i, p, me).start()
    for i, p in enumerate(others):
        back(i, p, p[1]).wait_recv()
    lanes = lax.broadcasted_iota(jnp.int32, (STEP, m * per_peer), 1)

    def settle(i, c):
        r = pl.ds(pl.multiple_of(i * STEP, STEP), STEP)
        chosen = jnp.where(sent[r, :] == lanes, 1.0, 0.0).astype(BF)
        tokens[r, :, :] = dg(chosen, inbox[...].reshape(m * per_peer, width), NN).reshape(STEP, 1, width)
        return c

    lax.fori_loop(0, REAL_DEV // STEP, settle, 0)
    for i, p in enumerate(peers):
        along(i, p, p[1]).wait_recv()
        along(i, p, me).wait_send()
    for i, p in enumerate(others):
        over(i, p, shard).wait_send()
        back(i, p, shard).wait_send()
    for j in range(n):
        swap(j).wait_send()
    for k in range(n - 1):
        @pl.when(n - 1 - k > h)
        def _():
            rise(k).wait_send()

        @pl.when(k < h)
        def _():
            fall(k).wait_send()
    carry.wait()
    if fill:
        for c in own_grad:
            c.wait()
        for i, p in enumerate(others):
            for c in grad(i, p, p[1]):
                c.wait_recv()
            for c in grad(i, p, shard):
                c.wait_send()


def z_finish(n, part, kept, scale, base, gain, share, small, sent, place, per_peer, collective_id, name, m, lhs, rhs, stacks):
    rows, width = part.shape[0], part.shape[1] // (2 * n)
    dma = pltpu.SemaphoreType.DMA
    wide, main = lhs.shape[1] // m, 4 * width
    fill = wide % 128 == 0
    if fill:
        kinds, arrays, extra = (), (), [lhs, rhs]
        made = [jax.ShapeDtypeStruct((m, wide, main), BF), jax.ShapeDtypeStruct((m, BETA, wide), BF)]
        room = [pltpu.VMEM((m, rows, wide), BF), pltpu.VMEM(rhs.shape, BF), pltpu.VMEM(made[0].shape, BF),
                pltpu.VMEM(made[1].shape, BF), dma((m,)), dma, dma((2, m)), dma((2, m)), dma((2,))]
    else:
        kinds = ("swap", "swap")
        arrays = (dg(lhs, rhs[:, :main], TN).astype(BF).reshape(m, wide, main),
                  dg(rhs[:, main:main + BETA], lhs, TN).astype(BF).reshape(BETA, m, wide).transpose(1, 0, 2))
        extra, made, room = [], [], []
    shapes, sems = carried(kinds, m, arrays)
    return pl.pallas_call(
        functools.partial(finish_kernel, n, width, m, kinds, int(fill), len(stacks)),
        out_shape=[jax.ShapeDtypeStruct((REAL_DEV, 1, width), F32), jax.ShapeDtypeStruct((2 * n,) + small.shape, F32)]
        + [jax.ShapeDtypeStruct(a.shape[1:], F32) for a in stacks] + made + shapes,
        in_specs=[HBM] + [VM] * 8 + [HBM] * (len(stacks) + len(extra) + len(shapes)),
        out_specs=[VM] * (2 + len(stacks)) + [HBM] * (len(made) + len(shapes)),
        scratch_shapes=[pltpu.VMEM(a.shape, BF) for a in stacks] + [pltpu.VMEM((rows, width), BF), pltpu.VMEM((8, width), F32)]
        + [pltpu.VMEM((m, per_peer, width), BF)] * 2 + [dma((m,))] * 2
        + [pltpu.VMEM((m,) + small.shape, F32), pltpu.VMEM(small.shape, F32), dma((m,)), dma((m,)), dma((2 * n,)), dma((2 * n,))]
        + [pltpu.VMEM((rows, width), F32), pltpu.VMEM((2 * n, rows // STEP, 8, STEP), F32), dma((2 * n,)), dma((2 * n,))]
        + [pltpu.VMEM((n, rows, width), BF)] * 2 + [pltpu.VMEM((n - 1, rows, width), BF)] * 2
        + [dma((n,))] * 3 + [dma((n - 1,))] * 4 + room + [dma((len(stacks),))] + sems,
        compiler_params=pltpu.CompilerParams(collective_id=collective_id, has_side_effects=True, vmem_limit_bytes=ROOM),
        cost_estimate=pl.CostEstimate(flops=0, bytes_accessed=LINK_COST, transcendentals=0),
        name=name,
    )(part, kept, scale, base, gain, share, small, sent, place, *stacks, *extra, *arrays)


CHUNKS = 4
SUBS = 4
UNITS = CHUNKS * SUBS
UNIT = CAP // UNITS


def turn_kernel(n, width, m, kinds, norm, *refs):
    if norm:
        (part, kept, scale, base, gain, share), (out, full, low, dgain), scratch, carry = carry_of(kinds, m, refs, 6, 4)
        tots, tot_s, tot_r = scratch[-3:]
        scratch = scratch[:-3]
    else:
        (part, base), (out, full, low), scratch, carry = carry_of(kinds, m, refs, 2, 3, True)
    (mine, theirs, from_below, from_above, here, core_s, core_r, up_s, up_r, down_s, down_r,
     gu_s, gu_r, gd_s, gd_r, gc_s, gc_r, flat) = scratch
    h, t, up, down, across = places()
    me = h * 2 + t
    chunks = CHUNKS

    def rows(u):
        return pl.ds(pl.multiple_of(u * UNIT, UNIT), UNIT)

    def wide(r):
        return pl.ds(pl.multiple_of(r * SUBS * UNIT, SUBS * UNIT), SUBS * UNIT)

    def lanes(j, c):
        return pl.ds(pl.multiple_of((j * 2 + c) * width, width), width)

    def remote(src, dst, ss, rs, to):
        return pltpu.make_async_remote_copy(src_ref=src, dst_ref=dst, send_sem=ss, recv_sem=rs, device_id=to, device_id_type=MESH)

    def swap(j, r):
        return remote(part.at[wide(r), lanes(j, 1 - t)], theirs.at[j, wide(r)], core_s.at[j, r], core_r.at[j, r], across)

    def own(j, r):
        return pltpu.make_async_copy(part.at[wide(r), lanes(j, t)], mine.at[j, wide(r)], here.at[j, r])

    def rise(k, u):
        return remote(mine.at[n - 1 - k, rows(u)], from_below.at[k, rows(u)], up_s.at[k, u], up_r.at[k, u], up)

    def fall(k, u):
        return remote(mine.at[k, rows(u)], from_above.at[k, rows(u)], down_s.at[k, u], down_r.at[k, u], down)

    def spread(j, u, src, ss, rs, to):
        return remote(src, full.at[rows(u), lanes(j, t)], ss.at[j, u], rs.at[j, u], to)

    def piece(j, u):
        return full.at[rows(u), lanes(j, t)]

    def tot_copy(i, p, dst):
        return remote(share, tots.at[dst], tot_s.at[i], tot_r.at[dst], p)

    order = [j for i in range(n // 2) for j in (n - 1 - i, i)]
    for r in range(chunks):
        for j in order:
            own(j, r).start()
    if norm:
        greet_group(n, carry.greet())
        for i, p in enumerate(group_peers(n)):
            tot_copy(i, p[0], me).start()
        dgain[...] = jnp.zeros_like(dgain)
    else:
        greet(n, h, up, down, across, carry.greet())
    for r in range(chunks):
        for j in order:
            swap(j, r).start()
    carry.start()

    def arrive(j, r):
        own(j, r).wait()
        swap(j, r).wait_recv()

    def both(j, u):
        return mine[j, rows(u), :].astype(F32) + theirs[j, rows(u), :].astype(F32)

    def climb(o, r, s):
        u = SUBS * r + s

        @pl.when(h <= o)
        def _():
            ku = o - h
            tu = n - 1 - ku
            if s == 0:
                arrive(tu, r)

            @pl.when(h == 0)
            def _():
                mine[tu, rows(u), :] = both(tu, u).astype(BF)

            @pl.when(h > 0)
            def _():
                rise(ku, u).wait_recv()
                mine[tu, rows(u), :] = (both(tu, u) + from_below[ku, rows(u), :].astype(F32)).astype(BF)

            rise(ku, u).start()

        @pl.when(h >= n - 1 - o)
        def _():
            kd = o - (n - 1 - h)
            if s == 0:
                arrive(kd, r)

            @pl.when(h == n - 1)
            def _():
                mine[kd, rows(u), :] = both(kd, u).astype(BF)

            @pl.when(h < n - 1)
            def _():
                fall(kd, u).wait_recv()
                mine[kd, rows(u), :] = (both(kd, u) + from_above[kd, rows(u), :].astype(F32)).astype(BF)

            fall(kd, u).start()

    def gather_totals():
        for i, p in enumerate(group_peers(n)):
            tot_copy(i, p[0], p[1]).wait_recv()
        tots[me] = share[...]
        for i, p in enumerate(group_peers(n)):
            tots[me] = tots[me] + tots[p[1]]

    def last(r, s):
        u = SUBS * r + s
        if s == 0:
            arrive(h, r)
        flat[rows(u), :] = both(h, u)

        @pl.when(h > 0)
        def _():
            k = n - 1 - h
            rise(k, u).wait_recv()
            flat[rows(u), :] = flat[rows(u), :] + from_below[k, rows(u), :].astype(F32)

        @pl.when(h < n - 1)
        def _():
            fall(h, u).wait_recv()
            flat[rows(u), :] = flat[rows(u), :] + from_above[h, rows(u), :].astype(F32)

        if norm:
            close(u)
        else:
            v = base[rows(u), :].astype(F32) + flat[rows(u), :]
            out[rows(u), :] = v
            low[rows(u), :] = v.astype(BF)
            set_out(u)

    def close(u):
        hi, lo = split(tots[me, u])
        eighth = jnp.full((8, 128), 0.125, BF)
        total_r = (dg(hi, eighth, TN) + dg(lo, eighth, TN))[:UNIT]
        sc = scale[rows(u), :]
        kp = kept[rows(u), :].astype(F32)
        dn = flat[rows(u), :]
        v = (base[rows(u), :].astype(F32) + sc * (gain[...] * dn)
             - kp * jnp.tile((sc * sc * sc) * (total_r * (1.0 / D)), (1, width // 128)))
        out[rows(u), :] = v
        low[rows(u), :] = v.astype(BF)
        dgain[...] += jnp.sum((dn * kp * sc).reshape(UNIT // 8, 8, width), axis=0)
        set_out(u)

    def set_out(u):
        src = low.at[rows(u)]

        @pl.when(h < n - 1)
        def _():
            spread(h, u, src, gu_s, gu_r, up).start()

        @pl.when(h > 0)
        def _():
            spread(h, u, src, gd_s, gd_r, down).start()

        spread(h, u, src, gc_s, gc_r, across).start()

    def pass_on(k, r, s):
        u = SUBS * r + s
        below, above = h - k, h + k

        @pl.when(below >= 0)
        def _():
            spread(below, u, piece(below, u), gu_s, gu_r, up).wait_recv()

            @pl.when(h < n - 1)
            def _():
                spread(below, u, piece(below, u), gu_s, gu_r, up).start()

            spread(below, u, piece(below, u), gc_s, gc_r, across).start()

        @pl.when(above < n)
        def _():
            spread(above, u, piece(above, u), gd_s, gd_r, down).wait_recv()

            @pl.when(h > 0)
            def _():
                spread(above, u, piece(above, u), gd_s, gd_r, down).start()

            spread(above, u, piece(above, u), gc_s, gc_r, across).start()

    def at(o, r, s):
        if o < n - 1:
            climb(o, r, s)
        elif o == n - 1:
            if norm and s == 0:
                @pl.when(r == 0)
                def _():
                    gather_totals()
            last(r, s)
        elif o < 2 * n - 1:
            pass_on(o - n + 1, r, s)

    def period(r, c):
        for e in range(len(kinds)):
            @pl.when(r == e + 1)
            def _():
                carry.relay(e)

        for o in range(n):
            for s in range(SUBS):
                @pl.when(r > 0)
                def _():
                    at(o + n, r - 1, s)

                @pl.when(r < chunks)
                def _():
                    at(o, r, s)
        return c

    lax.fori_loop(0, chunks + 1, period, 0)
    mine_out = pltpu.make_async_copy(low, full.at[:, lanes(h, t)], here.at[0, 0])
    mine_out.start()

    def drain(u, c):
        for j in range(n):
            back = remote(piece(j, u), full.at[rows(u), lanes(j, 1 - t)], gc_s.at[j, u], gc_r.at[j, u], across)
            back.wait_recv()
            back.wait_send()

            @pl.when((j <= h) & (h < n - 1))
            def _():
                spread(j, u, piece(j, u), gu_s, gu_r, up).wait_send()

            @pl.when((j >= h) & (h > 0))
            def _():
                spread(j, u, piece(j, u), gd_s, gd_r, down).wait_send()

        for k in range(n - 1):
            @pl.when(n - 1 - k > h)
            def _():
                rise(k, u).wait_send()

            @pl.when(k < h)
            def _():
                fall(k, u).wait_send()

        return c

    if norm:
        for i, p in enumerate(group_peers(n)):
            tot_copy(i, p[0], me).wait_send()
    lax.fori_loop(0, UNITS, drain, 0)
    for r in range(chunks):
        for j in range(n):
            swap(j, r).wait_send()
    mine_out.wait()
    carry.wait()


def z_turn(n, part, base, collective_id, name, m=1, kinds=(), arrays=(), norm=None):
    rows, width = part.shape[0], part.shape[1] // (2 * n)
    dma = pltpu.SemaphoreType.DMA
    shapes, sems = carried(kinds, m, arrays)
    shape = jax.ShapeDtypeStruct
    ins = [part, base] if norm is None else [part, norm[0], norm[1], base, norm[2], norm[3]]
    outs = [shape((rows, width), F32), shape((rows, 2 * n * width), BF), shape((rows, width), BF)]
    out_specs = [VM, HBM, VM]
    more = []
    if norm is not None:
        outs, out_specs = outs + [shape((8, width), F32)], out_specs + [VM]
        more = [pltpu.VMEM((2 * n, UNITS, 8, 128), F32), dma((2 * n,)), dma((2 * n,))]
    return pl.pallas_call(
        functools.partial(turn_kernel, n, width, m, kinds, norm is not None),
        out_shape=outs + shapes,
        in_specs=[HBM] + [VM] * (len(ins) - 1) + [HBM] * len(shapes), out_specs=out_specs + [HBM] * len(shapes),
        scratch_shapes=[pltpu.VMEM((n, rows, width), BF)] * 2 + [pltpu.VMEM((n - 1, rows, width), BF)] * 2
        + [dma((n, CHUNKS))] * 3 + [dma((n - 1, UNITS))] * 4 + [dma((n, UNITS))] * 6 + [pltpu.VMEM((rows, width), F32)]
        + more + sems,
        compiler_params=pltpu.CompilerParams(collective_id=collective_id, has_side_effects=True, vmem_limit_bytes=ROOM),
        cost_estimate=pl.CostEstimate(flops=0, bytes_accessed=LINK_COST, transcendentals=0),
        name=name,
    )(*ins, *arrays)


def rows_spec(rows, cols):
    return pl.BlockSpec((rows, cols), lambda i: (i, 0))


def fixed_spec(*shape):
    return pl.BlockSpec(shape, lambda i: (0,) * len(shape), pipeline_mode=pl.Buffered(1))


def by_rows(kernel, rows, ins, fixed, outs, lanes, flops, name):
    specs = [rows_spec(rows, a.shape[1]) for a in ins] + [fixed_spec(*a.shape) for a in fixed]
    out_specs = [rows_spec(rows, o.shape[1]) for o in outs]
    shapes = list(outs)
    if lanes:
        out_specs.append(pl.BlockSpec((lanes * rows // CAP, 8, 128), lambda i: (i, 0, 0)))
        shapes.append(jax.ShapeDtypeStruct((lanes, 8, 128), F32))
    return pl.pallas_call(
        kernel, grid=(CAP // rows,), out_shape=shapes, in_specs=specs, out_specs=out_specs,
        compiler_params=pltpu.CompilerParams(dimension_semantics=("arbitrary",), vmem_limit_bytes=ROOM),
        cost_estimate=pl.CostEstimate(flops=flops, bytes_accessed=20 * 2**20, transcendentals=0),
        name=name,
    )(*ins, *fixed)


def lane_sums(values, share):
    units, rows = share.shape[0], values.shape[0] // share.shape[0]
    hi, lo = split(values)
    ones = jnp.ones((8, values.shape[1]), BF)
    for i in range(units):
        r = slice(i * rows, (i + 1) * rows)
        share[i, :, :rows] = dg(ones, hi[r], NT) + dg(ones, lo[r], NT)
        if rows < 128:
            share[i, :, rows:] = jnp.zeros((8, 128 - rows), F32)


def normal(x, gain):
    x = x.astype(F32)
    scale = lax.rsqrt(jnp.mean(x * x, axis=1, keepdims=True) + EPSILON)
    return scale, (x * scale * gain).astype(BF)


def project_kernel(x, gain, w, wb, pre, normed, scale):
    sc, nb = normal(x[...], gain[...])
    scale[...] = sc
    normed[...] = nb
    main = w.shape[1]
    pre[:, :main] = dg(nb, w[...], NN)
    pre[:, main:main + BETA] = dg(nb, wb[...], NT)
    pre[:, main + BETA:] = jnp.zeros((nb.shape[0], PRE - main - BETA), F32)


def project(rows_full, gain, w_in, w_bt):
    sd = jax.ShapeDtypeStruct
    outs = [sd((CAP, PRE), F32), sd((CAP, D), BF), sd((CAP, 1), F32)]
    return by_rows(project_kernel, 256, [rows_full], [gain, w_in, w_bt], outs, 0, 2 * CAP * D * PRE, "project")


def ffn_kernel(x, cot, gain, w_ug, w_u, w_d, normed, product, d_gate, d_up, d_normed, scale, share):
    sc, nb = normal(x[...], gain[...])
    scale[...] = sc
    normed[...] = nb
    gate = dg(nb, w_ug[...], NT)
    up = dg(nb, w_u[...], NT)
    sig = sigmoid(gate)
    act = gate * sig
    product[...] = (act * up).astype(BF)
    d_product = dg(cot[...], w_d[...], NT)
    dgt = (d_product * up * sig * (1.0 + gate * (1.0 - sig))).astype(BF)
    dup = (d_product * act).astype(BF)
    d_gate[...] = dgt
    d_up[...] = dup
    d_normed[...] = (dg(dgt, w_ug[...], NN) + dg(dup, w_u[...], NN)).astype(BF)
    lane_sums((dgt.astype(F32) * gate + dup.astype(F32) * up) / sc, share)


def ffn(held_full, cot_full, gain, w_ug, w_u, w_d):
    sd = jax.ShapeDtypeStruct
    ff = w_u.shape[0]
    outs = [sd((CAP, D), BF)] + [sd((CAP, ff), BF)] * 3 + [sd((CAP, D), BF), sd((CAP, 1), F32)]
    return by_rows(ffn_kernel, CAP // CHUNKS, [held_full, cot_full], [gain, w_ug, w_u, w_d], outs, UNITS,
                   10 * CAP * D * ff, "feed_forward")


def unproject_kernel(d_pre, pre, scale, w, wb, d_normed, share):
    d = d_pre[...]
    main = w.shape[1]
    d_normed[...] = (dg(d[:, :main], w[...], NT) + dg(d_pre[:, main:main + BETA], wb[...], NN)).astype(BF)
    lane_sums(d.astype(F32) * pre[...] / scale[...], share)


def unproject(d_pre, pre, scale, w_in, w_bt):
    outs = [jax.ShapeDtypeStruct((CAP, D), BF)]
    return by_rows(unproject_kernel, 256, [d_pre, pre, scale], [w_in, w_bt], outs, CAP // STEP, 2 * CAP * D * PRE, "unproject")


def blocks_kernel(shard, a, x, b, y, *outs):
    tall = a.shape[1]
    first, second = dg(a[...], x[...], TN).astype(BF), dg(b[...], y[...], TN).astype(BF)
    for i, out in enumerate(outs):
        @pl.when(pl.program_id(0) == i)
        def _():
            out[:tall] = first
            out[tall:] = second


def grad_blocks(m, device, a, x, b, y):
    wide, tall = x.shape[1] // m, a.shape[1] + b.shape[1]
    if wide % 128:
        both = jnp.concatenate([dg(a, x, TN), dg(b, y, TN)], axis=0).astype(BF)
        return [lax.dynamic_slice_in_dim(both, lax.rem(device + i, m) * wide, wide, 1) for i in range(m)]

    def side(i, shard):
        return (0, lax.rem(shard[0] + i, m))

    def fixed(i, shard):
        return (0, 0)

    return pl.pallas_call(
        blocks_kernel,
        grid_spec=pltpu.PrefetchScalarGridSpec(
            num_scalar_prefetch=1, grid=(m,),
            in_specs=[pl.BlockSpec(a.shape, fixed, pipeline_mode=pl.Buffered(1)), pl.BlockSpec((CAP, wide), side),
                      pl.BlockSpec(b.shape, fixed, pipeline_mode=pl.Buffered(1)), pl.BlockSpec((CAP, wide), side)],
            out_specs=[pl.BlockSpec((tall, wide), fixed)] * m),
        out_shape=[jax.ShapeDtypeStruct((tall, wide), BF)] * m,
        compiler_params=pltpu.CompilerParams(dimension_semantics=("arbitrary",), vmem_limit_bytes=ROOM),
        cost_estimate=pl.CostEstimate(flops=2 * CAP * tall * x.shape[1], bytes_accessed=12 * 2**20, transcendentals=0),
        name="gradient_blocks",
    )(device[None], a, x, b, y)


GROUP = ("head", "tensor")


def mm(left, right, dims=NN):
    return lax.dot_general(left, right, dims, preferred_element_type=F32)


def full_rows(piece_in):
    return lax.all_gather(piece_in, GROUP, axis=1, tiled=True)


def shares(partial_sum):
    return lax.psum_scatter(partial_sum.astype(BF), GROUP, scatter_dimension=1, tiled=True).astype(F32)


def column_blocks(grad, m):
    rows, wide = grad.shape[0], grad.shape[1] // m
    if wide % 128 == 0:
        return "columns", grad
    return "swap", grad.reshape(rows, m, wide).transpose(1, 0, 2)


def side_by_side(wide):
    return "abreast" if wide % 128 == 0 else "pile"


def level(weights):
    if weights.ndim == 2:
        return weights
    return weights.transpose(1, 0, 2).reshape(weights.shape[1], -1)


def gather_ring(piece):
    shards, device = lax.axis_size("shard"), lax.axis_index("shard")
    wide = piece.shape[1]
    whole = jnp.zeros((piece.shape[0], shards * wide), piece.dtype)
    for i in range(shards):
        came = lax.ppermute(piece, "shard", [(o, (o + i) % shards) for o in range(shards)]) if i else piece
        whole = lax.dynamic_update_slice_in_dim(whole, came, lax.rem(device - i + shards, shards) * wide, 1)
    return whole


def swap_ring(a, x, b, y):
    shards, device = lax.axis_size("shard"), lax.axis_index("shard")
    blocks = grad_blocks(shards, device, a, x, b, y)
    total = blocks[0].astype(F32)
    for i in range(1, shards):
        total = total + lax.ppermute(blocks[i], "shard", [(o, (o + i) % shards) for o in range(shards)]).astype(F32)
    return total[:a.shape[1]], total[a.shape[1]:]


def sum_blocks(blocks):
    return jnp.sum(blocks.astype(F32), axis=0)


def body(tokens, seq_lengths, dealing, gain_mixer, w_query, w_key, w_value, w_gate, w_beta, conv_weight,
         gain_heads, w_out, gain_ffn, w_up_gate, w_up, w_down, cotangent):
    shards = lax.axis_size("shard")
    width = tokens.shape[2]
    col_start = lax.axis_index(GROUP) * width
    per_peer = (CAP // shards + SEQ_DEV + 15) // 16 * 16

    w_piece = jnp.concatenate([w_query, w_key, w_value, w_gate], axis=1)
    b_piece = jnp.pad(w_beta.T, ((0, BETA - w_beta.shape[1]), (0, 0)))

    own_rows = tokens.reshape(REAL_DEV, width)
    taps = conv_weight.reshape(3 * CONV, width)
    head_gain = gain_heads[None, :]

    n = lax.axis_size("head")
    side = side_by_side(w_up.shape[0])
    x_rows, rows_full, sent_slot, recv_slot, pos, filled_f, w_in, w_bt = z_gather(
        n, seq_lengths, dealing, own_rows, per_peer, 1, "gather_rows", shards,
        ("gather", side_by_side(b_piece.shape[1])), (w_piece, b_piece))
    w_bt = level(w_bt)
    rows_full, cot_piece, w_out = lax.optimization_barrier((rows_full, cotangent, w_out))
    w_o = gather_ring(w_out)
    cot_full = full_rows(cot_piece)
    pre, normed, scale_one = project(rows_full, gain_mixer[None, :], w_in, w_bt)
    mixed, *saved = mixer_fwd(pre, pos, filled_f, taps, head_gain)
    branch_part, cot_full = lax.optimization_barrier((mm(mixed, w_o).astype(BF), cot_full))
    hidden, held_full, held_low, w_ug, w_u, w_d = z_turn(
        n, branch_part, x_rows, 2, "turn_branch", shards, (side,) * 3, (w_up_gate.T, w_up.T, w_down))
    w_ug, w_u, w_d = level(w_ug), level(w_u), level(w_d)
    normed_two, product, d_gate, d_up, d_normed_two, scale_two, share_two = ffn(
        held_full, cot_full, gain_ffn[None, :], w_ug, w_u, w_d)
    down_kind, d_w_down = column_blocks(mm(product, cot_full, TN).astype(BF), shards)
    gate_kind, d_w_ug = column_blocks(mm(d_gate, normed_two, TN).astype(BF), shards)
    ffn_gain_part = lax.dynamic_slice_in_dim(gain_ffn, col_start, width)[None, :]
    d_hidden, d_branch_full, _, ffn_gain_grad, d_w_ug, d_w_down = z_turn(
        n, d_normed_two, cotangent, 4, "turn_normed_two", shards, (gate_kind, down_kind), (d_w_ug, d_w_down),
        norm=(held_low, scale_two, ffn_gain_part, share_two))
    out_part = mm(product, w_d).astype(BF)
    out_part, d_branch_full = lax.optimization_barrier((out_part, d_branch_full))
    d_w_u, d_w_out = swap_ring(d_up, normed_two, mixed, d_branch_full)
    out_sum = shares(out_part)
    d_mixed = mm(d_branch_full, w_o, NT)
    d_pre, d_taps, d_head_gain = mixer_bwd(d_mixed, pre, pos, filled_f, taps, head_gain, saved)
    d_normed, share_one = unproject(d_pre, pre, scale_one, w_in, w_bt)
    d_normed, out_sum = lax.optimization_barrier((d_normed, out_sum))
    block_out = (hidden + out_sum).astype(BF)
    mixer_gain_part = lax.dynamic_slice_in_dim(gain_mixer, col_start, width)[None, :]
    small = jnp.concatenate([
        jnp.sum(d_taps, axis=1), jnp.zeros((1, width), F32), jnp.sum(ffn_gain_grad, axis=0)[None, :],
        jnp.pad(jnp.sum(d_head_gain, axis=0), (0, width - HD))[None, :],
        jnp.zeros((1, width), F32)], axis=0)
    d_tokens, summed, d_w_ug, d_w_down, d_w_in, d_w_bt = z_finish(
        n, d_normed, x_rows, scale_one, d_hidden, mixer_gain_part, share_one, small,
        sent_slot, recv_slot, per_peer, 6, "finish_rows", shards, normed, d_pre, (d_w_ug, d_w_down))
    d_w_in = sum_blocks(d_w_in)
    by_row = summed.transpose(1, 0, 2).reshape(16, D)
    d_conv = by_row[:12].reshape(CONV, 3, D)
    d_gain_heads = jnp.sum(summed[:, 14, :HD], axis=0)
    cut = [0, width, 2 * width, 3 * width, 4 * width]
    return (
        block_out, d_tokens, by_row[12],
        d_w_in[:, cut[0]:cut[1]], d_w_in[:, cut[1]:cut[2]], d_w_in[:, cut[2]:cut[3]], d_w_in[:, cut[3]:cut[4]],
        sum_blocks(d_w_bt)[:w_beta.shape[1]].T,
        d_conv, d_gain_heads, d_w_out, by_row[13],
        d_w_ug.T, d_w_u.T, d_w_down,
    )


def solution(mesh):
    feat = ("head", "tensor")
    placed = (
        P(None, "shard", feat), P(), P(), P(),
        P("shard", feat), P("shard", feat), P("shard", feat), P("shard", feat), P("shard", feat),
        P(None, None, feat), P(), P(feat, "shard"), P(),
        P("shard", feat), P("shard", feat), P(feat, "shard"), P("shard", feat),
    )
    given = (
        P("shard", feat), P(None, "shard", feat), P(),
        P("shard", feat), P("shard", feat), P("shard", feat), P("shard", feat), P("shard", feat),
        P(), P(), P(feat, "shard"), P(),
        P("shard", feat), P("shard", feat), P(feat, "shard"),
    )
    return jax.shard_map(body, mesh=mesh, in_specs=placed, out_specs=given, check_vma=False)
```

```python
import functools
import jax
import jax.numpy as jnp
from jax import lax
from jax.experimental import pallas as pl
from jax.experimental.pallas import tpu as pltpu

from jax.sharding import PartitionSpec as P

D = 2048
HD = 128
CONV = 4
BLOCK = 64
SEQ_DEV = 4
REAL_DEV = 1152
CAP = 1280
NB = CAP // BLOCK
EPSILON = 1e-06
HEAD_FLOOR = 0.01
PRE = 1152
BETA = 16
F32 = jnp.float32
BF = jnp.bfloat16

def split(x):
    hi = x.astype(BF)
    return hi, (x - hi.astype(F32)).astype(BF)

NN=(((1,),(0,)),((),())); NT=(((1,),(1,)),((),())); TN=(((0,),(0,)),((),()))

def dg(a, b, dims):
    return lax.dot_general(a, b, dims, preferred_element_type=F32)

def d3(a, b, dims=NN):
    ah, al = split(a); bh, bl = split(b)
    return dg(ah, bh, dims) + (dg(ah, bl, dims) + dg(al, bh, dims))

def four_times(step):
    return lambda i, c: step(4 * i + 3, step(4 * i + 2, step(4 * i + 1, step(4 * i, c))))

def goes_on(pos_ref, n):
    first = pos_ref[pl.ds(pl.multiple_of(n * BLOCK, BLOCK), 8), :][:1]
    return jnp.where(first != 0, 1.0, 0.0)

def masks():
    ri = lax.broadcasted_iota(jnp.int32, (BLOCK, BLOCK), 0)
    ci = lax.broadcasted_iota(jnp.int32, (BLOCK, BLOCK), 1)
    return ri, ci

def sigmoid(x):
    return 1.0 / (1.0 + jnp.exp(-x))

def conv_rows(cur, tail, wt, pos):
    ext = jnp.concatenate([tail, cur], axis=0)
    out = wt[0] * cur
    for j in range(1, CONV):
        sh = pltpu.roll(ext, j, axis=0)[8:]
        out = out + wt[j] * jnp.where(pos >= j, sh, 0.0)
    return out

def inverses(lmats, ri, ci):
    apart = ri ^ ci
    xs = [jnp.where(apart == 0, 1.0, 0.0) - jnp.where(apart == 1, m, 0.0) for m in lmats]
    s = 2
    while s < BLOCK:
        at = (apart >= s) & (apart < 2 * s)
        ys = [d3(x, jnp.where(at, m, 0.0)) for x, m in zip(xs, lmats)]
        xs = [x - d3(y, x) for x, y in zip(xs, ys)]
        s *= 2
    return xs

def fwd_kernel(pre, pos_ref, fill_ref, cw, gain, mixed, *refs):
    given, (c_out, qk, w_out, u_out, u2_out, o_out, p_out, t_out, m_out, s_out, b_s), sem = refs[:10], refs[10:21], refs[21]
    held = (c_out, qk, w_out, u_out, u2_out, o_out, p_out, t_out, m_out, s_out)

    def keep(*which):
        for i in which:
            pltpu.make_async_copy(held[i], given[i], sem.at[i]).start()

    ri, ci = masks()
    heads = 2
    def phase_a(n, tails):
        r = pl.ds(pl.multiple_of(n * BLOCK, BLOCK), BLOCK)
        pos = pos_ref[r, :]; fil = fill_ref[r, :]
        new_tails = []
        acts = []
        for i in range(3):
            cur = pre[r, i*256:(i+1)*256]
            wt = [cw[j*3+i:j*3+i+1, :] for j in range(CONV)]
            cc = conv_rows(cur, tails[i], wt, pos)
            c_out[r, i*256:(i+1)*256] = cc
            acts.append(cc * sigmoid(cc) * fil)
            new_tails.append(cur[BLOCK-8:])
        beta = sigmoid(pre[r, 1024:1152])
        for h in range(heads):
            hs = slice(h*HD, (h+1)*HD)
            yq = acts[0][:, hs]; yk = acts[1][:, hs]; v = acts[2][:, hs]
            q = yq * lax.rsqrt(jnp.sum(yq*yq, axis=1, keepdims=True) + EPSILON)
            k = yk * lax.rsqrt(jnp.sum(yk*yk, axis=1, keepdims=True) + EPSILON)
            b = beta[:, h:h+1]
            qk[r, h*HD:(h+1)*HD] = q
            qk[r, 256+h*HD:256+(h+1)*HD] = k
            lmat = jnp.where(ri > ci, b * d3(k, k, NT), 0.0)
            p_out[n*2+h] = jnp.where(ri >= ci, d3(q, k, NT), 0.0)
            t_out[n*2+h] = lmat
            u_out[r, hs] = b*v
            w_out[r, hs] = b*k
        return tuple(new_tails)
    z8 = jnp.zeros((8, 256), F32)
    lax.fori_loop(0, NB // 4, four_times(phase_a), (z8, z8, z8))
    keep(0, 1, 6)
    GRP = 20
    def phase_t(i, _):
        ts = inverses([t_out[i*GRP+j] for j in range(GRP)], ri, ci)
        for j in range(GRP):
            t_out[i*GRP+j] = ts[j]
        return 0
    lax.fori_loop(0, 2*NB//GRP, phase_t, 0)
    keep(7)
    def phase_w(i, _):
        todo = [(n, pl.ds(pl.multiple_of(n * BLOCK, BLOCK), BLOCK), h, slice(h*HD, (h+1)*HD)) for n in (4*i, 4*i+1, 4*i+2, 4*i+3) for h in range(heads)]
        wu = [d3(t_out[n*2+h], jnp.concatenate([w_out[r, c], u_out[r, c]], axis=1)) for n, r, h, c in todo]
        mb = [d3(qk[r, 256+h*HD:256+(h+1)*HD], x, TN) for x, (n, r, h, c) in zip(wu, todo)]
        for x, y, (n, r, h, c) in zip(wu, mb, todo):
            w_out[r, c] = x[:, :HD]; u_out[r, c] = x[:, HD:]
            m_out[n*2+h] = y[:, :HD]; b_s[n*2+h] = y[:, HD:]
        return 0
    lax.fori_loop(0, NB//4, phase_w, 0)
    keep(2, 3, 8)
    def phase_b(n, ss):
        out = []
        for h in range(heads):
            e = n*2+h
            s = ss[h] * goes_on(pos_ref, n)
            s_out[e] = s
            out.append(s - d3(m_out[e], s) + b_s[e])
        return tuple(out)
    zs = jnp.zeros((HD, HD), F32)
    lax.fori_loop(0, NB, phase_b, (zs, zs))
    keep(9)
    def phase_c(i, _):
        todo = [(n, pl.ds(pl.multiple_of(n * BLOCK, BLOCK), BLOCK), h, slice(h*HD, (h+1)*HD)) for n in (4*i, 4*i+1, 4*i+2, 4*i+3) for h in range(heads)]
        rr = [d3(jnp.concatenate([w_out[r, c], qk[r, c]], axis=0), s_out[n*2+h]) for n, r, h, c in todo]
        u2 = [u_out[r, c] - v[:BLOCK] for v, (n, r, h, c) in zip(rr, todo)]
        os_ = [v[BLOCK:] + d3(p_out[n*2+h], u) for v, u, (n, r, h, c) in zip(rr, u2, todo)]
        for o, u, (n, r, h, c) in zip(os_, u2, todo):
            u2_out[r, c] = u
            o_out[r, c] = o
            ms = jnp.mean(o*o, axis=1, keepdims=True)
            sc = lax.rsqrt(jnp.maximum(ms, HEAD_FLOOR))
            gg = pre[r, 768+h*HD:768+(h+1)*HD]
            mixed[r, c] = (o * sc * gain[...] * (gg * sigmoid(gg))).astype(BF)
        return 0
    lax.fori_loop(0, NB // 4, phase_c, 0)
    keep(4, 5)
    for i in range(10):
        pltpu.make_async_copy(held[i], given[i], sem.at[i]).wait()

def sds(*s, dt=F32): return jax.ShapeDtypeStruct(s, dt)
VM = pl.BlockSpec(memory_space=pltpu.VMEM)
SM = pl.BlockSpec(memory_space=pltpu.SMEM)

def mixer_fwd(pre, pos, fil, cw, gain):
    outs = (sds(CAP,256,dt=BF), sds(CAP,768), sds(CAP,512), sds(CAP,256), sds(CAP,256), sds(CAP,256), sds(CAP,256),
            sds(2*NB,BLOCK,BLOCK), sds(2*NB,BLOCK,BLOCK), sds(2*NB,HD,HD), sds(2*NB,HD,HD))
    return pl.pallas_call(fwd_kernel, out_shape=outs, in_specs=[VM]*5, out_specs=[VM]+[pl.BlockSpec(memory_space=pltpu.HBM)]*(len(outs)-1),
        scratch_shapes=[pltpu.VMEM(o.shape,F32) for o in outs[1:]]+[pltpu.VMEM((2*NB,HD,HD),F32), pltpu.SemaphoreType.DMA((10,))],
        compiler_params=pltpu.CompilerParams(vmem_limit_bytes=60*2**20), cost_estimate=pl.CostEstimate(flops=0, bytes_accessed=140 * 2**20, transcendentals=0),
        name="mixer_forward")(pre, pos, fil, cw, gain)

def bwd_kernel(dmix, pre, pos_ref, fill_ref, cw, gain, *refs):
    kept, (dpre, dcw, dgain), held, (e_s, do_s, sem) = refs[:10], refs[10:13], refs[13:23], refs[23:]
    c_in, qk, w_in, u_in, u2_in, o_in, p_in, t_in, m_in, s_in = held

    def fetch(i):
        return pltpu.make_async_copy(kept[i], held[i], sem.at[i])

    for i in (5, 6, 1, 2, 8, 7, 9, 0, 3, 4):
        fetch(i).start()
    for i in (5, 6, 1, 2):
        fetch(i).wait()
    ri, ci = masks()
    heads = 2
    lane = lax.broadcasted_iota(jnp.int32, (BLOCK, HD), 1)
    dgain[...] = jnp.zeros_like(dgain)
    dcw[...] = jnp.zeros_like(dcw)
    def phase_a(n, _):
        r = pl.ds(pl.multiple_of(n * BLOCK, BLOCK), BLOCK)
        for h in range(heads):
            hs = slice(h*HD, (h+1)*HD)
            e = n*2+h
            o = o_in[r, hs]; dm = dmix[r, hs]
            gg = pre[r, 768+h*HD:768+(h+1)*HD]
            sg = sigmoid(gg); si = gg*sg
            ms = jnp.mean(o*o, axis=1, keepdims=True)
            sc = lax.rsqrt(jnp.maximum(ms, HEAD_FLOOR))
            on = o*sc
            gn = gain[...]
            dpre[r, 768+h*HD:768+(h+1)*HD] = (dm * on * gn * (sg * (1.0 + gg*(1.0-sg)))).astype(BF)
            dgs = dm * on * si
            dgain[...] += jnp.sum(dgs.reshape(8, 8, HD), axis=0)
            dn = dm * gn * si
            corr = jnp.where(ms > HEAD_FLOOR, jnp.mean(dn*on, axis=1, keepdims=True), 0.0)
            do = sc * (dn - on*corr)
            do_s[r, hs] = do
            pdo = d3(p_in[e], do, TN)
            qw = jnp.concatenate([qk[r, hs], w_in[r, hs]], axis=0)
            dd = jnp.concatenate([do, -pdo], axis=0)
            e_s[e] = d3(qw, dd, TN)
        return 0
    lax.fori_loop(0, NB // 4, four_times(phase_a), 0)
    fetch(8).wait()

    def phase_b(i, ds):
        n = NB-1-i
        out = []
        for h in range(heads):
            e = n*2+h
            d = ds[h]
            ee = e_s[e]
            e_s[e] = d
            out.append((d - d3(m_in[e], d, TN) + ee) * goes_on(pos_ref, n))
        return tuple(out)
    zs = jnp.zeros((HD, HD), F32)
    lax.fori_loop(0, NB, phase_b, (zs, zs))
    for i in (7, 9, 0, 3, 4):
        fetch(i).wait()

    def phase_c(i, heads_dc):
        blocks = tuple(NB - 1 - j - 4 * i for j in range(4))
        todo = [(n, pl.ds(pl.multiple_of(n * BLOCK, BLOCK), BLOCK), h, slice(h*HD, (h+1)*HD)) for n in blocks for h in range(heads)]
        def every(f, *lists):
            return [f(*v) for v in zip(*lists)]
        ns, rs, hh, hs = zip(*todo)
        es = [n*2+h for n, h in zip(ns, hh)]
        fil = [fill_ref[r, :] for r in rs]
        beta_t = [sigmoid(pre[r, 1024:1152]) for r in rs]
        q = [qk[r, c] for r, c in zip(rs, hs)]
        k = [qk[r, 256+h*HD:256+(h+1)*HD] for r, h in zip(rs, hh)]
        w = [w_in[r, c] for r, c in zip(rs, hs)]
        u = [u_in[r, c] for r, c in zip(rs, hs)]
        u2 = [u2_in[r, c] for r, c in zip(rs, hs)]
        do = [do_s[r, c] for r, c in zip(rs, hs)]
        p = [p_in[e] for e in es]
        t = [t_in[e] for e in es]
        s = [s_in[e] for e in es]
        ds = [e_s[e] for e in es]
        b = [x[:, h:h+1] for x, h in zip(beta_t, hh)]
        du2 = every(lambda p, do, k, ds: d3(p, do, TN) + d3(k, ds), p, do, k, ds)
        dp = every(lambda do, u2: jnp.where(ri >= ci, d3(do, u2, NT), 0.0), do, u2)
        g = every(lambda k: d3(k, k, NT), k)
        xs = every(lambda do, du2, s: d3(jnp.concatenate([do, -du2], axis=0), s, NT), do, du2, s)
        dq = every(lambda xs, dp, k: xs[:BLOCK] + d3(dp, k), xs, dp, k)
        xx = every(lambda t, xs, du2: d3(t, jnp.concatenate([xs[BLOCK:], du2], axis=1), TN), t, xs, du2)
        dk = every(lambda dp, q, u2, ds: d3(dp, q, TN) + d3(u2, ds, NT), dp, q, u2, ds)
        mm = every(lambda xx, w, u: jnp.where(ri > ci, -d3(xx, jnp.concatenate([w, u], axis=1), NT), 0.0), xx, w, u)
        cv = [c_in[r, 512+h*HD:512+(h+1)*HD] for r, h in zip(rs, hh)]
        sv = every(sigmoid, cv)
        bm = every(lambda b, mm: b*mm, b, mm)
        dk = every(lambda dk, bm, k, b, xx: dk + d3(bm + bm.T, k) + b*xx[:, :HD], dk, bm, k, b, xx)
        db = every(lambda mm, g, xx, k, cv, sv, fil: jnp.sum(mm*g, axis=1, keepdims=True)
                   + jnp.sum(xx[:, :HD]*k + xx[:, HD:]*(cv*sv*fil), axis=1, keepdims=True), mm, g, xx, k, cv, sv, fil)
        cq = [c_in[r, c] for r, c in zip(rs, hs)]
        ck = [c_in[r, 256+h*HD:256+(h+1)*HD] for r, h in zip(rs, hh)]
        def unit_back(c, fil, n, d):
            sg = sigmoid(c)
            y = c*sg*fil
            r = lax.rsqrt(jnp.sum(y*y, axis=1, keepdims=True) + EPSILON)
            return r*(d - n*jnp.sum(d*n, axis=1, keepdims=True))*fil*(sg*(1.0+c*(1.0-sg)))
        aq = every(unit_back, cq, fil, q, dq)
        ak = every(unit_back, ck, fil, k, dk)
        av = every(lambda b, xx, fil, sv, cv: b*xx[:, HD:]*fil*(sv*(1.0+cv*(1.0-sv))), b, xx, fil, sv, cv)
        for j, n in enumerate(blocks):
            r = rs[2*j]
            dbt = jnp.where(lane == 0, db[2*j], jnp.where(lane == 1, db[2*j+1], 0.0))
            dpre[r, 1024:1152] = (dbt*beta_t[2*j]*(1.0-beta_t[2*j])).astype(BF)
            pos = pos_ref[r, :]
            nxt = jnp.minimum(n+1, NB-1)
            posx = jnp.concatenate([pos, pos_ref[pl.ds(pl.multiple_of(nxt*BLOCK, BLOCK), 8), :]], axis=0)
            prv = jnp.maximum(n*BLOCK-8, 0)
            new = []
            for i, acts in enumerate((aq, ak, av)):
                dc = jnp.concatenate(acts[2*j:2*j+2], axis=1)
                ext = jnp.concatenate([dc, heads_dc[i]], axis=0)
                cur = pre[r, i*256:(i+1)*256]
                tail = pre[pl.ds(pl.multiple_of(prv, 8), 8), i*256:(i+1)*256]
                xext = jnp.concatenate([tail, cur], axis=0)
                dx = cw[i:i+1, :]*dc
                dcw[i] += jnp.sum((dc*cur).reshape(8, 8, 256), axis=0)
                for o in range(1, CONV):
                    z = jnp.where(posx >= o, ext, 0.0)
                    dx = dx + cw[o*3+i:o*3+i+1, :]*pltpu.roll(z, BLOCK+8-o, axis=0)[:BLOCK]
                    sh = pltpu.roll(xext, o, axis=0)[8:]
                    dcw[o*3+i] += jnp.sum(jnp.where(pos >= o, dc*sh, 0.0).reshape(8, 8, 256), axis=0)
                dpre[r, i*256:(i+1)*256] = dx.astype(BF)
                new.append(dc[:8])
            heads_dc = tuple(new)
        return heads_dc
    z8 = jnp.zeros((8, 256), F32)
    lax.fori_loop(0, NB // 4, phase_c, (z8, z8, z8))

def mixer_bwd(dmix, pre, pos, fil, cw, gain, saved):
    outs = (sds(CAP,1152,dt=BF), sds(12,8,256), sds(8,HD))
    return pl.pallas_call(bwd_kernel, out_shape=outs, in_specs=[VM]*6+[pl.BlockSpec(memory_space=pltpu.HBM)]*len(saved), out_specs=[VM]*3,
        scratch_shapes=[pltpu.VMEM(a.shape, F32) for a in saved]+[pltpu.VMEM((2*NB,HD,HD),F32), pltpu.VMEM((CAP,256),F32), pltpu.SemaphoreType.DMA((10,))],
        compiler_params=pltpu.CompilerParams(vmem_limit_bytes=60*2**20), cost_estimate=pl.CostEstimate(flops=0, bytes_accessed=200 * 2**20, transcendentals=0),
        name="mixer_backward")(dmix, pre, pos, fil, cw, gain, *saved)


MESH = pl.DeviceIdType.MESH
ROOM = 60 * 2**20
LINK_COST = 150 * 2**20
HBM = pl.BlockSpec(memory_space=pltpu.HBM)


def places():
    s, h, t = lax.axis_index("shard"), lax.axis_index("head"), lax.axis_index("tensor")
    return h, t, (s, h + 1, t), (s, h - 1, t), (s, h, 1 - t)


def shard_peers(m):
    s, h, t = lax.axis_index("shard"), lax.axis_index("head"), lax.axis_index("tensor")
    return [((lax.rem(s + i, m), h, t), lax.rem(s + i, m)) for i in range(1, m)]


def greet_shard(m):
    barrier = pltpu.get_barrier_semaphore()
    for p, _ in shard_peers(m):
        pl.semaphore_signal(barrier, inc=1, device_id=p, device_id_type=MESH)
    return m - 1


class Carry:
    def __init__(self, hops, kinds, m, ins, outs, send, recv, here):
        self.hops, self.kinds, self.m, self.ins, self.outs = hops, kinds, m, ins, outs
        self.send, self.recv, self.here = send, recv, here
        s, self.h, self.t = lax.axis_index("shard"), lax.axis_index("head"), lax.axis_index("tensor")
        self.me = s
        self.side = s + 1 - 2 * lax.rem(s, 2)
        self.over = lax.rem(s + 2, 4)
        self.corner = lax.rem(self.side + 2, 4)

    def relayed(self, e):
        return self.hops and self.m == 4 and self.kinds[e] in ("gather", "abreast")

    def part(self, e, src, half=None):
        rows = self.ins[e].shape[0]
        span = pl.ds(0, rows) if half is None else pl.ds(half * (rows // 2), rows // 2)
        if self.kinds[e] == "gather":
            first = src * rows + (0 if half is None else half * (rows // 2))
            return self.outs[e].at[pl.ds(pl.multiple_of(first, rows // 2), span.size)]
        if self.kinds[e] == "abreast":
            w = self.ins[e].shape[1]
            return self.outs[e].at[span, pl.ds(pl.multiple_of(src * w, w), w)]
        return self.outs[e].at[src]

    def given(self, e, dst):
        if self.kinds[e] == "columns":
            w = self.ins[e].shape[1] // self.m
            return self.ins[e].at[:, pl.ds(pl.multiple_of(dst * w, w), w)]
        return self.ins[e].at[dst] if self.kinds[e] == "swap" else self.ins[e]

    def move(self, e, src, dst, i, j, to):
        return pltpu.make_async_remote_copy(src_ref=src, dst_ref=dst, send_sem=self.send.at[e, i], recv_sem=self.recv.at[e, j],
                                            device_id=(to, self.h, self.t), device_id_type=MESH)

    def copy(self, e, i, to):
        return self.move(e, self.given(e, to), self.part(e, self.me), i, self.me, to)

    def came(self, e, src):
        return self.move(e, self.given(e, src), self.part(e, src), 0, src, src)

    def hand(self, e, half):
        src, to = (self.side, self.over) if half == 0 else (self.over, self.side)
        piece = self.part(e, src, half)
        return self.move(e, piece, piece, 2 + half, src if half == 0 else self.m, to)

    def handed(self, e, half):
        piece = self.part(e, self.corner, half)
        return self.move(e, piece, piece, 2 + half, self.corner if half == 0 else self.m, self.over if half == 0 else self.side)

    def local(self, e):
        return pltpu.make_async_copy(self.given(e, self.me), self.part(e, self.me), self.here.at[e])

    def targets(self, e):
        return [self.side, self.over] if self.relayed(e) else [p[1] for p in shard_peers(self.m)]

    def greet(self):
        return greet_shard(self.m) if self.kinds else 0

    def start(self):
        for e in range(len(self.kinds)):
            for i, to in enumerate(self.targets(e)):
                self.copy(e, i, to).start()
            self.local(e).start()

    def relay(self, e):
        if e < len(self.kinds) and self.relayed(e):
            self.came(e, self.side).wait_recv()
            self.hand(e, 0).start()
            self.came(e, self.over).wait_recv()
            self.hand(e, 1).start()

    def wait(self):
        for e in range(len(self.kinds)):
            self.local(e).wait()
            for i, to in enumerate(self.targets(e)):
                self.copy(e, i, to).wait_send()
                if not self.relayed(e):
                    self.came(e, to).wait_recv()
            if self.relayed(e):
                for half in range(2):
                    self.handed(e, half).wait_recv()
                    self.hand(e, half).wait_send()


def carried(kinds, m, arrays):
    dma = pltpu.SemaphoreType.DMA
    give = {"gather": lambda a: (m * a.shape[0], a.shape[1]), "swap": lambda a: a.shape,
            "abreast": lambda a: (a.shape[0], m * a.shape[1]), "pile": lambda a: (m,) + a.shape,
            "columns": lambda a: (m, a.shape[0], a.shape[1] // m)}
    shapes = [jax.ShapeDtypeStruct(give[k](a), a.dtype) for k, a in zip(kinds, arrays)]
    e = len(kinds)
    return shapes, ([dma((e, m + 1)), dma((e, m + 1)), dma((e,))] if e else [])


def carry_of(kinds, m, refs, n_in, n_out, hops=False):
    e = len(kinds)
    ins, refs = refs[:n_in], refs[n_in:]
    c_in, refs = refs[:e], refs[e:]
    outs, refs = refs[:n_out], refs[n_out:]
    c_out, refs = refs[:e], refs[e:]
    sems = (refs[-3:] if e else (None,) * 3)
    scratch = refs[:-3] if e else refs
    return ins, outs, scratch, Carry(hops, kinds, m, c_in, c_out, *sems)


def greet(n, h, up, down, across, more=0):
    barrier = pltpu.get_barrier_semaphore()
    pl.semaphore_signal(barrier, inc=1, device_id=across, device_id_type=MESH)

    @pl.when(h < n - 1)
    def _():
        pl.semaphore_signal(barrier, inc=1, device_id=up, device_id_type=MESH)

    @pl.when(h > 0)
    def _():
        pl.semaphore_signal(barrier, inc=1, device_id=down, device_id_type=MESH)

    pl.semaphore_wait(barrier, 1 + more + (h < n - 1).astype(jnp.int32) + (h > 0).astype(jnp.int32))


class Plan:
    def __init__(self, m, per_peer, lengths, dealing, starts):
        self.m, self.per_peer, self.lengths, self.dealing, self.starts = m, per_peer, lengths, dealing, starts
        self.shift = m.bit_length() - 1
        self.device = lax.axis_index("shard")

        def begin(q, total):
            starts[q] = total
            return total + lengths[q]

        lax.fori_loop(0, lengths.shape[0], begin, jnp.int32(0))

    def under(self, row, residue):
        return lax.shift_right_arithmetic(row - 1 - residue + self.m, self.shift + jnp.zeros_like(row))

    def members(self, g):
        at = [self.dealing[g * SEQ_DEV + i] for i in range(SEQ_DEV)]
        return [(self.starts[q], self.lengths[q]) for q in at]

    def sent(self, ids):
        packed = ids * self.m + self.device

        def group(g, slot):
            seqs = self.members(g)
            counts = [self.under(s + n, self.device) - self.under(s, self.device) for s, n in seqs]
            for s, n in seqs:
                first = g * self.per_peer - self.under(s, self.device)
                for (other, _), count in zip(seqs, counts):
                    first = first + jnp.where(other < s, count, 0)
                slot = slot + jnp.where((packed >= s) & (packed < s + n), first, 0)
            return slot

        return lax.fori_loop(0, self.lengths.shape[0] // SEQ_DEV, group, ids)

    def rows(self, ids):
        seqs = self.members(self.device)
        place, start, length, below = ids, jnp.zeros_like(ids), jnp.zeros_like(ids), jnp.int32(0)
        for s, n in seqs:
            here = ids >= below
            place = jnp.where(here, ids - below, place)
            start = jnp.where(here, s, start)
            length = jnp.where(here, n, length)
            below = below + lax.shift_right_arithmetic(n + BLOCK - 1, jnp.int32(6)) * BLOCK
        filled = place < length
        natural = start + place
        source = natural & (self.m - 1)
        slot = source * self.per_peer + self.under(natural, source) - self.under(start, source)
        for s, n in seqs:
            span = self.under(jnp.zeros_like(ids) + (s + n), source) - self.under(jnp.zeros_like(ids) + s, source)
            slot = slot + jnp.where(s < start, span, 0)
        return place, filled, jnp.where(filled, slot, -1)


def gather_kernel(n, width, m, kinds, *refs):
    (lengths, dealing, tokens), (x, out, sent_at, slot_at, pos_at, fill_at), scratch, carry = carry_of(kinds, m, refs, 3, 6)
    place_at, starts, outbox, inbox, deal_s, deal_r, here, up_s, up_r, down_s, down_r, core_s, core_r = scratch
    h, t, up, down, across = places()
    per_peer = outbox.shape[1]

    def cols(j):
        return out.at[:, pl.ds(pl.multiple_of((j * 2 + t) * width, width), width)]

    def other(j):
        return out.at[:, pl.ds(pl.multiple_of((j * 2 + 1 - t) * width, width), width)]

    def send(j, src, ss, rs, to):
        return pltpu.make_async_remote_copy(src_ref=src, dst_ref=cols(j), send_sem=ss.at[j], recv_sem=rs.at[j],
                                            device_id=to, device_id_type=MESH)

    greet(n, h, up, down, across, carry.greet())
    plan = Plan(m, per_peer, lengths, dealing, starts)
    peers = shard_peers(m)
    mine = lax.axis_index("shard")
    sent = plan.sent(lax.broadcasted_iota(jnp.int32, (1, REAL_DEV), 1))
    ids = lax.broadcasted_iota(jnp.int32, (per_peer, REAL_DEV), 0)

    def deal(i, p, src):
        return pltpu.make_async_remote_copy(src_ref=outbox.at[p[1]], dst_ref=inbox.at[src], send_sem=deal_s.at[i],
                                            recv_sem=deal_r.at[src], device_id=p[0], device_id_type=MESH)

    def pick(q):
        return dg(jnp.where(sent - q * per_peer == ids, 1.0, 0.0).astype(BF), tokens[...], NN).astype(BF)

    for i, p in enumerate(peers):
        outbox[p[1]] = pick(p[1])
        deal(i, p, mine).start()
    carry.start()
    inbox[mine] = pick(mine)
    place_at[...] = plan.rows(lax.broadcasted_iota(jnp.int32, (CAP, 1), 0))[2]
    for i, p in enumerate(peers):
        deal(i, p, p[1]).wait_recv()
    lanes = lax.broadcasted_iota(jnp.int32, (STEP, m * per_peer), 1)

    def settle(i, c):
        r = pl.ds(pl.multiple_of(i * STEP, STEP), STEP)
        chosen = jnp.where(place_at[r, :] == lanes, 1.0, 0.0).astype(BF)
        x[r, :] = dg(chosen, inbox[...].reshape(m * per_peer, width), NN).astype(BF)
        return c

    lax.fori_loop(0, CAP // STEP, settle, 0)
    local = pltpu.make_async_copy(x, cols(h), here)
    local.start()

    @pl.when(h < n - 1)
    def _():
        send(h, x, up_s, up_r, up).start()

    @pl.when(h > 0)
    def _():
        send(h, x, down_s, down_r, down).start()

    send(h, x, core_s, core_r, across).start()
    sent_at[...] = plan.sent(lax.broadcasted_iota(jnp.int32, (REAL_DEV, 1), 0))
    slot_at[...] = plan.rows(lax.broadcasted_iota(jnp.int32, (1, CAP), 1))[2]
    position, filled, _ = plan.rows(lax.broadcasted_iota(jnp.int32, (CAP, 1), 0))
    pos_at[...] = position
    fill_at[...] = jnp.where(filled, 1.0, 0.0)
    for k in range(1, n):
        below, above = h - k, h + k

        @pl.when(below >= 0)
        def _():
            send(below, cols(below), up_s, up_r, up).wait_recv()

            @pl.when(h < n - 1)
            def _():
                send(below, cols(below), up_s, up_r, up).start()

            send(below, cols(below), core_s, core_r, across).start()

        @pl.when(above < n)
        def _():
            send(above, cols(above), down_s, down_r, down).wait_recv()

            @pl.when(h > 0)
            def _():
                send(above, cols(above), down_s, down_r, down).start()

            send(above, cols(above), core_s, core_r, across).start()

    for j in range(n):
        back = pltpu.make_async_remote_copy(src_ref=cols(j), dst_ref=other(j), send_sem=core_s.at[j], recv_sem=core_r.at[j],
                                            device_id=across, device_id_type=MESH)
        back.wait_recv()
        back.wait_send()

        @pl.when((j <= h) & (h < n - 1))
        def _():
            send(j, cols(j), up_s, up_r, up).wait_send()

        @pl.when((j >= h) & (h > 0))
        def _():
            send(j, cols(j), down_s, down_r, down).wait_send()

    local.wait()
    for i, p in enumerate(peers):
        deal(i, p, mine).wait_send()
    carry.wait()


def z_gather(n, lengths, dealing, tokens, per_peer, collective_id, name, m, kinds, arrays):
    width = tokens.shape[1]
    dma = pltpu.SemaphoreType.DMA
    sd = jax.ShapeDtypeStruct
    shapes, sems = carried(kinds, m, arrays)
    return pl.pallas_call(
        functools.partial(gather_kernel, n, width, m, kinds),
        out_shape=[sd((CAP, width), BF), sd((CAP, 2 * n * width), BF), sd((REAL_DEV, 1), jnp.int32), sd((1, CAP), jnp.int32),
                   sd((CAP, 1), jnp.int32), sd((CAP, 1), F32)] + shapes,
        in_specs=[SM, SM, VM] + [HBM] * len(shapes), out_specs=[VM, HBM] + [VM] * 4 + [HBM] * len(shapes),
        scratch_shapes=[pltpu.VMEM((CAP, 1), jnp.int32), pltpu.SMEM(lengths.shape, jnp.int32)]
        + [pltpu.VMEM((m, per_peer, width), BF)] * 2 + [dma((m,)), dma((m,)), dma] + [dma((n,))] * 6 + sems,
        compiler_params=pltpu.CompilerParams(collective_id=collective_id, has_side_effects=True, vmem_limit_bytes=ROOM),
        cost_estimate=pl.CostEstimate(flops=0, bytes_accessed=LINK_COST, transcendentals=0),
        name=name,
    )(lengths, dealing, tokens, *arrays)


STEP = 128


def group_peers(n):
    s, h, t = lax.axis_index("shard"), lax.axis_index("head"), lax.axis_index("tensor")
    peers = []
    for i in range(1, 2 * n):
        hh, tt = lax.rem(h + i // 2, n), lax.rem(t + i % 2, 2)
        peers.append(((s, hh, tt), hh * 2 + tt))
    return peers


def greet_group(n, more=0):
    barrier = pltpu.get_barrier_semaphore()
    for p, _ in group_peers(n):
        pl.semaphore_signal(barrier, inc=1, device_id=p, device_id_type=MESH)
    pl.semaphore_wait(barrier, 2 * n - 1 + more)


def finish_kernel(n, width, m, kinds, fill, piles, *refs):
    (part, kept, scale, base, gain, share, small, sent, place, *left), (tokens, every, *grads), scratch, carry = carry_of(
        kinds, m, refs, 9 + piles + 2 * fill, 2 + piles + 2 * fill)
    stacks, left = left[:piles], left[piles:]
    added, grads = grads[:piles], grads[piles:]
    *scratch, pile_sem = scratch
    heaps, scratch = scratch[:piles], scratch[piles:]
    if fill:
        *scratch, l_buf, r_buf, blocks, strips, l_sem, r_sem, w_s, w_r, w_own = scratch
    (low, dgain, outbox, inbox, deal_s, deal_r, held, ours, shard_s, shard_r, group_s, group_r,
     acc, tots, wide_t, tot_s, tot_r, mine, theirs, from_below, from_above,
     here, core_s, core_r, up_s, up_r, down_s, down_r) = scratch
    h, t, up, down, across = places()

    def cols(j, c):
        return part.at[:, pl.ds(pl.multiple_of((j * 2 + c) * width, width), width)]

    def swap(j):
        return pltpu.make_async_remote_copy(src_ref=cols(j, 1 - t), dst_ref=theirs.at[j], send_sem=core_s.at[j],
                                            recv_sem=core_r.at[j], device_id=across, device_id_type=MESH)

    def own(j):
        return pltpu.make_async_copy(cols(j, t), mine.at[j], here.at[j])

    def rise(k):
        return pltpu.make_async_remote_copy(src_ref=mine.at[n - 1 - k], dst_ref=from_below.at[k], send_sem=up_s.at[k],
                                            recv_sem=up_r.at[k], device_id=up, device_id_type=MESH)

    def fall(k):
        return pltpu.make_async_remote_copy(src_ref=mine.at[k], dst_ref=from_above.at[k], send_sem=down_s.at[k],
                                            recv_sem=down_r.at[k], device_id=down, device_id_type=MESH)

    def total(j, extra):
        def step(i, c):
            r = pl.ds(pl.multiple_of(i * STEP, STEP), STEP)
            v = mine[j, r, :].astype(F32) + theirs[j, r, :].astype(F32)
            if extra is not None:
                v = v + extra(r).astype(F32)
            mine[j, r, :] = v.astype(BF)
            return c
        lax.fori_loop(0, CAP // STEP, step, 0)

    order = [j for i in range(n // 2) for j in (n - 1 - i, i)]
    for j in order:
        own(j).start()

    def load(i):
        return pltpu.make_async_copy(stacks[i], heaps[i], pile_sem.at[i])

    def add_up(i):
        load(i).wait()
        tall = heaps[i].shape[1] // 4

        def step(q, c):
            r = pl.ds(pl.multiple_of(q * tall, tall), tall)
            v = heaps[i][0, r, :].astype(F32)
            for b in range(1, m):
                v = v + heaps[i][b, r, :].astype(F32)
            added[i][r, :] = v
            return c

        lax.fori_loop(0, 4, step, 0)

    for i in range(piles):
        load(i).start()
    greet_group(n, greet_shard(m))
    me = h * 2 + t
    peers = group_peers(n)

    def tot_copy(i, p, dst):
        return pltpu.make_async_remote_copy(src_ref=share, dst_ref=tots.at[dst], send_sem=tot_s.at[i], recv_sem=tot_r.at[dst],
                                            device_id=p, device_id_type=MESH)

    for i, p in enumerate(peers):
        tot_copy(i, p[0], me).start()
    for j in order:
        swap(j).start()
    carry.start()
    shard = lax.axis_index("shard")
    others = shard_peers(m)
    if fill:
        lhs, rhs = left
        wide = lhs.shape[1] // m

        def columns(q):
            return lhs.at[:, pl.ds(pl.multiple_of(q * wide, wide), wide)]

        def fetch(i, q):
            return pltpu.make_async_copy(columns(q), l_buf.at[i], l_sem.at[i])

        made = (blocks, strips)

        def grad(i, p, src):
            return [pltpu.make_async_remote_copy(src_ref=made[e].at[i], dst_ref=grads[e].at[src], send_sem=w_s.at[e, i],
                                                 recv_sem=w_r.at[e, src], device_id=p[0], device_id_type=MESH) for e in range(2)]

        own_grad = [pltpu.make_async_copy(made[e].at[m - 1], grads[e].at[shard], w_own.at[e]) for e in range(2)]
        whole = pltpu.make_async_copy(rhs, r_buf, r_sem)
        whole.start()
        for i, p in enumerate(others):
            fetch(i, p[1]).start()
        fetch(m - 1, shard).start()

        def multiply(i):
            if i == 0:
                whole.wait()
            fetch(i, shard).wait()
            main = blocks.shape[2]
            strips[i] = dg(r_buf[:, main:main + BETA], l_buf[i], TN).astype(BF)
            blocks[i] = dg(l_buf[i], r_buf[:, :main], TN).astype(BF)
            for c in (grad(i, others[i], shard) if i < m - 1 else own_grad):
                c.start()

        multiply(0)

    def arrive(j):
        own(j).wait()
        swap(j).wait_recv()

    for tick in range(2 * n - 2):
        ku = tick - h
        tu = n - 1 - ku

        @pl.when((ku >= 0) & (tu > h))
        def _():
            arrive(tu)

            @pl.when(h == 0)
            def _():
                total(tu, None)

            @pl.when(h > 0)
            def _():
                rise(ku).wait_recv()
                total(tu, lambda r: from_below[ku, r, :])

            rise(ku).start()

        kd = tick - (n - 1 - h)

        @pl.when((kd >= 0) & (kd < h))
        def _():
            arrive(kd)

            @pl.when(h == n - 1)
            def _():
                total(kd, None)

            @pl.when(h < n - 1)
            def _():
                fall(kd).wait_recv()
                total(kd, lambda r: from_above[kd, r, :])

            fall(kd).start()

        if fill and tick + 1 < m:
            multiply(tick + 1)

        if tick >= 2 * n - 2 - piles:
            add_up(tick - (2 * n - 2 - piles))

    if fill:
        for i in range(2 * n - 1, m):
            multiply(i)
    arrive(h)
    for i, p in enumerate(peers):
        tot_copy(i, p[0], p[1]).wait_recv()
    v = share[...]
    for i, p in enumerate(peers):
        v = v + tots[p[1]]
    for i in range(CAP // STEP):
        wide_t[i] = jnp.broadcast_to(v[i:i + 1, :], (8, 128))
    dgain[...] = jnp.zeros_like(dgain)
    gains = gain[...]
    eighth = jnp.full((8, 128), 0.125, BF)

    def final(get):
        def step(i, c):
            r = pl.ds(pl.multiple_of(i * STEP, STEP), STEP)
            acc[r, :] = get(r)
            return c
        lax.fori_loop(0, CAP // STEP, step, 0)

    final(lambda r: mine[h, r, :].astype(F32) + theirs[h, r, :].astype(F32))

    def first(get):
        final(lambda r: acc[r, :] + get(r).astype(F32))

    @pl.when((h > 0) & (h < n - 1))
    def _():
        @pl.when(2 * h < n)
        def _():
            fall(h).wait_recv()
            first(lambda r: from_above[h, r, :])

        @pl.when(2 * h >= n)
        def _():
            rise(n - 1 - h).wait_recv()
            first(lambda r: from_below[n - 1 - h, r, :])

    by_below = (h > 0) & ((2 * h < n) | (h == n - 1))

    @pl.when(by_below)
    def _():
        rise(n - 1 - h).wait_recv()

    @pl.when(jnp.logical_not(by_below))
    def _():
        fall(h).wait_recv()

    def close(get):
        def step(i, c):
            r = pl.ds(pl.multiple_of(i * STEP, STEP), STEP)
            hi, lo = split(wide_t[i])
            total_r = dg(hi, eighth, TN) + dg(lo, eighth, TN)
            sc = scale[r, :]
            kp = kept[r, :].astype(F32)
            dn = acc[r, :] + get(r).astype(F32)
            back = base[r, :].astype(F32) + sc * (gains * dn) - kp * jnp.tile((sc * sc * sc) * (total_r * (1.0 / D)), (1, width // 128))
            low[r, :] = back.astype(BF)
            dgain[...] += jnp.sum((dn * kp * sc).reshape(STEP // 8, 8, width), axis=0)
            return c
        lax.fori_loop(0, CAP // STEP, step, 0)

    @pl.when(by_below)
    def _():
        close(lambda r: from_below[n - 1 - h, r, :])

    @pl.when(jnp.logical_not(by_below))
    def _():
        close(lambda r: from_above[h, r, :])

    for i, p in enumerate(peers):
        tot_copy(i, p[0], me).wait_send()

    per_peer = outbox.shape[1]
    ids = lax.broadcasted_iota(jnp.int32, (per_peer, place.shape[1]), 0)

    def back(i, p, src):
        return pltpu.make_async_remote_copy(src_ref=outbox.at[p[1]], dst_ref=inbox.at[src], send_sem=deal_s.at[i],
                                            recv_sem=deal_r.at[src], device_id=p[0], device_id_type=MESH)

    def pick(q):
        return dg(jnp.where(place[...] - q * per_peer == ids, 1.0, 0.0).astype(BF), low[...], NN).astype(BF)

    def over(i, p, src):
        return pltpu.make_async_remote_copy(src_ref=ours, dst_ref=held.at[src], send_sem=shard_s.at[i],
                                            recv_sem=shard_r.at[src], device_id=p[0], device_id_type=MESH)

    def along(i, p, src):
        return pltpu.make_async_remote_copy(src_ref=held.at[shard], dst_ref=every.at[src], send_sem=group_s.at[i],
                                            recv_sem=group_r.at[src], device_id=p[0], device_id_type=MESH)

    for i, p in enumerate(others):
        outbox[p[1]] = pick(p[1])
        back(i, p, shard).start()
    at = lax.broadcasted_iota(jnp.int32, small.shape, 0)
    ours[...] = small[...] + jnp.where(at == 12, jnp.sum(dgain[...], axis=0, keepdims=True), 0.0)
    for i, p in enumerate(others):
        over(i, p, shard).start()
    inbox[shard] = pick(shard)
    v = ours[...]
    for i, p in enumerate(others):
        over(i, p, p[1]).wait_recv()
        v = v + held[p[1]]
    held[shard] = v
    every[me] = v
    for i, p in enumerate(peers):
        along(i, p, me).start()
    for i, p in enumerate(others):
        back(i, p, p[1]).wait_recv()
    lanes = lax.broadcasted_iota(jnp.int32, (STEP, m * per_peer), 1)

    def settle(i, c):
        r = pl.ds(pl.multiple_of(i * STEP, STEP), STEP)
        chosen = jnp.where(sent[r, :] == lanes, 1.0, 0.0).astype(BF)
        tokens[r, :, :] = dg(chosen, inbox[...].reshape(m * per_peer, width), NN).reshape(STEP, 1, width)
        return c

    lax.fori_loop(0, REAL_DEV // STEP, settle, 0)
    for i, p in enumerate(peers):
        along(i, p, p[1]).wait_recv()
        along(i, p, me).wait_send()
    for i, p in enumerate(others):
        over(i, p, shard).wait_send()
        back(i, p, shard).wait_send()
    for j in range(n):
        swap(j).wait_send()
    for k in range(n - 1):
        @pl.when(n - 1 - k > h)
        def _():
            rise(k).wait_send()

        @pl.when(k < h)
        def _():
            fall(k).wait_send()
    carry.wait()
    if fill:
        for c in own_grad:
            c.wait()
        for i, p in enumerate(others):
            for c in grad(i, p, p[1]):
                c.wait_recv()
            for c in grad(i, p, shard):
                c.wait_send()


def z_finish(n, part, kept, scale, base, gain, share, small, sent, place, per_peer, collective_id, name, m, lhs, rhs, stacks):
    rows, width = part.shape[0], part.shape[1] // (2 * n)
    dma = pltpu.SemaphoreType.DMA
    wide, main = lhs.shape[1] // m, 4 * width
    fill = wide % 128 == 0
    if fill:
        kinds, arrays, extra = (), (), [lhs, rhs]
        made = [jax.ShapeDtypeStruct((m, wide, main), BF), jax.ShapeDtypeStruct((m, BETA, wide), BF)]
        room = [pltpu.VMEM((m, rows, wide), BF), pltpu.VMEM(rhs.shape, BF), pltpu.VMEM(made[0].shape, BF),
                pltpu.VMEM(made[1].shape, BF), dma((m,)), dma, dma((2, m)), dma((2, m)), dma((2,))]
    else:
        kinds = ("swap", "swap")
        arrays = (dg(lhs, rhs[:, :main], TN).astype(BF).reshape(m, wide, main),
                  dg(rhs[:, main:main + BETA], lhs, TN).astype(BF).reshape(BETA, m, wide).transpose(1, 0, 2))
        extra, made, room = [], [], []
    shapes, sems = carried(kinds, m, arrays)
    return pl.pallas_call(
        functools.partial(finish_kernel, n, width, m, kinds, int(fill), len(stacks)),
        out_shape=[jax.ShapeDtypeStruct((REAL_DEV, 1, width), F32), jax.ShapeDtypeStruct((2 * n,) + small.shape, F32)]
        + [jax.ShapeDtypeStruct(a.shape[1:], F32) for a in stacks] + made + shapes,
        in_specs=[HBM] + [VM] * 8 + [HBM] * (len(stacks) + len(extra) + len(shapes)),
        out_specs=[VM] * (2 + len(stacks)) + [HBM] * (len(made) + len(shapes)),
        scratch_shapes=[pltpu.VMEM(a.shape, BF) for a in stacks] + [pltpu.VMEM((rows, width), BF), pltpu.VMEM((8, width), F32)]
        + [pltpu.VMEM((m, per_peer, width), BF)] * 2 + [dma((m,))] * 2
        + [pltpu.VMEM((m,) + small.shape, F32), pltpu.VMEM(small.shape, F32), dma((m,)), dma((m,)), dma((2 * n,)), dma((2 * n,))]
        + [pltpu.VMEM((rows, width), F32), pltpu.VMEM((2 * n, 16, 128), F32), pltpu.VMEM((rows // STEP, 8, STEP), F32),
           dma((2 * n,)), dma((2 * n,))]
        + [pltpu.VMEM((n, rows, width), BF)] * 2 + [pltpu.VMEM((n - 1, rows, width), BF)] * 2
        + [dma((n,))] * 3 + [dma((n - 1,))] * 4 + room + [dma((len(stacks),))] + sems,
        compiler_params=pltpu.CompilerParams(collective_id=collective_id, has_side_effects=True, vmem_limit_bytes=ROOM),
        cost_estimate=pl.CostEstimate(flops=0, bytes_accessed=LINK_COST, transcendentals=0),
        name=name,
    )(part, kept, scale, base, gain, share, small, sent, place, *stacks, *extra, *arrays)


CHUNKS = 4
SUBS = 4
UNITS = CHUNKS * SUBS
UNIT = CAP // UNITS


def turn_kernel(n, width, m, kinds, norm, *refs):
    if norm:
        (part, kept, scale, base, gain, share), (out, full, low, dgain), scratch, carry = carry_of(kinds, m, refs, 6, 4)
        tots, wide_t, tot_s, tot_r = scratch[-4:]
        scratch = scratch[:-4]
    else:
        (part, base), (out, full, low), scratch, carry = carry_of(kinds, m, refs, 2, 3, True)
    (mine, theirs, from_below, from_above, here, core_s, core_r, up_s, up_r, down_s, down_r,
     gu_s, gu_r, gd_s, gd_r, gc_s, gc_r, flat) = scratch
    h, t, up, down, across = places()
    me = h * 2 + t
    chunks = CHUNKS

    def rows(u):
        return pl.ds(pl.multiple_of(u * UNIT, UNIT), UNIT)

    def wide(r):
        return pl.ds(pl.multiple_of(r * SUBS * UNIT, SUBS * UNIT), SUBS * UNIT)

    def lanes(j, c):
        return pl.ds(pl.multiple_of((j * 2 + c) * width, width), width)

    def remote(src, dst, ss, rs, to):
        return pltpu.make_async_remote_copy(src_ref=src, dst_ref=dst, send_sem=ss, recv_sem=rs, device_id=to, device_id_type=MESH)

    def swap(j, r):
        return remote(part.at[wide(r), lanes(j, 1 - t)], theirs.at[j, wide(r)], core_s.at[j, r], core_r.at[j, r], across)

    def own(j, r):
        return pltpu.make_async_copy(part.at[wide(r), lanes(j, t)], mine.at[j, wide(r)], here.at[j, r])

    def rise(k, u):
        return remote(mine.at[n - 1 - k, rows(u)], from_below.at[k, rows(u)], up_s.at[k, u], up_r.at[k, u], up)

    def fall(k, u):
        return remote(mine.at[k, rows(u)], from_above.at[k, rows(u)], down_s.at[k, u], down_r.at[k, u], down)

    def spread(j, u, src, ss, rs, to):
        return remote(src, full.at[rows(u), lanes(j, t)], ss.at[j, u], rs.at[j, u], to)

    def piece(j, u):
        return full.at[rows(u), lanes(j, t)]

    def tot_copy(i, p, dst):
        return remote(share, tots.at[dst], tot_s.at[i], tot_r.at[dst], p)

    order = [j for i in range(n // 2) for j in (n - 1 - i, i)]
    for r in range(chunks):
        for j in order:
            own(j, r).start()
    if norm:
        greet_group(n, carry.greet())
        for i, p in enumerate(group_peers(n)):
            tot_copy(i, p[0], me).start()
        dgain[...] = jnp.zeros_like(dgain)
    else:
        greet(n, h, up, down, across, carry.greet())
    for r in range(chunks):
        for j in order:
            swap(j, r).start()
    carry.start()

    def arrive(j, r):
        own(j, r).wait()
        swap(j, r).wait_recv()

    def both(j, u):
        return mine[j, rows(u), :].astype(F32) + theirs[j, rows(u), :].astype(F32)

    def climb(o, r, s):
        u = SUBS * r + s

        @pl.when(h <= o)
        def _():
            ku = o - h
            tu = n - 1 - ku
            if s == 0:
                arrive(tu, r)

            @pl.when(h == 0)
            def _():
                mine[tu, rows(u), :] = both(tu, u).astype(BF)

            @pl.when(h > 0)
            def _():
                rise(ku, u).wait_recv()
                mine[tu, rows(u), :] = (both(tu, u) + from_below[ku, rows(u), :].astype(F32)).astype(BF)

            rise(ku, u).start()

        @pl.when(h >= n - 1 - o)
        def _():
            kd = o - (n - 1 - h)
            if s == 0:
                arrive(kd, r)

            @pl.when(h == n - 1)
            def _():
                mine[kd, rows(u), :] = both(kd, u).astype(BF)

            @pl.when(h < n - 1)
            def _():
                fall(kd, u).wait_recv()
                mine[kd, rows(u), :] = (both(kd, u) + from_above[kd, rows(u), :].astype(F32)).astype(BF)

            fall(kd, u).start()

    def gather_totals():
        for i, p in enumerate(group_peers(n)):
            tot_copy(i, p[0], p[1]).wait_recv()
        v = share[...]
        for i, p in enumerate(group_peers(n)):
            v = v + tots[p[1]]
        for i in range(UNITS):
            wide_t[i] = jnp.broadcast_to(v[i:i + 1, :], (8, 128))

    def last(r, s):
        u = SUBS * r + s
        if s == 0:
            arrive(h, r)
        flat[rows(u), :] = both(h, u)

        @pl.when(h > 0)
        def _():
            k = n - 1 - h
            rise(k, u).wait_recv()
            flat[rows(u), :] = flat[rows(u), :] + from_below[k, rows(u), :].astype(F32)

        @pl.when(h < n - 1)
        def _():
            fall(h, u).wait_recv()
            flat[rows(u), :] = flat[rows(u), :] + from_above[h, rows(u), :].astype(F32)

        if norm:
            close(u)
        else:
            v = base[rows(u), :].astype(F32) + flat[rows(u), :]
            out[rows(u), :] = v
            low[rows(u), :] = v.astype(BF)
            set_out(u)

    def close(u):
        hi, lo = split(wide_t[u])
        eighth = jnp.full((8, 128), 0.125, BF)
        total_r = (dg(hi, eighth, TN) + dg(lo, eighth, TN))[:UNIT]
        sc = scale[rows(u), :]
        kp = kept[rows(u), :].astype(F32)
        dn = flat[rows(u), :]
        v = (base[rows(u), :].astype(F32) + sc * (gain[...] * dn)
             - kp * jnp.tile((sc * sc * sc) * (total_r * (1.0 / D)), (1, width // 128)))
        out[rows(u), :] = v
        low[rows(u), :] = v.astype(BF)
        dgain[...] += jnp.sum((dn * kp * sc).reshape(UNIT // 8, 8, width), axis=0)
        set_out(u)

    def set_out(u):
        src = low.at[rows(u)]

        @pl.when(h < n - 1)
        def _():
            spread(h, u, src, gu_s, gu_r, up).start()

        @pl.when(h > 0)
        def _():
            spread(h, u, src, gd_s, gd_r, down).start()

        spread(h, u, src, gc_s, gc_r, across).start()

    def pass_on(k, r, s):
        u = SUBS * r + s
        below, above = h - k, h + k

        @pl.when(below >= 0)
        def _():
            spread(below, u, piece(below, u), gu_s, gu_r, up).wait_recv()

            @pl.when(h < n - 1)
            def _():
                spread(below, u, piece(below, u), gu_s, gu_r, up).start()

            spread(below, u, piece(below, u), gc_s, gc_r, across).start()

        @pl.when(above < n)
        def _():
            spread(above, u, piece(above, u), gd_s, gd_r, down).wait_recv()

            @pl.when(h > 0)
            def _():
                spread(above, u, piece(above, u), gd_s, gd_r, down).start()

            spread(above, u, piece(above, u), gc_s, gc_r, across).start()

    def at(o, r, s):
        if o < n - 1:
            climb(o, r, s)
        elif o == n - 1:
            if norm and s == 0:
                @pl.when(r == 0)
                def _():
                    gather_totals()
            last(r, s)
        elif o < 2 * n - 1:
            pass_on(o - n + 1, r, s)

    def period(r, c):
        for e in range(len(kinds)):
            @pl.when(r == e + 1)
            def _():
                carry.relay(e)

        for o in range(n):
            for s in range(SUBS):
                @pl.when(r > 0)
                def _():
                    at(o + n, r - 1, s)

                @pl.when(r < chunks)
                def _():
                    at(o, r, s)
        return c

    lax.fori_loop(0, chunks + 1, period, 0)
    mine_out = pltpu.make_async_copy(low, full.at[:, lanes(h, t)], here.at[0, 0])
    mine_out.start()

    def drain(u, c):
        for j in range(n):
            back = remote(piece(j, u), full.at[rows(u), lanes(j, 1 - t)], gc_s.at[j, u], gc_r.at[j, u], across)
            back.wait_recv()
            back.wait_send()

            @pl.when((j <= h) & (h < n - 1))
            def _():
                spread(j, u, piece(j, u), gu_s, gu_r, up).wait_send()

            @pl.when((j >= h) & (h > 0))
            def _():
                spread(j, u, piece(j, u), gd_s, gd_r, down).wait_send()

        for k in range(n - 1):
            @pl.when(n - 1 - k > h)
            def _():
                rise(k, u).wait_send()

            @pl.when(k < h)
            def _():
                fall(k, u).wait_send()

        return c

    if norm:
        for i, p in enumerate(group_peers(n)):
            tot_copy(i, p[0], me).wait_send()
    lax.fori_loop(0, UNITS, drain, 0)
    for r in range(chunks):
        for j in range(n):
            swap(j, r).wait_send()
    mine_out.wait()
    carry.wait()


def z_turn(n, part, base, collective_id, name, m=1, kinds=(), arrays=(), norm=None):
    rows, width = part.shape[0], part.shape[1] // (2 * n)
    dma = pltpu.SemaphoreType.DMA
    shapes, sems = carried(kinds, m, arrays)
    shape = jax.ShapeDtypeStruct
    ins = [part, base] if norm is None else [part, norm[0], norm[1], base, norm[2], norm[3]]
    outs = [shape((rows, width), F32), shape((rows, 2 * n * width), BF), shape((rows, width), BF)]
    out_specs = [VM, HBM, VM]
    more = []
    if norm is not None:
        outs, out_specs = outs + [shape((8, width), F32)], out_specs + [VM]
        more = [pltpu.VMEM((2 * n, 16, 128), F32), pltpu.VMEM((UNITS, 8, 128), F32), dma((2 * n,)), dma((2 * n,))]
    return pl.pallas_call(
        functools.partial(turn_kernel, n, width, m, kinds, norm is not None),
        out_shape=outs + shapes,
        in_specs=[HBM] + [VM] * (len(ins) - 1) + [HBM] * len(shapes), out_specs=out_specs + [HBM] * len(shapes),
        scratch_shapes=[pltpu.VMEM((n, rows, width), BF)] * 2 + [pltpu.VMEM((n - 1, rows, width), BF)] * 2
        + [dma((n, CHUNKS))] * 3 + [dma((n - 1, UNITS))] * 4 + [dma((n, UNITS))] * 6 + [pltpu.VMEM((rows, width), F32)]
        + more + sems,
        compiler_params=pltpu.CompilerParams(collective_id=collective_id, has_side_effects=True, vmem_limit_bytes=ROOM),
        cost_estimate=pl.CostEstimate(flops=0, bytes_accessed=LINK_COST, transcendentals=0),
        name=name,
    )(*ins, *arrays)


def rows_spec(rows, cols):
    return pl.BlockSpec((rows, cols), lambda i: (i, 0))


def fixed_spec(*shape):
    return pl.BlockSpec(shape, lambda i: (0,) * len(shape), pipeline_mode=pl.Buffered(1))


def by_rows(kernel, rows, ins, fixed, outs, lanes, flops, name):
    specs = [rows_spec(rows, a.shape[1]) for a in ins] + [fixed_spec(*a.shape) for a in fixed]
    out_specs = [rows_spec(rows, o.shape[1]) for o in outs]
    shapes = list(outs)
    if lanes:
        out_specs.append(pl.BlockSpec((lanes * rows // CAP, 8, 128), lambda i: (i, 0, 0)))
        shapes.append(jax.ShapeDtypeStruct((lanes, 8, 128), F32))
    return pl.pallas_call(
        kernel, grid=(CAP // rows,), out_shape=shapes, in_specs=specs, out_specs=out_specs,
        compiler_params=pltpu.CompilerParams(dimension_semantics=("arbitrary",), vmem_limit_bytes=ROOM),
        cost_estimate=pl.CostEstimate(flops=flops, bytes_accessed=20 * 2**20, transcendentals=0),
        name=name,
    )(*ins, *fixed)


def lane_sums(values, share):
    units, rows = share.shape[0], values.shape[0] // share.shape[0]
    hi, lo = split(values)
    ones = jnp.ones((8, values.shape[1]), BF)
    for i in range(units):
        r = slice(i * rows, (i + 1) * rows)
        share[i, :, :rows] = dg(ones, hi[r], NT) + dg(ones, lo[r], NT)
        if rows < 128:
            share[i, :, rows:] = jnp.zeros((8, 128 - rows), F32)


def normal(x, gain):
    x = x.astype(F32)
    scale = lax.rsqrt(jnp.mean(x * x, axis=1, keepdims=True) + EPSILON)
    return scale, (x * scale * gain).astype(BF)


def project_kernel(x, gain, w, wb, pre, normed, scale):
    sc, nb = normal(x[...], gain[...])
    scale[...] = sc
    normed[...] = nb
    main = w.shape[1]
    pre[:, :main] = dg(nb, w[...], NN)
    pre[:, main:main + BETA] = dg(nb, wb[...], NT)
    pre[:, main + BETA:] = jnp.zeros((nb.shape[0], PRE - main - BETA), F32)


def project(rows_full, gain, w_in, w_bt):
    sd = jax.ShapeDtypeStruct
    outs = [sd((CAP, PRE), F32), sd((CAP, D), BF), sd((CAP, 1), F32)]
    return by_rows(project_kernel, 256, [rows_full], [gain, w_in, w_bt], outs, 0, 2 * CAP * D * PRE, "project")


def ffn_kernel(x, cot, gain, w_ug, w_u, w_d, normed, product, d_gate, d_up, d_normed, scale, share):
    sc, nb = normal(x[...], gain[...])
    scale[...] = sc
    normed[...] = nb
    gate = dg(nb, w_ug[...], NT)
    up = dg(nb, w_u[...], NT)
    sig = sigmoid(gate)
    act = gate * sig
    product[...] = (act * up).astype(BF)
    d_product = dg(cot[...], w_d[...], NT)
    dgt = (d_product * up * sig * (1.0 + gate * (1.0 - sig))).astype(BF)
    dup = (d_product * act).astype(BF)
    d_gate[...] = dgt
    d_up[...] = dup
    d_normed[...] = (dg(dgt, w_ug[...], NN) + dg(dup, w_u[...], NN)).astype(BF)
    lane_sums((dgt.astype(F32) * gate + dup.astype(F32) * up) / sc, share)


def ffn(held_full, cot_full, gain, w_ug, w_u, w_d):
    sd = jax.ShapeDtypeStruct
    ff = w_u.shape[0]
    outs = [sd((CAP, D), BF)] + [sd((CAP, ff), BF)] * 3 + [sd((CAP, D), BF), sd((CAP, 1), F32)]
    return by_rows(ffn_kernel, CAP // CHUNKS, [held_full, cot_full], [gain, w_ug, w_u, w_d], outs, UNITS,
                   10 * CAP * D * ff, "feed_forward")


def unproject_kernel(d_pre, pre, scale, w, wb, d_normed, share):
    d = d_pre[...]
    main = w.shape[1]
    d_normed[...] = (dg(d[:, :main], w[...], NT) + dg(d_pre[:, main:main + BETA], wb[...], NN)).astype(BF)
    lane_sums(d.astype(F32) * pre[...] / scale[...], share)


def unproject(d_pre, pre, scale, w_in, w_bt):
    outs = [jax.ShapeDtypeStruct((CAP, D), BF)]
    return by_rows(unproject_kernel, 256, [d_pre, pre, scale], [w_in, w_bt], outs, CAP // STEP, 2 * CAP * D * PRE, "unproject")


def blocks_kernel(shard, a, x, b, y, *outs):
    tall = a.shape[1]
    first, second = dg(a[...], x[...], TN).astype(BF), dg(b[...], y[...], TN).astype(BF)
    for i, out in enumerate(outs):
        @pl.when(pl.program_id(0) == i)
        def _():
            out[:tall] = first
            out[tall:] = second


def grad_blocks(m, device, a, x, b, y):
    wide, tall = x.shape[1] // m, a.shape[1] + b.shape[1]
    if wide % 128:
        both = jnp.concatenate([dg(a, x, TN), dg(b, y, TN)], axis=0).astype(BF)
        return [lax.dynamic_slice_in_dim(both, lax.rem(device + i, m) * wide, wide, 1) for i in range(m)]

    def side(i, shard):
        return (0, lax.rem(shard[0] + i, m))

    def fixed(i, shard):
        return (0, 0)

    return pl.pallas_call(
        blocks_kernel,
        grid_spec=pltpu.PrefetchScalarGridSpec(
            num_scalar_prefetch=1, grid=(m,),
            in_specs=[pl.BlockSpec(a.shape, fixed, pipeline_mode=pl.Buffered(1)), pl.BlockSpec((CAP, wide), side),
                      pl.BlockSpec(b.shape, fixed, pipeline_mode=pl.Buffered(1)), pl.BlockSpec((CAP, wide), side)],
            out_specs=[pl.BlockSpec((tall, wide), fixed)] * m),
        out_shape=[jax.ShapeDtypeStruct((tall, wide), BF)] * m,
        compiler_params=pltpu.CompilerParams(dimension_semantics=("arbitrary",), vmem_limit_bytes=ROOM),
        cost_estimate=pl.CostEstimate(flops=2 * CAP * tall * x.shape[1], bytes_accessed=12 * 2**20, transcendentals=0),
        name="gradient_blocks",
    )(device[None], a, x, b, y)


GROUP = ("head", "tensor")


def mm(left, right, dims=NN):
    return lax.dot_general(left, right, dims, preferred_element_type=F32)


def full_rows(piece_in):
    return lax.all_gather(piece_in, GROUP, axis=1, tiled=True)


def shares(partial_sum):
    return lax.psum_scatter(partial_sum.astype(BF), GROUP, scatter_dimension=1, tiled=True).astype(F32)


def column_blocks(grad, m):
    rows, wide = grad.shape[0], grad.shape[1] // m
    if wide % 128 == 0:
        return "columns", grad
    return "swap", grad.reshape(rows, m, wide).transpose(1, 0, 2)


def side_by_side(wide):
    return "abreast" if wide % 128 == 0 else "pile"


def level(weights):
    if weights.ndim == 2:
        return weights
    return weights.transpose(1, 0, 2).reshape(weights.shape[1], -1)


def sixteen(share):
    return jnp.pad(share[:, 0, :], ((0, 16 - share.shape[0]), (0, 0)))


def gather_ring(piece):
    shards, device = lax.axis_size("shard"), lax.axis_index("shard")
    wide = piece.shape[1]
    whole = jnp.zeros((piece.shape[0], shards * wide), piece.dtype)
    for i in range(shards):
        came = lax.ppermute(piece, "shard", [(o, (o + i) % shards) for o in range(shards)]) if i else piece
        whole = lax.dynamic_update_slice_in_dim(whole, came, lax.rem(device - i + shards, shards) * wide, 1)
    return whole


def swap_ring(a, x, b, y):
    shards, device = lax.axis_size("shard"), lax.axis_index("shard")
    blocks = grad_blocks(shards, device, a, x, b, y)
    total = blocks[0].astype(F32)
    for i in range(1, shards):
        total = total + lax.ppermute(blocks[i], "shard", [(o, (o + i) % shards) for o in range(shards)]).astype(F32)
    return total[:a.shape[1]], total[a.shape[1]:]


def sum_blocks(blocks):
    return jnp.sum(blocks.astype(F32), axis=0)


def body(tokens, seq_lengths, dealing, gain_mixer, w_query, w_key, w_value, w_gate, w_beta, conv_weight,
         gain_heads, w_out, gain_ffn, w_up_gate, w_up, w_down, cotangent):
    shards = lax.axis_size("shard")
    width = tokens.shape[2]
    col_start = lax.axis_index(GROUP) * width
    per_peer = (CAP // shards + SEQ_DEV + 15) // 16 * 16

    w_piece = jnp.concatenate([w_query, w_key, w_value, w_gate], axis=1)
    b_piece = jnp.pad(w_beta.T, ((0, BETA - w_beta.shape[1]), (0, 0)))

    own_rows = tokens.reshape(REAL_DEV, width)
    taps = conv_weight.reshape(3 * CONV, width)
    head_gain = gain_heads[None, :]

    n = lax.axis_size("head")
    side = side_by_side(w_up.shape[0])
    x_rows, rows_full, sent_slot, recv_slot, pos, filled_f, w_in, w_bt = z_gather(
        n, seq_lengths, dealing, own_rows, per_peer, 1, "gather_rows", shards,
        ("gather", side_by_side(b_piece.shape[1])), (w_piece, b_piece))
    w_bt = level(w_bt)
    rows_full, cot_piece, w_out = lax.optimization_barrier((rows_full, cotangent, w_out))
    w_o = gather_ring(w_out)
    cot_full = full_rows(cot_piece)
    pre, normed, scale_one = project(rows_full, gain_mixer[None, :], w_in, w_bt)
    mixed, *saved = mixer_fwd(pre, pos, filled_f, taps, head_gain)
    branch_part, cot_full = lax.optimization_barrier((mm(mixed, w_o).astype(BF), cot_full))
    hidden, held_full, held_low, w_ug, w_u, w_d = z_turn(
        n, branch_part, x_rows, 2, "turn_branch", shards, (side,) * 3, (w_up_gate.T, w_up.T, w_down))
    w_ug, w_u, w_d = level(w_ug), level(w_u), level(w_d)
    normed_two, product, d_gate, d_up, d_normed_two, scale_two, share_two = ffn(
        held_full, cot_full, gain_ffn[None, :], w_ug, w_u, w_d)
    down_kind, d_w_down = column_blocks(mm(product, cot_full, TN).astype(BF), shards)
    gate_kind, d_w_ug = column_blocks(mm(d_gate, normed_two, TN).astype(BF), shards)
    ffn_gain_part = lax.dynamic_slice_in_dim(gain_ffn, col_start, width)[None, :]
    d_hidden, d_branch_full, _, ffn_gain_grad, d_w_ug, d_w_down = z_turn(
        n, d_normed_two, cotangent, 4, "turn_normed_two", shards, (gate_kind, down_kind), (d_w_ug, d_w_down),
        norm=(held_low, scale_two, ffn_gain_part, sixteen(share_two)))
    out_part = mm(product, w_d).astype(BF)
    out_part, d_branch_full = lax.optimization_barrier((out_part, d_branch_full))
    d_w_u, d_w_out = swap_ring(d_up, normed_two, mixed, d_branch_full)
    out_sum = shares(out_part)
    d_mixed = mm(d_branch_full, w_o, NT)
    d_pre, d_taps, d_head_gain = mixer_bwd(d_mixed, pre, pos, filled_f, taps, head_gain, saved)
    d_normed, share_one = unproject(d_pre, pre, scale_one, w_in, w_bt)
    d_normed, out_sum = lax.optimization_barrier((d_normed, out_sum))
    block_out = (hidden + out_sum).astype(BF)
    mixer_gain_part = lax.dynamic_slice_in_dim(gain_mixer, col_start, width)[None, :]
    small = jnp.concatenate([
        jnp.sum(d_taps, axis=1), jnp.zeros((1, width), F32), jnp.sum(ffn_gain_grad, axis=0)[None, :],
        jnp.pad(jnp.sum(d_head_gain, axis=0), (0, width - HD))[None, :],
        jnp.zeros((1, width), F32)], axis=0)
    d_tokens, summed, d_w_ug, d_w_down, d_w_in, d_w_bt = z_finish(
        n, d_normed, x_rows, scale_one, d_hidden, mixer_gain_part, sixteen(share_one), small,
        sent_slot, recv_slot, per_peer, 6, "finish_rows", shards, normed, d_pre, (d_w_ug, d_w_down))
    d_w_in = sum_blocks(d_w_in)
    by_row = summed.transpose(1, 0, 2).reshape(16, D)
    d_conv = by_row[:12].reshape(CONV, 3, D)
    d_gain_heads = jnp.sum(summed[:, 14, :HD], axis=0)
    cut = [0, width, 2 * width, 3 * width, 4 * width]
    return (
        block_out, d_tokens, by_row[12],
        d_w_in[:, cut[0]:cut[1]], d_w_in[:, cut[1]:cut[2]], d_w_in[:, cut[2]:cut[3]], d_w_in[:, cut[3]:cut[4]],
        sum_blocks(d_w_bt)[:w_beta.shape[1]].T,
        d_conv, d_gain_heads, d_w_out, by_row[13],
        d_w_ug.T, d_w_u.T, d_w_down,
    )


def solution(mesh):
    feat = ("head", "tensor")
    placed = (
        P(None, "shard", feat), P(), P(), P(),
        P("shard", feat), P("shard", feat), P("shard", feat), P("shard", feat), P("shard", feat),
        P(None, None, feat), P(), P(feat, "shard"), P(),
        P("shard", feat), P("shard", feat), P(feat, "shard"), P("shard", feat),
    )
    given = (
        P("shard", feat), P(None, "shard", feat), P(),
        P("shard", feat), P("shard", feat), P("shard", feat), P("shard", feat), P("shard", feat),
        P(), P(), P(feat, "shard"), P(),
        P("shard", feat), P("shard", feat), P(feat, "shard"),
    )
    return jax.shard_map(body, mesh=mesh, in_specs=placed, out_specs=given, check_vma=False)
```

```python
import functools
import jax
import jax.numpy as jnp
from jax import lax
from jax.experimental import pallas as pl
from jax.experimental.pallas import tpu as pltpu

from jax.sharding import PartitionSpec as P

D = 2048
HD = 128
CONV = 4
BLOCK = 64
SEQ_DEV = 4
REAL_DEV = 1152
CAP = 1280
NB = CAP // BLOCK
EPSILON = 1e-06
HEAD_FLOOR = 0.01
PRE = 1152
BETA = 16
F32 = jnp.float32
BF = jnp.bfloat16

def split(x):
    hi = x.astype(BF)
    return hi, (x - hi.astype(F32)).astype(BF)

NN=(((1,),(0,)),((),())); NT=(((1,),(1,)),((),())); TN=(((0,),(0,)),((),()))

def dg(a, b, dims):
    return lax.dot_general(a, b, dims, preferred_element_type=F32)

def d3(a, b, dims=NN):
    ah, al = split(a); bh, bl = split(b)
    return dg(ah, bh, dims) + (dg(ah, bl, dims) + dg(al, bh, dims))

def four_times(step):
    return lambda i, c: step(4 * i + 3, step(4 * i + 2, step(4 * i + 1, step(4 * i, c))))

def goes_on(pos_ref, n):
    first = pos_ref[pl.ds(pl.multiple_of(n * BLOCK, BLOCK), 8), :][:1]
    return jnp.where(first != 0, 1.0, 0.0)

def masks():
    ri = lax.broadcasted_iota(jnp.int32, (BLOCK, BLOCK), 0)
    ci = lax.broadcasted_iota(jnp.int32, (BLOCK, BLOCK), 1)
    return ri, ci

def sigmoid(x):
    return 1.0 / (1.0 + jnp.exp(-x))

def conv_rows(cur, tail, wt, pos):
    ext = jnp.concatenate([tail, cur], axis=0)
    out = wt[0] * cur
    for j in range(1, CONV):
        sh = pltpu.roll(ext, j, axis=0)[8:]
        out = out + wt[j] * jnp.where(pos >= j, sh, 0.0)
    return out

def inverses(lmats, ri, ci):
    apart = ri ^ ci
    xs = [jnp.where(apart == 0, 1.0, 0.0) - jnp.where(apart == 1, m, 0.0) for m in lmats]
    s = 2
    while s < BLOCK:
        at = (apart >= s) & (apart < 2 * s)
        ys = [d3(x, jnp.where(at, m, 0.0)) for x, m in zip(xs, lmats)]
        xs = [x - d3(y, x) for x, y in zip(xs, ys)]
        s *= 2
    return xs

def fwd_kernel(pre, pos_ref, fill_ref, cw, gain, mixed, *refs):
    given, (c_out, qk, w_out, u_out, u2_out, o_out, p_out, t_out, m_out, s_out, b_s), sem = refs[:10], refs[10:21], refs[21]
    held = (c_out, qk, w_out, u_out, u2_out, o_out, p_out, t_out, m_out, s_out)

    def keep(*which):
        for i in which:
            pltpu.make_async_copy(held[i], given[i], sem.at[i]).start()

    ri, ci = masks()
    heads = 2
    def phase_a(n, tails):
        r = pl.ds(pl.multiple_of(n * BLOCK, BLOCK), BLOCK)
        pos = pos_ref[r, :]; fil = fill_ref[r, :]
        new_tails = []
        acts = []
        for i in range(3):
            cur = pre[r, i*256:(i+1)*256]
            wt = [cw[j*3+i:j*3+i+1, :] for j in range(CONV)]
            cc = conv_rows(cur, tails[i], wt, pos)
            c_out[r, i*256:(i+1)*256] = cc
            acts.append(cc * sigmoid(cc) * fil)
            new_tails.append(cur[BLOCK-8:])
        beta = sigmoid(pre[r, 1024:1152])
        for h in range(heads):
            hs = slice(h*HD, (h+1)*HD)
            yq = acts[0][:, hs]; yk = acts[1][:, hs]; v = acts[2][:, hs]
            q = yq * lax.rsqrt(jnp.sum(yq*yq, axis=1, keepdims=True) + EPSILON)
            k = yk * lax.rsqrt(jnp.sum(yk*yk, axis=1, keepdims=True) + EPSILON)
            b = beta[:, h:h+1]
            qk[r, h*HD:(h+1)*HD] = q
            qk[r, 256+h*HD:256+(h+1)*HD] = k
            lmat = jnp.where(ri > ci, b * d3(k, k, NT), 0.0)
            p_out[n*2+h] = jnp.where(ri >= ci, d3(q, k, NT), 0.0)
            t_out[n*2+h] = lmat
            u_out[r, hs] = b*v
            w_out[r, hs] = b*k
        return tuple(new_tails)
    z8 = jnp.zeros((8, 256), F32)
    lax.fori_loop(0, NB // 4, four_times(phase_a), (z8, z8, z8))
    keep(0, 1, 6)
    GRP = 20
    def phase_t(i, _):
        ts = inverses([t_out[i*GRP+j] for j in range(GRP)], ri, ci)
        for j in range(GRP):
            t_out[i*GRP+j] = ts[j]
        return 0
    lax.fori_loop(0, 2*NB//GRP, phase_t, 0)
    keep(7)
    def phase_w(i, _):
        todo = [(n, pl.ds(pl.multiple_of(n * BLOCK, BLOCK), BLOCK), h, slice(h*HD, (h+1)*HD)) for n in (4*i, 4*i+1, 4*i+2, 4*i+3) for h in range(heads)]
        wu = [d3(t_out[n*2+h], jnp.concatenate([w_out[r, c], u_out[r, c]], axis=1)) for n, r, h, c in todo]
        mb = [d3(qk[r, 256+h*HD:256+(h+1)*HD], x, TN) for x, (n, r, h, c) in zip(wu, todo)]
        for x, y, (n, r, h, c) in zip(wu, mb, todo):
            w_out[r, c] = x[:, :HD]; u_out[r, c] = x[:, HD:]
            m_out[n*2+h] = y[:, :HD]; b_s[n*2+h] = y[:, HD:]
        return 0
    lax.fori_loop(0, NB//4, phase_w, 0)
    keep(2, 3, 8)
    def phase_b(n, ss):
        out = []
        for h in range(heads):
            e = n*2+h
            s = ss[h] * goes_on(pos_ref, n)
            s_out[e] = s
            out.append(s - d3(m_out[e], s) + b_s[e])
        return tuple(out)
    zs = jnp.zeros((HD, HD), F32)
    lax.fori_loop(0, NB // 4, four_times(phase_b), (zs, zs))
    keep(9)
    def phase_c(i, _):
        todo = [(n, pl.ds(pl.multiple_of(n * BLOCK, BLOCK), BLOCK), h, slice(h*HD, (h+1)*HD)) for n in (4*i, 4*i+1, 4*i+2, 4*i+3) for h in range(heads)]
        rr = [d3(jnp.concatenate([w_out[r, c], qk[r, c]], axis=0), s_out[n*2+h]) for n, r, h, c in todo]
        u2 = [u_out[r, c] - v[:BLOCK] for v, (n, r, h, c) in zip(rr, todo)]
        os_ = [v[BLOCK:] + d3(p_out[n*2+h], u) for v, u, (n, r, h, c) in zip(rr, u2, todo)]
        for o, u, (n, r, h, c) in zip(os_, u2, todo):
            u2_out[r, c] = u
            o_out[r, c] = o
            ms = jnp.mean(o*o, axis=1, keepdims=True)
            sc = lax.rsqrt(jnp.maximum(ms, HEAD_FLOOR))
            gg = pre[r, 768+h*HD:768+(h+1)*HD]
            mixed[r, c] = (o * sc * gain[...] * (gg * sigmoid(gg))).astype(BF)
        return 0
    lax.fori_loop(0, NB // 4, phase_c, 0)
    keep(4, 5)
    for i in range(10):
        pltpu.make_async_copy(held[i], given[i], sem.at[i]).wait()

def sds(*s, dt=F32): return jax.ShapeDtypeStruct(s, dt)
VM = pl.BlockSpec(memory_space=pltpu.VMEM)
SM = pl.BlockSpec(memory_space=pltpu.SMEM)

def mixer_fwd(pre, pos, fil, cw, gain):
    outs = (sds(CAP,256,dt=BF), sds(CAP,768), sds(CAP,512), sds(CAP,256), sds(CAP,256), sds(CAP,256), sds(CAP,256),
            sds(2*NB,BLOCK,BLOCK), sds(2*NB,BLOCK,BLOCK), sds(2*NB,HD,HD), sds(2*NB,HD,HD))
    return pl.pallas_call(fwd_kernel, out_shape=outs, in_specs=[VM]*5, out_specs=[VM]+[pl.BlockSpec(memory_space=pltpu.HBM)]*(len(outs)-1),
        scratch_shapes=[pltpu.VMEM(o.shape,F32) for o in outs[1:]]+[pltpu.VMEM((2*NB,HD,HD),F32), pltpu.SemaphoreType.DMA((10,))],
        compiler_params=pltpu.CompilerParams(vmem_limit_bytes=60*2**20), cost_estimate=pl.CostEstimate(flops=0, bytes_accessed=140 * 2**20, transcendentals=0),
        name="mixer_forward")(pre, pos, fil, cw, gain)

def bwd_kernel(dmix, pre, pos_ref, fill_ref, cw, gain, *refs):
    kept, (dpre, dcw, dgain), held, (e_s, do_s, sem) = refs[:10], refs[10:13], refs[13:23], refs[23:]
    c_in, qk, w_in, u_in, u2_in, o_in, p_in, t_in, m_in, s_in = held

    def fetch(i):
        return pltpu.make_async_copy(kept[i], held[i], sem.at[i])

    for i in (5, 6, 1, 2, 8, 7, 9, 0, 3, 4):
        fetch(i).start()
    for i in (5, 6, 1, 2):
        fetch(i).wait()
    ri, ci = masks()
    heads = 2
    lane = lax.broadcasted_iota(jnp.int32, (BLOCK, HD), 1)
    dgain[...] = jnp.zeros_like(dgain)
    dcw[...] = jnp.zeros_like(dcw)
    def phase_a(n, _):
        r = pl.ds(pl.multiple_of(n * BLOCK, BLOCK), BLOCK)
        for h in range(heads):
            hs = slice(h*HD, (h+1)*HD)
            e = n*2+h
            o = o_in[r, hs]; dm = dmix[r, hs]
            gg = pre[r, 768+h*HD:768+(h+1)*HD]
            sg = sigmoid(gg); si = gg*sg
            ms = jnp.mean(o*o, axis=1, keepdims=True)
            sc = lax.rsqrt(jnp.maximum(ms, HEAD_FLOOR))
            on = o*sc
            gn = gain[...]
            dpre[r, 768+h*HD:768+(h+1)*HD] = (dm * on * gn * (sg * (1.0 + gg*(1.0-sg)))).astype(BF)
            dgs = dm * on * si
            dgain[...] += jnp.sum(dgs.reshape(8, 8, HD), axis=0)
            dn = dm * gn * si
            corr = jnp.where(ms > HEAD_FLOOR, jnp.mean(dn*on, axis=1, keepdims=True), 0.0)
            do = sc * (dn - on*corr)
            do_s[r, hs] = do
            pdo = d3(p_in[e], do, TN)
            qw = jnp.concatenate([qk[r, hs], w_in[r, hs]], axis=0)
            dd = jnp.concatenate([do, -pdo], axis=0)
            e_s[e] = d3(qw, dd, TN)
        return 0
    lax.fori_loop(0, NB // 4, four_times(phase_a), 0)
    fetch(8).wait()

    def phase_b(i, ds):
        n = NB-1-i
        out = []
        for h in range(heads):
            e = n*2+h
            d = ds[h]
            ee = e_s[e]
            e_s[e] = d
            out.append((d - d3(m_in[e], d, TN) + ee) * goes_on(pos_ref, n))
        return tuple(out)
    zs = jnp.zeros((HD, HD), F32)
    lax.fori_loop(0, NB // 4, four_times(phase_b), (zs, zs))
    for i in (7, 9, 0, 3, 4):
        fetch(i).wait()

    def phase_c(i, heads_dc):
        blocks = tuple(NB - 1 - j - 4 * i for j in range(4))
        todo = [(n, pl.ds(pl.multiple_of(n * BLOCK, BLOCK), BLOCK), h, slice(h*HD, (h+1)*HD)) for n in blocks for h in range(heads)]
        def every(f, *lists):
            return [f(*v) for v in zip(*lists)]
        ns, rs, hh, hs = zip(*todo)
        es = [n*2+h for n, h in zip(ns, hh)]
        fil = [fill_ref[r, :] for r in rs]
        beta_t = [sigmoid(pre[r, 1024:1152]) for r in rs]
        q = [qk[r, c] for r, c in zip(rs, hs)]
        k = [qk[r, 256+h*HD:256+(h+1)*HD] for r, h in zip(rs, hh)]
        w = [w_in[r, c] for r, c in zip(rs, hs)]
        u = [u_in[r, c] for r, c in zip(rs, hs)]
        u2 = [u2_in[r, c] for r, c in zip(rs, hs)]
        do = [do_s[r, c] for r, c in zip(rs, hs)]
        p = [p_in[e] for e in es]
        t = [t_in[e] for e in es]
        s = [s_in[e] for e in es]
        ds = [e_s[e] for e in es]
        b = [x[:, h:h+1] for x, h in zip(beta_t, hh)]
        du2 = every(lambda p, do, k, ds: d3(p, do, TN) + d3(k, ds), p, do, k, ds)
        dp = every(lambda do, u2: jnp.where(ri >= ci, d3(do, u2, NT), 0.0), do, u2)
        g = every(lambda k: d3(k, k, NT), k)
        xs = every(lambda do, du2, s: d3(jnp.concatenate([do, -du2], axis=0), s, NT), do, du2, s)
        dq = every(lambda xs, dp, k: xs[:BLOCK] + d3(dp, k), xs, dp, k)
        xx = every(lambda t, xs, du2: d3(t, jnp.concatenate([xs[BLOCK:], du2], axis=1), TN), t, xs, du2)
        dk = every(lambda dp, q, u2, ds: d3(dp, q, TN) + d3(u2, ds, NT), dp, q, u2, ds)
        mm = every(lambda xx, w, u: jnp.where(ri > ci, -d3(xx, jnp.concatenate([w, u], axis=1), NT), 0.0), xx, w, u)
        cv = [c_in[r, 512+h*HD:512+(h+1)*HD] for r, h in zip(rs, hh)]
        sv = every(sigmoid, cv)
        bm = every(lambda b, mm: b*mm, b, mm)
        dk = every(lambda dk, bm, k, b, xx: dk + d3(bm + bm.T, k) + b*xx[:, :HD], dk, bm, k, b, xx)
        db = every(lambda mm, g, xx, k, cv, sv, fil: jnp.sum(mm*g, axis=1, keepdims=True)
                   + jnp.sum(xx[:, :HD]*k + xx[:, HD:]*(cv*sv*fil), axis=1, keepdims=True), mm, g, xx, k, cv, sv, fil)
        cq = [c_in[r, c] for r, c in zip(rs, hs)]
        ck = [c_in[r, 256+h*HD:256+(h+1)*HD] for r, h in zip(rs, hh)]
        def unit_back(c, fil, n, d):
            sg = sigmoid(c)
            y = c*sg*fil
            r = lax.rsqrt(jnp.sum(y*y, axis=1, keepdims=True) + EPSILON)
            return r*(d - n*jnp.sum(d*n, axis=1, keepdims=True))*fil*(sg*(1.0+c*(1.0-sg)))
        aq = every(unit_back, cq, fil, q, dq)
        ak = every(unit_back, ck, fil, k, dk)
        av = every(lambda b, xx, fil, sv, cv: b*xx[:, HD:]*fil*(sv*(1.0+cv*(1.0-sv))), b, xx, fil, sv, cv)
        for j, n in enumerate(blocks):
            r = rs[2*j]
            dbt = jnp.where(lane == 0, db[2*j], jnp.where(lane == 1, db[2*j+1], 0.0))
            dpre[r, 1024:1152] = (dbt*beta_t[2*j]*(1.0-beta_t[2*j])).astype(BF)
            pos = pos_ref[r, :]
            nxt = jnp.minimum(n+1, NB-1)
            posx = jnp.concatenate([pos, pos_ref[pl.ds(pl.multiple_of(nxt*BLOCK, BLOCK), 8), :]], axis=0)
            prv = jnp.maximum(n*BLOCK-8, 0)
            new = []
            for i, acts in enumerate((aq, ak, av)):
                dc = jnp.concatenate(acts[2*j:2*j+2], axis=1)
                ext = jnp.concatenate([dc, heads_dc[i]], axis=0)
                cur = pre[r, i*256:(i+1)*256]
                tail = pre[pl.ds(pl.multiple_of(prv, 8), 8), i*256:(i+1)*256]
                xext = jnp.concatenate([tail, cur], axis=0)
                dx = cw[i:i+1, :]*dc
                dcw[i] += jnp.sum((dc*cur).reshape(8, 8, 256), axis=0)
                for o in range(1, CONV):
                    z = jnp.where(posx >= o, ext, 0.0)
                    dx = dx + cw[o*3+i:o*3+i+1, :]*pltpu.roll(z, BLOCK+8-o, axis=0)[:BLOCK]
                    sh = pltpu.roll(xext, o, axis=0)[8:]
                    dcw[o*3+i] += jnp.sum(jnp.where(pos >= o, dc*sh, 0.0).reshape(8, 8, 256), axis=0)
                dpre[r, i*256:(i+1)*256] = dx.astype(BF)
                new.append(dc[:8])
            heads_dc = tuple(new)
        return heads_dc
    z8 = jnp.zeros((8, 256), F32)
    lax.fori_loop(0, NB // 4, phase_c, (z8, z8, z8))

def mixer_bwd(dmix, pre, pos, fil, cw, gain, saved):
    outs = (sds(CAP,1152,dt=BF), sds(12,8,256), sds(8,HD))
    return pl.pallas_call(bwd_kernel, out_shape=outs, in_specs=[VM]*6+[pl.BlockSpec(memory_space=pltpu.HBM)]*len(saved), out_specs=[VM]*3,
        scratch_shapes=[pltpu.VMEM(a.shape, F32) for a in saved]+[pltpu.VMEM((2*NB,HD,HD),F32), pltpu.VMEM((CAP,256),F32), pltpu.SemaphoreType.DMA((10,))],
        compiler_params=pltpu.CompilerParams(vmem_limit_bytes=60*2**20), cost_estimate=pl.CostEstimate(flops=0, bytes_accessed=200 * 2**20, transcendentals=0),
        name="mixer_backward")(dmix, pre, pos, fil, cw, gain, *saved)


MESH = pl.DeviceIdType.MESH
ROOM = 60 * 2**20
LINK_COST = 150 * 2**20
HBM = pl.BlockSpec(memory_space=pltpu.HBM)


def places():
    s, h, t = lax.axis_index("shard"), lax.axis_index("head"), lax.axis_index("tensor")
    return h, t, (s, h + 1, t), (s, h - 1, t), (s, h, 1 - t)


def shard_peers(m):
    s, h, t = lax.axis_index("shard"), lax.axis_index("head"), lax.axis_index("tensor")
    return [((lax.rem(s + i, m), h, t), lax.rem(s + i, m)) for i in range(1, m)]


def greet_shard(m):
    barrier = pltpu.get_barrier_semaphore()
    for p, _ in shard_peers(m):
        pl.semaphore_signal(barrier, inc=1, device_id=p, device_id_type=MESH)
    return m - 1


class Carry:
    def __init__(self, hops, kinds, m, ins, outs, send, recv, here):
        self.hops, self.kinds, self.m, self.ins, self.outs = hops, kinds, m, ins, outs
        self.send, self.recv, self.here = send, recv, here
        s, self.h, self.t = lax.axis_index("shard"), lax.axis_index("head"), lax.axis_index("tensor")
        self.me = s
        self.side = s + 1 - 2 * lax.rem(s, 2)
        self.over = lax.rem(s + 2, 4)
        self.corner = lax.rem(self.side + 2, 4)

    def relayed(self, e):
        return self.hops and self.m == 4 and self.kinds[e] in ("gather", "abreast")

    def part(self, e, src, half=None):
        rows = self.ins[e].shape[0]
        span = pl.ds(0, rows) if half is None else pl.ds(half * (rows // 2), rows // 2)
        if self.kinds[e] == "gather":
            first = src * rows + (0 if half is None else half * (rows // 2))
            return self.outs[e].at[pl.ds(pl.multiple_of(first, rows // 2), span.size)]
        if self.kinds[e] == "abreast":
            w = self.ins[e].shape[1]
            return self.outs[e].at[span, pl.ds(pl.multiple_of(src * w, w), w)]
        return self.outs[e].at[src]

    def given(self, e, dst):
        if self.kinds[e] == "columns":
            w = self.ins[e].shape[1] // self.m
            return self.ins[e].at[:, pl.ds(pl.multiple_of(dst * w, w), w)]
        return self.ins[e].at[dst] if self.kinds[e] == "swap" else self.ins[e]

    def move(self, e, src, dst, i, j, to):
        return pltpu.make_async_remote_copy(src_ref=src, dst_ref=dst, send_sem=self.send.at[e, i], recv_sem=self.recv.at[e, j],
                                            device_id=(to, self.h, self.t), device_id_type=MESH)

    def copy(self, e, i, to):
        return self.move(e, self.given(e, to), self.part(e, self.me), i, self.me, to)

    def came(self, e, src):
        return self.move(e, self.given(e, src), self.part(e, src), 0, src, src)

    def hand(self, e, half):
        src, to = (self.side, self.over) if half == 0 else (self.over, self.side)
        piece = self.part(e, src, half)
        return self.move(e, piece, piece, 2 + half, src if half == 0 else self.m, to)

    def handed(self, e, half):
        piece = self.part(e, self.corner, half)
        return self.move(e, piece, piece, 2 + half, self.corner if half == 0 else self.m, self.over if half == 0 else self.side)

    def local(self, e):
        return pltpu.make_async_copy(self.given(e, self.me), self.part(e, self.me), self.here.at[e])

    def targets(self, e):
        return [self.side, self.over] if self.relayed(e) else [p[1] for p in shard_peers(self.m)]

    def greet(self):
        return greet_shard(self.m) if self.kinds else 0

    def start(self):
        for e in range(len(self.kinds)):
            for i, to in enumerate(self.targets(e)):
                self.copy(e, i, to).start()
            self.local(e).start()

    def relay(self, e):
        if e < len(self.kinds) and self.relayed(e):
            self.came(e, self.side).wait_recv()
            self.hand(e, 0).start()
            self.came(e, self.over).wait_recv()
            self.hand(e, 1).start()

    def wait(self):
        for e in range(len(self.kinds)):
            self.local(e).wait()
            for i, to in enumerate(self.targets(e)):
                self.copy(e, i, to).wait_send()
                if not self.relayed(e):
                    self.came(e, to).wait_recv()
            if self.relayed(e):
                for half in range(2):
                    self.handed(e, half).wait_recv()
                    self.hand(e, half).wait_send()


def carried(kinds, m, arrays):
    dma = pltpu.SemaphoreType.DMA
    give = {"gather": lambda a: (m * a.shape[0], a.shape[1]), "swap": lambda a: a.shape,
            "abreast": lambda a: (a.shape[0], m * a.shape[1]), "pile": lambda a: (m,) + a.shape,
            "columns": lambda a: (m, a.shape[0], a.shape[1] // m)}
    shapes = [jax.ShapeDtypeStruct(give[k](a), a.dtype) for k, a in zip(kinds, arrays)]
    e = len(kinds)
    return shapes, ([dma((e, m + 1)), dma((e, m + 1)), dma((e,))] if e else [])


def carry_of(kinds, m, refs, n_in, n_out, hops=False):
    e = len(kinds)
    ins, refs = refs[:n_in], refs[n_in:]
    c_in, refs = refs[:e], refs[e:]
    outs, refs = refs[:n_out], refs[n_out:]
    c_out, refs = refs[:e], refs[e:]
    sems = (refs[-3:] if e else (None,) * 3)
    scratch = refs[:-3] if e else refs
    return ins, outs, scratch, Carry(hops, kinds, m, c_in, c_out, *sems)


def greet(n, h, up, down, across, more=0):
    barrier = pltpu.get_barrier_semaphore()
    pl.semaphore_signal(barrier, inc=1, device_id=across, device_id_type=MESH)

    @pl.when(h < n - 1)
    def _():
        pl.semaphore_signal(barrier, inc=1, device_id=up, device_id_type=MESH)

    @pl.when(h > 0)
    def _():
        pl.semaphore_signal(barrier, inc=1, device_id=down, device_id_type=MESH)

    pl.semaphore_wait(barrier, 1 + more + (h < n - 1).astype(jnp.int32) + (h > 0).astype(jnp.int32))


class Plan:
    def __init__(self, m, per_peer, lengths, dealing, starts):
        self.m, self.per_peer, self.lengths, self.dealing, self.starts = m, per_peer, lengths, dealing, starts
        self.shift = m.bit_length() - 1
        self.device = lax.axis_index("shard")

        def begin(q, total):
            starts[q] = total
            return total + lengths[q]

        lax.fori_loop(0, lengths.shape[0], begin, jnp.int32(0))

    def under(self, row, residue):
        return lax.shift_right_arithmetic(row - 1 - residue + self.m, self.shift + jnp.zeros_like(row))

    def members(self, g):
        at = [self.dealing[g * SEQ_DEV + i] for i in range(SEQ_DEV)]
        return [(self.starts[q], self.lengths[q]) for q in at]

    def sent(self, ids):
        packed = ids * self.m + self.device

        def group(g, slot):
            seqs = self.members(g)
            counts = [self.under(s + n, self.device) - self.under(s, self.device) for s, n in seqs]
            for s, n in seqs:
                first = g * self.per_peer - self.under(s, self.device)
                for (other, _), count in zip(seqs, counts):
                    first = first + jnp.where(other < s, count, 0)
                slot = slot + jnp.where((packed >= s) & (packed < s + n), first, 0)
            return slot

        return lax.fori_loop(0, self.lengths.shape[0] // SEQ_DEV, group, ids)

    def rows(self, ids):
        seqs = self.members(self.device)
        place, start, length, below = ids, jnp.zeros_like(ids), jnp.zeros_like(ids), jnp.int32(0)
        for s, n in seqs:
            here = ids >= below
            place = jnp.where(here, ids - below, place)
            start = jnp.where(here, s, start)
            length = jnp.where(here, n, length)
            below = below + lax.shift_right_arithmetic(n + BLOCK - 1, jnp.int32(6)) * BLOCK
        filled = place < length
        natural = start + place
        source = natural & (self.m - 1)
        slot = source * self.per_peer + self.under(natural, source) - self.under(start, source)
        for s, n in seqs:
            span = self.under(jnp.zeros_like(ids) + (s + n), source) - self.under(jnp.zeros_like(ids) + s, source)
            slot = slot + jnp.where(s < start, span, 0)
        return place, filled, jnp.where(filled, slot, -1)


def gather_kernel(n, width, m, kinds, *refs):
    (lengths, dealing, tokens), (x, out, sent_at, slot_at, pos_at, fill_at), scratch, carry = carry_of(kinds, m, refs, 3, 6)
    place_at, starts, outbox, inbox, deal_s, deal_r, here, up_s, up_r, down_s, down_r, core_s, core_r = scratch
    h, t, up, down, across = places()
    per_peer = outbox.shape[1]

    def cols(j):
        return out.at[:, pl.ds(pl.multiple_of((j * 2 + t) * width, width), width)]

    def other(j):
        return out.at[:, pl.ds(pl.multiple_of((j * 2 + 1 - t) * width, width), width)]

    def send(j, src, ss, rs, to):
        return pltpu.make_async_remote_copy(src_ref=src, dst_ref=cols(j), send_sem=ss.at[j], recv_sem=rs.at[j],
                                            device_id=to, device_id_type=MESH)

    greet(n, h, up, down, across, carry.greet())
    plan = Plan(m, per_peer, lengths, dealing, starts)
    peers = shard_peers(m)
    mine = lax.axis_index("shard")
    sent = plan.sent(lax.broadcasted_iota(jnp.int32, (1, REAL_DEV), 1))
    ids = lax.broadcasted_iota(jnp.int32, (per_peer, REAL_DEV), 0)

    def deal(i, p, src):
        return pltpu.make_async_remote_copy(src_ref=outbox.at[p[1]], dst_ref=inbox.at[src], send_sem=deal_s.at[i],
                                            recv_sem=deal_r.at[src], device_id=p[0], device_id_type=MESH)

    def pick(q):
        return dg(jnp.where(sent - q * per_peer == ids, 1.0, 0.0).astype(BF), tokens[...], NN).astype(BF)

    for i, p in enumerate(peers):
        outbox[p[1]] = pick(p[1])
        deal(i, p, mine).start()
    carry.start()
    inbox[mine] = pick(mine)
    place_at[...] = plan.rows(lax.broadcasted_iota(jnp.int32, (CAP, 1), 0))[2]
    for i, p in enumerate(peers):
        deal(i, p, p[1]).wait_recv()
    lanes = lax.broadcasted_iota(jnp.int32, (STEP, m * per_peer), 1)

    def settle(i, c):
        r = pl.ds(pl.multiple_of(i * STEP, STEP), STEP)
        chosen = jnp.where(place_at[r, :] == lanes, 1.0, 0.0).astype(BF)
        x[r, :] = dg(chosen, inbox[...].reshape(m * per_peer, width), NN).astype(BF)
        return c

    lax.fori_loop(0, CAP // STEP, settle, 0)
    local = pltpu.make_async_copy(x, cols(h), here)
    local.start()

    @pl.when(h < n - 1)
    def _():
        send(h, x, up_s, up_r, up).start()

    @pl.when(h > 0)
    def _():
        send(h, x, down_s, down_r, down).start()

    send(h, x, core_s, core_r, across).start()
    sent_at[...] = plan.sent(lax.broadcasted_iota(jnp.int32, (REAL_DEV, 1), 0))
    slot_at[...] = plan.rows(lax.broadcasted_iota(jnp.int32, (1, CAP), 1))[2]
    position, filled, _ = plan.rows(lax.broadcasted_iota(jnp.int32, (CAP, 1), 0))
    pos_at[...] = position
    fill_at[...] = jnp.where(filled, 1.0, 0.0)
    for k in range(1, n):
        below, above = h - k, h + k

        @pl.when(below >= 0)
        def _():
            send(below, cols(below), up_s, up_r, up).wait_recv()

            @pl.when(h < n - 1)
            def _():
                send(below, cols(below), up_s, up_r, up).start()

            send(below, cols(below), core_s, core_r, across).start()

        @pl.when(above < n)
        def _():
            send(above, cols(above), down_s, down_r, down).wait_recv()

            @pl.when(h > 0)
            def _():
                send(above, cols(above), down_s, down_r, down).start()

            send(above, cols(above), core_s, core_r, across).start()

    for j in range(n):
        back = pltpu.make_async_remote_copy(src_ref=cols(j), dst_ref=other(j), send_sem=core_s.at[j], recv_sem=core_r.at[j],
                                            device_id=across, device_id_type=MESH)
        back.wait_recv()
        back.wait_send()

        @pl.when((j <= h) & (h < n - 1))
        def _():
            send(j, cols(j), up_s, up_r, up).wait_send()

        @pl.when((j >= h) & (h > 0))
        def _():
            send(j, cols(j), down_s, down_r, down).wait_send()

    local.wait()
    for i, p in enumerate(peers):
        deal(i, p, mine).wait_send()
    carry.wait()


def z_gather(n, lengths, dealing, tokens, per_peer, collective_id, name, m, kinds, arrays):
    width = tokens.shape[1]
    dma = pltpu.SemaphoreType.DMA
    sd = jax.ShapeDtypeStruct
    shapes, sems = carried(kinds, m, arrays)
    return pl.pallas_call(
        functools.partial(gather_kernel, n, width, m, kinds),
        out_shape=[sd((CAP, width), BF), sd((CAP, 2 * n * width), BF), sd((REAL_DEV, 1), jnp.int32), sd((1, CAP), jnp.int32),
                   sd((CAP, 1), jnp.int32), sd((CAP, 1), F32)] + shapes,
        in_specs=[SM, SM, VM] + [HBM] * len(shapes), out_specs=[VM, HBM] + [VM] * 4 + [HBM] * len(shapes),
        scratch_shapes=[pltpu.VMEM((CAP, 1), jnp.int32), pltpu.SMEM(lengths.shape, jnp.int32)]
        + [pltpu.VMEM((m, per_peer, width), BF)] * 2 + [dma((m,)), dma((m,)), dma] + [dma((n,))] * 6 + sems,
        compiler_params=pltpu.CompilerParams(collective_id=collective_id, has_side_effects=True, vmem_limit_bytes=ROOM),
        cost_estimate=pl.CostEstimate(flops=0, bytes_accessed=LINK_COST, transcendentals=0),
        name=name,
    )(lengths, dealing, tokens, *arrays)


STEP = 128


def group_peers(n):
    s, h, t = lax.axis_index("shard"), lax.axis_index("head"), lax.axis_index("tensor")
    peers = []
    for i in range(1, 2 * n):
        hh, tt = lax.rem(h + i // 2, n), lax.rem(t + i % 2, 2)
        peers.append(((s, hh, tt), hh * 2 + tt))
    return peers


def greet_group(n, more=0):
    barrier = pltpu.get_barrier_semaphore()
    for p, _ in group_peers(n):
        pl.semaphore_signal(barrier, inc=1, device_id=p, device_id_type=MESH)
    pl.semaphore_wait(barrier, 2 * n - 1 + more)


def finish_kernel(n, width, m, kinds, fill, piles, *refs):
    (part, kept, scale, base, gain, share, small, sent, place, *left), (tokens, every, *grads), scratch, carry = carry_of(
        kinds, m, refs, 9 + piles + 2 * fill, 2 + piles + 2 * fill)
    stacks, left = left[:piles], left[piles:]
    added, grads = grads[:piles], grads[piles:]
    *scratch, pile_sem = scratch
    heaps, scratch = scratch[:piles], scratch[piles:]
    if fill:
        *scratch, l_buf, r_buf, blocks, strips, l_sem, r_sem, w_s, w_r, w_own = scratch
    (low, dgain, outbox, inbox, deal_s, deal_r, held, ours, shard_s, shard_r, group_s, group_r,
     acc, tots, wide_t, tot_s, tot_r, mine, theirs, from_below, from_above,
     here, core_s, core_r, up_s, up_r, down_s, down_r) = scratch
    h, t, up, down, across = places()

    def cols(j, c):
        return part.at[:, pl.ds(pl.multiple_of((j * 2 + c) * width, width), width)]

    def swap(j):
        return pltpu.make_async_remote_copy(src_ref=cols(j, 1 - t), dst_ref=theirs.at[j], send_sem=core_s.at[j],
                                            recv_sem=core_r.at[j], device_id=across, device_id_type=MESH)

    def own(j):
        return pltpu.make_async_copy(cols(j, t), mine.at[j], here.at[j])

    def rise(k):
        return pltpu.make_async_remote_copy(src_ref=mine.at[n - 1 - k], dst_ref=from_below.at[k], send_sem=up_s.at[k],
                                            recv_sem=up_r.at[k], device_id=up, device_id_type=MESH)

    def fall(k):
        return pltpu.make_async_remote_copy(src_ref=mine.at[k], dst_ref=from_above.at[k], send_sem=down_s.at[k],
                                            recv_sem=down_r.at[k], device_id=down, device_id_type=MESH)

    def total(j, extra):
        def step(i, c):
            r = pl.ds(pl.multiple_of(i * STEP, STEP), STEP)
            v = mine[j, r, :].astype(F32) + theirs[j, r, :].astype(F32)
            if extra is not None:
                v = v + extra(r).astype(F32)
            mine[j, r, :] = v.astype(BF)
            return c
        lax.fori_loop(0, CAP // STEP, step, 0)

    order = [j for i in range(n // 2) for j in (n - 1 - i, i)]
    for j in order:
        own(j).start()

    def load(i):
        return pltpu.make_async_copy(stacks[i], heaps[i], pile_sem.at[i])

    def add_up(i):
        load(i).wait()
        tall = heaps[i].shape[1] // 4

        def step(q, c):
            r = pl.ds(pl.multiple_of(q * tall, tall), tall)
            v = heaps[i][0, r, :].astype(F32)
            for b in range(1, m):
                v = v + heaps[i][b, r, :].astype(F32)
            added[i][r, :] = v
            return c

        lax.fori_loop(0, 4, step, 0)

    for i in range(piles):
        load(i).start()
    greet_group(n, greet_shard(m))
    me = h * 2 + t
    peers = group_peers(n)

    def tot_copy(i, p, dst):
        return pltpu.make_async_remote_copy(src_ref=share, dst_ref=tots.at[dst], send_sem=tot_s.at[i], recv_sem=tot_r.at[dst],
                                            device_id=p, device_id_type=MESH)

    for i, p in enumerate(peers):
        tot_copy(i, p[0], me).start()
    for j in order:
        swap(j).start()
    carry.start()
    shard = lax.axis_index("shard")
    others = shard_peers(m)
    if fill:
        lhs, rhs = left
        wide = lhs.shape[1] // m

        def columns(q):
            return lhs.at[:, pl.ds(pl.multiple_of(q * wide, wide), wide)]

        def fetch(i, q):
            return pltpu.make_async_copy(columns(q), l_buf.at[i], l_sem.at[i])

        made = (blocks, strips)

        def grad(i, p, src):
            return [pltpu.make_async_remote_copy(src_ref=made[e].at[i], dst_ref=grads[e].at[src], send_sem=w_s.at[e, i],
                                                 recv_sem=w_r.at[e, src], device_id=p[0], device_id_type=MESH) for e in range(2)]

        own_grad = [pltpu.make_async_copy(made[e].at[m - 1], grads[e].at[shard], w_own.at[e]) for e in range(2)]
        whole = pltpu.make_async_copy(rhs, r_buf, r_sem)
        whole.start()
        for i, p in enumerate(others):
            fetch(i, p[1]).start()
        fetch(m - 1, shard).start()

        def multiply(i):
            if i == 0:
                whole.wait()
            fetch(i, shard).wait()
            main = blocks.shape[2]
            strips[i] = dg(r_buf[:, main:main + BETA], l_buf[i], TN).astype(BF)
            blocks[i] = dg(l_buf[i], r_buf[:, :main], TN).astype(BF)
            for c in (grad(i, others[i], shard) if i < m - 1 else own_grad):
                c.start()

        multiply(0)

    def arrive(j):
        own(j).wait()
        swap(j).wait_recv()

    for tick in range(2 * n - 2):
        ku = tick - h
        tu = n - 1 - ku

        @pl.when((ku >= 0) & (tu > h))
        def _():
            arrive(tu)

            @pl.when(h == 0)
            def _():
                total(tu, None)

            @pl.when(h > 0)
            def _():
                rise(ku).wait_recv()
                total(tu, lambda r: from_below[ku, r, :])

            rise(ku).start()

        kd = tick - (n - 1 - h)

        @pl.when((kd >= 0) & (kd < h))
        def _():
            arrive(kd)

            @pl.when(h == n - 1)
            def _():
                total(kd, None)

            @pl.when(h < n - 1)
            def _():
                fall(kd).wait_recv()
                total(kd, lambda r: from_above[kd, r, :])

            fall(kd).start()

        if fill and tick + 1 < m:
            multiply(tick + 1)

        if tick >= 2 * n - 2 - piles:
            add_up(tick - (2 * n - 2 - piles))

    if fill:
        for i in range(2 * n - 1, m):
            multiply(i)
    arrive(h)
    for i, p in enumerate(peers):
        tot_copy(i, p[0], p[1]).wait_recv()
    v = share[...]
    for i, p in enumerate(peers):
        v = v + tots[p[1]]
    for i in range(CAP // STEP):
        wide_t[i] = jnp.broadcast_to(v[i:i + 1, :], (8, 128))
    dgain[...] = jnp.zeros_like(dgain)
    gains = gain[...]
    eighth = jnp.full((8, 128), 0.125, BF)

    def final(get):
        def step(i, c):
            r = pl.ds(pl.multiple_of(i * STEP, STEP), STEP)
            acc[r, :] = get(r)
            return c
        lax.fori_loop(0, CAP // STEP, step, 0)

    final(lambda r: mine[h, r, :].astype(F32) + theirs[h, r, :].astype(F32))

    def first(get):
        final(lambda r: acc[r, :] + get(r).astype(F32))

    @pl.when((h > 0) & (h < n - 1))
    def _():
        @pl.when(2 * h < n)
        def _():
            fall(h).wait_recv()
            first(lambda r: from_above[h, r, :])

        @pl.when(2 * h >= n)
        def _():
            rise(n - 1 - h).wait_recv()
            first(lambda r: from_below[n - 1 - h, r, :])

    by_below = (h > 0) & ((2 * h < n) | (h == n - 1))

    @pl.when(by_below)
    def _():
        rise(n - 1 - h).wait_recv()

    @pl.when(jnp.logical_not(by_below))
    def _():
        fall(h).wait_recv()

    def close(get):
        def step(i, c):
            r = pl.ds(pl.multiple_of(i * STEP, STEP), STEP)
            hi, lo = split(wide_t[i])
            total_r = dg(hi, eighth, TN) + dg(lo, eighth, TN)
            sc = scale[r, :]
            kp = kept[r, :].astype(F32)
            dn = acc[r, :] + get(r).astype(F32)
            back = base[r, :].astype(F32) + sc * (gains * dn) - kp * jnp.tile((sc * sc * sc) * (total_r * (1.0 / D)), (1, width // 128))
            low[r, :] = back.astype(BF)
            dgain[...] += jnp.sum((dn * kp * sc).reshape(STEP // 8, 8, width), axis=0)
            return c
        lax.fori_loop(0, CAP // STEP, step, 0)

    @pl.when(by_below)
    def _():
        close(lambda r: from_below[n - 1 - h, r, :])

    @pl.when(jnp.logical_not(by_below))
    def _():
        close(lambda r: from_above[h, r, :])

    for i, p in enumerate(peers):
        tot_copy(i, p[0], me).wait_send()

    per_peer = outbox.shape[1]
    ids = lax.broadcasted_iota(jnp.int32, (per_peer, place.shape[1]), 0)

    def back(i, p, src):
        return pltpu.make_async_remote_copy(src_ref=outbox.at[p[1]], dst_ref=inbox.at[src], send_sem=deal_s.at[i],
                                            recv_sem=deal_r.at[src], device_id=p[0], device_id_type=MESH)

    def pick(q):
        return dg(jnp.where(place[...] - q * per_peer == ids, 1.0, 0.0).astype(BF), low[...], NN).astype(BF)

    def over(i, p, src):
        return pltpu.make_async_remote_copy(src_ref=ours, dst_ref=held.at[src], send_sem=shard_s.at[i],
                                            recv_sem=shard_r.at[src], device_id=p[0], device_id_type=MESH)

    def along(i, p, src):
        return pltpu.make_async_remote_copy(src_ref=held.at[shard], dst_ref=every.at[src], send_sem=group_s.at[i],
                                            recv_sem=group_r.at[src], device_id=p[0], device_id_type=MESH)

    for i, p in enumerate(others):
        outbox[p[1]] = pick(p[1])
        back(i, p, shard).start()
    at = lax.broadcasted_iota(jnp.int32, small.shape, 0)
    ours[...] = small[...] + jnp.where(at == 12, jnp.sum(dgain[...], axis=0, keepdims=True), 0.0)
    for i, p in enumerate(others):
        over(i, p, shard).start()
    inbox[shard] = pick(shard)
    v = ours[...]
    for i, p in enumerate(others):
        over(i, p, p[1]).wait_recv()
        v = v + held[p[1]]
    held[shard] = v
    every[me] = v
    for i, p in enumerate(peers):
        along(i, p, me).start()
    for i, p in enumerate(others):
        back(i, p, p[1]).wait_recv()
    lanes = lax.broadcasted_iota(jnp.int32, (STEP, m * per_peer), 1)

    def settle(i, c):
        r = pl.ds(pl.multiple_of(i * STEP, STEP), STEP)
        chosen = jnp.where(sent[r, :] == lanes, 1.0, 0.0).astype(BF)
        tokens[r, :, :] = dg(chosen, inbox[...].reshape(m * per_peer, width), NN).reshape(STEP, 1, width)
        return c

    lax.fori_loop(0, REAL_DEV // STEP, settle, 0)
    for i, p in enumerate(peers):
        along(i, p, p[1]).wait_recv()
        along(i, p, me).wait_send()
    for i, p in enumerate(others):
        over(i, p, shard).wait_send()
        back(i, p, shard).wait_send()
    for j in range(n):
        swap(j).wait_send()
    for k in range(n - 1):
        @pl.when(n - 1 - k > h)
        def _():
            rise(k).wait_send()

        @pl.when(k < h)
        def _():
            fall(k).wait_send()
    carry.wait()
    if fill:
        for c in own_grad:
            c.wait()
        for i, p in enumerate(others):
            for c in grad(i, p, p[1]):
                c.wait_recv()
            for c in grad(i, p, shard):
                c.wait_send()


def z_finish(n, part, kept, scale, base, gain, share, small, sent, place, per_peer, collective_id, name, m, lhs, rhs, stacks):
    rows, width = part.shape[0], part.shape[1] // (2 * n)
    dma = pltpu.SemaphoreType.DMA
    wide, main = lhs.shape[1] // m, 4 * width
    fill = wide % 128 == 0
    if fill:
        kinds, arrays, extra = (), (), [lhs, rhs]
        made = [jax.ShapeDtypeStruct((m, wide, main), BF), jax.ShapeDtypeStruct((m, BETA, wide), BF)]
        room = [pltpu.VMEM((m, rows, wide), BF), pltpu.VMEM(rhs.shape, BF), pltpu.VMEM(made[0].shape, BF),
                pltpu.VMEM(made[1].shape, BF), dma((m,)), dma, dma((2, m)), dma((2, m)), dma((2,))]
    else:
        kinds = ("swap", "swap")
        arrays = (dg(lhs, rhs[:, :main], TN).astype(BF).reshape(m, wide, main),
                  dg(rhs[:, main:main + BETA], lhs, TN).astype(BF).reshape(BETA, m, wide).transpose(1, 0, 2))
        extra, made, room = [], [], []
    shapes, sems = carried(kinds, m, arrays)
    return pl.pallas_call(
        functools.partial(finish_kernel, n, width, m, kinds, int(fill), len(stacks)),
        out_shape=[jax.ShapeDtypeStruct((REAL_DEV, 1, width), F32), jax.ShapeDtypeStruct((2 * n,) + small.shape, F32)]
        + [jax.ShapeDtypeStruct(a.shape[1:], F32) for a in stacks] + made + shapes,
        in_specs=[HBM] + [VM] * 8 + [HBM] * (len(stacks) + len(extra) + len(shapes)),
        out_specs=[VM] * (2 + len(stacks)) + [HBM] * (len(made) + len(shapes)),
        scratch_shapes=[pltpu.VMEM(a.shape, BF) for a in stacks] + [pltpu.VMEM((rows, width), BF), pltpu.VMEM((8, width), F32)]
        + [pltpu.VMEM((m, per_peer, width), BF)] * 2 + [dma((m,))] * 2
        + [pltpu.VMEM((m,) + small.shape, F32), pltpu.VMEM(small.shape, F32), dma((m,)), dma((m,)), dma((2 * n,)), dma((2 * n,))]
        + [pltpu.VMEM((rows, width), F32), pltpu.VMEM((2 * n, 16, 128), F32), pltpu.VMEM((rows // STEP, 8, STEP), F32),
           dma((2 * n,)), dma((2 * n,))]
        + [pltpu.VMEM((n, rows, width), BF)] * 2 + [pltpu.VMEM((n - 1, rows, width), BF)] * 2
        + [dma((n,))] * 3 + [dma((n - 1,))] * 4 + room + [dma((len(stacks),))] + sems,
        compiler_params=pltpu.CompilerParams(collective_id=collective_id, has_side_effects=True, vmem_limit_bytes=ROOM),
        cost_estimate=pl.CostEstimate(flops=0, bytes_accessed=LINK_COST, transcendentals=0),
        name=name,
    )(part, kept, scale, base, gain, share, small, sent, place, *stacks, *extra, *arrays)


CHUNKS = 4
SUBS = 4
UNITS = CHUNKS * SUBS
UNIT = CAP // UNITS


def turn_kernel(n, width, m, kinds, norm, *refs):
    if norm:
        (part, kept, scale, base, gain, share), (out, full, low, dgain), scratch, carry = carry_of(kinds, m, refs, 6, 4)
        tots, wide_t, tot_s, tot_r = scratch[-4:]
        scratch = scratch[:-4]
    else:
        (part, base), (out, full, low), scratch, carry = carry_of(kinds, m, refs, 2, 3, True)
    (mine, theirs, from_below, from_above, here, core_s, core_r, up_s, up_r, down_s, down_r,
     gu_s, gu_r, gd_s, gd_r, gc_s, gc_r, flat) = scratch
    h, t, up, down, across = places()
    me = h * 2 + t
    chunks = CHUNKS

    def rows(u):
        return pl.ds(pl.multiple_of(u * UNIT, UNIT), UNIT)

    def wide(r):
        return pl.ds(pl.multiple_of(r * SUBS * UNIT, SUBS * UNIT), SUBS * UNIT)

    def lanes(j, c):
        return pl.ds(pl.multiple_of((j * 2 + c) * width, width), width)

    def remote(src, dst, ss, rs, to):
        return pltpu.make_async_remote_copy(src_ref=src, dst_ref=dst, send_sem=ss, recv_sem=rs, device_id=to, device_id_type=MESH)

    def swap(j, r):
        return remote(part.at[wide(r), lanes(j, 1 - t)], theirs.at[j, wide(r)], core_s.at[j, r], core_r.at[j, r], across)

    def own(j, r):
        return pltpu.make_async_copy(part.at[wide(r), lanes(j, t)], mine.at[j, wide(r)], here.at[j, r])

    def rise(k, u):
        return remote(mine.at[n - 1 - k, rows(u)], from_below.at[k, rows(u)], up_s.at[k, u], up_r.at[k, u], up)

    def fall(k, u):
        return remote(mine.at[k, rows(u)], from_above.at[k, rows(u)], down_s.at[k, u], down_r.at[k, u], down)

    def spread(j, u, src, ss, rs, to):
        return remote(src, full.at[rows(u), lanes(j, t)], ss.at[j, u], rs.at[j, u], to)

    def piece(j, u):
        return full.at[rows(u), lanes(j, t)]

    def tot_copy(i, p, dst):
        return remote(share, tots.at[dst], tot_s.at[i], tot_r.at[dst], p)

    order = [j for i in range(n // 2) for j in (n - 1 - i, i)]
    for r in range(chunks):
        for j in order:
            own(j, r).start()
    if norm:
        greet_group(n, carry.greet())
        for i, p in enumerate(group_peers(n)):
            tot_copy(i, p[0], me).start()
        dgain[...] = jnp.zeros_like(dgain)
    else:
        greet(n, h, up, down, across, carry.greet())
    for r in range(chunks):
        for j in order:
            swap(j, r).start()
    carry.start()

    def arrive(j, r):
        own(j, r).wait()
        swap(j, r).wait_recv()

    def both(j, u):
        return mine[j, rows(u), :].astype(F32) + theirs[j, rows(u), :].astype(F32)

    def climb(o, r, s):
        u = SUBS * r + s

        @pl.when(h <= o)
        def _():
            ku = o - h
            tu = n - 1 - ku
            if s == 0:
                arrive(tu, r)

            @pl.when(h == 0)
            def _():
                mine[tu, rows(u), :] = both(tu, u).astype(BF)

            @pl.when(h > 0)
            def _():
                rise(ku, u).wait_recv()
                mine[tu, rows(u), :] = (both(tu, u) + from_below[ku, rows(u), :].astype(F32)).astype(BF)

            rise(ku, u).start()

        @pl.when(h >= n - 1 - o)
        def _():
            kd = o - (n - 1 - h)
            if s == 0:
                arrive(kd, r)

            @pl.when(h == n - 1)
            def _():
                mine[kd, rows(u), :] = both(kd, u).astype(BF)

            @pl.when(h < n - 1)
            def _():
                fall(kd, u).wait_recv()
                mine[kd, rows(u), :] = (both(kd, u) + from_above[kd, rows(u), :].astype(F32)).astype(BF)

            fall(kd, u).start()

    def gather_totals():
        for i, p in enumerate(group_peers(n)):
            tot_copy(i, p[0], p[1]).wait_recv()
        v = share[...]
        for i, p in enumerate(group_peers(n)):
            v = v + tots[p[1]]
        for i in range(UNITS):
            wide_t[i] = jnp.broadcast_to(v[i:i + 1, :], (8, 128))

    def last(r, s):
        u = SUBS * r + s
        if s == 0:
            arrive(h, r)
        flat[rows(u), :] = both(h, u)

        @pl.when(h > 0)
        def _():
            k = n - 1 - h
            rise(k, u).wait_recv()
            flat[rows(u), :] = flat[rows(u), :] + from_below[k, rows(u), :].astype(F32)

        @pl.when(h < n - 1)
        def _():
            fall(h, u).wait_recv()
            flat[rows(u), :] = flat[rows(u), :] + from_above[h, rows(u), :].astype(F32)

        if norm:
            close(u)
        else:
            v = base[rows(u), :].astype(F32) + flat[rows(u), :]
            out[rows(u), :] = v
            low[rows(u), :] = v.astype(BF)
            set_out(u)

    def close(u):
        hi, lo = split(wide_t[u])
        eighth = jnp.full((8, 128), 0.125, BF)
        total_r = (dg(hi, eighth, TN) + dg(lo, eighth, TN))[:UNIT]
        sc = scale[rows(u), :]
        kp = kept[rows(u), :].astype(F32)
        dn = flat[rows(u), :]
        v = (base[rows(u), :].astype(F32) + sc * (gain[...] * dn)
             - kp * jnp.tile((sc * sc * sc) * (total_r * (1.0 / D)), (1, width // 128)))
        out[rows(u), :] = v
        low[rows(u), :] = v.astype(BF)
        dgain[...] += jnp.sum((dn * kp * sc).reshape(UNIT // 8, 8, width), axis=0)
        set_out(u)

    def set_out(u):
        src = low.at[rows(u)]

        @pl.when(h < n - 1)
        def _():
            spread(h, u, src, gu_s, gu_r, up).start()

        @pl.when(h > 0)
        def _():
            spread(h, u, src, gd_s, gd_r, down).start()

        spread(h, u, src, gc_s, gc_r, across).start()

    def pass_on(k, r, s):
        u = SUBS * r + s
        below, above = h - k, h + k

        @pl.when(below >= 0)
        def _():
            spread(below, u, piece(below, u), gu_s, gu_r, up).wait_recv()

            @pl.when(h < n - 1)
            def _():
                spread(below, u, piece(below, u), gu_s, gu_r, up).start()

            spread(below, u, piece(below, u), gc_s, gc_r, across).start()

        @pl.when(above < n)
        def _():
            spread(above, u, piece(above, u), gd_s, gd_r, down).wait_recv()

            @pl.when(h > 0)
            def _():
                spread(above, u, piece(above, u), gd_s, gd_r, down).start()

            spread(above, u, piece(above, u), gc_s, gc_r, across).start()

    def at(o, r, s):
        if o < n - 1:
            climb(o, r, s)
        elif o == n - 1:
            if norm and s == 0:
                @pl.when(r == 0)
                def _():
                    gather_totals()
            last(r, s)
        elif o < 2 * n - 1:
            pass_on(o - n + 1, r, s)

    def period(r, c):
        for e in range(len(kinds)):
            @pl.when(r == e + 1)
            def _():
                carry.relay(e)

        for o in range(n):
            for s in range(SUBS):
                @pl.when(r > 0)
                def _():
                    at(o + n, r - 1, s)

                @pl.when(r < chunks)
                def _():
                    at(o, r, s)
        return c

    lax.fori_loop(0, chunks + 1, period, 0)
    mine_out = pltpu.make_async_copy(low, full.at[:, lanes(h, t)], here.at[0, 0])
    mine_out.start()

    def drain(u, c):
        for j in range(n):
            back = remote(piece(j, u), full.at[rows(u), lanes(j, 1 - t)], gc_s.at[j, u], gc_r.at[j, u], across)
            back.wait_recv()
            back.wait_send()

            @pl.when((j <= h) & (h < n - 1))
            def _():
                spread(j, u, piece(j, u), gu_s, gu_r, up).wait_send()

            @pl.when((j >= h) & (h > 0))
            def _():
                spread(j, u, piece(j, u), gd_s, gd_r, down).wait_send()

        for k in range(n - 1):
            @pl.when(n - 1 - k > h)
            def _():
                rise(k, u).wait_send()

            @pl.when(k < h)
            def _():
                fall(k, u).wait_send()

        return c

    if norm:
        for i, p in enumerate(group_peers(n)):
            tot_copy(i, p[0], me).wait_send()
    lax.fori_loop(0, UNITS, drain, 0)
    for r in range(chunks):
        for j in range(n):
            swap(j, r).wait_send()
    mine_out.wait()
    carry.wait()


def z_turn(n, part, base, collective_id, name, m=1, kinds=(), arrays=(), norm=None):
    rows, width = part.shape[0], part.shape[1] // (2 * n)
    dma = pltpu.SemaphoreType.DMA
    shapes, sems = carried(kinds, m, arrays)
    shape = jax.ShapeDtypeStruct
    ins = [part, base] if norm is None else [part, norm[0], norm[1], base, norm[2], norm[3]]
    outs = [shape((rows, width), F32), shape((rows, 2 * n * width), BF), shape((rows, width), BF)]
    out_specs = [VM, HBM, VM]
    more = []
    if norm is not None:
        outs, out_specs = outs + [shape((8, width), F32)], out_specs + [VM]
        more = [pltpu.VMEM((2 * n, 16, 128), F32), pltpu.VMEM((UNITS, 8, 128), F32), dma((2 * n,)), dma((2 * n,))]
    return pl.pallas_call(
        functools.partial(turn_kernel, n, width, m, kinds, norm is not None),
        out_shape=outs + shapes,
        in_specs=[HBM] + [VM] * (len(ins) - 1) + [HBM] * len(shapes), out_specs=out_specs + [HBM] * len(shapes),
        scratch_shapes=[pltpu.VMEM((n, rows, width), BF)] * 2 + [pltpu.VMEM((n - 1, rows, width), BF)] * 2
        + [dma((n, CHUNKS))] * 3 + [dma((n - 1, UNITS))] * 4 + [dma((n, UNITS))] * 6 + [pltpu.VMEM((rows, width), F32)]
        + more + sems,
        compiler_params=pltpu.CompilerParams(collective_id=collective_id, has_side_effects=True, vmem_limit_bytes=ROOM),
        cost_estimate=pl.CostEstimate(flops=0, bytes_accessed=LINK_COST, transcendentals=0),
        name=name,
    )(*ins, *arrays)


def rows_spec(rows, cols):
    return pl.BlockSpec((rows, cols), lambda i: (i, 0))


def fixed_spec(*shape):
    return pl.BlockSpec(shape, lambda i: (0,) * len(shape), pipeline_mode=pl.Buffered(1))


def by_rows(kernel, rows, ins, fixed, outs, lanes, flops, name):
    specs = [rows_spec(rows, a.shape[1]) for a in ins] + [fixed_spec(*a.shape) for a in fixed]
    out_specs = [rows_spec(rows, o.shape[1]) for o in outs]
    shapes = list(outs)
    if lanes:
        out_specs.append(pl.BlockSpec((lanes * rows // CAP, 8, 128), lambda i: (i, 0, 0)))
        shapes.append(jax.ShapeDtypeStruct((lanes, 8, 128), F32))
    return pl.pallas_call(
        kernel, grid=(CAP // rows,), out_shape=shapes, in_specs=specs, out_specs=out_specs,
        compiler_params=pltpu.CompilerParams(dimension_semantics=("arbitrary",), vmem_limit_bytes=ROOM),
        cost_estimate=pl.CostEstimate(flops=flops, bytes_accessed=20 * 2**20, transcendentals=0),
        name=name,
    )(*ins, *fixed)


def lane_sums(values, share):
    units, rows = share.shape[0], values.shape[0] // share.shape[0]
    hi, lo = split(values)
    ones = jnp.ones((8, values.shape[1]), BF)
    for i in range(units):
        r = slice(i * rows, (i + 1) * rows)
        share[i, :, :rows] = dg(ones, hi[r], NT) + dg(ones, lo[r], NT)
        if rows < 128:
            share[i, :, rows:] = jnp.zeros((8, 128 - rows), F32)


def normal(x, gain):
    x = x.astype(F32)
    scale = lax.rsqrt(jnp.mean(x * x, axis=1, keepdims=True) + EPSILON)
    return scale, (x * scale * gain).astype(BF)


def project_kernel(x, gain, w, wb, pre, normed, scale):
    sc, nb = normal(x[...], gain[...])
    scale[...] = sc
    normed[...] = nb
    main = w.shape[1]
    pre[:, :main] = dg(nb, w[...], NN)
    pre[:, main:main + BETA] = dg(nb, wb[...], NT)
    pre[:, main + BETA:] = jnp.zeros((nb.shape[0], PRE - main - BETA), F32)


def project(rows_full, gain, w_in, w_bt):
    sd = jax.ShapeDtypeStruct
    outs = [sd((CAP, PRE), F32), sd((CAP, D), BF), sd((CAP, 1), F32)]
    return by_rows(project_kernel, 256, [rows_full], [gain, w_in, w_bt], outs, 0, 2 * CAP * D * PRE, "project")


def ffn_kernel(x, cot, gain, w_ug, w_u, w_d, normed, product, d_gate, d_up, d_normed, scale, share):
    sc, nb = normal(x[...], gain[...])
    scale[...] = sc
    normed[...] = nb
    gate = dg(nb, w_ug[...], NT)
    up = dg(nb, w_u[...], NT)
    sig = sigmoid(gate)
    act = gate * sig
    product[...] = (act * up).astype(BF)
    d_product = dg(cot[...], w_d[...], NT)
    dgt = (d_product * up * sig * (1.0 + gate * (1.0 - sig))).astype(BF)
    dup = (d_product * act).astype(BF)
    d_gate[...] = dgt
    d_up[...] = dup
    d_normed[...] = (dg(dgt, w_ug[...], NN) + dg(dup, w_u[...], NN)).astype(BF)
    lane_sums((dgt.astype(F32) * gate + dup.astype(F32) * up) / sc, share)


def ffn(held_full, cot_full, gain, w_ug, w_u, w_d):
    sd = jax.ShapeDtypeStruct
    ff = w_u.shape[0]
    outs = [sd((CAP, D), BF)] + [sd((CAP, ff), BF)] * 3 + [sd((CAP, D), BF), sd((CAP, 1), F32)]
    return by_rows(ffn_kernel, CAP // CHUNKS, [held_full, cot_full], [gain, w_ug, w_u, w_d], outs, UNITS,
                   10 * CAP * D * ff, "feed_forward")


def unproject_kernel(d_pre, pre, scale, w, wb, d_normed, share):
    d = d_pre[...]
    main = w.shape[1]
    d_normed[...] = (dg(d[:, :main], w[...], NT) + dg(d_pre[:, main:main + BETA], wb[...], NN)).astype(BF)
    lane_sums(d.astype(F32) * pre[...] / scale[...], share)


def unproject(d_pre, pre, scale, w_in, w_bt):
    outs = [jax.ShapeDtypeStruct((CAP, D), BF)]
    return by_rows(unproject_kernel, 256, [d_pre, pre, scale], [w_in, w_bt], outs, CAP // STEP, 2 * CAP * D * PRE, "unproject")


def blocks_kernel(shard, a, x, b, y, *outs):
    tall = a.shape[1]
    first, second = dg(a[...], x[...], TN).astype(BF), dg(b[...], y[...], TN).astype(BF)
    for i, out in enumerate(outs):
        @pl.when(pl.program_id(0) == i)
        def _():
            out[:tall] = first
            out[tall:] = second


def grad_blocks(m, device, a, x, b, y):
    wide, tall = x.shape[1] // m, a.shape[1] + b.shape[1]
    if wide % 128:
        both = jnp.concatenate([dg(a, x, TN), dg(b, y, TN)], axis=0).astype(BF)
        return [lax.dynamic_slice_in_dim(both, lax.rem(device + i, m) * wide, wide, 1) for i in range(m)]

    def side(i, shard):
        return (0, lax.rem(shard[0] + i, m))

    def fixed(i, shard):
        return (0, 0)

    return pl.pallas_call(
        blocks_kernel,
        grid_spec=pltpu.PrefetchScalarGridSpec(
            num_scalar_prefetch=1, grid=(m,),
            in_specs=[pl.BlockSpec(a.shape, fixed, pipeline_mode=pl.Buffered(1)), pl.BlockSpec((CAP, wide), side),
                      pl.BlockSpec(b.shape, fixed, pipeline_mode=pl.Buffered(1)), pl.BlockSpec((CAP, wide), side)],
            out_specs=[pl.BlockSpec((tall, wide), fixed)] * m),
        out_shape=[jax.ShapeDtypeStruct((tall, wide), BF)] * m,
        compiler_params=pltpu.CompilerParams(dimension_semantics=("arbitrary",), vmem_limit_bytes=ROOM),
        cost_estimate=pl.CostEstimate(flops=2 * CAP * tall * x.shape[1], bytes_accessed=12 * 2**20, transcendentals=0),
        name="gradient_blocks",
    )(device[None], a, x, b, y)


GROUP = ("head", "tensor")


def mm(left, right, dims=NN):
    return lax.dot_general(left, right, dims, preferred_element_type=F32)


def full_rows(piece_in):
    return lax.all_gather(piece_in, GROUP, axis=1, tiled=True)


def shares(partial_sum):
    return lax.psum_scatter(partial_sum.astype(BF), GROUP, scatter_dimension=1, tiled=True).astype(F32)


def column_blocks(grad, m):
    rows, wide = grad.shape[0], grad.shape[1] // m
    if wide % 128 == 0:
        return "columns", grad
    return "swap", grad.reshape(rows, m, wide).transpose(1, 0, 2)


def side_by_side(wide):
    return "abreast" if wide % 128 == 0 else "pile"


def level(weights):
    if weights.ndim == 2:
        return weights
    return weights.transpose(1, 0, 2).reshape(weights.shape[1], -1)


def sixteen(share):
    return jnp.pad(share[:, 0, :], ((0, 16 - share.shape[0]), (0, 0)))


def gather_ring(piece):
    shards, device = lax.axis_size("shard"), lax.axis_index("shard")
    wide = piece.shape[1]
    whole = jnp.zeros((piece.shape[0], shards * wide), piece.dtype)
    for i in range(shards):
        came = lax.ppermute(piece, "shard", [(o, (o + i) % shards) for o in range(shards)]) if i else piece
        whole = lax.dynamic_update_slice_in_dim(whole, came, lax.rem(device - i + shards, shards) * wide, 1)
    return whole


def swap_ring(a, x, b, y):
    shards, device = lax.axis_size("shard"), lax.axis_index("shard")
    blocks = grad_blocks(shards, device, a, x, b, y)
    total = blocks[0].astype(F32)
    for i in range(1, shards):
        total = total + lax.ppermute(blocks[i], "shard", [(o, (o + i) % shards) for o in range(shards)]).astype(F32)
    return total[:a.shape[1]], total[a.shape[1]:]


def sum_blocks(blocks):
    return jnp.sum(blocks.astype(F32), axis=0)


def body(tokens, seq_lengths, dealing, gain_mixer, w_query, w_key, w_value, w_gate, w_beta, conv_weight,
         gain_heads, w_out, gain_ffn, w_up_gate, w_up, w_down, cotangent):
    shards = lax.axis_size("shard")
    width = tokens.shape[2]
    col_start = lax.axis_index(GROUP) * width
    per_peer = (CAP // shards + SEQ_DEV + 15) // 16 * 16

    w_piece = jnp.concatenate([w_query, w_key, w_value, w_gate], axis=1)
    b_piece = jnp.pad(w_beta.T, ((0, BETA - w_beta.shape[1]), (0, 0)))

    own_rows = tokens.reshape(REAL_DEV, width)
    taps = conv_weight.reshape(3 * CONV, width)
    head_gain = gain_heads[None, :]

    n = lax.axis_size("head")
    side = side_by_side(w_up.shape[0])
    x_rows, rows_full, sent_slot, recv_slot, pos, filled_f, w_in, w_bt = z_gather(
        n, seq_lengths, dealing, own_rows, per_peer, 1, "gather_rows", shards,
        ("gather", side_by_side(b_piece.shape[1])), (w_piece, b_piece))
    w_bt = level(w_bt)
    rows_full, cot_piece, w_out = lax.optimization_barrier((rows_full, cotangent, w_out))
    w_o = gather_ring(w_out)
    cot_full = full_rows(cot_piece)
    pre, normed, scale_one = project(rows_full, gain_mixer[None, :], w_in, w_bt)
    mixed, *saved = mixer_fwd(pre, pos, filled_f, taps, head_gain)
    branch_part, cot_full = lax.optimization_barrier((mm(mixed, w_o).astype(BF), cot_full))
    hidden, held_full, held_low, w_ug, w_u, w_d = z_turn(
        n, branch_part, x_rows, 2, "turn_branch", shards, (side,) * 3, (w_up_gate.T, w_up.T, w_down))
    w_ug, w_u, w_d = level(w_ug), level(w_u), level(w_d)
    normed_two, product, d_gate, d_up, d_normed_two, scale_two, share_two = ffn(
        held_full, cot_full, gain_ffn[None, :], w_ug, w_u, w_d)
    down_kind, d_w_down = column_blocks(mm(product, cot_full, TN).astype(BF), shards)
    gate_kind, d_w_ug = column_blocks(mm(d_gate, normed_two, TN).astype(BF), shards)
    ffn_gain_part = lax.dynamic_slice_in_dim(gain_ffn, col_start, width)[None, :]
    d_hidden, d_branch_full, _, ffn_gain_grad, d_w_ug, d_w_down = z_turn(
        n, d_normed_two, cotangent, 4, "turn_normed_two", shards, (gate_kind, down_kind), (d_w_ug, d_w_down),
        norm=(held_low, scale_two, ffn_gain_part, sixteen(share_two)))
    out_part = mm(product, w_d).astype(BF)
    out_part, d_branch_full = lax.optimization_barrier((out_part, d_branch_full))
    d_w_u, d_w_out = swap_ring(d_up, normed_two, mixed, d_branch_full)
    out_sum = shares(out_part)
    d_mixed = mm(d_branch_full, w_o, NT)
    d_pre, d_taps, d_head_gain = mixer_bwd(d_mixed, pre, pos, filled_f, taps, head_gain, saved)
    d_normed, share_one = unproject(d_pre, pre, scale_one, w_in, w_bt)
    d_normed, out_sum = lax.optimization_barrier((d_normed, out_sum))
    block_out = (hidden + out_sum).astype(BF)
    mixer_gain_part = lax.dynamic_slice_in_dim(gain_mixer, col_start, width)[None, :]
    small = jnp.concatenate([
        jnp.sum(d_taps, axis=1), jnp.zeros((1, width), F32), jnp.sum(ffn_gain_grad, axis=0)[None, :],
        jnp.pad(jnp.sum(d_head_gain, axis=0), (0, width - HD))[None, :],
        jnp.zeros((1, width), F32)], axis=0)
    d_tokens, summed, d_w_ug, d_w_down, d_w_in, d_w_bt = z_finish(
        n, d_normed, x_rows, scale_one, d_hidden, mixer_gain_part, sixteen(share_one), small,
        sent_slot, recv_slot, per_peer, 6, "finish_rows", shards, normed, d_pre, (d_w_ug, d_w_down))
    d_w_in = sum_blocks(d_w_in)
    by_row = summed.transpose(1, 0, 2).reshape(16, D)
    d_conv = by_row[:12].reshape(CONV, 3, D)
    d_gain_heads = jnp.sum(summed[:, 14, :HD], axis=0)
    cut = [0, width, 2 * width, 3 * width, 4 * width]
    return (
        block_out, d_tokens, by_row[12],
        d_w_in[:, cut[0]:cut[1]], d_w_in[:, cut[1]:cut[2]], d_w_in[:, cut[2]:cut[3]], d_w_in[:, cut[3]:cut[4]],
        sum_blocks(d_w_bt)[:w_beta.shape[1]].T,
        d_conv, d_gain_heads, d_w_out, by_row[13],
        d_w_ug.T, d_w_u.T, d_w_down,
    )


def solution(mesh):
    feat = ("head", "tensor")
    placed = (
        P(None, "shard", feat), P(), P(), P(),
        P("shard", feat), P("shard", feat), P("shard", feat), P("shard", feat), P("shard", feat),
        P(None, None, feat), P(), P(feat, "shard"), P(),
        P("shard", feat), P("shard", feat), P(feat, "shard"), P("shard", feat),
    )
    given = (
        P("shard", feat), P(None, "shard", feat), P(),
        P("shard", feat), P("shard", feat), P("shard", feat), P("shard", feat), P("shard", feat),
        P(), P(), P(feat, "shard"), P(),
        P("shard", feat), P("shard", feat), P(feat, "shard"),
    )
    return jax.shard_map(body, mesh=mesh, in_specs=placed, out_specs=given, check_vma=False)
```
